32 devices in a mesh: dp: 8 (over z, x), seq: 4 (over y, core).
Axes of the slice: x: 2, y: 2, z: 4, core: 2. Of those that a mesh axis runs over, the one named last changes fastest.
Arguments:
- layer_input: bfloat16 [16, 2048, 1024], P('dp', 'seq'), may hold values from -6 to 6
- segment_ids: int32 [16, 2048], P('dp'), may hold values from 0 to 7, never falling along the last dimension, each value on 1 to 1024 neighbouring positions
- gain_attn: bfloat16 [1024], P(('dp', 'seq')), may hold values from 0.5 to 1.5
- w_query: bfloat16 [1024, 256], P(('dp', 'seq')), may hold values from -0.1875 to 0.1875
- w_key: bfloat16 [1024, 256], P(('dp', 'seq')), may hold values from -0.1875 to 0.1875
- w_value: bfloat16 [1024, 1024], P(('dp', 'seq')), may hold values from -0.1875 to 0.1875
- w_out: bfloat16 [1024, 1024], P(('dp', 'seq')), may hold values from -2 to 2
- gain_mlp: bfloat16 [1024], P(('dp', 'seq')), may hold values from 0.5 to 1.5
- w_gate: bfloat16 [1024, 2752], P(('dp', 'seq')), may hold values from -0.1875 to 0.1875
- w_up: bfloat16 [1024, 2752], P(('dp', 'seq')), may hold values from -0.1875 to 0.1875
- w_down: bfloat16 [2752, 1024], P(None, ('dp', 'seq')), may hold values from -0.109375 to 0.109375
- grad_output: bfloat16 [16, 2048, 1024], P('dp', 'seq'), may hold values from -6 to 6
Outputs:
- layer_output: bfloat16 [16, 2048, 1024], P('dp', 'seq')
- grad_input: float32 [16, 2048, 1024], P('dp', 'seq')
- grad_gain_attn: float32 [1024], P(('dp', 'seq'))
- grad_query: float32 [1024, 256], P(('dp', 'seq'))
- grad_key: float32 [1024, 256], P(('dp', 'seq'))
- grad_value: float32 [1024, 1024], P(('dp', 'seq'))
- grad_out: float32 [1024, 1024], P(('dp', 'seq'))
- grad_gain_mlp: float32 [1024], P(('dp', 'seq'))
- grad_gate: float32 [1024, 2752], P(('dp', 'seq'))
- grad_up: float32 [1024, 2752], P(('dp', 'seq'))
- grad_down: float32 [2752, 1024], P(None, ('dp', 'seq'))
The draws below stay inside these ranges and needn't reach their ends.
Inputs may be any that keep to these rules, and one draw needn't show every extreme that they name: `segment_ids`: within each row the ids never fall; each document has 1 to 1024 positions, and one has exactly 1024.
All inputs are finite; a program needn't handle non-finite values.
Results may differ from the reference program's by a relative error of at most 0.0099.
Values may be sent and summed in bfloat16 or wider, within the bound.
No kernel may reach another device: no remote copies, remote signals or barrier semaphores. Data moves between devices by JAX's collectives and lax.ppermute only.
A program may use at most 256 MiB of HBM per device.

```python
import math
import jax
import jax.numpy as jnp
import numpy as np
from jax import lax

D = 1024
HEADS = 16
FEAT = 16
FF = 2752
LEN = 2048
SEGS = 8
NROWS = 16


def shard_levels(key, shape, split, least, largest):
    def one(dim, shards_of):
        steps = jax.random.uniform(jax.random.fold_in(jax.random.fold_in(key, 6), dim), (shards_of,), jnp.float32, least / len(split), largest / len(split))
        return jnp.repeat(jnp.exp(steps), shape[dim] // shards_of).reshape((-1,) + (1,) * (len(shape) - dim - 1))

    factor_of = one(*split[0])
    for cut in split[1:]:
        factor_of = factor_of * one(*cut)
    return factor_of


def split_up(amount, total, limit, slope):
    weights = [(1 << 20) // math.isqrt(standing ** slope) + 1 for standing in range(2, amount + 1)]
    spare, holding = total - limit - (amount - 1), [1] * (amount - 1)
    while spare > 0:
        candidates = [i for i in range(amount - 1) if holding[i] < limit]
        pool, remaining = sum([weights[i] for i in candidates]), spare
        for i in candidates:
            extra = min(limit - holding[i], max(1, remaining * weights[i] // pool), spare)
            holding[i] = holding[i] + extra
            spare = spare - extra
    return np.array([limit] + holding)


def ragged_sizes(key, amount, total, bound, lean):
    if amount == 2:
        one = jax.random.randint(key, (), max(1, total - bound), min(bound, total - 1) + 1)
        return jnp.stack([one, total - one])
    lengths = jnp.asarray(split_up(amount, total, bound, lean), jnp.int32)
    couples = (amount - 1) // 2
    giver, taker = lengths[1:1 + 2 * couples:2], lengths[2:2 + 2 * couples:2]
    margin = jnp.minimum(giver - 1, bound - taker)
    passed = jax.random.randint(jax.random.fold_in(key, 1), (couples,), 0, 1 << 20) % (margin + 1)
    lengths = lengths.at[1:1 + 2 * couples:2].set(giver - passed).at[2:2 + 2 * couples:2].set(taker + passed)
    return lengths[jax.random.permutation(jax.random.fold_in(key, 2), amount)]


def normal_values(own_key, shape, deviation, bound, pieces=(), dtype=jnp.bfloat16):
    factor_of = shard_levels(own_key, shape, pieces, -0.22, 0.18) if pieces else 1.0
    drawn = jax.random.normal(own_key, shape, jnp.float32) * deviation * factor_of
    return jnp.minimum(jnp.maximum(drawn, -bound), bound).astype(dtype)


def setup_inputs(seed: int = 0) -> dict:
    splits = jax.random.split(jax.random.key(seed), 13)
    return {
        "layer_input": normal_values(splits[0], (NROWS, LEN, D), 1.0, 6.0, ((0, 8), (1, 4))),
        "segment_ids": jax.vmap(lambda own: jnp.searchsorted(jnp.cumsum(ragged_sizes(own, SEGS, LEN, LEN // 2, 1)), jnp.arange(LEN), side="right"))(jax.random.split(splits[1], NROWS)).reshape((NROWS, LEN)).astype(jnp.int32),
        "gain_attn": jnp.clip(1.0 + 0.1 * jax.random.normal(splits[2], (D,), jnp.float32), 0.5, 1.5).astype(jnp.bfloat16),
        "w_query": normal_values(splits[3], (D, HEADS * FEAT), D ** -0.5, 0.1875, ((0, 32),)),
        "w_key": normal_values(splits[4], (D, HEADS * FEAT), D ** -0.5, 0.1875, ((0, 32),)),
        "w_value": normal_values(splits[5], (D, D), D ** -0.5, 0.1875, ((0, 32),)),
        "w_out": normal_values(splits[6], (D, D), (D // 128) ** -0.5, 2.0, ((0, 32),)),
        "gain_mlp": jnp.clip(1.0 + 0.1 * jax.random.normal(splits[7], (D,), jnp.float32), 0.5, 1.5).astype(jnp.bfloat16),
        "w_gate": normal_values(splits[8], (D, FF), D ** -0.5, 0.1875, ((0, 32),)),
        "w_up": normal_values(splits[9], (D, FF), D ** -0.5, 0.1875, ((0, 32),)),
        "w_down": normal_values(splits[10], (FF, D), FF ** -0.5, 0.109375, ((1, 32),)),
        "grad_output": normal_values(splits[11], (NROWS, LEN, D), 1.0, 6.0, ((0, 8), (1, 4))),
    }


@jax.custom_vjp
def low(v):
    return lax.optimization_barrier(v.astype(jnp.bfloat16)).astype(jnp.float32)

@jax.custom_vjp
def low_back(v):
    return v

def low_keep(v):
    return (low(v), None)

def low_pass(kept, grad):
    return (grad,)

def back_keep(v):
    return (v, None)

def back_low(kept, grad):
    return (low(grad),)
low.defvjp(low_keep, low_pass)
low_back.defvjp(back_keep, back_low)
maximum_precision = lax.Precision.HIGHEST

def rms_norm(value, gain):
    return value * lax.rsqrt(lax.optimization_barrier(jnp.mean(value * value, axis=-1, keepdims=True)) + 1e-05) * gain

def mix_head(query_rows, key_rows, values, segments):
    scores = jnp.dot(query_rows, key_rows.T, precision=maximum_precision) * FEAT ** (-0.5)
    places = jnp.arange(LEN)
    kept_mask = (places[:, None] >= places[None, :]) & (segments[:, None] == segments[None, :])
    weights = jnp.where(kept_mask, 1.0 + scores + 0.5 * scores * scores, 0.0)
    numerator = jnp.dot(weights, values, precision=maximum_precision)
    denominator = lax.optimization_barrier(jnp.sum(weights, axis=1, keepdims=True))
    return numerator / denominator

def layer(xf, gain_attn, w_query, w_key, w_value, w_out, gain_mlp, w_gate, w_up, w_down, segments):
    a_one = low(rms_norm(xf, gain_attn))
    query_rows = low_back(low(jnp.dot(a_one, w_query, precision=maximum_precision)))
    key_rows = low_back(low(jnp.dot(a_one, w_key, precision=maximum_precision)))
    values = low_back(low(jnp.dot(a_one, w_value, precision=maximum_precision)))
    query_rows = query_rows.reshape(LEN, HEADS, FEAT).transpose(1, 0, 2)
    key_rows = key_rows.reshape(LEN, HEADS, FEAT).transpose(1, 0, 2)
    values = values.reshape(LEN, HEADS, D // HEADS).transpose(1, 0, 2)
    per_head = jax.checkpoint(lambda triple: mix_head(triple[0], triple[1], triple[2], segments))
    mixed = lax.map(per_head, (query_rows, key_rows, values))
    mixed = low_back(low(mixed.transpose(1, 0, 2).reshape(LEN, D)))
    branch = low_back(jnp.dot(mixed, w_out, precision=maximum_precision))
    x_two = xf + branch
    a_two = low(rms_norm(x_two, gain_mlp))
    gate = low_back(jnp.dot(a_two, w_gate, precision=maximum_precision))
    up_values = low_back(jnp.dot(a_two, w_up, precision=maximum_precision))
    hidden = low(jax.nn.silu(gate) * up_values)
    return x_two + jnp.dot(hidden, w_down, precision=maximum_precision)

def reference(layer_input, segment_ids, gain_attn, w_query, w_key, w_value, w_out, gain_mlp, w_gate, w_up, w_down, grad_output):
    weights_f = tuple((p.astype(jnp.float32) for p in (gain_attn, w_query, w_key, w_value, w_out, gain_mlp, w_gate, w_up, w_down)))

    def one_row(totals, triple):
        row_input, segments, cotangent = triple

        def forward(xf, *weights):
            return layer(xf, *weights, segments)
        result, pullback = jax.vjp(forward, row_input.astype(jnp.float32), *weights_f)
        gradients = pullback(cotangent.astype(jnp.float32))
        totals = tuple((t + g for t, g in zip(totals, gradients[1:])))
        return (totals, (result.astype(jnp.bfloat16), gradients[0]))
    begin_position = tuple((jnp.zeros_like(p) for p in weights_f))
    totals, (outputs, d_inputs) = lax.scan(one_row, begin_position, (layer_input, segment_ids, grad_output))
    return (outputs, d_inputs, totals[0], totals[1], totals[2], totals[3], totals[4], totals[5], totals[6], totals[7], totals[8])
```

```python
import functools

import jax
import jax.numpy as jnp
import numpy as np
from jax import lax
from jax.experimental import pallas as pl
from jax.experimental.pallas import tpu as pltpu
from jax.sharding import PartitionSpec as P

HEADS = 16
FEAT = 16
LEN = 2048
BLOCK = 512


epsilon = 1e-05
maximum_precision = lax.Precision.HIGHEST


def across_rows(left, right):
    return lax.dot_general(
        left, right, (((0,), (0,)), ((), ())), preferred_element_type=jnp.float32
    )


def against(left, matrix):
    return lax.dot_general(
        left, matrix, (((1,), (1,)), ((), ())), preferred_element_type=jnp.float32
    )


def split_packed(packed):
    query_rows = packed[..., :FEAT]
    key_rows = packed[..., FEAT : 2 * FEAT]
    values = packed[..., 2 * FEAT :].astype(jnp.float32)
    return (query_rows, key_rows, values)


def block_terms(query_rows, key_rows, segments, begin_position):
    stop_position = begin_position + BLOCK
    scores = jnp.einsum(
        "pyg,jyg->ypj",
        query_rows[begin_position:stop_position],
        key_rows[:stop_position],
        preferred_element_type=jnp.float32,
    ) * FEAT ** (-0.5)
    q_places = begin_position + jnp.arange(BLOCK)
    k_places = jnp.arange(stop_position)
    kept_mask = (q_places[:, None] >= k_places[None, :]) & (
        segments[begin_position:stop_position][:, None] == segments[:stop_position][None, :]
    )
    weights = jnp.where(kept_mask[None], 1.0 + scores + 0.5 * scores * scores, 0.0)
    return (scores, kept_mask[None], weights)


def attend_row(pair):
    packed, segments = pair
    query_rows, key_rows, values = split_packed(packed)
    mixed_parts = []
    denom_parts = []
    for begin_position in range(0, LEN, BLOCK):
        scores, kept_mask, weights = block_terms(query_rows, key_rows, segments, begin_position)
        numerator = jnp.einsum(
            "hqk,khc->qhc", weights, values[: begin_position + BLOCK], precision=maximum_precision
        )
        denominator = jnp.sum(weights, axis=2).T
        mixed_parts.append(numerator / denominator[:, :, None])
        denom_parts.append(denominator)
    return (jnp.concatenate(mixed_parts, 0), jnp.concatenate(denom_parts, 0))


def attend_back(bundle):
    packed, segments, mixed, denominator, d_mixed = bundle
    query_rows, key_rows, values = split_packed(packed)
    complete_query_rows = query_rows.astype(jnp.float32)
    complete_key_rows = key_rows.astype(jnp.float32)
    d_mixed = d_mixed.astype(jnp.float32)
    d_numer = d_mixed / denominator[:, :, None]
    d_denom = -jnp.sum(d_mixed * mixed, axis=2) / denominator
    d_query_parts = []
    d_keys = jnp.zeros_like(complete_key_rows)
    d_values = jnp.zeros_like(values)
    for begin_position in range(0, LEN, BLOCK):
        stop_position = begin_position + BLOCK
        scores, kept_mask, weights = block_terms(query_rows, key_rows, segments, begin_position)
        d_weights = jnp.einsum(
            "qhc,khc->hqk",
            d_numer[begin_position:stop_position],
            values[:stop_position],
            precision=maximum_precision,
        )
        d_weights = jnp.where(
            kept_mask, d_weights + d_denom[begin_position:stop_position].T[:, :, None], 0.0
        )
        d_values = d_values.at[:stop_position].add(
            jnp.einsum(
                "hqk,qhc->khc",
                weights,
                d_numer[begin_position:stop_position],
                precision=maximum_precision,
            )
        )
        score_gradient = d_weights * (1.0 + scores) * FEAT ** (-0.5)
        d_query_parts.append(
            jnp.einsum(
                "ouw,wor->uor",
                score_gradient,
                complete_key_rows[:stop_position],
                precision=maximum_precision,
            )
        )
        d_keys = d_keys.at[:stop_position].add(
            jnp.einsum(
                "urs,ruw->suw",
                score_gradient,
                complete_query_rows[begin_position:stop_position],
                precision=maximum_precision,
            )
        )
    d_query = jnp.concatenate(d_query_parts, 0)
    return jnp.concatenate([d_query, d_keys, d_values], axis=2).astype(jnp.bfloat16)


def norm_forward(values):
    scale = lax.rsqrt(jnp.mean(values * values, axis=1, keepdims=True) + epsilon)
    return (scale, values * scale)


def norm_backward(d_scaled, gain, scale, normed):
    d_normed = d_scaled * gain
    return scale * (d_normed - normed * jnp.mean(d_normed * normed, axis=1, keepdims=True))


def fold(count):
    return [0] + list(range(1, count, 2)) + list(range(2, count, 2))[::-1]


class Line:
    def __init__(self, axis, axis_size, stride, count):
        self.axis, self.stride, self.count = axis, stride, count
        self.order = fold(count)
        self.pairs = []
        for index in range(axis_size):
            place = (index // stride) % count
            ring = self.order.index(place)
            goal = self.order[(ring + 1) % count]
            self.pairs.append((index, index + (goal - place) * stride))

    def send(self, array):
        return lax.ppermute(array, self.axis, self.pairs)

    def place_back(self, steps):
        own = (lax.axis_index(self.axis) // self.stride) % self.count
        rank = jnp.asarray([self.order.index(p) for p in range(self.count)], jnp.int32)[own]
        return jnp.asarray(self.order, jnp.int32)[(rank - steps) % self.count]


class Slice:
    def __init__(self, dp, seq):
        self.dp, self.seq, self.devices = dp, seq, dp * seq
        self.lines = {
            "z": Line("dp", dp, 2, dp // 2),
            "x": Line("dp", dp, 1, 2),
            "y": Line("seq", seq, 2, seq // 2),
            "c": Line("seq", seq, 1, 2),
        }

    def device_of(self, back):
        at = {d: self.lines[d].place_back(back[d]) for d in "zxyc"}
        return ((at["z"] * 2 + at["x"]) * (self.seq // 2) + at["y"]) * 2 + at["c"]


def assemble(pieces, places, block, devices):
    columns = pieces[0].shape[1]
    counts = [piece.shape[0] // block for piece in pieces]

    def kernel(places_ref, *refs):
        piece_refs, out_ref, held, in_sems, out_sems = (
            refs[: len(pieces)],
            *refs[len(pieces) :],
        )
        loads, begin = [], 0
        for number, piece_ref in enumerate(piece_refs):
            rows = counts[number] * block
            load = pltpu.make_async_copy(
                piece_ref, held.at[pl.ds(begin * block, rows)], in_sems.at[number]
            )
            load.start()
            loads.append(load)
            begin += counts[number]
        stores, begin = [], 0
        for number, load in enumerate(loads):
            load.wait()
            for i in range(begin, begin + counts[number]):
                to = pl.multiple_of(places_ref[i] * block, block)
                store = pltpu.make_async_copy(
                    held.at[pl.ds(i * block, block)], out_ref.at[pl.ds(to, block)], out_sems.at[i]
                )
                store.start()
                stores.append(store)
            begin += counts[number]
        for store in stores:
            store.wait()

    size = devices * block * columns * pieces[0].dtype.itemsize
    return pl.pallas_call(
        kernel,
        out_shape=jax.ShapeDtypeStruct((devices * block, columns), pieces[0].dtype),
        in_specs=[pl.BlockSpec(memory_space=pltpu.SMEM)]
        + [pl.BlockSpec(memory_space=pl.ANY)] * len(pieces),
        out_specs=pl.BlockSpec(memory_space=pl.ANY),
        scratch_shapes=[
            pltpu.VMEM((devices * block, columns), pieces[0].dtype),
            pltpu.SemaphoreType.DMA((len(pieces),)),
            pltpu.SemaphoreType.DMA((devices,)),
        ],
        cost_estimate=pl.CostEstimate(flops=0, bytes_accessed=2 * size, transcendentals=0),
        name="assemble",
    )(places, *pieces)


def gather_rows(part, shape, route):
    block, columns = part.shape
    if block % 16:
        return lax.all_gather(part, ("dp", "seq"), axis=0, tiled=True)
    held = [(part, [dict(z=0, x=0, y=0, c=0)])]
    for dim in route:
        if len(held) > 1 and sum(len(names) for _, names in held) <= 4:
            held = [
                (jnp.concatenate([a for a, _ in held], 0), [n for _, names in held for n in names])
            ]
        came = []
        for array, names in held:
            for step in range(1, shape.lines[dim].count):
                array = shape.lines[dim].send(array)
                came.append((array, [dict(n, **{dim: step}) for n in names]))
        held = held + came
    places = jnp.stack([shape.device_of(n) for _, names in held for n in names])
    return assemble([a for a, _ in held], places, block, shape.devices)


def column_order(shape, width, route):
    block = width // shape.devices
    names = [dict()]
    for dim in route:
        names = [dict(n, **{dim: s}) for n in names for s in range(shape.lines[dim].count)]
    places = jnp.stack([shape.device_of(n) for n in names])
    return (places[:, None] * block + jnp.arange(block)[None, :]).reshape(width)


def reorder(left, order):
    width = left.shape[1]
    pick = (jnp.arange(width)[:, None] == order[None, :]).astype(jnp.bfloat16)
    return jnp.dot(left, pick, preferred_element_type=jnp.float32).astype(jnp.bfloat16)


def scatter_rows(left, right, shape, route):
    width = left.shape[1]
    if (width // shape.devices) % 16:
        return lax.psum_scatter(
            across_rows(left, right), ("dp", "seq"), scatter_dimension=0, tiled=True
        )
    left = reorder(left, column_order(shape, width, route))
    first, second = (shape.lines[d] for d in route[:2])
    half = width // first.count
    came = None
    for step in range(1, first.count):
        term = across_rows(left[:, step * half : (step + 1) * half], right)
        term = term if came is None else term + came.astype(jnp.float32)
        came = first.send(term.astype(jnp.bfloat16))
    rows = half // second.count
    arrived, came = came, None

    def term_of(step):
        low, high = step * rows, (step + 1) * rows
        return across_rows(left[:, low:high], right) + arrived[low:high].astype(jnp.float32)

    for step in range(1, second.count):
        term = term_of(step)
        term = term if came is None else term + came.astype(jnp.float32)
        came = second.send(term.astype(jnp.bfloat16))
    total = term_of(0) + came.astype(jnp.float32)
    for dim in route[2:]:
        line = shape.lines[dim]
        rows = total.shape[0] // line.count
        came = None
        for step in range(1, line.count):
            term = total[step * rows : (step + 1) * rows]
            term = term if came is None else term + came.astype(jnp.float32)
            came = line.send(term.astype(jnp.bfloat16))
        total = total[:rows] + came.astype(jnp.float32)
    return total


def gain_gradient(weights, gradients, gain):
    products = jnp.sum(weights.astype(jnp.float32) * gradients, axis=1)
    return products / gain.astype(jnp.float32)


def per_device(
    shape,
    layer_input,
    segment_ids,
    gain_attn,
    w_query,
    w_key,
    w_value,
    w_out,
    gain_mlp,
    w_gate,
    w_up,
    w_down,
    grad_output,
):
    rows, shard_len, width = layer_input.shape
    count = rows * shard_len
    value_dim = width // HEADS
    features = HEADS * FEAT
    qkv_part = jnp.concatenate([w_query, w_key, w_value], axis=1)
    down_part = w_down.T
    gains = jnp.stack([gain_attn, gain_mlp], axis=1)
    gains = jnp.pad(gains, ((0, 0), (0, 126)))
    head = gather_rows(jnp.concatenate([qkv_part, gains], axis=1), shape, "zxyc")
    qkv_w = head[:, : 2 * features + width]
    gain_one = head[:, 2 * features + width].astype(jnp.float32)
    gain_two = head[:, 2 * features + width + 1].astype(jnp.float32)
    out_w = gather_rows(w_out, shape, "xyzc")
    gate_w = gather_rows(w_gate, shape, "zxyc")
    up_w = gather_rows(w_up, shape, "zyxc")
    down_w = gather_rows(down_part, shape, "xyzc")

    tokens = layer_input.reshape(count, width).astype(jnp.float32)
    scale_one, normed_one = norm_forward(tokens)
    a_one = (normed_one * gain_one).astype(jnp.bfloat16)
    qkv = jnp.dot(a_one, qkv_w, preferred_element_type=jnp.float32).astype(jnp.bfloat16)
    packed = jnp.concatenate(
        [
            qkv[:, :features].reshape(rows, shard_len, HEADS, FEAT),
            qkv[:, features : 2 * features].reshape(rows, shard_len, HEADS, FEAT),
            qkv[:, 2 * features :].reshape(rows, shard_len, HEADS, value_dim),
        ],
        axis=3,
    )
    by_heads = lax.all_to_all(packed, "seq", split_axis=2, concat_axis=1, tiled=True)
    mixed, denominator = lax.map(attend_row, (by_heads, segment_ids))
    mixed_seq = lax.all_to_all(
        mixed.astype(jnp.bfloat16), "seq", split_axis=1, concat_axis=2, tiled=True
    )
    mixed_cat = mixed_seq.reshape(count, width)
    x_two = tokens + jnp.dot(mixed_cat, out_w, preferred_element_type=jnp.float32)
    scale_two, normed_two = norm_forward(x_two)
    a_two = (normed_two * gain_two).astype(jnp.bfloat16)
    gate = jnp.dot(a_two, gate_w, preferred_element_type=jnp.float32)
    up_values = jnp.dot(a_two, up_w, preferred_element_type=jnp.float32)
    sigma = jax.nn.sigmoid(gate)
    silu_gate = gate * sigma
    hidden = (silu_gate * up_values).astype(jnp.bfloat16)
    result = (x_two + against(hidden, down_w)).astype(jnp.bfloat16)

    cotangent = grad_output.reshape(count, width)
    grad_down = scatter_rows(cotangent, hidden, shape, "czxy")
    d_hidden = jnp.dot(cotangent, down_w, preferred_element_type=jnp.float32)
    d_gate = (d_hidden * up_values * sigma * (1.0 + gate * (1.0 - sigma))).astype(jnp.bfloat16)
    d_up = (d_hidden * silu_gate).astype(jnp.bfloat16)
    grad_gate = scatter_rows(a_two, d_gate, shape, "cyxz")
    grad_up = scatter_rows(a_two, d_up, shape, "cxyz")
    d_a_two = against(d_gate, gate_w) + against(d_up, up_w)
    d_x_two = cotangent.astype(jnp.float32) + norm_backward(
        d_a_two, gain_two, scale_two, normed_two
    )
    d_branch = d_x_two.astype(jnp.bfloat16)
    grad_out = scatter_rows(mixed_cat, d_branch, shape, "cxyz")
    d_mixed = (
        against(d_branch, out_w).astype(jnp.bfloat16).reshape(rows, shard_len, HEADS, value_dim)
    )
    d_mixed_heads = lax.all_to_all(d_mixed, "seq", split_axis=2, concat_axis=1, tiled=True)
    d_packed = lax.map(attend_back, (by_heads, segment_ids, mixed, denominator, d_mixed_heads))
    d_packed_seq = lax.all_to_all(d_packed, "seq", split_axis=1, concat_axis=2, tiled=True)
    d_qkv = jnp.concatenate(
        [
            d_packed_seq[..., :FEAT].reshape(count, features),
            d_packed_seq[..., FEAT : 2 * FEAT].reshape(count, features),
            d_packed_seq[..., 2 * FEAT :].reshape(count, width),
        ],
        axis=1,
    )
    grad_qkv = scatter_rows(a_one, d_qkv, shape, "cyxz")
    d_a_one = against(d_qkv, qkv_w)
    d_tokens = d_x_two + norm_backward(d_a_one, gain_one, scale_one, normed_one)
    return (
        result.reshape(rows, shard_len, width),
        d_tokens.reshape(rows, shard_len, width),
        gain_gradient(qkv_part, grad_qkv, gain_attn),
        grad_qkv[:, :features],
        grad_qkv[:, features : 2 * features],
        grad_qkv[:, 2 * features :],
        grad_out,
        gain_gradient(
            jnp.concatenate([w_gate, w_up], axis=1),
            jnp.concatenate([grad_gate, grad_up], axis=1),
            gain_mlp,
        ),
        grad_gate,
        grad_up,
        grad_down.T,
    )


def solution(mesh):
    placed = (
        P("dp", "seq", None),
        P("dp", None),
        P(("dp", "seq")),
        P(("dp", "seq"), None),
        P(("dp", "seq"), None),
        P(("dp", "seq"), None),
        P(("dp", "seq"), None),
        P(("dp", "seq")),
        P(("dp", "seq"), None),
        P(("dp", "seq"), None),
        P(None, ("dp", "seq")),
        P("dp", "seq", None),
    )
    return jax.shard_map(
        functools.partial(per_device, Slice(mesh.shape["dp"], mesh.shape["seq"])),
        mesh=mesh,
        in_specs=placed,
        out_specs=(
            P("dp", "seq", None),
            P("dp", "seq", None),
            P(("dp", "seq")),
            P(("dp", "seq"), None),
            P(("dp", "seq"), None),
            P(("dp", "seq"), None),
            P(("dp", "seq"), None),
            P(("dp", "seq")),
            P(("dp", "seq"), None),
            P(("dp", "seq"), None),
            P(None, ("dp", "seq")),
        ),
        check_vma=False,
    )
```

```python
import functools

import jax
import jax.numpy as jnp
import numpy as np
from jax import lax
from jax.experimental import pallas as pl
from jax.experimental.pallas import tpu as pltpu
from jax.sharding import PartitionSpec as P

LONGEST = 1024
HEADS = 16
FEAT = 16
LANES = 128
GROUP = LANES // FEAT
PIECES = FEAT // 2 + 2
WIDE = PIECES * LANES


def dot(left, right, dims=((1,), (0,))):
    return lax.dot_general(left, right, (dims, ((), ())), preferred_element_type=jnp.float32)


def rolls(scaled):
    table = np.zeros((LANES, WIDE), np.float32)
    for d in range(FEAT // 2 + 1):
        factor = (1 / 32 if d == 0 else 1 / 16) if scaled else 1.0
        for lane in range(LANES):
            head, a = divmod(lane, FEAT)
            if d < FEAT // 2 or a < FEAT // 2:
                table[head * FEAT + (a + d) % FEAT, (d + 1) * LANES + lane] = factor
    return table


def piece_of(number, rows, factors, lin, axis):
    if number == 0:
        return rows.astype(jnp.float32) * lin
    products = rows.astype(jnp.float32) * factors
    if number < PIECES - 1:
        return products
    place = lax.broadcasted_iota(jnp.int32, products.shape, axis)
    return jnp.where(place % FEAT == FEAT // 2, 1.0, products)


def head_mask(lanes_per_head, first_head, shape):
    row_head = lax.broadcasted_iota(jnp.int32, shape, 0) // FEAT
    lane_head = lax.broadcasted_iota(jnp.int32, shape, 1) // lanes_per_head + first_head
    return row_head == lane_head


def fold_heads(full, value_dim):
    per = LANES // value_dim
    total = None
    for part in range(full.shape[1] // LANES):
        piece = full[:, part * LANES : (part + 1) * LANES]
        piece = jnp.where(head_mask(value_dim, part * per, piece.shape), piece, 0.0)
        total = piece if total is None else total + piece
    return total + pltpu.roll(total, value_dim, 1)


def halves(state):
    state = state.astype(jnp.float32)
    turned = pltpu.roll(state, LANES // 2, 1)
    low = lax.broadcasted_iota(jnp.int32, state.shape, 1) < LANES // 2
    return jnp.where(low, state, turned), jnp.where(low, turned, state)


def spread_heads(values, value_dim, width):
    per = LANES // value_dim
    return jnp.concatenate(
        [
            jnp.where(head_mask(value_dim, part * per, values.shape), values, 0.0)
            for part in range(width // LANES)
        ],
        axis=1,
    )


def turned(block):
    return block.astype(jnp.float32).T.astype(jnp.bfloat16)


def tail_kernel(value_dim, k_ref, v_ref, seg_ref, pick_ref, out_ref):
    seg = seg_ref[...]
    last = seg[-1:, :]
    keep = (seg == last).astype(jnp.float32)
    values = (v_ref[...].astype(jnp.float32) * keep).astype(jnp.bfloat16)
    ones = jnp.broadcast_to(keep, (seg.shape[0], LANES)).astype(jnp.bfloat16)
    keys = turned(k_ref[...])
    low = lax.broadcasted_iota(jnp.int32, (LANES, LANES), 1) < value_dim
    for number in range(PIECES):
        span = slice(number * LANES, (number + 1) * LANES)
        factors = dot(pick_ref[span, :], keys) if number else None
        piece = piece_of(number, keys, factors, 1.0, 0).astype(jnp.bfloat16)
        folded = fold_heads(dot(piece, values), value_dim)
        out_ref[0, 0, span, :] = jnp.where(low, folded, dot(piece, ones)).astype(out_ref.dtype)


def masks_of(seg_ref, seg_row_ref, begin, block):
    stop = begin + block
    rows = begin + lax.broadcasted_iota(jnp.int32, (block, stop), 0)
    columns = lax.broadcasted_iota(jnp.int32, (block, stop), 1)
    same = seg_ref[begin:stop, :] == seg_row_ref[0, :, :stop]
    return ((rows >= columns) & same).astype(jnp.float32)


def own_lanes(array, lanes_per_head, head):
    place = lax.broadcasted_iota(jnp.int32, array.shape, 1) // lanes_per_head
    return jnp.where(place == head, array, jnp.zeros_like(array))


def near_kernel(value_dim, block, q_ref, k_ref, v_ref, seg_ref, seg_row_ref, top_ref, den_ref):
    length = q_ref.shape[0]
    per = LANES // value_dim
    low = lax.broadcasted_iota(jnp.int32, (block, LANES), 1) < value_dim
    for begin in range(0, length, block):
        stop = begin + block
        mask = masks_of(seg_ref, seg_row_ref, begin, block)
        queries = q_ref[begin:stop, :] * jnp.bfloat16(FEAT ** (-0.5))
        keys = k_ref[:stop, :]
        ones = jnp.ones((stop, LANES), jnp.bfloat16)
        for pair in range(GROUP // per):
            span = slice(pair * LANES, (pair + 1) * LANES)
            values = jnp.concatenate([v_ref[:stop, span], ones], axis=1)
            sides = []
            for side in range(per):
                scores = dot(
                    own_lanes(queries, FEAT, pair * per + side), keys, ((1,), (1,))
                )
                weights = (((0.5 * scores + 1.0) * scores + 1.0) * mask).astype(jnp.bfloat16)
                sides.append(dot(weights, values))
            top_ref[begin:stop, span] = jnp.where(low, sides[0][:, :LANES], sides[1][:, :LANES])
            den_ref[begin:stop, span] = jnp.where(low, sides[0][:, LANES:], sides[1][:, LANES:])


def features(rows, pick_ref, lin):
    pieces = []
    for number in range(PIECES):
        span = slice(number * LANES, (number + 1) * LANES)
        factors = dot(rows, pick_ref[:, span]) if number else None
        pieces.append(piece_of(number, rows, factors, lin, 1).astype(jnp.bfloat16))
    return jnp.concatenate(pieces, axis=1)


def far_kernel(
    value_dim, q_ref, seg_ref, state_ref, top_ref, den_ref, pick_ref, y_ref, inverse_ref,
    values_ref, sums_ref,
):
    width = top_ref.shape[1]
    for number in range(PIECES):
        span = slice(number * LANES, (number + 1) * LANES)
        values, sums = halves(state_ref[0, 0, span, :])
        values_ref[span, :] = spread_heads(values, value_dim, width).astype(jnp.bfloat16)
        sums_ref[span, :] = spread_heads(sums, value_dim, width).astype(jnp.bfloat16)
    seg = seg_ref[...]
    keep = (seg == seg[:1, :]).astype(jnp.float32)
    phi = features(q_ref[...], pick_ref, FEAT ** (-0.5))
    top = top_ref[...] + keep * dot(phi, values_ref[...])
    inverse = 1.0 / (den_ref[...] + keep * dot(phi, sums_ref[...]))
    y_ref[...] = (top * inverse).astype(y_ref.dtype)
    inverse_ref[...] = inverse


def lane_sums(product, value_dim, side):
    place = lax.broadcasted_iota(jnp.int32, product.shape, 1) // value_dim
    return jnp.sum(jnp.where(place == side, product, 0.0), axis=1, keepdims=True)


def d_den_of(pair, value_dim, dy_ref, y_ref, inverse_ref):
    span = slice(pair * LANES, (pair + 1) * LANES)
    product = dy_ref[:, span].astype(jnp.float32) * y_ref[:, span].astype(jnp.float32)
    product = product * inverse_ref[:, span]
    return [-lane_sums(product, value_dim, side) for side in range(LANES // value_dim)]


def d_den_lanes(value_dim, dy_ref, y_ref, inverse_ref):
    per = LANES // value_dim
    shape = (dy_ref.shape[0], LANES)
    place = lax.broadcasted_iota(jnp.int32, shape, 1) // FEAT
    total = jnp.zeros(shape, jnp.float32)
    for pair in range(GROUP // per):
        for side, column in enumerate(d_den_of(pair, value_dim, dy_ref, y_ref, inverse_ref)):
            total = jnp.where(place == pair * per + side, column, total)
    return total


def head_kernel(
    value_dim, q_ref, dy_ref, y_ref, inverse_ref, seg_ref, pick_ref, out_ref
):
    seg = seg_ref[...]
    keep = (seg == seg[:1, :]).astype(jnp.float32)
    d_top = (dy_ref[...].astype(jnp.float32) * inverse_ref[...] * keep).astype(jnp.bfloat16)
    d_den = (d_den_lanes(value_dim, dy_ref, y_ref, inverse_ref) * keep).astype(jnp.bfloat16)
    queries = turned(q_ref[...])
    low = lax.broadcasted_iota(jnp.int32, (LANES, LANES), 1) < value_dim
    for number in range(PIECES):
        span = slice(number * LANES, (number + 1) * LANES)
        factors = dot(pick_ref[span, :], queries) if number else None
        piece = piece_of(number, queries, factors, FEAT ** (-0.5), 0).astype(jnp.bfloat16)
        folded = fold_heads(dot(piece, d_top), value_dim)
        sums = jnp.where(head_mask(FEAT, 0, (LANES, LANES)), dot(piece, d_den), 0.0)
        sums = jnp.sum(sums, axis=1, keepdims=True) * (1 / FEAT)
        out_ref[0, 0, span, :] = jnp.where(low, folded, sums).astype(out_ref.dtype)


def from_features(d_phi, rows, pick_ref, lin):
    total = d_phi[:, :LANES] * lin
    x = rows.astype(jnp.float32)
    scaled = []
    for number in range(1, PIECES):
        span = slice(number * LANES, (number + 1) * LANES)
        total = total + d_phi[:, span] * dot(rows, pick_ref[:, span])
        scaled.append((d_phi[:, span] * x).astype(jnp.bfloat16))
    return total + dot(jnp.concatenate(scaled, axis=1), pick_ref[:, LANES:], ((1,), (1,)))


def near_back_kernel(
    value_dim, block, q_ref, k_ref, v_ref, dy_ref, y_ref, inverse_ref, seg_ref, seg_row_ref,
    state_ref, pick_ref, dq_ref, dk_ref, dv_ref, values_ref, sums_ref, dq_sum,
):
    length, width = dy_ref.shape
    per = LANES // value_dim
    seg = seg_ref[...]
    keep = (seg == seg[:1, :]).astype(jnp.float32)
    for number in range(PIECES):
        span = slice(number * LANES, (number + 1) * LANES)
        values, sums = halves(state_ref[0, 0, span, :])
        values_ref[span, :] = spread_heads(values, value_dim, width).astype(jnp.bfloat16)
        sums = jnp.where(head_mask(FEAT, 0, sums.shape), sums, 0.0) * (1 / FEAT)
        sums_ref[span, :] = sums.astype(jnp.bfloat16)
    d_top = (dy_ref[...].astype(jnp.float32) * inverse_ref[...] * keep).astype(jnp.bfloat16)
    d_den = (d_den_lanes(value_dim, dy_ref, y_ref, inverse_ref) * keep).astype(jnp.bfloat16)
    d_phi = dot(d_top, values_ref[...], ((1,), (1,))) + dot(d_den, sums_ref[...], ((1,), (1,)))
    dq_sum[...] = from_features(d_phi, q_ref[...], pick_ref, FEAT ** (-0.5))
    dk_ref[...] = jnp.zeros_like(dk_ref)
    dv_ref[...] = jnp.zeros_like(dv_ref)
    for begin in range(0, length, block):
        stop = begin + block
        mask = masks_of(seg_ref, seg_row_ref, begin, block)
        queries = q_ref[begin:stop, :] * jnp.bfloat16(FEAT ** (-0.5))
        keys = k_ref[:stop, :] * jnp.bfloat16(FEAT ** (-0.5))
        for pair in range(GROUP // per):
            span = slice(pair * LANES, (pair + 1) * LANES)
            d_mixed = dy_ref[begin:stop, span].astype(jnp.float32)
            inverse = inverse_ref[begin:stop, span]
            d_numer = (d_mixed * inverse).astype(jnp.bfloat16)
            product = d_mixed * inverse * y_ref[begin:stop, span].astype(jnp.float32)
            values = v_ref[:stop, span]
            for side in range(per):
                head = pair * per + side
                own_q = own_lanes(queries, FEAT, head)
                own_dn = own_lanes(d_numer, value_dim, side)
                scores = dot(own_q, k_ref[:stop, :], ((1,), (1,)))
                weights = (((0.5 * scores + 1.0) * scores + 1.0) * mask).astype(jnp.bfloat16)
                d_weights = dot(own_dn, values, ((1,), (1,))) - lane_sums(product, value_dim, side)
                d_scores = (d_weights * ((scores + 1.0) * mask)).astype(jnp.bfloat16)
                dv_ref[:stop, span] += dot(weights, own_dn, ((0,), (0,)))
                dq_sum[begin:stop, :] += dot(d_scores, own_lanes(keys, FEAT, head))
                dk_ref[:stop, :] += dot(d_scores, own_q, ((0,), (0,)))
    dq_ref[...] = dq_sum[...].astype(dq_ref.dtype)


def far_back_kernel(
    value_dim, k_ref, v_ref, seg_ref, state_ref, dk_in_ref, dv_in_ref, pick_ref, dk_ref, dv_ref,
    values_ref, sums_ref,
):
    length, width = dv_ref.shape
    for number in range(PIECES):
        span = slice(number * LANES, (number + 1) * LANES)
        values, sums = halves(state_ref[0, 0, span, :])
        values_ref[span, :] = spread_heads(values, value_dim, width).astype(jnp.bfloat16)
        sums_ref[span, :] = (sums * (1 / LANES)).astype(jnp.bfloat16)
    seg = seg_ref[...]
    keep = (seg == seg[-1:, :]).astype(jnp.float32)
    keys = k_ref[...]
    ones = jnp.ones((length, LANES), jnp.bfloat16)
    d_phi = dot(v_ref[...], values_ref[...], ((1,), (1,))) + dot(ones, sums_ref[...], ((1,), (1,)))
    dk = dk_in_ref[...] + keep * from_features(d_phi, keys, pick_ref, 1.0)
    dk_ref[...] = dk.astype(dk_ref.dtype)
    phi = features(keys, pick_ref, 1.0)
    dv_ref[...] = (dv_in_ref[...] + keep * dot(phi, values_ref[...])).astype(dv_ref.dtype)


class Attention:
    def __init__(self, rows, length, width):
        self.rows, self.length = rows, length
        self.value_dim = width // HEADS
        self.groups = HEADS // GROUP
        self.wide = GROUP * self.value_dim
        self.block = min(256, length)
        self.count = rows * length
        length_, groups, wide = length, self.groups, self.wide
        self.q = pl.BlockSpec((length, LANES), lambda r, g: (r, g))
        self.k = pl.BlockSpec((length, LANES), lambda r, g: (r, groups + g))
        self.v = pl.BlockSpec((length, wide), lambda r, g: (r, 2 * groups * LANES // wide + g))
        self.y = pl.BlockSpec((length, wide), lambda r, g: (r, g))
        self.seg = pl.BlockSpec((length, 1), lambda r, g: (r, 0))
        self.seg_row = pl.BlockSpec((1, 1, length), lambda r, g: (r, 0, 0))
        self.state = pl.BlockSpec((1, 1, WIDE, LANES), lambda r, g: (r, g, 0, 0))
        self.whole = pl.BlockSpec((LANES, WIDE), lambda r, g: (0, 0))
        self.whole_t = pl.BlockSpec((WIDE, LANES), lambda r, g: (0, 0))
        self.scaled = jnp.asarray(rolls(True), jnp.bfloat16)
        self.plain = jnp.asarray(rolls(False), jnp.bfloat16)
        self.state_shape = jax.ShapeDtypeStruct((rows, groups, WIDE, LANES), jnp.bfloat16)
        self.narrow = HEADS * FEAT

    def shape(self, columns, dtype):
        return jax.ShapeDtypeStruct((self.count, columns), dtype)

    def call(self, kernel, specs, outs, out_specs, scratch, passes, name):
        flops = self.rows * self.groups * GROUP * passes * 2 * 256**3
        return pl.pallas_call(
            kernel,
            grid=(self.rows, self.groups),
            in_specs=specs,
            out_specs=out_specs,
            out_shape=outs,
            scratch_shapes=scratch,
            compiler_params=pltpu.CompilerParams(
                dimension_semantics=("arbitrary", "arbitrary"), vmem_limit_bytes=48 * 2**20
            ),
            cost_estimate=pl.CostEstimate(
                flops=flops, bytes_accessed=2**22, transcendentals=0
            ),
            name=name,
        )

    def tail(self, qkv, seg):
        return self.call(
            functools.partial(tail_kernel, self.value_dim),
            [self.k, self.v, self.seg, self.whole_t],
            self.state_shape, self.state, [], 5, "attn_tail",
        )(qkv, qkv, seg, self.plain.T)

    def near(self, qkv, seg, seg_row):
        out = self.shape(self.groups * self.wide, jnp.float32)
        return self.call(
            functools.partial(near_kernel, self.value_dim, self.block),
            [self.q, self.k, self.v, self.seg, self.seg_row],
            [out, out], [self.y, self.y], [], 8, "attn_near",
        )(qkv, qkv, qkv, seg, seg_row)

    def states(self):
        return pltpu.VMEM((WIDE, self.wide), jnp.bfloat16)

    def far(self, qkv, seg, state, top, den):
        out = self.groups * self.wide
        return self.call(
            functools.partial(far_kernel, self.value_dim),
            [self.q, self.seg, self.state, self.y, self.y, self.whole],
            [self.shape(out, jnp.bfloat16), self.shape(out, jnp.float32)],
            [self.y, self.y], [self.states(), self.states()], 8, "attn_far",
        )(qkv, seg, state, top, den, self.scaled)

    def head(self, qkv, dy, y, inverse, seg):
        return self.call(
            functools.partial(head_kernel, self.value_dim),
            [self.q, self.y, self.y, self.y, self.seg, self.whole_t],
            self.state_shape, self.state, [], 5, "attn_head",
        )(qkv, dy, y, inverse, seg, self.scaled.T)

    def near_back(self, qkv, dy, y, inverse, seg, seg_row, state):
        wide = self.groups * self.wide
        return self.call(
            functools.partial(near_back_kernel, self.value_dim, self.block),
            [self.q, self.k, self.v, self.y, self.y, self.y, self.seg, self.seg_row, self.state,
             self.whole],
            [self.shape(self.narrow, jnp.bfloat16), self.shape(self.narrow, jnp.float32),
             self.shape(wide, jnp.float32)],
            [self.q, self.q, self.y],
            [self.states(), pltpu.VMEM((WIDE, LANES), jnp.bfloat16),
             pltpu.VMEM((self.length, LANES), jnp.float32)], 24, "attn_near_back",
        )(qkv, qkv, qkv, dy, y, inverse, seg, seg_row, state, self.scaled)

    def far_back(self, qkv, seg, state, dk, dv):
        wide = self.groups * self.wide
        return self.call(
            functools.partial(far_back_kernel, self.value_dim),
            [self.k, self.v, self.seg, self.state, self.q, self.y, self.whole],
            [self.shape(self.narrow, jnp.bfloat16), self.shape(wide, jnp.bfloat16)],
            [self.q, self.y],
            [self.states(), pltpu.VMEM((WIDE, LANES), jnp.bfloat16)], 9, "attn_far_back",
        )(qkv, qkv, seg, state, dk, dv, self.plain)


def pass_states(own, whole, linked, steps, axis, shift, size):
    pairs = [(i, i + shift) for i in range(size) if 0 <= i + shift < size]
    pick = lambda flag, array: jnp.where(flag[:, None, None, None], array, jnp.zeros_like(array))
    came = None
    for _ in range(steps):
        total = own if came is None else own + pick(whole, came)
        came = pick(linked, lax.ppermute(total, axis, pairs))
    return came


epsilon = 1e-05


def across_rows(left, right):
    return dot(left, right, ((0,), (0,)))


def against(left, matrix):
    return dot(left, matrix, ((1,), (1,)))


def norm_forward(values):
    scale = lax.rsqrt(jnp.mean(values * values, axis=1, keepdims=True) + epsilon)
    return (scale, values * scale)


def norm_backward(d_scaled, gain, scale, normed):
    d_normed = d_scaled * gain
    return scale * (d_normed - normed * jnp.mean(d_normed * normed, axis=1, keepdims=True))


def fold(count):
    return [0] + list(range(1, count, 2)) + list(range(2, count, 2))[::-1]


class Line:
    def __init__(self, axis, axis_size, stride, count):
        self.axis, self.stride, self.count = axis, stride, count
        self.order = fold(count)
        self.pairs = []
        for index in range(axis_size):
            place = (index // stride) % count
            ring = self.order.index(place)
            goal = self.order[(ring + 1) % count]
            self.pairs.append((index, index + (goal - place) * stride))

    def send(self, array):
        return lax.ppermute(array, self.axis, self.pairs)

    def place_back(self, steps):
        own = (lax.axis_index(self.axis) // self.stride) % self.count
        rank = jnp.asarray([self.order.index(p) for p in range(self.count)], jnp.int32)[own]
        return jnp.asarray(self.order, jnp.int32)[(rank - steps) % self.count]


class Slice:
    def __init__(self, dp, seq):
        self.dp, self.seq, self.devices = dp, seq, dp * seq
        self.lines = {
            "z": Line("dp", dp, 2, dp // 2),
            "x": Line("dp", dp, 1, 2),
            "y": Line("seq", seq, 2, seq // 2),
            "c": Line("seq", seq, 1, 2),
        }

    def device_of(self, back):
        at = {d: self.lines[d].place_back(back[d]) for d in "zxyc"}
        return ((at["z"] * 2 + at["x"]) * (self.seq // 2) + at["y"]) * 2 + at["c"]


def assemble(pieces, places, block, devices):
    columns = pieces[0].shape[1]
    counts = [piece.shape[0] // block for piece in pieces]

    def kernel(places_ref, *refs):
        piece_refs, out_ref, held, in_sems, out_sems = (
            refs[: len(pieces)],
            *refs[len(pieces) :],
        )
        loads, begin = [], 0
        for number, piece_ref in enumerate(piece_refs):
            rows = counts[number] * block
            load = pltpu.make_async_copy(
                piece_ref, held.at[pl.ds(begin * block, rows)], in_sems.at[number]
            )
            load.start()
            loads.append(load)
            begin += counts[number]
        stores, begin = [], 0
        for number, load in enumerate(loads):
            load.wait()
            for i in range(begin, begin + counts[number]):
                to = pl.multiple_of(places_ref[i] * block, block)
                store = pltpu.make_async_copy(
                    held.at[pl.ds(i * block, block)], out_ref.at[pl.ds(to, block)], out_sems.at[i]
                )
                store.start()
                stores.append(store)
            begin += counts[number]
        for store in stores:
            store.wait()

    size = devices * block * columns * pieces[0].dtype.itemsize
    return pl.pallas_call(
        kernel,
        out_shape=jax.ShapeDtypeStruct((devices * block, columns), pieces[0].dtype),
        in_specs=[pl.BlockSpec(memory_space=pltpu.SMEM)]
        + [pl.BlockSpec(memory_space=pl.ANY)] * len(pieces),
        out_specs=pl.BlockSpec(memory_space=pl.ANY),
        scratch_shapes=[
            pltpu.VMEM((devices * block, columns), pieces[0].dtype),
            pltpu.SemaphoreType.DMA((len(pieces),)),
            pltpu.SemaphoreType.DMA((devices,)),
        ],
        cost_estimate=pl.CostEstimate(flops=0, bytes_accessed=2 * size, transcendentals=0),
        name="assemble",
    )(places, *pieces)


def gather_rows(part, shape, route):
    block, columns = part.shape
    if block % 16:
        return lax.all_gather(part, ("dp", "seq"), axis=0, tiled=True)
    held = [(part, [dict(z=0, x=0, y=0, c=0)])]
    for dim in route:
        if len(held) > 1 and sum(len(names) for _, names in held) <= 4:
            held = [
                (jnp.concatenate([a for a, _ in held], 0), [n for _, names in held for n in names])
            ]
        came = []
        for array, names in held:
            for step in range(1, shape.lines[dim].count):
                array = shape.lines[dim].send(array)
                came.append((array, [dict(n, **{dim: step}) for n in names]))
        held = held + came
    places = jnp.stack([shape.device_of(n) for _, names in held for n in names])
    return assemble([a for a, _ in held], places, block, shape.devices)


def column_order(shape, width, route):
    block = width // shape.devices
    names = [dict()]
    for dim in route:
        names = [dict(n, **{dim: s}) for n in names for s in range(shape.lines[dim].count)]
    places = jnp.stack([shape.device_of(n) for n in names])
    return (places[:, None] * block + jnp.arange(block)[None, :]).reshape(width)


def reorder(left, order):
    width = left.shape[1]
    pick = (jnp.arange(width)[:, None] == order[None, :]).astype(jnp.bfloat16)
    return jnp.dot(left, pick, preferred_element_type=jnp.float32).astype(jnp.bfloat16)


def scatter_rows(left, right, shape, route):
    width = left.shape[1]
    if (width // shape.devices) % 16:
        return lax.psum_scatter(
            across_rows(left, right), ("dp", "seq"), scatter_dimension=0, tiled=True
        )
    left = reorder(left, column_order(shape, width, route))
    first, second = (shape.lines[d] for d in route[:2])
    half = width // first.count
    came = None
    for step in range(1, first.count):
        term = across_rows(left[:, step * half : (step + 1) * half], right)
        term = term if came is None else term + came.astype(jnp.float32)
        came = first.send(term.astype(jnp.bfloat16))
    rows = half // second.count
    arrived, came = came, None

    def term_of(step):
        low, high = step * rows, (step + 1) * rows
        return across_rows(left[:, low:high], right) + arrived[low:high].astype(jnp.float32)

    for step in range(1, second.count):
        term = term_of(step)
        term = term if came is None else term + came.astype(jnp.float32)
        came = second.send(term.astype(jnp.bfloat16))
    total = term_of(0) + came.astype(jnp.float32)
    for dim in route[2:]:
        line = shape.lines[dim]
        rows = total.shape[0] // line.count
        came = None
        for step in range(1, line.count):
            term = total[step * rows : (step + 1) * rows]
            term = term if came is None else term + came.astype(jnp.float32)
            came = line.send(term.astype(jnp.bfloat16))
        total = total[:rows] + came.astype(jnp.float32)
    return total


def gain_gradient(weights, gradients, gain):
    products = jnp.sum(weights.astype(jnp.float32) * gradients, axis=1)
    return products / gain.astype(jnp.float32)


def per_device(
    shape,
    layer_input,
    segment_ids,
    gain_attn,
    w_query,
    w_key,
    w_value,
    w_out,
    gain_mlp,
    w_gate,
    w_up,
    w_down,
    grad_output,
):
    rows, shard_len, width = layer_input.shape
    count = rows * shard_len
    narrow = HEADS * FEAT
    qkv_part = jnp.concatenate([w_query, w_key, w_value], axis=1)
    down_part = w_down.T
    gains = jnp.stack([gain_attn, gain_mlp], axis=1)
    gains = jnp.pad(gains, ((0, 0), (0, 126)))
    head = gather_rows(jnp.concatenate([qkv_part, gains], axis=1), shape, "zxyc")
    qkv_w = head[:, : 2 * narrow + width]
    gain_one = head[:, 2 * narrow + width].astype(jnp.float32)
    gain_two = head[:, 2 * narrow + width + 1].astype(jnp.float32)
    out_w = gather_rows(w_out, shape, "xyzc")
    gate_w = gather_rows(w_gate, shape, "zxyc")
    up_w = gather_rows(w_up, shape, "zyxc")
    down_w = gather_rows(down_part, shape, "xyzc")

    tokens = layer_input.reshape(count, width).astype(jnp.float32)
    scale_one, normed_one = norm_forward(tokens)
    a_one = (normed_one * gain_one).astype(jnp.bfloat16)
    qkv = jnp.dot(a_one, qkv_w, preferred_element_type=jnp.float32).astype(jnp.bfloat16)
    attention = Attention(rows, shard_len, width)
    place = lax.axis_index("seq")
    own_seg = lax.dynamic_slice_in_dim(segment_ids, place * shard_len, shard_len, 1)
    before = jnp.maximum(place * shard_len - 1, 0)
    after = jnp.minimum((place + 1) * shard_len, segment_ids.shape[1] - 1)
    first, last = own_seg[:, 0], own_seg[:, -1]
    from_before = lax.dynamic_index_in_dim(segment_ids, before, 1, keepdims=False) == first
    from_after = lax.dynamic_index_in_dim(segment_ids, after, 1, keepdims=False) == last
    seg, seg_row = own_seg.reshape(count, 1), own_seg.reshape(rows, 1, shard_len)
    reach = min(shape.seq - 1, -(-(LONGEST - 1) // shard_len))
    tail = attention.tail(qkv, seg)
    earlier = pass_states(tail, first == last, from_before, reach, "seq", 1, shape.seq)
    top, den = attention.near(qkv, seg, seg_row)
    mixed_cat, inverse = attention.far(qkv, seg, earlier, top, den)
    x_two = tokens + jnp.dot(mixed_cat, out_w, preferred_element_type=jnp.float32)
    scale_two, normed_two = norm_forward(x_two)
    a_two = (normed_two * gain_two).astype(jnp.bfloat16)
    gate = jnp.dot(a_two, gate_w, preferred_element_type=jnp.float32)
    up_values = jnp.dot(a_two, up_w, preferred_element_type=jnp.float32)
    sigma = jax.nn.sigmoid(gate)
    silu_gate = gate * sigma
    hidden = (silu_gate * up_values).astype(jnp.bfloat16)
    result = (x_two + against(hidden, down_w)).astype(jnp.bfloat16)

    cotangent = grad_output.reshape(count, width)
    grad_down = scatter_rows(cotangent, hidden, shape, "czxy")
    d_hidden = jnp.dot(cotangent, down_w, preferred_element_type=jnp.float32)
    d_gate = (d_hidden * up_values * sigma * (1.0 + gate * (1.0 - sigma))).astype(jnp.bfloat16)
    d_up = (d_hidden * silu_gate).astype(jnp.bfloat16)
    grad_gate = scatter_rows(a_two, d_gate, shape, "cyxz")
    grad_up = scatter_rows(a_two, d_up, shape, "cxyz")
    d_a_two = against(d_gate, gate_w) + against(d_up, up_w)
    d_x_two = cotangent.astype(jnp.float32) + norm_backward(
        d_a_two, gain_two, scale_two, normed_two
    )
    d_branch = d_x_two.astype(jnp.bfloat16)
    grad_out = scatter_rows(mixed_cat, d_branch, shape, "cxyz")
    d_mixed = against(d_branch, out_w).astype(jnp.bfloat16)
    ahead = attention.head(qkv, d_mixed, mixed_cat, inverse, seg)
    later = pass_states(ahead, first == last, from_after, reach, "seq", -1, shape.seq)
    d_query, d_keys, d_values = attention.near_back(
        qkv, d_mixed, mixed_cat, inverse, seg, seg_row, earlier
    )
    d_keys, d_values = attention.far_back(qkv, seg, later, d_keys, d_values)
    d_qkv = jnp.concatenate([d_query, d_keys, d_values], axis=1)
    grad_qkv = scatter_rows(a_one, d_qkv, shape, "cyxz")
    d_a_one = against(d_qkv, qkv_w)
    d_tokens = d_x_two + norm_backward(d_a_one, gain_one, scale_one, normed_one)
    return (
        result.reshape(rows, shard_len, width),
        d_tokens.reshape(rows, shard_len, width),
        gain_gradient(qkv_part, grad_qkv, gain_attn),
        grad_qkv[:, :narrow],
        grad_qkv[:, narrow : 2 * narrow],
        grad_qkv[:, 2 * narrow :],
        grad_out,
        gain_gradient(
            jnp.concatenate([w_gate, w_up], axis=1),
            jnp.concatenate([grad_gate, grad_up], axis=1),
            gain_mlp,
        ),
        grad_gate,
        grad_up,
        grad_down.T,
    )


def solution(mesh):
    placed = (
        P("dp", "seq", None),
        P("dp", None),
        P(("dp", "seq")),
        P(("dp", "seq"), None),
        P(("dp", "seq"), None),
        P(("dp", "seq"), None),
        P(("dp", "seq"), None),
        P(("dp", "seq")),
        P(("dp", "seq"), None),
        P(("dp", "seq"), None),
        P(None, ("dp", "seq")),
        P("dp", "seq", None),
    )
    return jax.shard_map(
        functools.partial(per_device, Slice(mesh.shape["dp"], mesh.shape["seq"])),
        mesh=mesh,
        in_specs=placed,
        out_specs=(
            P("dp", "seq", None),
            P("dp", "seq", None),
            P(("dp", "seq")),
            P(("dp", "seq"), None),
            P(("dp", "seq"), None),
            P(("dp", "seq"), None),
            P(("dp", "seq"), None),
            P(("dp", "seq")),
            P(("dp", "seq"), None),
            P(("dp", "seq"), None),
            P(None, ("dp", "seq")),
        ),
        check_vma=False,
    )
```

```python
import functools

import jax
import jax.numpy as jnp
import numpy as np
from jax import lax
from jax.experimental import pallas as pl
from jax.experimental.pallas import tpu as pltpu
from jax.sharding import PartitionSpec as P

LONGEST = 1024
HEADS = 16
FEAT = 16
LANES = 128
GROUP = LANES // FEAT
PIECES = FEAT // 2 + 2
WIDE = PIECES * LANES


def dot(left, right, dims=((1,), (0,))):
    return lax.dot_general(left, right, (dims, ((), ())), preferred_element_type=jnp.float32)


def rolls(scaled):
    table = np.zeros((LANES, WIDE), np.float32)
    for d in range(FEAT // 2 + 1):
        factor = (1 / 32 if d == 0 else 1 / 16) if scaled else 1.0
        for lane in range(LANES):
            head, a = divmod(lane, FEAT)
            if d < FEAT // 2 or a < FEAT // 2:
                table[head * FEAT + (a + d) % FEAT, (d + 1) * LANES + lane] = factor
    return table


def piece_of(number, rows, factors, lin, axis):
    if number == 0:
        return rows.astype(jnp.float32) * lin
    products = rows.astype(jnp.float32) * factors
    if number < PIECES - 1:
        return products
    place = lax.broadcasted_iota(jnp.int32, products.shape, axis)
    return jnp.where(place % FEAT == FEAT // 2, 1.0, products)


def head_mask(lanes_per_head, first_head, shape):
    row_head = lax.broadcasted_iota(jnp.int32, shape, 0) // FEAT
    lane_head = lax.broadcasted_iota(jnp.int32, shape, 1) // lanes_per_head + first_head
    return row_head == lane_head


def fold_heads(full, value_dim):
    per = LANES // value_dim
    total = None
    for part in range(full.shape[1] // LANES):
        piece = full[:, part * LANES : (part + 1) * LANES]
        piece = jnp.where(head_mask(value_dim, part * per, piece.shape), piece, 0.0)
        total = piece if total is None else total + piece
    return total + pltpu.roll(total, value_dim, 1)


def halves(state):
    state = state.astype(jnp.float32)
    turned = pltpu.roll(state, LANES // 2, 1)
    low = lax.broadcasted_iota(jnp.int32, state.shape, 1) < LANES // 2
    return jnp.where(low, state, turned), jnp.where(low, turned, state)


def spread_heads(values, value_dim, width):
    per = LANES // value_dim
    return jnp.concatenate(
        [
            jnp.where(head_mask(value_dim, part * per, values.shape), values, 0.0)
            for part in range(width // LANES)
        ],
        axis=1,
    )


def turned(block):
    return block.astype(jnp.float32).T.astype(jnp.bfloat16)


def tail_kernel(value_dim, k_ref, v_ref, seg_ref, pick_ref, out_ref):
    seg = seg_ref[...]
    last = seg[-1:, :]
    keep = (seg == last).astype(jnp.float32)
    values = (v_ref[...].astype(jnp.float32) * keep).astype(jnp.bfloat16)
    ones = jnp.broadcast_to(keep, (seg.shape[0], LANES)).astype(jnp.bfloat16)
    keys = turned(k_ref[...])
    low = lax.broadcasted_iota(jnp.int32, (LANES, LANES), 1) < value_dim
    for number in range(PIECES):
        span = slice(number * LANES, (number + 1) * LANES)
        factors = dot(pick_ref[span, :], keys) if number else None
        piece = piece_of(number, keys, factors, 1.0, 0).astype(jnp.bfloat16)
        folded = fold_heads(dot(piece, values), value_dim)
        out_ref[0, 0, span, :] = jnp.where(low, folded, dot(piece, ones)).astype(out_ref.dtype)


def masks_of(seg_ref, seg_row_ref, begin, block):
    stop = begin + block
    rows = begin + lax.broadcasted_iota(jnp.int32, (block, stop), 0)
    columns = lax.broadcasted_iota(jnp.int32, (block, stop), 1)
    same = seg_ref[begin:stop, :] == seg_row_ref[0, :, :stop]
    return ((rows >= columns) & same).astype(jnp.float32)


def own_lanes(array, lanes_per_head, head):
    place = lax.broadcasted_iota(jnp.int32, array.shape, 1) // lanes_per_head
    return jnp.where(place == head, array, jnp.zeros_like(array))


def near_kernel(value_dim, block, q_ref, k_ref, v_ref, seg_ref, seg_row_ref, top_ref, den_ref):
    length = q_ref.shape[0]
    per = LANES // value_dim
    low = lax.broadcasted_iota(jnp.int32, (block, LANES), 1) < value_dim
    for begin in range(0, length, block):
        stop = begin + block
        mask = masks_of(seg_ref, seg_row_ref, begin, block)
        queries = q_ref[begin:stop, :] * jnp.bfloat16(FEAT ** (-0.5))
        keys = k_ref[:stop, :]
        ones = jnp.ones((stop, LANES), jnp.bfloat16)
        for pair in range(GROUP // per):
            span = slice(pair * LANES, (pair + 1) * LANES)
            values = jnp.concatenate([v_ref[:stop, span], ones], axis=1)
            sides = []
            for side in range(per):
                scores = dot(
                    own_lanes(queries, FEAT, pair * per + side), keys, ((1,), (1,))
                )
                weights = (((0.5 * scores + 1.0) * scores + 1.0) * mask).astype(jnp.bfloat16)
                sides.append(dot(weights, values))
            top_ref[begin:stop, span] = jnp.where(low, sides[0][:, :LANES], sides[1][:, :LANES])
            den_ref[begin:stop, span] = jnp.where(low, sides[0][:, LANES:], sides[1][:, LANES:])


def features(rows, pick_ref, lin):
    pieces = []
    for number in range(PIECES):
        span = slice(number * LANES, (number + 1) * LANES)
        factors = dot(rows, pick_ref[:, span]) if number else None
        pieces.append(piece_of(number, rows, factors, lin, 1).astype(jnp.bfloat16))
    return jnp.concatenate(pieces, axis=1)


def far_kernel(
    value_dim, q_ref, seg_ref, state_ref, top_ref, den_ref, pick_ref, y_ref, inverse_ref,
    values_ref, sums_ref,
):
    width = top_ref.shape[1]
    for number in range(PIECES):
        span = slice(number * LANES, (number + 1) * LANES)
        values, sums = halves(state_ref[0, 0, span, :])
        values_ref[span, :] = spread_heads(values, value_dim, width).astype(jnp.bfloat16)
        sums_ref[span, :] = spread_heads(sums, value_dim, width).astype(jnp.bfloat16)
    seg = seg_ref[...]
    keep = (seg == seg[:1, :]).astype(jnp.float32)
    phi = features(q_ref[...], pick_ref, FEAT ** (-0.5))
    top = top_ref[...] + keep * dot(phi, values_ref[...])
    inverse = 1.0 / (den_ref[...] + keep * dot(phi, sums_ref[...]))
    y_ref[...] = (top * inverse).astype(y_ref.dtype)
    inverse_ref[...] = inverse


def lane_sums(product, value_dim, side):
    place = lax.broadcasted_iota(jnp.int32, product.shape, 1) // value_dim
    return jnp.sum(jnp.where(place == side, product, 0.0), axis=1, keepdims=True)


def d_den_of(pair, value_dim, dy_ref, y_ref, inverse_ref):
    span = slice(pair * LANES, (pair + 1) * LANES)
    product = dy_ref[:, span].astype(jnp.float32) * y_ref[:, span].astype(jnp.float32)
    product = product * inverse_ref[:, span]
    return [-lane_sums(product, value_dim, side) for side in range(LANES // value_dim)]


def d_den_lanes(value_dim, dy_ref, y_ref, inverse_ref):
    per = LANES // value_dim
    shape = (dy_ref.shape[0], LANES)
    place = lax.broadcasted_iota(jnp.int32, shape, 1) // FEAT
    total = jnp.zeros(shape, jnp.float32)
    for pair in range(GROUP // per):
        for side, column in enumerate(d_den_of(pair, value_dim, dy_ref, y_ref, inverse_ref)):
            total = jnp.where(place == pair * per + side, column, total)
    return total


def head_kernel(
    value_dim, q_ref, dy_ref, y_ref, inverse_ref, seg_ref, pick_ref, out_ref
):
    seg = seg_ref[...]
    keep = (seg == seg[:1, :]).astype(jnp.float32)
    d_top = (dy_ref[...].astype(jnp.float32) * inverse_ref[...] * keep).astype(jnp.bfloat16)
    d_den = (d_den_lanes(value_dim, dy_ref, y_ref, inverse_ref) * keep).astype(jnp.bfloat16)
    queries = turned(q_ref[...])
    low = lax.broadcasted_iota(jnp.int32, (LANES, LANES), 1) < value_dim
    for number in range(PIECES):
        span = slice(number * LANES, (number + 1) * LANES)
        factors = dot(pick_ref[span, :], queries) if number else None
        piece = piece_of(number, queries, factors, FEAT ** (-0.5), 0).astype(jnp.bfloat16)
        folded = fold_heads(dot(piece, d_top), value_dim)
        sums = jnp.where(head_mask(FEAT, 0, (LANES, LANES)), dot(piece, d_den), 0.0)
        sums = jnp.sum(sums, axis=1, keepdims=True) * (1 / FEAT)
        out_ref[0, 0, span, :] = jnp.where(low, folded, sums).astype(out_ref.dtype)


def from_features(d_phi, rows, pick_ref, lin):
    total = d_phi[:, :LANES] * lin
    x = rows.astype(jnp.float32)
    scaled = []
    for number in range(1, PIECES):
        span = slice(number * LANES, (number + 1) * LANES)
        total = total + d_phi[:, span] * dot(rows, pick_ref[:, span])
        scaled.append((d_phi[:, span] * x).astype(jnp.bfloat16))
    return total + dot(jnp.concatenate(scaled, axis=1), pick_ref[:, LANES:], ((1,), (1,)))


def near_back_kernel(
    value_dim, block, q_ref, k_ref, v_ref, dy_ref, y_ref, inverse_ref, seg_ref, seg_row_ref,
    state_ref, pick_ref, dq_ref, dk_ref, dv_ref, values_ref, sums_ref, dq_sum,
):
    length, width = dy_ref.shape
    per = LANES // value_dim
    seg = seg_ref[...]
    keep = (seg == seg[:1, :]).astype(jnp.float32)
    for number in range(PIECES):
        span = slice(number * LANES, (number + 1) * LANES)
        values, sums = halves(state_ref[0, 0, span, :])
        values_ref[span, :] = spread_heads(values, value_dim, width).astype(jnp.bfloat16)
        sums = jnp.where(head_mask(FEAT, 0, sums.shape), sums, 0.0) * (1 / FEAT)
        sums_ref[span, :] = sums.astype(jnp.bfloat16)
    d_top = (dy_ref[...].astype(jnp.float32) * inverse_ref[...] * keep).astype(jnp.bfloat16)
    d_den = (d_den_lanes(value_dim, dy_ref, y_ref, inverse_ref) * keep).astype(jnp.bfloat16)
    d_phi = dot(d_top, values_ref[...], ((1,), (1,))) + dot(d_den, sums_ref[...], ((1,), (1,)))
    dq_sum[...] = from_features(d_phi, q_ref[...], pick_ref, FEAT ** (-0.5))
    dk_ref[...] = jnp.zeros_like(dk_ref)
    dv_ref[...] = jnp.zeros_like(dv_ref)
    for begin in range(0, length, block):
        stop = begin + block
        mask = masks_of(seg_ref, seg_row_ref, begin, block)
        queries = q_ref[begin:stop, :] * jnp.bfloat16(FEAT ** (-0.5))
        keys = k_ref[:stop, :] * jnp.bfloat16(FEAT ** (-0.5))
        for pair in range(GROUP // per):
            span = slice(pair * LANES, (pair + 1) * LANES)
            d_mixed = dy_ref[begin:stop, span].astype(jnp.float32)
            inverse = inverse_ref[begin:stop, span]
            d_numer = (d_mixed * inverse).astype(jnp.bfloat16)
            product = d_mixed * inverse * y_ref[begin:stop, span].astype(jnp.float32)
            values = v_ref[:stop, span]
            for side in range(per):
                head = pair * per + side
                own_q = own_lanes(queries, FEAT, head)
                own_dn = own_lanes(d_numer, value_dim, side)
                scores = dot(own_q, k_ref[:stop, :], ((1,), (1,)))
                weights = (((0.5 * scores + 1.0) * scores + 1.0) * mask).astype(jnp.bfloat16)
                d_weights = dot(own_dn, values, ((1,), (1,))) - lane_sums(product, value_dim, side)
                d_scores = (d_weights * ((scores + 1.0) * mask)).astype(jnp.bfloat16)
                dv_ref[:stop, span] += dot(weights, own_dn, ((0,), (0,)))
                dq_sum[begin:stop, :] += dot(d_scores, own_lanes(keys, FEAT, head))
                dk_ref[:stop, :] += dot(d_scores, own_q, ((0,), (0,)))
    dq_ref[...] = dq_sum[...].astype(dq_ref.dtype)


def far_back_kernel(
    value_dim, k_ref, v_ref, seg_ref, state_ref, dk_in_ref, dv_in_ref, pick_ref, dk_ref, dv_ref,
    values_ref, sums_ref,
):
    length, width = dv_ref.shape
    for number in range(PIECES):
        span = slice(number * LANES, (number + 1) * LANES)
        values, sums = halves(state_ref[0, 0, span, :])
        values_ref[span, :] = spread_heads(values, value_dim, width).astype(jnp.bfloat16)
        sums_ref[span, :] = (sums * (1 / LANES)).astype(jnp.bfloat16)
    seg = seg_ref[...]
    keep = (seg == seg[-1:, :]).astype(jnp.float32)
    keys = k_ref[...]
    ones = jnp.ones((length, LANES), jnp.bfloat16)
    d_phi = dot(v_ref[...], values_ref[...], ((1,), (1,))) + dot(ones, sums_ref[...], ((1,), (1,)))
    dk = dk_in_ref[...] + keep * from_features(d_phi, keys, pick_ref, 1.0)
    dk_ref[...] = dk.astype(dk_ref.dtype)
    phi = features(keys, pick_ref, 1.0)
    dv_ref[...] = (dv_in_ref[...] + keep * dot(phi, values_ref[...])).astype(dv_ref.dtype)


class Attention:
    def __init__(self, rows, length, width):
        self.rows, self.length = rows, length
        self.value_dim = width // HEADS
        self.groups = HEADS // GROUP
        self.wide = GROUP * self.value_dim
        self.block = min(256, length)
        self.count = rows * length
        length_, groups, wide = length, self.groups, self.wide
        self.q = pl.BlockSpec((length, LANES), lambda r, g: (r, g))
        self.k = pl.BlockSpec((length, LANES), lambda r, g: (r, groups + g))
        self.v = pl.BlockSpec((length, wide), lambda r, g: (r, 2 * groups * LANES // wide + g))
        self.y = pl.BlockSpec((length, wide), lambda r, g: (r, g))
        self.seg = pl.BlockSpec((length, 1), lambda r, g: (r, 0))
        self.seg_row = pl.BlockSpec((1, 1, length), lambda r, g: (r, 0, 0))
        self.state = pl.BlockSpec((1, 1, WIDE, LANES), lambda r, g: (r, g, 0, 0))
        self.whole = pl.BlockSpec((LANES, WIDE), lambda r, g: (0, 0))
        self.whole_t = pl.BlockSpec((WIDE, LANES), lambda r, g: (0, 0))
        self.scaled = jnp.asarray(rolls(True), jnp.bfloat16)
        self.plain = jnp.asarray(rolls(False), jnp.bfloat16)
        self.state_shape = jax.ShapeDtypeStruct((rows, groups, WIDE, LANES), jnp.bfloat16)
        self.narrow = HEADS * FEAT

    def shape(self, columns, dtype):
        return jax.ShapeDtypeStruct((self.count, columns), dtype)

    def call(self, kernel, specs, outs, out_specs, scratch, passes, name):
        flops = self.rows * self.groups * GROUP * passes * 2 * 256**3
        return pl.pallas_call(
            kernel,
            grid=(self.rows, self.groups),
            in_specs=specs,
            out_specs=out_specs,
            out_shape=outs,
            scratch_shapes=scratch,
            compiler_params=pltpu.CompilerParams(
                dimension_semantics=("arbitrary", "arbitrary"), vmem_limit_bytes=48 * 2**20
            ),
            cost_estimate=pl.CostEstimate(
                flops=flops, bytes_accessed=2**22, transcendentals=0
            ),
            name=name,
        )

    def tail(self, qkv, seg):
        return self.call(
            functools.partial(tail_kernel, self.value_dim),
            [self.k, self.v, self.seg, self.whole_t],
            self.state_shape, self.state, [], 5, "attn_tail",
        )(qkv, qkv, seg, self.plain.T)

    def near(self, qkv, seg, seg_row):
        out = self.shape(self.groups * self.wide, jnp.float32)
        return self.call(
            functools.partial(near_kernel, self.value_dim, self.block),
            [self.q, self.k, self.v, self.seg, self.seg_row],
            [out, out], [self.y, self.y], [], 8, "attn_near",
        )(qkv, qkv, qkv, seg, seg_row)

    def states(self):
        return pltpu.VMEM((WIDE, self.wide), jnp.bfloat16)

    def far(self, qkv, seg, state, top, den):
        out = self.groups * self.wide
        return self.call(
            functools.partial(far_kernel, self.value_dim),
            [self.q, self.seg, self.state, self.y, self.y, self.whole],
            [self.shape(out, jnp.bfloat16), self.shape(out, jnp.float32)],
            [self.y, self.y], [self.states(), self.states()], 8, "attn_far",
        )(qkv, seg, state, top, den, self.scaled)

    def head(self, qkv, dy, y, inverse, seg):
        return self.call(
            functools.partial(head_kernel, self.value_dim),
            [self.q, self.y, self.y, self.y, self.seg, self.whole_t],
            self.state_shape, self.state, [], 5, "attn_head",
        )(qkv, dy, y, inverse, seg, self.scaled.T)

    def near_back(self, qkv, dy, y, inverse, seg, seg_row, state):
        wide = self.groups * self.wide
        return self.call(
            functools.partial(near_back_kernel, self.value_dim, self.block),
            [self.q, self.k, self.v, self.y, self.y, self.y, self.seg, self.seg_row, self.state,
             self.whole],
            [self.shape(self.narrow, jnp.bfloat16), self.shape(self.narrow, jnp.float32),
             self.shape(wide, jnp.float32)],
            [self.q, self.q, self.y],
            [self.states(), pltpu.VMEM((WIDE, LANES), jnp.bfloat16),
             pltpu.VMEM((self.length, LANES), jnp.float32)], 24, "attn_near_back",
        )(qkv, qkv, qkv, dy, y, inverse, seg, seg_row, state, self.scaled)

    def far_back(self, qkv, seg, state, dk, dv):
        wide = self.groups * self.wide
        return self.call(
            functools.partial(far_back_kernel, self.value_dim),
            [self.k, self.v, self.seg, self.state, self.q, self.y, self.whole],
            [self.shape(self.narrow, jnp.bfloat16), self.shape(wide, jnp.bfloat16)],
            [self.q, self.y],
            [self.states(), pltpu.VMEM((WIDE, LANES), jnp.bfloat16)], 9, "attn_far_back",
        )(qkv, qkv, seg, state, dk, dv, self.plain)


def pass_states(own, whole, linked, steps, axis, shift, size):
    pairs = [(i, i + shift) for i in range(size) if 0 <= i + shift < size]
    pick = lambda flag, array: jnp.where(flag[:, None, None, None], array, jnp.zeros_like(array))
    came = None
    for _ in range(steps):
        total = own if came is None else own + pick(whole, came)
        came = pick(linked, lax.ppermute(total, axis, pairs))
    return came


epsilon = 1e-05


def against(left, matrix):
    return dot(left, matrix, ((1,), (1,)))


def norm_forward(values):
    scale = lax.rsqrt(jnp.mean(values * values, axis=1, keepdims=True) + epsilon)
    return (scale, values * scale)


def norm_backward(d_scaled, gain, scale, normed):
    d_normed = d_scaled * gain
    return scale * (d_normed - normed * jnp.mean(d_normed * normed, axis=1, keepdims=True))


def fold(count):
    return [0] + list(range(1, count, 2)) + list(range(2, count, 2))[::-1]


class Line:
    def __init__(self, axis, axis_size, stride, count):
        self.axis, self.stride, self.count = axis, stride, count
        self.order = fold(count)
        self.pairs = []
        for index in range(axis_size):
            place = (index // stride) % count
            ring = self.order.index(place)
            goal = self.order[(ring + 1) % count]
            self.pairs.append((index, index + (goal - place) * stride))

    def send(self, array):
        return lax.ppermute(array, self.axis, self.pairs)

    def place_back(self, steps):
        own = (lax.axis_index(self.axis) // self.stride) % self.count
        rank = jnp.asarray([self.order.index(p) for p in range(self.count)], jnp.int32)[own]
        return jnp.asarray(self.order, jnp.int32)[(rank - steps) % self.count]


class Slice:
    def __init__(self, dp, seq):
        self.dp, self.seq, self.devices = dp, seq, dp * seq
        self.lines = {
            "z": Line("dp", dp, 2, dp // 2),
            "x": Line("dp", dp, 1, 2),
            "y": Line("seq", seq, 2, seq // 2),
            "c": Line("seq", seq, 1, 2),
        }

    def device_of(self, back):
        at = {d: self.lines[d].place_back(back[d]) for d in "zxyc"}
        return ((at["z"] * 2 + at["x"]) * (self.seq // 2) + at["y"]) * 2 + at["c"]


def assemble(pieces, columns, block, devices, shape):
    arrays = [array for array, _, _ in pieces]
    counts = [len(names) for _, names, _ in pieces]
    places = jnp.stack([shape.device_of(n) for _, names, _ in pieces for n in names])
    held = sum(array.size for array in arrays) // columns

    def kernel(places_ref, *refs):
        piece_refs = refs[: len(pieces)]
        out_ref = refs[len(pieces)]
        buffers = refs[len(pieces) + 1 : 2 * len(pieces) + 1]
        in_sems, out_sems = refs[2 * len(pieces) + 1 :]
        loads = []
        for number, piece_ref in enumerate(piece_refs):
            load = pltpu.make_async_copy(piece_ref, buffers[number], in_sems.at[number])
            load.start()
            loads.append(load)
        stores, begin = [], 0
        for number, load in enumerate(loads):
            load.wait()
            span = pl.ds(pieces[number][2], arrays[number].shape[1])
            for i in range(counts[number]):
                to = pl.multiple_of(places_ref[begin + i] * block, block)
                store = pltpu.make_async_copy(
                    buffers[number].at[pl.ds(i * block, block)],
                    out_ref.at[pl.ds(to, block), span],
                    out_sems.at[begin + i],
                )
                store.start()
                stores.append(store)
            begin += counts[number]
        for store in stores:
            store.wait()

    size = held * columns * arrays[0].dtype.itemsize
    return pl.pallas_call(
        kernel,
        out_shape=jax.ShapeDtypeStruct((devices * block, columns), arrays[0].dtype),
        in_specs=[pl.BlockSpec(memory_space=pltpu.SMEM)]
        + [pl.BlockSpec(memory_space=pl.ANY)] * len(pieces),
        out_specs=pl.BlockSpec(memory_space=pl.ANY),
        scratch_shapes=[pltpu.VMEM(array.shape, array.dtype) for array in arrays]
        + [
            pltpu.SemaphoreType.DMA((len(pieces),)),
            pltpu.SemaphoreType.DMA((sum(counts),)),
        ],
        cost_estimate=pl.CostEstimate(flops=0, bytes_accessed=2 * size, transcendentals=0),
        name="assemble",
    )(places, *arrays)


class Gathering:
    def __init__(self, shape, array, names=None):
        self.shape, self.array = shape, array
        self.names = names or [dict(z=0, x=0, y=0, c=0)]

    def came(self, dim):
        line, array, out = self.shape.lines[dim], self.array, []
        for step in range(1, line.count):
            array = line.send(array)
            out.append((array, [dict(n, **{dim: step}) for n in self.names]))
        return out

    def along(self, dim):
        came = self.came(dim)
        array = jnp.concatenate([self.array] + [a for a, _ in came], 0)
        return Gathering(self.shape, array, self.names + [n for _, names in came for n in names])

    def columns(self, low, high):
        return Gathering(self.shape, self.array[:, low:high], self.names)

    def pieces(self, dim, first_column=0):
        found = [(self.array, self.names)] + self.came(dim)
        return [(array, names, first_column) for array, names in found]


def small_blocks(part):
    return part.shape[0] % 16 != 0


def gather_rows(part, shape, route):
    if small_blocks(part):
        return lax.all_gather(part, ("dp", "seq"), axis=0, tiled=True)
    held = Gathering(shape, part)
    for dim in route[:-1]:
        held = held.along(dim)
    return assemble(held.pieces(route[-1]), part.shape[1], part.shape[0], shape.devices, shape)


def gather_first(part, shape, waiting):
    if small_blocks(part):
        return lax.all_gather(part, ("dp", "seq"), axis=0, tiled=True), waiting
    columns = part.shape[1]
    cut = columns // 2 // LANES * LANES + LANES
    held = Gathering(shape, part).along("z")
    one, two = held.columns(0, cut).along("x"), held.columns(cut, columns).along("y")
    one.array, two.array, waiting = lax.optimization_barrier((one.array, two.array, waiting))
    one, two = one.along("y"), two.along("x")
    pieces = one.pieces("c") + two.pieces("c", cut)
    return assemble(pieces, columns, part.shape[0], shape.devices, shape), waiting


LAYOUT = "cyxz"


def picker(shape, width):
    block = width // shape.devices
    if block % 16:
        order = jnp.arange(width)
    else:
        names = [dict()]
        for dim in LAYOUT:
            names = [dict(n, **{dim: s}) for n in names for s in range(shape.lines[dim].count)]
        places = jnp.stack([shape.device_of(n) for n in names])
        order = (places[:, None] * block + jnp.arange(block)[None, :]).reshape(width)
    return (jnp.arange(width)[:, None] == order[None, :]).astype(jnp.bfloat16)


def turned_rows(pick, left):
    return dot(pick, left, ((0,), (1,))).astype(jnp.bfloat16)


def scatter_rows(kept, sent, shape, route):
    half, columns = kept.shape
    block = 2 * half // shape.devices
    if block % 16:
        whole = jnp.concatenate([kept, sent], 0)
        return lax.psum_scatter(
            whole.astype(jnp.float32), ("dp", "seq"), scatter_dimension=0, tiled=True
        )
    dims = list(LAYOUT[1:])
    form = [shape.lines[d].count for d in dims] + [block, columns]
    arrived = shape.lines["c"].send(sent).reshape(form)
    total = kept.reshape(form)
    for dim in route:
        line, axis = shape.lines[dim], dims.index(dim)

        def term_of(step):
            term = lax.index_in_dim(total, step, axis, False).astype(jnp.float32)
            if arrived is not None:
                term = term + lax.index_in_dim(arrived, step, axis, False).astype(jnp.float32)
            return term

        came = None
        for step in range(1, line.count):
            term = term_of(step)
            term = term if came is None else term + came.astype(jnp.float32)
            came = line.send(term.astype(jnp.bfloat16))
        total, arrived = term_of(0) + came.astype(jnp.float32), None
        dims.pop(axis)
    return total.reshape(block, columns)


def scatter_product(turned, right, shape, route):
    half = turned.shape[0] // 2
    sent = dot(turned[half:], right).astype(jnp.bfloat16)
    kept = dot(turned[:half], right).astype(jnp.bfloat16)
    return scatter_rows(kept, sent, shape, route)


FF_TILE = 256


def mlp_kernel(
    block, a_ref, g_ref, at_ref, gt_ref, x_ref, gain_ref, gate_ref, up_ref, down_ref, y_ref,
    dx_ref, dxo_ref, *rest,
):
    grads, (out_sum, hidden_ref, d_gate_ref, d_up_ref) = rest[:6], rest[6:]
    count = a_ref.shape[0]
    step = pl.program_id(0)

    @pl.when(step == 0)
    def _():
        out_sum[...] = jnp.zeros_like(out_sum)
        dx_ref[...] = jnp.zeros_like(dx_ref)

    for begin in range(0, count, block):
        span = slice(begin, begin + block)
        a, g = a_ref[span, :], g_ref[span, :]
        gate, up = dot(a, gate_ref[...]), dot(a, up_ref[...])
        d_hidden = dot(g, down_ref[...])
        sigma = jax.nn.sigmoid(gate)
        silu = gate * sigma
        hidden = (silu * up).astype(jnp.bfloat16)
        d_gate = (d_hidden * up * (sigma + silu * (1.0 - sigma))).astype(jnp.bfloat16)
        d_up = (d_hidden * silu).astype(jnp.bfloat16)
        hidden_ref[span, :], d_gate_ref[span, :], d_up_ref[span, :] = hidden, d_gate, d_up
        out_sum[span, :] += dot(hidden, down_ref[...], ((1,), (1,)))
        dx_ref[span, :] += dot(d_gate, gate_ref[...], ((1,), (1,))) + dot(
            d_up, up_ref[...], ((1,), (1,))
        )
    half = at_ref.shape[0] // 2
    for number, (left, right) in enumerate(
        ((at_ref, d_gate_ref), (at_ref, d_up_ref), (gt_ref, hidden_ref))
    ):
        for part in range(2):
            rows = slice(part * half, (part + 1) * half)
            grads[2 * number + part][...] = dot(left[rows, :], right[...]).astype(jnp.bfloat16)

    @pl.when(step == pl.num_programs(0) - 1)
    def _():
        for begin in range(0, count, block):
            span = slice(begin, begin + block)
            x = x_ref[span, :]
            y_ref[span, :] = (x + out_sum[span, :]).astype(y_ref.dtype)
            scale = lax.rsqrt(jnp.mean(x * x, axis=1, keepdims=True) + epsilon)
            normed = x * scale
            d_normed = dx_ref[span, :] * gain_ref[...]
            mean = jnp.mean(d_normed * normed, axis=1, keepdims=True)
            dx = g_ref[span, :].astype(jnp.float32) + scale * (d_normed - normed * mean)
            dx_ref[span, :] = dx
            dxo_ref[span, :] = dx.astype(dxo_ref.dtype)


def feed_forward(a, g, a_turned, g_turned, x, gain, gate_w, up_w, down_w):
    count, width = a.shape
    hidden = gate_w.shape[1]
    tiles = hidden // FF_TILE
    half = width // 2

    def held(rows, columns):
        return pl.BlockSpec((rows, columns), lambda j: (0, 0), pipeline_mode=pl.Buffered(1))

    def tile(rows):
        return pl.BlockSpec((rows, FF_TILE), lambda j: (0, j))

    out = pl.pallas_call(
        functools.partial(mlp_kernel, min(256, count)),
        grid=(tiles,),
        in_specs=[held(count, width)] * 2
        + [held(width, count)] * 2
        + [held(count, width), held(1, width)]
        + [tile(width)] * 3,
        out_specs=[held(count, width)] * 3 + [tile(half)] * 6,
        out_shape=[
            jax.ShapeDtypeStruct((count, width), jnp.bfloat16),
            jax.ShapeDtypeStruct((count, width), jnp.float32),
            jax.ShapeDtypeStruct((count, width), jnp.bfloat16),
        ]
        + [jax.ShapeDtypeStruct((half, hidden), jnp.bfloat16)] * 6,
        scratch_shapes=[pltpu.VMEM((count, width), jnp.float32)]
        + [pltpu.VMEM((count, FF_TILE), jnp.bfloat16)] * 3,
        compiler_params=pltpu.CompilerParams(
            dimension_semantics=("arbitrary",), vmem_limit_bytes=60 * 2**20
        ),
        cost_estimate=pl.CostEstimate(
            flops=18 * count * width * hidden,
            bytes_accessed=12 * width * hidden + 20 * count * width,
            transcendentals=count * hidden,
        ),
        name="mlp",
    )(a, g, a_turned, g_turned, x, gain, gate_w, up_w, down_w)
    return out[0], out[1], out[2], out[3:5], out[5:7], out[7:9]


def gain_gradient(weights, gradients, gain):
    products = jnp.sum(weights.astype(jnp.float32) * gradients, axis=1)
    return products / gain.astype(jnp.float32)


def per_device(
    shape,
    layer_input,
    segment_ids,
    gain_attn,
    w_query,
    w_key,
    w_value,
    w_out,
    gain_mlp,
    w_gate,
    w_up,
    w_down,
    grad_output,
):
    rows, shard_len, width = layer_input.shape
    count = rows * shard_len
    narrow, hidden = HEADS * FEAT, w_gate.shape[1]
    qkv_columns = 2 * narrow + width
    qkv_part = jnp.concatenate([w_query, w_key, w_value], axis=1)
    gains = jnp.pad(jnp.stack([gain_attn, gain_mlp], axis=1), ((0, 0), (0, LANES - 2)))
    spare = ((0, 0), (0, -hidden % FF_TILE))
    parts = (
        w_out,
        jnp.pad(w_gate, spare),
        jnp.pad(w_up, spare),
        jnp.pad(w_down.T, spare),
    )
    first_part = jnp.concatenate([qkv_part, gains], axis=1)
    gathered, parts = gather_first(first_part, shape, parts)
    qkv_w = gathered[:, :qkv_columns]
    gain_one = gathered[:, qkv_columns].astype(jnp.float32)[None, :]
    gain_two = gathered[:, qkv_columns + 1].astype(jnp.float32)[None, :]
    out_w = gather_rows(parts[0], shape, "zyxc")
    gate_w = gather_rows(parts[1], shape, "zxyc")
    up_w = gather_rows(parts[2], shape, "zyxc")
    down_w = gather_rows(parts[3], shape, "xyzc")

    pick = picker(shape, width)
    cotangent = grad_output.reshape(count, width)
    tokens = layer_input.reshape(count, width).astype(jnp.float32)
    scale_one, normed_one = norm_forward(tokens)
    a_one = (normed_one * gain_one).astype(jnp.bfloat16)
    qkv = jnp.dot(a_one, qkv_w, preferred_element_type=jnp.float32).astype(jnp.bfloat16)
    attention = Attention(rows, shard_len, width)
    place = lax.axis_index("seq")
    own_seg = lax.dynamic_slice_in_dim(segment_ids, place * shard_len, shard_len, 1)
    before = jnp.maximum(place * shard_len - 1, 0)
    after = jnp.minimum((place + 1) * shard_len, segment_ids.shape[1] - 1)
    first, last = own_seg[:, 0], own_seg[:, -1]
    from_before = lax.dynamic_index_in_dim(segment_ids, before, 1, keepdims=False) == first
    from_after = lax.dynamic_index_in_dim(segment_ids, after, 1, keepdims=False) == last
    seg, seg_row = own_seg.reshape(count, 1), own_seg.reshape(rows, 1, shard_len)
    reach = min(shape.seq - 1, -(-(LONGEST - 1) // shard_len))
    tail = attention.tail(qkv, seg)
    earlier = pass_states(tail, first == last, from_before, reach, "seq", 1, shape.seq)
    top, den = attention.near(qkv, seg, seg_row)
    mixed_cat, inverse = attention.far(qkv, seg, earlier, top, den)
    x_two = tokens + jnp.dot(mixed_cat, out_w, preferred_element_type=jnp.float32)
    scale_two, normed_two = norm_forward(x_two)
    a_two = (normed_two * gain_two).astype(jnp.bfloat16)
    result, d_x_two, d_branch, gate_sums, up_sums, down_sums = feed_forward(
        a_two,
        cotangent,
        turned_rows(pick, a_two),
        turned_rows(pick, cotangent),
        x_two,
        gain_two,
        gate_w,
        up_w,
        down_w,
    )
    grad_gate = scatter_rows(*gate_sums, shape, "yxz")[:, :hidden]
    grad_up = scatter_rows(*up_sums, shape, "xyz")[:, :hidden]
    grad_down = scatter_rows(*down_sums, shape, "zxy")[:, :hidden]
    grad_out = scatter_product(turned_rows(pick, mixed_cat), d_branch, shape, "xyz")
    d_mixed = against(d_branch, out_w).astype(jnp.bfloat16)
    ahead = attention.head(qkv, d_mixed, mixed_cat, inverse, seg)
    later = pass_states(ahead, first == last, from_after, reach, "seq", -1, shape.seq)
    d_query, d_keys, d_values = attention.near_back(
        qkv, d_mixed, mixed_cat, inverse, seg, seg_row, earlier
    )
    d_keys, d_values = attention.far_back(qkv, seg, later, d_keys, d_values)
    d_qkv = jnp.concatenate([d_query, d_keys, d_values], axis=1)
    grad_qkv = scatter_product(turned_rows(pick, a_one), d_qkv, shape, "yxz")
    d_a_one = against(d_qkv, qkv_w)
    d_tokens = d_x_two + norm_backward(d_a_one, gain_one, scale_one, normed_one)
    return (
        result.reshape(rows, shard_len, width),
        d_tokens.reshape(rows, shard_len, width),
        gain_gradient(qkv_part, grad_qkv, gain_attn),
        grad_qkv[:, :narrow],
        grad_qkv[:, narrow : 2 * narrow],
        grad_qkv[:, 2 * narrow :],
        grad_out,
        gain_gradient(
            jnp.concatenate([w_gate, w_up], axis=1),
            jnp.concatenate([grad_gate, grad_up], axis=1),
            gain_mlp,
        ),
        grad_gate,
        grad_up,
        grad_down.T,
    )


def solution(mesh):
    placed = (
        P("dp", "seq", None),
        P("dp", None),
        P(("dp", "seq")),
        P(("dp", "seq"), None),
        P(("dp", "seq"), None),
        P(("dp", "seq"), None),
        P(("dp", "seq"), None),
        P(("dp", "seq")),
        P(("dp", "seq"), None),
        P(("dp", "seq"), None),
        P(None, ("dp", "seq")),
        P("dp", "seq", None),
    )
    return jax.shard_map(
        functools.partial(per_device, Slice(mesh.shape["dp"], mesh.shape["seq"])),
        mesh=mesh,
        in_specs=placed,
        out_specs=(
            P("dp", "seq", None),
            P("dp", "seq", None),
            P(("dp", "seq")),
            P(("dp", "seq"), None),
            P(("dp", "seq"), None),
            P(("dp", "seq"), None),
            P(("dp", "seq"), None),
            P(("dp", "seq")),
            P(("dp", "seq"), None),
            P(("dp", "seq"), None),
            P(None, ("dp", "seq")),
        ),
        check_vma=False,
    )
```

```python
import functools

import jax
import jax.numpy as jnp
import numpy as np
from jax import lax
from jax.experimental import pallas as pl
from jax.experimental.pallas import tpu as pltpu
from jax.sharding import PartitionSpec as P

LONGEST = 1024
HEADS = 16
FEAT = 16
LANES = 128
GROUP = LANES // FEAT
PIECES = FEAT // 2 + 2
WIDE = PIECES * LANES
PACKED = WIDE // 2 + 16


def dot(left, right, dims=((1,), (0,))):
    return lax.dot_general(left, right, (dims, ((), ())), preferred_element_type=jnp.float32)


def rolls(scaled):
    zero = lax.optimization_barrier(jnp.int32(0))
    row = lax.broadcasted_iota(jnp.int32, (LANES, WIDE), 0) + zero
    column = lax.broadcasted_iota(jnp.int32, (LANES, WIDE), 1)
    d, lane = column // LANES - 1, column % LANES
    a = lane % FEAT
    goal = lane - a + (a + d) % FEAT
    found = (row == goal) & (d >= 0) & ((d < FEAT // 2) | (a < FEAT // 2))
    factor = jnp.where(d == 0, 1 / 32, 1 / 16) if scaled else 1.0
    return jnp.where(found, factor, 0.0).astype(jnp.bfloat16)


def features(rows, factors, lin, axis):
    x = rows.astype(jnp.float32)
    pieces = [x * lin]
    for number in range(PIECES - 1):
        span = slice(number * LANES, (number + 1) * LANES)
        piece = x * (factors[:, span] if axis else factors[span, :])
        if number == PIECES - 2:
            place = lax.broadcasted_iota(jnp.int32, piece.shape, axis)
            piece = jnp.where(place % FEAT == FEAT // 2, 1.0, piece)
        pieces.append(piece)
    return jnp.concatenate([piece.astype(jnp.bfloat16) for piece in pieces], axis=axis)


def turned_features(rows, turned_pick_ref, lin):
    turned = rows.astype(jnp.float32).T.astype(jnp.bfloat16)
    return features(turned, dot(turned_pick_ref[LANES:, :], turned), lin, 0)


def upright_features(rows, pick_ref, lin):
    return features(rows, dot(rows, pick_ref[:, LANES:]), lin, 1)


def head_mask(lanes_per_head, first_head):
    row_head = lax.broadcasted_iota(jnp.int32, (LANES, LANES), 0) // FEAT
    lane_head = lax.broadcasted_iota(jnp.int32, (LANES, LANES), 1) // lanes_per_head + first_head
    return row_head == lane_head


def head_masks(value_dim):
    per = LANES // value_dim
    return [head_mask(value_dim, part * per) for part in range(GROUP // per)]


def low_half():
    return lax.broadcasted_iota(jnp.int32, (LANES, LANES), 1) < LANES // 2


def piece_spans():
    return [slice(number * LANES, (number + 1) * LANES) for number in range(PIECES)]


def fold_heads(rows, masks):
    total = None
    for part, mask in enumerate(masks):
        piece = jnp.where(mask, rows[:, part * LANES : (part + 1) * LANES], 0.0)
        total = piece if total is None else total + piece
    return total + pltpu.roll(total, LANES // 2, 1)


def diagonal():
    row = lax.broadcasted_iota(jnp.int32, (LANES, LANES), 0)
    return row == lax.broadcasted_iota(jnp.int32, (LANES, LANES), 1)


def pack_state(out_ref, pieces):
    low, straight = low_half(), diagonal()
    for number in range(0, PIECES, 2):
        rows = slice(number // 2 * LANES, (number // 2 + 1) * LANES)
        values = jnp.where(low, pieces[number][0], pieces[number + 1][0])
        out_ref[0, 0, rows, :] = values.astype(out_ref.dtype)
    sums = [jnp.sum(jnp.where(straight, s, 0.0), axis=0, keepdims=True) for _, s in pieces]
    sums.append(jnp.zeros((PACKED - WIDE // 2 - PIECES, LANES), jnp.float32))
    out_ref[0, 0, WIDE // 2 :, :] = jnp.concatenate(sums, axis=0).astype(out_ref.dtype)


def spread_state(state_ref, wide_ref, value_dim, sums_of):
    masks, low, straight = head_masks(value_dim), low_half(), diagonal()
    all_sums = state_ref[0, 0, WIDE // 2 :, :].astype(jnp.float32)
    for number, span in enumerate(piece_spans()):
        rows = slice(number // 2 * LANES, (number // 2 + 1) * LANES)
        state = state_ref[0, 0, rows, :].astype(jnp.float32)
        turned = pltpu.roll(state, LANES // 2, 1)
        values = jnp.where(low, turned, state) if number % 2 else jnp.where(low, state, turned)
        sums = jnp.where(straight, all_sums[number : number + 1, :], 0.0)
        sums = jnp.broadcast_to(jnp.sum(sums, axis=1, keepdims=True), (LANES, LANES))
        parts = [jnp.where(mask, values, 0.0) for mask in masks] + sums_of(sums, masks)
        for place, part in enumerate(parts):
            wide_ref[span, slice(place * LANES, (place + 1) * LANES)] = part.astype(jnp.bfloat16)


def own_lanes(array, lanes_per_head, head):
    place = lax.broadcasted_iota(jnp.int32, array.shape, 1) // lanes_per_head
    return jnp.where(place == head, array, jnp.zeros_like(array))


Q, K, V = slice(0, LANES), slice(LANES, 2 * LANES), slice(2 * LANES, None)


def tail_kernel(value_dim, x_ref, seg_ref, pick_ref, out_ref):
    seg = seg_ref[...]
    keep = (seg == seg[-1:, :]).astype(jnp.float32)
    values = (x_ref[:, V].astype(jnp.float32) * keep).astype(jnp.bfloat16)
    ones = jnp.broadcast_to(keep, (seg.shape[0], LANES)).astype(jnp.bfloat16)
    phi = turned_features(x_ref[:, K], pick_ref, 1.0)
    full = dot(phi, jnp.concatenate([values, ones], axis=1))
    width, masks = values.shape[1], head_masks(value_dim)
    pack_state(
        out_ref,
        [(fold_heads(full[span, :width], masks), full[span, width:]) for span in piece_spans()],
    )


def masks_of(seg_ref, seg_row_ref, begin, block):
    stop = begin + block
    rows = begin + lax.broadcasted_iota(jnp.int32, (block, stop), 0)
    columns = lax.broadcasted_iota(jnp.int32, (block, stop), 1)
    same = seg_ref[begin:stop, :] == seg_row_ref[0, :, :stop]
    return ((rows >= columns) & same).astype(jnp.float32)


def near_kernel(value_dim, block, x_ref, seg_ref, seg_row_ref, top_ref, den_ref):
    length = x_ref.shape[0]
    low = lax.broadcasted_iota(jnp.int32, (block, LANES), 1) < value_dim
    for begin in range(0, length, block):
        stop = begin + block
        mask = masks_of(seg_ref, seg_row_ref, begin, block)
        queries = x_ref[begin:stop, Q] * jnp.bfloat16(FEAT ** (-0.5))
        keys = x_ref[:stop, K]
        ones = jnp.ones((stop, LANES), jnp.bfloat16)
        for pair in range(GROUP // 2):
            span = slice(pair * LANES, (pair + 1) * LANES)
            first = 2 * LANES + pair * LANES
            values = jnp.concatenate([x_ref[:stop, first : first + LANES], ones], axis=1)
            sides = []
            for head in (2 * pair, 2 * pair + 1):
                scores = dot(own_lanes(queries, FEAT, head), keys, ((1,), (1,)))
                weights = (((0.5 * scores + 1.0) * scores + 1.0) * mask).astype(jnp.bfloat16)
                sides.append(dot(weights, values))
            top_ref[begin:stop, span] = jnp.where(low, sides[0][:, :LANES], sides[1][:, :LANES])
            den_ref[begin:stop, span] = jnp.where(low, sides[0][:, LANES:], sides[1][:, LANES:])


def far_kernel(value_dim, x_ref, seg_ref, state_ref, top_ref, den_ref, pick_ref, *rest):
    y_ref, inverse_ref, state_wide = rest[-3:]
    width = top_ref.shape[1]
    spread_state(
        state_ref, state_wide, value_dim,
        lambda sums, masks: [jnp.where(mask, sums, 0.0) for mask in masks],
    )
    seg = seg_ref[...]
    keep = (seg == seg[:1, :]).astype(jnp.float32)
    far = dot(upright_features(x_ref[:, Q], pick_ref, FEAT ** (-0.5)), state_wide[...])
    top = top_ref[...] + keep * far[:, :width]
    inverse = 1.0 / (den_ref[...] + keep * far[:, width:])
    y_ref[...] = (top * inverse).astype(y_ref.dtype)
    inverse_ref[...] = inverse


def head_kernel(
    value_dim, x_ref, dy_ref, y_ref, inverse_ref, seg_ref, pick_ref, out_ref, dn_ref, dd_ref
):
    width = dy_ref.shape[1]
    d_top = dy_ref[...].astype(jnp.float32) * inverse_ref[...]
    product = d_top * y_ref[...].astype(jnp.float32)
    large = product.astype(jnp.bfloat16)
    small = (product - large.astype(jnp.float32)).astype(jnp.bfloat16)
    row = lax.broadcasted_iota(jnp.int32, (width, LANES), 0) // value_dim
    lane = lax.broadcasted_iota(jnp.int32, (width, LANES), 1) // FEAT
    adder = jnp.where(row == lane, -1.0, 0.0).astype(jnp.bfloat16)
    d_den = dot(large, adder) + dot(small, adder)
    rounded = d_den.astype(jnp.bfloat16).astype(jnp.float32)
    place = lax.broadcasted_iota(jnp.int32, d_den.shape, 1) % FEAT
    d_den = jnp.where(place < FEAT // 2, rounded, d_den - rounded)
    seg = seg_ref[...]
    keep = (seg == seg[:1, :]).astype(jnp.float32)
    dn_ref[...] = d_top.astype(jnp.bfloat16)
    dd_ref[...] = d_den.astype(jnp.bfloat16)
    d_both = [(d_top * keep).astype(jnp.bfloat16), (d_den * keep).astype(jnp.bfloat16)]
    full = dot(
        turned_features(x_ref[:, Q], pick_ref, FEAT ** (-0.5)), jnp.concatenate(d_both, axis=1)
    )
    masks, own, pieces = head_masks(value_dim), head_mask(FEAT, 0), []
    for span in piece_spans():
        sums = jnp.where(own, full[span, width:], 0.0)
        sums = jnp.sum(sums, axis=1, keepdims=True) * (2 / FEAT)
        pieces.append((fold_heads(full[span, :width], masks), sums))
    pack_state(out_ref, pieces)


def from_features(d_phi, rows, pick_ref, lin):
    x = rows.astype(jnp.float32)
    factors = dot(rows, pick_ref[:, LANES:])
    total, scaled = d_phi[:, :LANES] * lin, []
    for number in range(PIECES - 1):
        span = slice(number * LANES, (number + 1) * LANES)
        piece = d_phi[:, (number + 1) * LANES : (number + 2) * LANES]
        total = total + piece * factors[:, span]
        scaled.append((piece * x).astype(jnp.bfloat16))
    return total + dot(jnp.concatenate(scaled, axis=1), pick_ref[:, LANES:], ((1,), (1,)))


def near_back_kernel(
    value_dim, block, x_ref, dn_ref, dd_ref, seg_ref, seg_row_ref, state_ref, pick_ref,
    dq_ref, dk_ref, dv_ref, state_wide, dq_sum,
):
    length, width = dn_ref.shape
    own = head_mask(FEAT, 0)
    spread_state(
        state_ref, state_wide, value_dim,
        lambda sums, masks: [jnp.where(own, sums, 0.0) * (2 / FEAT)],
    )
    keep = seg_ref[...] == seg_ref[:1, :]
    d_both = jnp.concatenate([dn_ref[...], dd_ref[...]], axis=1)
    d_phi = dot(jnp.where(keep, d_both, jnp.zeros_like(d_both)), state_wide[...], ((1,), (1,)))
    dq_sum[...] = from_features(d_phi, x_ref[:, Q], pick_ref, FEAT ** (-0.5))
    scale = jnp.bfloat16(FEAT ** (-0.5))
    low = lax.broadcasted_iota(jnp.int32, (block, LANES), 1) < value_dim
    for begin in range(0, length, block):
        stop, count = begin + block, length - begin
        key_place = lax.broadcasted_iota(jnp.int32, (block, count), 0)
        query_place = lax.broadcasted_iota(jnp.int32, (block, count), 1)
        same = seg_ref[begin:stop, :] == seg_row_ref[0, :, begin:]
        mask = ((query_place >= key_place) & same).astype(jnp.float32)
        queries = x_ref[begin:, Q] * scale
        keys = x_ref[begin:stop, K]
        dd = dd_ref[begin:, :]
        dk = jnp.zeros((block, LANES), jnp.float32)
        for pair in range(GROUP // 2):
            span = slice(pair * LANES, (pair + 1) * LANES)
            first = 2 * LANES + pair * LANES
            values = x_ref[begin:stop, first : first + LANES]
            dn = dn_ref[begin:, span]
            d_both = jnp.concatenate([dn, dd], axis=1)
            sides = []
            for side in range(2):
                head = 2 * pair + side
                own_keys = own_lanes(keys, FEAT, head)
                ones = own_lanes(jnp.full((block, LANES), 2 / FEAT, jnp.bfloat16), FEAT, head)
                own_values = own_lanes(values, value_dim, side)
                scores = dot(own_keys, queries, ((1,), (1,)))
                weights = (((0.5 * scores + 1.0) * scores + 1.0) * mask).astype(jnp.bfloat16)
                d_weights = dot(
                    jnp.concatenate([own_values, ones], axis=1), d_both, ((1,), (1,))
                )
                d_scores = (d_weights * ((scores + 1.0) * mask)).astype(jnp.bfloat16)
                sides.append(dot(weights, dn))
                dk = dk + own_lanes(dot(d_scores, queries), FEAT, head)
                dq_sum[begin:, :] += dot(d_scores, own_keys * scale, ((0,), (0,)))
            dv_ref[begin:stop, span] = jnp.where(low, sides[0], sides[1])
        dk_ref[begin:stop, :] = dk
    dq_ref[...] = dq_sum[...].astype(dq_ref.dtype)


def far_back_kernel(
    value_dim, x_ref, seg_ref, state_ref, dq_ref, dk_ref, dv_ref, pick_ref, out_ref, state_wide
):
    length, width = dv_ref.shape
    spread_state(state_ref, state_wide, value_dim, lambda sums, masks: [sums * (1 / LANES)])
    seg = seg_ref[...]
    keep = (seg == seg[-1:, :]).astype(jnp.float32)
    keys = x_ref[:, K]
    ones = jnp.ones((length, LANES), jnp.bfloat16)
    d_phi = dot(jnp.concatenate([x_ref[:, V], ones], axis=1), state_wide[...], ((1,), (1,)))
    dk = dk_ref[...] + keep * from_features(d_phi, keys, pick_ref, 1.0)
    dv = dv_ref[...] + keep * dot(upright_features(keys, pick_ref, 1.0), state_wide[:, :width])
    out_ref[:, Q] = dq_ref[...]
    out_ref[:, K] = dk.astype(out_ref.dtype)
    out_ref[:, V] = dv.astype(out_ref.dtype)


class Attention:
    def __init__(self, rows, length, width):
        self.rows, self.length = rows, length
        self.value_dim = width // HEADS
        self.groups = HEADS // GROUP
        self.wide = GROUP * self.value_dim
        self.across = 2 * LANES + self.wide
        self.block = min(256, length)
        self.count = rows * length
        self.scaled, self.plain = rolls(True), rolls(False)
        self.all = range(self.groups)

    def specs(self, groups, own=False):
        first = 0 if own else groups[0]

        def rows_of(columns):
            return pl.BlockSpec((self.length, columns), lambda r, g: (r, first + g))

        return dict(
            x=rows_of(self.across),
            values=rows_of(self.wide),
            narrow=rows_of(LANES),
            seg=pl.BlockSpec((self.length, 1), lambda r, g: (r, 0)),
            seg_row=pl.BlockSpec((1, 1, self.length), lambda r, g: (r, 0, 0)),
            state=pl.BlockSpec((1, 1, PACKED, LANES), lambda r, g: (r, first + g, 0, 0)),
            pick=pl.BlockSpec((LANES, WIDE), lambda r, g: (0, 0)),
            turned_pick=pl.BlockSpec((WIDE, LANES), lambda r, g: (0, 0)),
        )

    def shape(self, columns, dtype, groups):
        return jax.ShapeDtypeStruct((self.count, columns * len(groups)), dtype)

    def state_shape(self, groups):
        return jax.ShapeDtypeStruct((self.rows, len(groups), PACKED, LANES), jnp.bfloat16)

    def wide_state(self, columns):
        return pltpu.VMEM((WIDE, columns), jnp.bfloat16)

    def call(self, kernel, groups, specs, outs, out_specs, scratch, passes, name):
        return pl.pallas_call(
            functools.partial(kernel, self.value_dim),
            grid=(self.rows, len(groups)),
            in_specs=specs,
            out_specs=out_specs,
            out_shape=outs,
            scratch_shapes=scratch,
            compiler_params=pltpu.CompilerParams(
                dimension_semantics=("arbitrary", "arbitrary"), vmem_limit_bytes=56 * 2**20
            ),
            cost_estimate=pl.CostEstimate(
                flops=self.rows * len(groups) * GROUP * passes * 2**26 * self.length // 512,
                bytes_accessed=2**21,
                transcendentals=0,
            ),
            name=name,
        )

    def tail(self, x, seg):
        at = self.specs(self.all)
        return self.call(
            tail_kernel, self.all, [at["x"], at["seg"], at["turned_pick"]],
            self.state_shape(self.all), at["state"], [], 5, "attn_tail",
        )(x, seg, self.plain.T)

    def near(self, x, seg, seg_row):
        def kernel(value_dim, *refs):
            near_kernel(value_dim, self.block, *refs)

        at = self.specs(self.all)
        out = self.shape(self.wide, jnp.float32, self.all)
        return self.call(
            kernel, self.all, [at["x"], at["seg"], at["seg_row"]],
            [out, out], [at["values"]] * 2, [], 8, "attn_near",
        )(x, seg, seg_row)

    def far(self, x, seg, state, top, den):
        at = self.specs(self.all)
        return self.call(
            far_kernel, self.all,
            [at["x"], at["seg"], at["state"], at["values"], at["values"], at["pick"]],
            [self.shape(self.wide, dtype, self.all) for dtype in (jnp.bfloat16, jnp.float32)],
            [at["values"]] * 2, [self.wide_state(2 * self.wide)], 8, "attn_far",
        )(x, seg, state, top, den, self.scaled)

    def head(self, x, dy, y, inverse, seg):
        at = self.specs(self.all)
        return self.call(
            head_kernel, self.all,
            [at["x"], at["values"], at["values"], at["values"], at["seg"], at["turned_pick"]],
            [self.state_shape(self.all), self.shape(self.wide, jnp.bfloat16, self.all),
             self.shape(LANES, jnp.bfloat16, self.all)],
            [at["state"], at["values"], at["narrow"]], [], 5, "attn_head",
        )(x, dy, y, inverse, seg, self.scaled.T)

    def near_back(self, x, dn, dd, seg, seg_row, state, groups):
        def kernel(value_dim, *refs):
            near_back_kernel(value_dim, self.block, *refs)

        at, out = self.specs(groups), self.specs(groups, own=True)
        return self.call(
            kernel, groups,
            [at["x"], at["values"], at["narrow"], at["seg"], at["seg_row"], at["state"],
             at["pick"]],
            [self.shape(LANES, jnp.bfloat16, groups), self.shape(LANES, jnp.float32, groups),
             self.shape(self.wide, jnp.float32, groups)],
            [out["narrow"], out["narrow"], out["values"]],
            [self.wide_state(self.wide + LANES), pltpu.VMEM((self.length, LANES), jnp.float32)],
            24, "attn_near_back",
        )(x, dn, dd, seg, seg_row, state, self.scaled)

    def far_back(self, x, seg, state, dq, dk, dv, groups):
        at, out = self.specs(groups), self.specs(groups, own=True)
        return self.call(
            far_back_kernel, groups,
            [at["x"], at["seg"], at["state"], out["narrow"], out["narrow"], out["values"],
             at["pick"]],
            self.shape(self.across, jnp.bfloat16, groups), out["x"],
            [self.wide_state(self.wide + LANES)], 9, "attn_far_back",
        )(x, seg, state, dq, dk, dv, self.plain)


class Passing:
    def __init__(self, whole, steps, size):
        self.whole, self.steps, self.size = whole, steps, size

    def start(self, own, linked, shift):
        self.own, self.linked, self.left = own, linked, self.steps
        self.pairs = [(i, i + shift) for i in range(self.size) if 0 <= i + shift < self.size]
        self.go(own)

    def go(self, array):
        self.sent, self.left = array, self.left - 1
        self.came = self.pick(self.linked, lax.ppermute(array, "seq", self.pairs))

    @staticmethod
    def pick(flag, array):
        return jnp.where(flag[:, None, None, None], array, jnp.zeros_like(array))

    def rest(self, *hold):
        while self.left:
            came = after(self.came, *hold) if hold else self.came
            self.go(self.own + self.pick(self.whole, came))


epsilon = 1e-05


def against(left, matrix):
    return dot(left, matrix, ((1,), (1,)))


def norm_forward(values):
    scale = lax.rsqrt(jnp.mean(values * values, axis=1, keepdims=True) + epsilon)
    return (scale, values * scale)


def norm_backward(d_scaled, gain, scale, normed):
    d_normed = d_scaled * gain
    return scale * (d_normed - normed * jnp.mean(d_normed * normed, axis=1, keepdims=True))


def fold(count):
    return [0] + list(range(1, count, 2)) + list(range(2, count, 2))[::-1]


class Line:
    def __init__(self, axis, axis_size, stride, count):
        self.axis, self.size, self.stride, self.count = axis, axis_size, stride, count
        self.order = fold(count)

    def send(self, array, steps=1):
        pairs = []
        for index in range(self.size):
            place = (index // self.stride) % self.count
            goal = self.order[(self.order.index(place) + steps) % self.count]
            pairs.append((index, index + (goal - place) * self.stride))
        return lax.ppermute(array, self.axis, pairs)

    def place_back(self, steps):
        own = (lax.axis_index(self.axis) // self.stride) % self.count
        rank = jnp.asarray([self.order.index(p) for p in range(self.count)], jnp.int32)[own]
        return jnp.asarray(self.order, jnp.int32)[(rank - steps) % self.count]


class Slice:
    def __init__(self, dp, seq):
        self.dp, self.seq, self.devices = dp, seq, dp * seq
        self.lines = {
            "z": Line("dp", dp, 2, dp // 2),
            "x": Line("dp", dp, 1, 2),
            "y": Line("seq", seq, 2, seq // 2),
            "c": Line("seq", seq, 1, 2),
        }
        if dp % 4 == 0:
            self.lines["w"] = Line("dp", dp, 4, dp // 4)
            self.lines["u"] = Line("dp", dp, 2, 2)

    def device_of(self, back):
        at = {d: self.lines[d].place_back(back[d]) for d in back}
        z = at["z"] if "z" in at else at["w"] * 2 + at["u"]
        return ((z * 2 + at["x"]) * (self.seq // 2) + at["y"]) * 2 + at["c"]


def after(array, *others):
    return lax.optimization_barrier((array, *others))[0]


def assemble(pieces, widths, block, shape):
    arrays = [array for array, _, _ in pieces]
    dtype = arrays[0].dtype
    places = jnp.stack([shape.device_of(n) for _, names, _ in pieces for n in names])
    copies = sum(len(names) * len(spans) for _, names, spans in pieces)
    windows = [
        (min(span[0] for span in spans), max(span[0] + span[1] for span in spans))
        for _, _, spans in pieces
    ]
    held = [(array.shape[0], high - low) for array, (low, high) in zip(arrays, windows)]

    def kernel(places_ref, *refs):
        piece_refs, refs = refs[: len(pieces)], refs[len(pieces) :]
        out_refs, refs = refs[: len(widths)], refs[len(widths) :]
        buffers, (in_sems, out_sems) = refs[: len(pieces)], refs[len(pieces) :]
        loads = []
        for number, piece_ref in enumerate(piece_refs):
            low, high = windows[number]
            load = pltpu.make_async_copy(
                piece_ref.at[:, pl.ds(low, high - low)], buffers[number], in_sems.at[number]
            )
            load.start()
            loads.append(load)
        stores, begin = [], 0
        for number, (load, (_, names, spans)) in enumerate(zip(loads, pieces)):
            load.wait()
            for i in range(len(names)):
                to = pl.multiple_of(places_ref[begin + i] * block, block)
                for low, width, output, column in spans:
                    store = pltpu.make_async_copy(
                        buffers[number].at[pl.ds(i * block, block), pl.ds(low - windows[number][0], width)],
                        out_refs[output].at[pl.ds(to, block), pl.ds(column, width)],
                        out_sems.at[len(stores)],
                    )
                    store.start()
                    stores.append(store)
            begin += len(names)
        for store in stores:
            store.wait()

    size = sum(tall * wide for tall, wide in held) * dtype.itemsize
    return pl.pallas_call(
        kernel,
        out_shape=[jax.ShapeDtypeStruct((shape.devices * block, w), dtype) for w in widths],
        in_specs=[pl.BlockSpec(memory_space=pltpu.SMEM)]
        + [pl.BlockSpec(memory_space=pl.ANY)] * len(pieces),
        out_specs=[pl.BlockSpec(memory_space=pl.ANY)] * len(widths),
        scratch_shapes=[pltpu.VMEM(size, dtype) for size in held]
        + [
            pltpu.SemaphoreType.DMA((len(pieces),)),
            pltpu.SemaphoreType.DMA((copies,)),
        ],
        cost_estimate=pl.CostEstimate(flops=0, bytes_accessed=2 * size, transcendentals=0),
        name="assemble",
    )(places, *arrays)


class Gathering:
    def __init__(self, shape, array, names=None):
        self.shape, self.array = shape, array
        self.names = names or [dict(z=0, x=0, y=0, c=0)]

    def came(self, dim, direct=False, hold=()):
        line, array, out = self.shape.lines[dim], self.array, []
        for step in range(1, line.count):
            array = line.send(self.array, step) if direct else line.send(array)
            if step <= len(hold):
                array = after(array, *hold[step - 1])
            out.append((array, [dict(n, **{dim: step}) for n in self.names]))
        return out

    def along(self, dim, direct=False, hold=()):
        came = self.came(dim, direct, hold)
        array = jnp.concatenate([self.array] + [a for a, _ in came], 0)
        return Gathering(self.shape, array, self.names + [n for _, names in came for n in names])

    def columns(self, low, high):
        return Gathering(self.shape, self.array[:, low:high], self.names)

    def pieces(self, dim, spans):
        found = [(self.array, self.names)] + self.came(dim)
        return [(array, names, spans) for array, names in found]


def spans_of(low, high, homes):
    spans = []
    for begin, width, output, column in homes:
        first, last = max(low, begin), min(high, begin + width)
        if first < last:
            spans.append((first - low, last - first, output, column + first - begin))
    return spans


def side_by_side(widths):
    return [(sum(widths[:i]), width, i, 0) for i, width in enumerate(widths)]


class TwoWays:
    def __init__(self, parts, shape, homes=None, widths=None):
        own = [part.shape[1] for part in parts]
        self.homes, self.widths = homes or side_by_side(own), widths or own
        self.block, self.shape = parts[0].shape[0], shape
        self.columns = sum(own)
        self.cut = -(-self.columns // 2 // LANES) * LANES
        self.held = Gathering(shape, jnp.concatenate(parts, axis=1))

    def first(self, *hold):
        self.held = self.held.along("z", True, [hold] * 8 if hold else ())

    def second(self, *hold):
        hold = [hold] if hold else ()
        self.one = self.held.columns(0, self.cut).along("x", False, hold)
        self.two = self.held.columns(self.cut, self.columns).along("y", False, hold)

    def third(self, *hold):
        hold = [hold] if hold else ()
        self.one, self.two = self.one.along("y", False, hold), self.two.along("x", False, hold)

    def last(self):
        self.ends = [self.one.came("c"), self.two.came("c")]

    def output(self, *outputs):
        homes = [(b, w, outputs.index(o), c) for b, w, o, c in self.homes if o in outputs]
        pieces = []
        for half, low, high, came in (
            (self.one, 0, self.cut, self.ends[0]),
            (self.two, self.cut, self.columns, self.ends[1]),
        ):
            spans = spans_of(low, high, homes)
            found = [(half.array, half.names)] + came
            pieces += [(array, names, spans) for array, names in found if spans]
        return assemble(pieces, [self.widths[o] for o in outputs], self.block, self.shape)


LAYOUT = "cyxwu"


def picker(shape, width):
    block = width // shape.devices
    if block % 16:
        order = jnp.arange(width)
    else:
        names = [dict()]
        for dim in LAYOUT:
            names = [dict(n, **{dim: s}) for n in names for s in range(shape.lines[dim].count)]
        places = jnp.stack([shape.device_of(n) for n in names])
        order = (places[:, None] * block + jnp.arange(block)[None, :]).reshape(width)
    return (jnp.arange(width)[:, None] == order[None, :]).astype(jnp.bfloat16)


def turned_rows(pick, left):
    return dot(pick, left, ((0,), (1,))).astype(jnp.bfloat16)


class Scattering:
    def __init__(self, shape, kept, arrived):
        half, columns = kept.shape
        self.shape, self.dims = shape, LAYOUT[1:]
        form = [shape.lines[d].count for d in self.dims] + [2 * half // shape.devices, columns]
        self.parts = [[kept.reshape(form), arrived.reshape(form)]]

    def beside(self, other):
        self.parts = self.parts + other.parts
        return self

    def term_of(self, step):
        found = []
        for terms in self.parts:
            own = [lax.index_in_dim(t, step, self.axis, False) for t in terms]
            found.append(functools.reduce(jnp.add, [t.astype(jnp.float32) for t in own]))
        return jnp.concatenate(found, axis=-1)

    def start(self, dim, *hold):
        self.line, self.axis, self.step = self.shape.lines[dim], self.dims.index(dim), 1
        self.dims = self.dims.replace(dim, "")
        if hold:
            self.parts = [[after(t, *hold) for t in terms] for terms in self.parts]
        self.sent = self.term_of(1).astype(jnp.bfloat16)
        self.came = self.line.send(self.sent)
        return self

    def advance(self, *hold):
        came = after(self.came, *hold) if hold else self.came
        self.step += 1
        total = self.term_of(self.step % self.line.count) + came.astype(jnp.float32)
        if self.step < self.line.count:
            self.sent = total.astype(jnp.bfloat16)
            self.came = self.line.send(self.sent)
        else:
            self.parts, self.came = [[total]], None
        return self

    def along(self, dim):
        self.start(dim)
        while self.came is not None:
            self.advance()
        return self


def scatter_whole(kept, sent):
    whole = jnp.concatenate([kept, sent], 0).astype(jnp.float32)
    return lax.psum_scatter(whole, ("dp", "seq"), scatter_dimension=0, tiled=True)


FF_TILE = 256


def mlp_kernel(
    block, begins, ends, a_ref, g_ref, at_ref, gt_ref, gate_ref, up_ref, down_ref, *refs
):
    if not begins:
        y_in_ref, da_in_ref, *refs = refs
    if ends:
        x_ref, gain_ref, y_ref, dxo_ref, da_sum, kept_ref, sent_ref, *refs, y_sum = refs
    else:
        y_sum, da_sum, kept_ref, sent_ref, *refs = refs
    hidden_ref, d_gate_ref, d_up_ref = refs
    count = a_ref.shape[0]
    step = pl.program_id(0)

    @pl.when(step == 0)
    def _():
        y_sum[...] = jnp.zeros_like(y_sum) if begins else y_in_ref[...]
        da_sum[...] = jnp.zeros_like(da_sum) if begins else da_in_ref[...]

    for begin in range(0, count, block):
        span = slice(begin, begin + block)
        a, g = a_ref[span, :], g_ref[span, :]
        gate, up = dot(a, gate_ref[...]), dot(a, up_ref[...])
        d_hidden = dot(g, down_ref[...])
        sigma = jax.nn.sigmoid(gate)
        silu = gate * sigma
        hidden = (silu * up).astype(jnp.bfloat16)
        d_gate = (d_hidden * up * (sigma + silu * (1.0 - sigma))).astype(jnp.bfloat16)
        d_up = (d_hidden * silu).astype(jnp.bfloat16)
        hidden_ref[span, :], d_gate_ref[span, :], d_up_ref[span, :] = hidden, d_gate, d_up
        y_sum[span, :] += dot(hidden, down_ref[...], ((1,), (1,)))
        da_sum[span, :] += dot(d_gate, gate_ref[...], ((1,), (1,))) + dot(
            d_up, up_ref[...], ((1,), (1,))
        )
    half = at_ref.shape[0] // 2
    for number, (left, right) in enumerate(
        ((at_ref, d_gate_ref), (at_ref, d_up_ref), (gt_ref, hidden_ref))
    ):
        kept_ref[number] = dot(left[:half, :], right[...]).astype(jnp.bfloat16)
        sent_ref[number] = dot(left[half:, :], right[...]).astype(jnp.bfloat16)
    if not ends:
        return

    @pl.when(step == pl.num_programs(0) - 1)
    def _():
        for begin in range(0, count, block):
            span = slice(begin, begin + block)
            x = x_ref[span, :]
            y_ref[span, :] = (x + y_sum[span, :]).astype(y_ref.dtype)
            scale = lax.rsqrt(jnp.mean(x * x, axis=1, keepdims=True) + epsilon)
            normed = x * scale
            d_normed = da_sum[span, :] * gain_ref[...]
            mean = jnp.mean(d_normed * normed, axis=1, keepdims=True)
            dx = g_ref[span, :].astype(jnp.float32) + scale * (d_normed - normed * mean)
            da_sum[span, :] = dx
            dxo_ref[span, :] = dx.astype(dxo_ref.dtype)


def feed_forward(a, g, a_turned, g_turned, weights, tiles, sums=None, ending=None):
    count, width = a.shape
    half = width // 2

    def held(rows, columns):
        return pl.BlockSpec((rows, columns), lambda j: (0, 0), pipeline_mode=pl.Buffered(1))

    def tile(first):
        return pl.BlockSpec((width, FF_TILE), lambda j: (0, first + j))

    def shape(dtype):
        return jax.ShapeDtypeStruct((count, width), dtype)

    full = held(count, width)
    given = [a, g, a_turned, g_turned] + [array for array, _ in weights]
    specs = [full, full] + [held(width, count)] * 2 + [tile(first) for _, first in weights]
    scratch = [pltpu.VMEM((count, FF_TILE), jnp.bfloat16)] * 3
    if sums is not None:
        given, specs = given + list(sums), specs + [full] * 2
    if ending is not None:
        given, specs = given + list(ending), specs + [full, held(1, width)]
        outs = [shape(jnp.bfloat16), shape(jnp.bfloat16), shape(jnp.float32)]
        scratch = scratch + [pltpu.VMEM((count, width), jnp.float32)]
    else:
        outs = [shape(jnp.float32)] * 2
    hidden = tiles * FF_TILE
    return pl.pallas_call(
        functools.partial(mlp_kernel, min(512, count), sums is None, ending is not None),
        grid=(tiles,),
        in_specs=specs,
        out_specs=[full] * len(outs)
        + [pl.BlockSpec((3, half, FF_TILE), lambda j: (0, 0, j))] * 2,
        out_shape=outs + [jax.ShapeDtypeStruct((3, half, hidden), jnp.bfloat16)] * 2,
        scratch_shapes=scratch,
        compiler_params=pltpu.CompilerParams(
            dimension_semantics=("arbitrary",), vmem_limit_bytes=60 * 2**20
        ),
        cost_estimate=pl.CostEstimate(
            flops=18 * count * width * hidden,
            bytes_accessed=12 * width * hidden + 20 * count * width,
            transcendentals=count * hidden,
        ),
        name="mlp",
    )(*given)


def gain_gradient(weights, gradients, gain):
    products = jnp.sum(weights.astype(jnp.float32) * gradients, axis=1)
    return products / gain.astype(jnp.float32)


def per_device(
    shape,
    layer_input,
    segment_ids,
    gain_attn,
    w_query,
    w_key,
    w_value,
    w_out,
    gain_mlp,
    w_gate,
    w_up,
    w_down,
    grad_output,
):
    rows, shard_len, width = layer_input.shape
    count = rows * shard_len
    narrow, hidden = HEADS * FEAT, w_gate.shape[1]
    attention = Attention(rows, shard_len, width)
    groups, wide, across = attention.groups, attention.wide, attention.across
    gains = jnp.pad(jnp.stack([gain_attn, gain_mlp], axis=1), ((0, 0), (0, LANES - 2)))
    first_parts = [w_query, w_key, w_value, gains]
    homes, grouped = [], []
    for g in range(groups):
        for part, begin, size, place in (
            (w_query, 0, LANES, 0),
            (w_key, narrow, LANES, LANES),
            (w_value, 2 * narrow, wide, 2 * LANES),
        ):
            homes.append((begin + g * size, size, 0, g * across + place))
            grouped.append(part[:, g * size : (g + 1) * size])
    homes.append((groups * across, LANES, 0, groups * across))
    spare = ((0, 0), (0, -hidden % FF_TILE))
    gate_part, up_part, down_part = (
        jnp.pad(part, spare) for part in (w_gate, w_up, w_down.T)
    )
    tiles = gate_part.shape[1] // FF_TILE
    ringed = gains.shape[0] % 16 == 0
    if ringed:
        early = TwoWays(first_parts, shape, homes, [groups * across + LANES])
        rest = TwoWays([gate_part, w_out, up_part], shape)
        early.first()
        early.second()
        early.third()
        begun = [early.one.array, early.two.array]
        rest.first(*begun)
        down = Gathering(shape, down_part).along("x", False, [begun])
        early.last()
        (gathered,) = early.output(0)
    else:
        first_part = jnp.concatenate(grouped + [gains], axis=1)
        gathered, out_w, gate_w, up_w, down_w = (
            lax.all_gather(part, ("dp", "seq"), axis=0, tiled=True)
            for part in (first_part, w_out, gate_part, up_part, down_part)
        )
    qkv_w = gathered[:, : groups * across]
    gain_one = gathered[:, groups * across].astype(jnp.float32)[None, :]
    gain_two = gathered[:, groups * across + 1].astype(jnp.float32)[None, :]

    pick = picker(shape, width)
    cotangent = grad_output.reshape(count, width)
    tokens = layer_input.reshape(count, width).astype(jnp.float32)
    scale_one, normed_one = norm_forward(tokens)
    a_one = (normed_one * gain_one).astype(jnp.bfloat16)
    a_one = after(a_one, rest.held.array, down.array) if ringed else a_one
    qkv = jnp.dot(a_one, qkv_w, preferred_element_type=jnp.float32).astype(jnp.bfloat16)
    place = lax.axis_index("seq")
    own_seg = lax.dynamic_slice_in_dim(segment_ids, place * shard_len, shard_len, 1)
    before = jnp.maximum(place * shard_len - 1, 0)
    behind = jnp.minimum((place + 1) * shard_len, segment_ids.shape[1] - 1)
    first, last = own_seg[:, 0], own_seg[:, -1]
    from_before = lax.dynamic_index_in_dim(segment_ids, before, 1, keepdims=False) == first
    from_behind = lax.dynamic_index_in_dim(segment_ids, behind, 1, keepdims=False) == last
    seg, seg_row = own_seg.reshape(count, 1), own_seg.reshape(rows, 1, shard_len)
    reach = min(shape.seq - 1, -(-(LONGEST - 1) // shard_len))
    states = Passing(first == last, reach, shape.seq)
    tail = attention.tail(qkv, seg)
    if ringed:
        rest.second(tail)
        down = down.along("y", False, [[tail]])
        states.start(tail, from_before, 1)
        top, den = attention.near(
            after(qkv, states.sent, rest.one.array, rest.two.array, down.array), seg, seg_row
        )
        states.rest(den)
        rest.third(den, states.sent)
        rest.last()
        down = down.along("z", False, [[den], [rest.one.array, rest.two.array]])
        down_ends = down.pieces("c", [(0, tiles * FF_TILE, 0, 0)])
        earlier = after(states.came, rest.one.array, rest.two.array)
        mixed_cat, inverse = attention.far(qkv, seg, earlier, top, den)
        (out_w,) = rest.output(1)
    else:
        states.start(tail, from_before, 1)
        states.rest()
        earlier = states.came
        top, den = attention.near(qkv, seg, seg_row)
        mixed_cat, inverse = attention.far(qkv, seg, earlier, top, den)
    x_two = tokens + jnp.dot(mixed_cat, out_w, preferred_element_type=jnp.float32)
    scale_two, normed_two = norm_forward(x_two)
    a_two = (normed_two * gain_two).astype(jnp.bfloat16)
    if ringed:
        gate_w, up_w = rest.output(0, 2)
        (down_w,) = assemble(down_ends, [tiles * FF_TILE], down_part.shape[0], shape)
    result, d_branch, d_x_two, kept, sent = feed_forward(
        a_two,
        cotangent,
        turned_rows(pick, a_two),
        turned_rows(pick, cotangent),
        [(gate_w, 0), (up_w, 0), (down_w, 0)],
        tiles,
        None,
        (x_two, gain_two),
    )
    turned_mixed, turned_one = turned_rows(pick, mixed_cat), turned_rows(pick, a_one)
    half = width // 2
    out_kept, out_sent = (
        dot(t, d_branch).astype(jnp.bfloat16) for t in (turned_mixed[:half], turned_mixed[half:])
    )
    d_mixed = against(d_branch, out_w).astype(jnp.bfloat16)
    d_qkv, grad_qkv = [], []
    if ringed:
        send_core = shape.lines["c"].send
        arrived, out_arrived = send_core(sent), send_core(out_sent)
        d_mixed = after(d_mixed, out_sent, out_kept)
        ahead, d_top, d_den = attention.head(qkv, d_mixed, mixed_cat, inverse, seg)
        states.start(ahead, from_behind, -1)
        arrived = after(arrived, ahead)
        gate_sum, up_sum, down_sum = (Scattering(shape, kept[i], arrived[i]) for i in range(3))
        gate_sum.beside(Scattering(shape, out_kept, out_arrived)).start("y")
        up_sum.start("x")
        down_sum.start("u")
        d_top = after(d_top, states.sent, gate_sum.sent, up_sum.sent, down_sum.sent)
        d_near = [None, None]
        d_near[0] = attention.near_back(qkv, d_top, d_den, seg, seg_row, earlier, range(0, 1))
        states.rest(d_near[0][0])
        d_top = after(d_top, states.sent, d_near[0][0])
        d_near[1] = attention.near_back(qkv, d_top, d_den, seg, seg_row, earlier, range(1, 2))
        near = d_near[1][0]
        down_sum.advance(near).start("w")
        gate_sum.advance(near).start("x")
        up_sum.advance(near).start("y")
        later = after(states.came, near, down_sum.sent, gate_sum.sent, up_sum.sent)

        turned = [turned_one[:half], turned_one[half:]]

        def products(right):
            own_sent = dot(turned[1], right).astype(jnp.bfloat16)
            own_kept = dot(turned[0], right).astype(jnp.bfloat16)
            own_sum = Scattering(shape, own_kept, send_core(own_sent))
            own_sum.sent = own_sent
            return own_sum

        far = attention.far_back(qkv, seg, later, *d_near[0], range(0, 1))
        d_qkv.append(far)
        qkv_a = products(far)
        later = after(later, qkv_a.sent)
        far = attention.far_back(qkv, seg, later, *d_near[1], range(1, 2))
        d_qkv.append(far)
        qkv_a.start("y", far)
        qkv_b = products(after(far, qkv_a.sent))
        down_sum.advance(qkv_b.sent).start("x")
        both = gate_sum.advance(qkv_b.sent).beside(up_sum.advance(qkv_b.sent)).start("u")
        qkv_b.start("x", both.sent)
        qkv_a.advance(both.sent).start("x")
        down_sum.advance(both.sent).start("y")
        qkv_b.advance().start("y")
        both.advance(qkv_b.sent).start("w")
        qkv_sum = qkv_a.advance(qkv_b.sent).beside(qkv_b.advance()).start("u")
        down_sum.advance(both.sent)
        qkv_sum.advance().start("w")
        both.advance()
        qkv_sum.advance()
        grad_qkv, both, down_sum = (part.parts[0][0] for part in (qkv_sum, both, down_sum))
        grad_qkv = [grad_qkv[:, g * across : (g + 1) * across] for g in range(groups)]
        padded = tiles * FF_TILE
        grad_gate, grad_out = both[:, :hidden], both[:, padded : padded + width]
        grad_up = both[:, padded + width : padded + width + hidden]
        grad_down = down_sum[:, :hidden]
    else:
        ahead, d_top, d_den = attention.head(qkv, d_mixed, mixed_cat, inverse, seg)
        states.start(ahead, from_behind, -1)
        states.rest()
        grad_gate, grad_up, grad_down = (
            scatter_whole(kept[i], sent[i])[:, :hidden] for i in range(3)
        )
        grad_out = scatter_whole(out_kept, out_sent)
        for g in range(groups):
            only = range(g, g + 1)
            d_near = attention.near_back(qkv, d_top, d_den, seg, seg_row, earlier, only)
            d_qkv.append(attention.far_back(qkv, seg, states.came, *d_near, only))
            grad_qkv.append(
                scatter_whole(dot(turned_one[:half], d_qkv[g]), dot(turned_one[half:], d_qkv[g]))
            )
    d_a_one = None
    for g in range(groups):
        term = against(d_qkv[g], qkv_w[:, g * across : (g + 1) * across])
        d_a_one = term if d_a_one is None else d_a_one + term
    d_tokens = d_x_two + norm_backward(d_a_one, gain_one, scale_one, normed_one)
    return (
        result.reshape(rows, shard_len, width),
        d_tokens.reshape(rows, shard_len, width),
        gain_gradient(jnp.concatenate(grouped, axis=1), jnp.concatenate(grad_qkv, axis=1), gain_attn),
        jnp.concatenate([part[:, Q] for part in grad_qkv], axis=1),
        jnp.concatenate([part[:, K] for part in grad_qkv], axis=1),
        jnp.concatenate([part[:, V] for part in grad_qkv], axis=1),
        grad_out,
        gain_gradient(
            jnp.concatenate([w_gate, w_up], axis=1),
            jnp.concatenate([grad_gate, grad_up], axis=1),
            gain_mlp,
        ),
        grad_gate,
        grad_up,
        grad_down.T,
    )


def solution(mesh):
    placed = (
        P("dp", "seq", None),
        P("dp", None),
        P(("dp", "seq")),
        P(("dp", "seq"), None),
        P(("dp", "seq"), None),
        P(("dp", "seq"), None),
        P(("dp", "seq"), None),
        P(("dp", "seq")),
        P(("dp", "seq"), None),
        P(("dp", "seq"), None),
        P(None, ("dp", "seq")),
        P("dp", "seq", None),
    )
    return jax.shard_map(
        functools.partial(per_device, Slice(mesh.shape["dp"], mesh.shape["seq"])),
        mesh=mesh,
        in_specs=placed,
        out_specs=(
            P("dp", "seq", None),
            P("dp", "seq", None),
            P(("dp", "seq")),
            P(("dp", "seq"), None),
            P(("dp", "seq"), None),
            P(("dp", "seq"), None),
            P(("dp", "seq"), None),
            P(("dp", "seq")),
            P(("dp", "seq"), None),
            P(("dp", "seq"), None),
            P(None, ("dp", "seq")),
        ),
        check_vma=False,
    )
```

```python
import functools

import jax
import jax.numpy as jnp
import numpy as np
from jax import lax
from jax.experimental import pallas as pl
from jax.experimental.pallas import tpu as pltpu
from jax.sharding import PartitionSpec as P

LONGEST = 1024
HEADS = 16
FEAT = 16
LANES = 128
GROUP = LANES // FEAT
PIECES = FEAT // 2 + 2
WIDE = PIECES * LANES
PACKED = WIDE // 2 + 16


def dot(left, right, dims=((1,), (0,))):
    return lax.dot_general(left, right, (dims, ((), ())), preferred_element_type=jnp.float32)


def rolls(scaled):
    zero = lax.optimization_barrier(jnp.int32(0))
    row = lax.broadcasted_iota(jnp.int32, (LANES, WIDE), 0) + zero
    column = lax.broadcasted_iota(jnp.int32, (LANES, WIDE), 1)
    d, lane = column // LANES - 1, column % LANES
    a = lane % FEAT
    goal = lane - a + (a + d) % FEAT
    found = (row == goal) & (d >= 0) & ((d < FEAT // 2) | (a < FEAT // 2))
    factor = jnp.where(d == 0, 1 / 32, 1 / 16) if scaled else 1.0
    return jnp.where(found, factor, 0.0).astype(jnp.bfloat16)


def features(rows, factors, lin, axis):
    x = rows.astype(jnp.float32)
    pieces = [x * lin]
    for number in range(PIECES - 1):
        span = slice(number * LANES, (number + 1) * LANES)
        piece = x * (factors[:, span] if axis else factors[span, :])
        if number == PIECES - 2:
            place = lax.broadcasted_iota(jnp.int32, piece.shape, axis)
            piece = jnp.where(place % FEAT == FEAT // 2, 1.0, piece)
        pieces.append(piece)
    return jnp.concatenate([piece.astype(jnp.bfloat16) for piece in pieces], axis=axis)


def turned_features(rows, turned_pick_ref, lin):
    turned = rows.astype(jnp.float32).T.astype(jnp.bfloat16)
    return features(turned, dot(turned_pick_ref[LANES:, :], turned), lin, 0)


def upright_features(rows, pick_ref, lin):
    return features(rows, dot(rows, pick_ref[:, LANES:]), lin, 1)


def head_mask(lanes_per_head, first_head):
    row_head = lax.broadcasted_iota(jnp.int32, (LANES, LANES), 0) // FEAT
    lane_head = lax.broadcasted_iota(jnp.int32, (LANES, LANES), 1) // lanes_per_head + first_head
    return row_head == lane_head


def head_masks(value_dim):
    per = LANES // value_dim
    return [head_mask(value_dim, part * per) for part in range(GROUP // per)]


def low_half():
    return lax.broadcasted_iota(jnp.int32, (LANES, LANES), 1) < LANES // 2


def piece_spans():
    return [slice(number * LANES, (number + 1) * LANES) for number in range(PIECES)]


def fold_heads(rows, masks):
    total = None
    for part, mask in enumerate(masks):
        piece = jnp.where(mask, rows[:, part * LANES : (part + 1) * LANES], 0.0)
        total = piece if total is None else total + piece
    return total + pltpu.roll(total, LANES // 2, 1)


def diagonal():
    row = lax.broadcasted_iota(jnp.int32, (LANES, LANES), 0)
    return row == lax.broadcasted_iota(jnp.int32, (LANES, LANES), 1)


def pack_state(out_ref, pieces):
    low, straight = low_half(), diagonal()
    for number in range(0, PIECES, 2):
        rows = slice(number // 2 * LANES, (number // 2 + 1) * LANES)
        values = jnp.where(low, pieces[number][0], pieces[number + 1][0])
        out_ref[0, 0, rows, :] = values.astype(out_ref.dtype)
    sums = [jnp.sum(jnp.where(straight, s, 0.0), axis=0, keepdims=True) for _, s in pieces]
    sums.append(jnp.zeros((PACKED - WIDE // 2 - PIECES, LANES), jnp.float32))
    out_ref[0, 0, WIDE // 2 :, :] = jnp.concatenate(sums, axis=0).astype(out_ref.dtype)


def spread_state(state_ref, wide_ref, value_dim, sums_of):
    masks, low, straight = head_masks(value_dim), low_half(), diagonal()
    all_sums = state_ref[0, 0, WIDE // 2 :, :].astype(jnp.float32)
    for number, span in enumerate(piece_spans()):
        rows = slice(number // 2 * LANES, (number // 2 + 1) * LANES)
        state = state_ref[0, 0, rows, :].astype(jnp.float32)
        turned = pltpu.roll(state, LANES // 2, 1)
        values = jnp.where(low, turned, state) if number % 2 else jnp.where(low, state, turned)
        sums = jnp.where(straight, all_sums[number : number + 1, :], 0.0)
        sums = jnp.broadcast_to(jnp.sum(sums, axis=1, keepdims=True), (LANES, LANES))
        parts = [jnp.where(mask, values, 0.0) for mask in masks] + sums_of(sums, masks)
        for place, part in enumerate(parts):
            wide_ref[span, slice(place * LANES, (place + 1) * LANES)] = part.astype(jnp.bfloat16)


def own_lanes(array, lanes_per_head, head):
    place = lax.broadcasted_iota(jnp.int32, array.shape, 1) // lanes_per_head
    return jnp.where(place == head, array, jnp.zeros_like(array))


Q, K, V = slice(0, LANES), slice(LANES, 2 * LANES), slice(2 * LANES, None)


def tail_kernel(value_dim, x_ref, seg_ref, pick_ref, out_ref):
    seg = seg_ref[...]
    keep = (seg == seg[-1:, :]).astype(jnp.float32)
    values = (x_ref[:, V].astype(jnp.float32) * keep).astype(jnp.bfloat16)
    ones = jnp.broadcast_to(keep, (seg.shape[0], LANES)).astype(jnp.bfloat16)
    phi = turned_features(x_ref[:, K], pick_ref, 1.0)
    full = dot(phi, jnp.concatenate([values, ones], axis=1))
    width, masks = values.shape[1], head_masks(value_dim)
    pack_state(
        out_ref,
        [(fold_heads(full[span, :width], masks), full[span, width:]) for span in piece_spans()],
    )


def masks_of(seg_ref, seg_row_ref, begin, block):
    stop = begin + block
    rows = begin + lax.broadcasted_iota(jnp.int32, (block, stop), 0)
    columns = lax.broadcasted_iota(jnp.int32, (block, stop), 1)
    same = seg_ref[begin:stop, :] == seg_row_ref[0, :, :stop]
    return ((rows >= columns) & same).astype(jnp.float32)


def near_kernel(value_dim, block, x_ref, seg_ref, seg_row_ref, top_ref, den_ref):
    length = x_ref.shape[0]
    low = lax.broadcasted_iota(jnp.int32, (block, LANES), 1) < value_dim
    for begin in range(0, length, block):
        stop = begin + block
        mask = masks_of(seg_ref, seg_row_ref, begin, block)
        queries = x_ref[begin:stop, Q] * jnp.bfloat16(FEAT ** (-0.5))
        keys = x_ref[:stop, K]
        ones = jnp.ones((stop, LANES), jnp.bfloat16)
        for pair in range(GROUP // 2):
            span = slice(pair * LANES, (pair + 1) * LANES)
            first = 2 * LANES + pair * LANES
            values = jnp.concatenate([x_ref[:stop, first : first + LANES], ones], axis=1)
            sides = []
            for head in (2 * pair, 2 * pair + 1):
                scores = dot(own_lanes(queries, FEAT, head), keys, ((1,), (1,)))
                weights = (((0.5 * scores + 1.0) * scores + 1.0) * mask).astype(jnp.bfloat16)
                sides.append(dot(weights, values))
            top_ref[begin:stop, span] = jnp.where(low, sides[0][:, :LANES], sides[1][:, :LANES])
            den_ref[begin:stop, span] = jnp.where(low, sides[0][:, LANES:], sides[1][:, LANES:])


def far_kernel(value_dim, x_ref, seg_ref, state_ref, top_ref, den_ref, pick_ref, *rest):
    y_ref, inverse_ref, state_wide = rest[-3:]
    width = top_ref.shape[1]
    spread_state(
        state_ref, state_wide, value_dim,
        lambda sums, masks: [jnp.where(mask, sums, 0.0) for mask in masks],
    )
    seg = seg_ref[...]
    keep = (seg == seg[:1, :]).astype(jnp.float32)
    far = dot(upright_features(x_ref[:, Q], pick_ref, FEAT ** (-0.5)), state_wide[...])
    top = top_ref[...] + keep * far[:, :width]
    inverse = 1.0 / (den_ref[...] + keep * far[:, width:])
    y_ref[...] = (top * inverse).astype(y_ref.dtype)
    inverse_ref[...] = inverse


def head_kernel(
    value_dim, x_ref, dy_ref, y_ref, inverse_ref, seg_ref, pick_ref, out_ref, dn_ref, dd_ref
):
    width = dy_ref.shape[1]
    d_top = dy_ref[...].astype(jnp.float32) * inverse_ref[...]
    product = d_top * y_ref[...].astype(jnp.float32)
    large = product.astype(jnp.bfloat16)
    small = (product - large.astype(jnp.float32)).astype(jnp.bfloat16)
    row = lax.broadcasted_iota(jnp.int32, (width, LANES), 0) // value_dim
    lane = lax.broadcasted_iota(jnp.int32, (width, LANES), 1) // FEAT
    adder = jnp.where(row == lane, -1.0, 0.0).astype(jnp.bfloat16)
    d_den = dot(large, adder) + dot(small, adder)
    rounded = d_den.astype(jnp.bfloat16).astype(jnp.float32)
    place = lax.broadcasted_iota(jnp.int32, d_den.shape, 1) % FEAT
    d_den = jnp.where(place < FEAT // 2, rounded, d_den - rounded)
    seg = seg_ref[...]
    keep = (seg == seg[:1, :]).astype(jnp.float32)
    dn_ref[...] = d_top.astype(jnp.bfloat16)
    dd_ref[...] = d_den.astype(jnp.bfloat16)
    d_both = [(d_top * keep).astype(jnp.bfloat16), (d_den * keep).astype(jnp.bfloat16)]
    full = dot(
        turned_features(x_ref[:, Q], pick_ref, FEAT ** (-0.5)), jnp.concatenate(d_both, axis=1)
    )
    masks, own, pieces = head_masks(value_dim), head_mask(FEAT, 0), []
    for span in piece_spans():
        sums = jnp.where(own, full[span, width:], 0.0)
        sums = jnp.sum(sums, axis=1, keepdims=True) * (2 / FEAT)
        pieces.append((fold_heads(full[span, :width], masks), sums))
    pack_state(out_ref, pieces)


def from_features(d_phi, rows, pick_ref, lin):
    x = rows.astype(jnp.float32)
    factors = dot(rows, pick_ref[:, LANES:])
    total, scaled = d_phi[:, :LANES] * lin, []
    for number in range(PIECES - 1):
        span = slice(number * LANES, (number + 1) * LANES)
        piece = d_phi[:, (number + 1) * LANES : (number + 2) * LANES]
        total = total + piece * factors[:, span]
        scaled.append((piece * x).astype(jnp.bfloat16))
    return total + dot(jnp.concatenate(scaled, axis=1), pick_ref[:, LANES:], ((1,), (1,)))


def near_back_kernel(
    value_dim, block, x_ref, dn_ref, dd_ref, seg_ref, seg_row_ref, state_ref, pick_ref,
    dq_ref, dk_ref, dv_ref, state_wide, dq_sum,
):
    length, width = dn_ref.shape
    own = head_mask(FEAT, 0)
    spread_state(
        state_ref, state_wide, value_dim,
        lambda sums, masks: [jnp.where(own, sums, 0.0) * (2 / FEAT)],
    )
    keep = seg_ref[...] == seg_ref[:1, :]
    d_both = jnp.concatenate([dn_ref[...], dd_ref[...]], axis=1)
    d_phi = dot(jnp.where(keep, d_both, jnp.zeros_like(d_both)), state_wide[...], ((1,), (1,)))
    dq_sum[...] = from_features(d_phi, x_ref[:, Q], pick_ref, FEAT ** (-0.5))
    scale = jnp.bfloat16(FEAT ** (-0.5))
    low = lax.broadcasted_iota(jnp.int32, (block, LANES), 1) < value_dim
    for begin in range(0, length, block):
        stop, count = begin + block, length - begin
        key_place = lax.broadcasted_iota(jnp.int32, (block, count), 0)
        query_place = lax.broadcasted_iota(jnp.int32, (block, count), 1)
        same = seg_ref[begin:stop, :] == seg_row_ref[0, :, begin:]
        mask = ((query_place >= key_place) & same).astype(jnp.float32)
        queries = x_ref[begin:, Q] * scale
        keys = x_ref[begin:stop, K]
        dd = dd_ref[begin:, :]
        dk = jnp.zeros((block, LANES), jnp.float32)
        for pair in range(GROUP // 2):
            span = slice(pair * LANES, (pair + 1) * LANES)
            first = 2 * LANES + pair * LANES
            values = x_ref[begin:stop, first : first + LANES]
            dn = dn_ref[begin:, span]
            d_both = jnp.concatenate([dn, dd], axis=1)
            sides = []
            for side in range(2):
                head = 2 * pair + side
                own_keys = own_lanes(keys, FEAT, head)
                ones = own_lanes(jnp.full((block, LANES), 2 / FEAT, jnp.bfloat16), FEAT, head)
                own_values = own_lanes(values, value_dim, side)
                scores = dot(own_keys, queries, ((1,), (1,)))
                weights = (((0.5 * scores + 1.0) * scores + 1.0) * mask).astype(jnp.bfloat16)
                d_weights = dot(
                    jnp.concatenate([own_values, ones], axis=1), d_both, ((1,), (1,))
                )
                d_scores = (d_weights * ((scores + 1.0) * mask)).astype(jnp.bfloat16)
                sides.append(dot(weights, dn))
                dk = dk + own_lanes(dot(d_scores, queries), FEAT, head)
                dq_sum[begin:, :] += dot(d_scores, own_keys * scale, ((0,), (0,)))
            dv_ref[begin:stop, span] = jnp.where(low, sides[0], sides[1])
        dk_ref[begin:stop, :] = dk
    dq_ref[...] = dq_sum[...].astype(dq_ref.dtype)


def far_back_kernel(
    value_dim, x_ref, seg_ref, state_ref, dq_ref, dk_ref, dv_ref, pick_ref, out_ref, state_wide
):
    length, width = dv_ref.shape
    spread_state(state_ref, state_wide, value_dim, lambda sums, masks: [sums * (1 / LANES)])
    seg = seg_ref[...]
    keep = (seg == seg[-1:, :]).astype(jnp.float32)
    keys = x_ref[:, K]
    ones = jnp.ones((length, LANES), jnp.bfloat16)
    d_phi = dot(jnp.concatenate([x_ref[:, V], ones], axis=1), state_wide[...], ((1,), (1,)))
    dk = dk_ref[...] + keep * from_features(d_phi, keys, pick_ref, 1.0)
    dv = dv_ref[...] + keep * dot(upright_features(keys, pick_ref, 1.0), state_wide[:, :width])
    out_ref[:, Q] = dq_ref[...]
    out_ref[:, K] = dk.astype(out_ref.dtype)
    out_ref[:, V] = dv.astype(out_ref.dtype)


class Attention:
    def __init__(self, rows, length, width):
        self.rows, self.length = rows, length
        self.value_dim = width // HEADS
        self.groups = HEADS // GROUP
        self.wide = GROUP * self.value_dim
        self.across = 2 * LANES + self.wide
        self.block = min(256, length)
        self.count = rows * length
        self.scaled, self.plain = rolls(True), rolls(False)
        self.all = range(self.groups)

    def specs(self, groups, own=False):
        first = 0 if own else groups[0]

        def rows_of(columns):
            return pl.BlockSpec((self.length, columns), lambda r, g: (r, first + g))

        return dict(
            x=rows_of(self.across),
            values=rows_of(self.wide),
            narrow=rows_of(LANES),
            seg=pl.BlockSpec((self.length, 1), lambda r, g: (r, 0)),
            seg_row=pl.BlockSpec((1, 1, self.length), lambda r, g: (r, 0, 0)),
            state=pl.BlockSpec((1, 1, PACKED, LANES), lambda r, g: (r, first + g, 0, 0)),
            pick=pl.BlockSpec((LANES, WIDE), lambda r, g: (0, 0)),
            turned_pick=pl.BlockSpec((WIDE, LANES), lambda r, g: (0, 0)),
        )

    def shape(self, columns, dtype, groups):
        return jax.ShapeDtypeStruct((self.count, columns * len(groups)), dtype)

    def state_shape(self, groups):
        return jax.ShapeDtypeStruct((self.rows, len(groups), PACKED, LANES), jnp.bfloat16)

    def wide_state(self, columns):
        return pltpu.VMEM((WIDE, columns), jnp.bfloat16)

    def call(self, kernel, groups, specs, outs, out_specs, scratch, passes, name):
        return pl.pallas_call(
            functools.partial(kernel, self.value_dim),
            grid=(self.rows, len(groups)),
            in_specs=specs,
            out_specs=out_specs,
            out_shape=outs,
            scratch_shapes=scratch,
            compiler_params=pltpu.CompilerParams(
                dimension_semantics=("arbitrary", "arbitrary"), vmem_limit_bytes=56 * 2**20
            ),
            cost_estimate=pl.CostEstimate(
                flops=self.rows * len(groups) * GROUP * passes * 2**26 * self.length // 512,
                bytes_accessed=2**21,
                transcendentals=0,
            ),
            name=name,
        )

    def tail(self, x, seg):
        at = self.specs(self.all)
        return self.call(
            tail_kernel, self.all, [at["x"], at["seg"], at["turned_pick"]],
            self.state_shape(self.all), at["state"], [], 5, "attn_tail",
        )(x, seg, self.plain.T)

    def near(self, x, seg, seg_row):
        def kernel(value_dim, *refs):
            near_kernel(value_dim, self.block, *refs)

        at = self.specs(self.all)
        out = self.shape(self.wide, jnp.float32, self.all)
        return self.call(
            kernel, self.all, [at["x"], at["seg"], at["seg_row"]],
            [out, out], [at["values"]] * 2, [], 8, "attn_near",
        )(x, seg, seg_row)

    def far(self, x, seg, state, top, den):
        at = self.specs(self.all)
        return self.call(
            far_kernel, self.all,
            [at["x"], at["seg"], at["state"], at["values"], at["values"], at["pick"]],
            [self.shape(self.wide, dtype, self.all) for dtype in (jnp.bfloat16, jnp.float32)],
            [at["values"]] * 2, [self.wide_state(2 * self.wide)], 8, "attn_far",
        )(x, seg, state, top, den, self.scaled)

    def head(self, x, dy, y, inverse, seg):
        at = self.specs(self.all)
        return self.call(
            head_kernel, self.all,
            [at["x"], at["values"], at["values"], at["values"], at["seg"], at["turned_pick"]],
            [self.state_shape(self.all), self.shape(self.wide, jnp.bfloat16, self.all),
             self.shape(LANES, jnp.bfloat16, self.all)],
            [at["state"], at["values"], at["narrow"]], [], 5, "attn_head",
        )(x, dy, y, inverse, seg, self.scaled.T)

    def near_back(self, x, dn, dd, seg, seg_row, state):
        def kernel(value_dim, *refs):
            near_back_kernel(value_dim, self.block, *refs)

        at, groups = self.specs(self.all), self.all
        return self.call(
            kernel, groups,
            [at["x"], at["values"], at["narrow"], at["seg"], at["seg_row"], at["state"],
             at["pick"]],
            [self.shape(LANES, jnp.bfloat16, groups), self.shape(LANES, jnp.float32, groups),
             self.shape(self.wide, jnp.float32, groups)],
            [at["narrow"], at["narrow"], at["values"]],
            [self.wide_state(self.wide + LANES), pltpu.VMEM((self.length, LANES), jnp.float32)],
            24, "attn_near_back",
        )(x, dn, dd, seg, seg_row, state, self.scaled)

    def far_back(self, x, seg, state, dq, dk, dv, groups):
        at, out = self.specs(groups), self.specs(groups, own=True)
        return self.call(
            far_back_kernel, groups,
            [at["x"], at["seg"], at["state"], at["narrow"], at["narrow"], at["values"],
             at["pick"]],
            self.shape(self.across, jnp.bfloat16, groups), out["x"],
            [self.wide_state(self.wide + LANES)], 9, "attn_far_back",
        )(x, seg, state, dq, dk, dv, self.plain)


class Passing:
    def __init__(self, segment_ids, length, reach, size):
        self.ids, self.length, self.reach, self.size = segment_ids, length, reach, size
        self.place = lax.axis_index("seq")

    def id_at(self, device, last):
        position = jnp.clip(device, 0, self.size - 1) * self.length + last * (self.length - 1)
        return lax.dynamic_index_in_dim(self.ids, position, 1, keepdims=False)

    def start(self, own, shift):
        self.shift, self.came = shift, []
        for k in range(1, self.reach + 1):
            goals = [(i, i + shift * k) for i in range(self.size)]
            pairs = [(i, goal) for i, goal in goals if 0 <= goal < self.size]
            self.came.append(lax.ppermute(own, "seq", pairs))

    def end(self, *hold):
        before = self.shift > 0
        own_id, total = self.id_at(self.place, not before), 0.0
        for k, came in enumerate(self.came, 1):
            linked = self.id_at(self.place - self.shift * k, before) == own_id
            came = after(came, *hold) if hold else came
            total = total + jnp.where(linked[:, None, None, None], came.astype(jnp.float32), 0.0)
        return total.astype(jnp.bfloat16)


epsilon = 1e-05


def against(left, matrix):
    return dot(left, matrix, ((1,), (1,)))


def norm_forward(values):
    scale = lax.rsqrt(jnp.mean(values * values, axis=1, keepdims=True) + epsilon)
    return (scale, values * scale)


def norm_backward(d_scaled, gain, scale, normed):
    d_normed = d_scaled * gain
    return scale * (d_normed - normed * jnp.mean(d_normed * normed, axis=1, keepdims=True))


def fold(count):
    return [0] + list(range(1, count, 2)) + list(range(2, count, 2))[::-1]


class Line:
    def __init__(self, axis, axis_size, stride, count):
        self.axis, self.size, self.stride, self.count = axis, axis_size, stride, count
        self.order = fold(count)

    def send(self, array, steps=1):
        pairs = []
        for index in range(self.size):
            place = (index // self.stride) % self.count
            goal = self.order[(self.order.index(place) + steps) % self.count]
            pairs.append((index, index + (goal - place) * self.stride))
        return lax.ppermute(array, self.axis, pairs)

    def place_back(self, steps):
        own = (lax.axis_index(self.axis) // self.stride) % self.count
        rank = jnp.asarray([self.order.index(p) for p in range(self.count)], jnp.int32)[own]
        return jnp.asarray(self.order, jnp.int32)[(rank - steps) % self.count]


class Slice:
    def __init__(self, dp, seq):
        self.dp, self.seq, self.devices = dp, seq, dp * seq
        self.lines = {
            "z": Line("dp", dp, 2, dp // 2),
            "x": Line("dp", dp, 1, 2),
            "y": Line("seq", seq, 2, seq // 2),
            "c": Line("seq", seq, 1, 2),
        }
        if dp % 4 == 0:
            self.lines["w"] = Line("dp", dp, 4, dp // 4)
            self.lines["u"] = Line("dp", dp, 2, 2)

    def device_of(self, back):
        at = {d: self.lines[d].place_back(back[d]) for d in back}
        z = at["z"] if "z" in at else at["w"] * 2 + at["u"]
        return ((z * 2 + at["x"]) * (self.seq // 2) + at["y"]) * 2 + at["c"]


def after(array, *others):
    return lax.optimization_barrier((array, *others))[0]


def assemble(pieces, widths, block, shape):
    arrays = [array for array, _, _ in pieces]
    dtype = arrays[0].dtype
    places = jnp.stack([shape.device_of(n) for _, names, _ in pieces for n in names])
    copies = sum(len(names) * len(spans) for _, names, spans in pieces)
    windows = [
        (min(span[0] for span in spans), max(span[0] + span[1] for span in spans))
        for _, _, spans in pieces
    ]
    held = [(array.shape[0], high - low) for array, (low, high) in zip(arrays, windows)]

    def kernel(places_ref, *refs):
        piece_refs, refs = refs[: len(pieces)], refs[len(pieces) :]
        out_refs, refs = refs[: len(widths)], refs[len(widths) :]
        buffers, (in_sems, out_sems) = refs[: len(pieces)], refs[len(pieces) :]
        loads = []
        for number, piece_ref in enumerate(piece_refs):
            low, high = windows[number]
            load = pltpu.make_async_copy(
                piece_ref.at[:, pl.ds(low, high - low)], buffers[number], in_sems.at[number]
            )
            load.start()
            loads.append(load)
        stores, begin = [], 0
        for number, (load, (_, names, spans)) in enumerate(zip(loads, pieces)):
            load.wait()
            for i in range(len(names)):
                to = pl.multiple_of(places_ref[begin + i] * block, block)
                for low, width, output, column in spans:
                    store = pltpu.make_async_copy(
                        buffers[number].at[pl.ds(i * block, block), pl.ds(low - windows[number][0], width)],
                        out_refs[output].at[pl.ds(to, block), pl.ds(column, width)],
                        out_sems.at[len(stores)],
                    )
                    store.start()
                    stores.append(store)
            begin += len(names)
        for store in stores:
            store.wait()

    size = sum(tall * wide for tall, wide in held) * dtype.itemsize
    return pl.pallas_call(
        kernel,
        out_shape=[jax.ShapeDtypeStruct((shape.devices * block, w), dtype) for w in widths],
        in_specs=[pl.BlockSpec(memory_space=pltpu.SMEM)]
        + [pl.BlockSpec(memory_space=pl.ANY)] * len(pieces),
        out_specs=[pl.BlockSpec(memory_space=pl.ANY)] * len(widths),
        scratch_shapes=[pltpu.VMEM(size, dtype) for size in held]
        + [
            pltpu.SemaphoreType.DMA((len(pieces),)),
            pltpu.SemaphoreType.DMA((copies,)),
        ],
        cost_estimate=pl.CostEstimate(flops=0, bytes_accessed=2 * size, transcendentals=0),
        name="assemble",
    )(places, *arrays)


class Gathering:
    def __init__(self, shape, array, names=None):
        self.shape, self.array = shape, array
        self.names = names or [dict(z=0, x=0, y=0, c=0)]

    def came(self, dim, direct=False, hold=()):
        line, array, out = self.shape.lines[dim], self.array, []
        for step in range(1, line.count):
            array = line.send(self.array, step) if direct else line.send(array)
            if step <= len(hold):
                array = after(array, *hold[step - 1])
            out.append((array, [dict(n, **{dim: step}) for n in self.names]))
        return out

    def along(self, dim, direct=False, hold=()):
        came = self.came(dim, direct, hold)
        array = jnp.concatenate([self.array] + [a for a, _ in came], 0)
        return Gathering(self.shape, array, self.names + [n for _, names in came for n in names])

    def ring(self, dim):
        return RingGathering(self, dim)

    def columns(self, low, high):
        return Gathering(self.shape, self.array[:, low:high], self.names)

    def pieces(self, dim, spans):
        found = [(self.array, self.names)] + self.came(dim)
        return [(array, names, spans) for array, names in found]


class RingGathering:
    def __init__(self, held, dim):
        self.held, self.dim, self.line = held, dim, held.shape.lines[dim]
        self.arrays = [held.array]
        self.came = self.line.send(held.array)

    def next(self, *hold):
        if len(self.arrays) == self.line.count - 1:
            return self.came
        self.arrays.append(after(self.came, *hold))
        self.came = self.line.send(self.arrays[-1])
        return self.arrays[-1]

    def end(self):
        while len(self.arrays) < self.line.count - 1:
            self.next()
        self.arrays.append(self.came)
        names = [dict(n, **{self.dim: s}) for s in range(self.line.count) for n in self.held.names]
        return Gathering(self.held.shape, jnp.concatenate(self.arrays, 0), names)


def spans_of(low, high, homes):
    spans = []
    for begin, width, output, column in homes:
        first, last = max(low, begin), min(high, begin + width)
        if first < last:
            spans.append((first - low, last - first, output, column + first - begin))
    return spans


def side_by_side(widths):
    return [(sum(widths[:i]), width, i, 0) for i, width in enumerate(widths)]


class TwoWays:
    def __init__(self, parts, shape, homes=None, widths=None):
        own = [part.shape[1] for part in parts]
        self.homes, self.widths = homes or side_by_side(own), widths or own
        self.block, self.shape = parts[0].shape[0], shape
        self.columns = sum(own)
        self.cut = -(-self.columns // 2 // LANES) * LANES
        self.held = Gathering(shape, jnp.concatenate(parts, axis=1))

    def first(self, *hold):
        self.held = self.held.along("z", True, [hold] * 8 if hold else ())

    def second(self, *hold):
        hold = [hold] if hold else ()
        self.one = self.held.columns(0, self.cut).along("x", False, hold)
        self.two = self.held.columns(self.cut, self.columns).along("y", False, hold)

    def third(self, *hold):
        hold = [hold] if hold else ()
        self.one, self.two = self.one.along("y", False, hold), self.two.along("x", False, hold)

    def last(self):
        self.ends = [self.one.came("c"), self.two.came("c")]

    def output(self, *outputs):
        homes = [(b, w, outputs.index(o), c) for b, w, o, c in self.homes if o in outputs]
        pieces = []
        for half, low, high, came in (
            (self.one, 0, self.cut, self.ends[0]),
            (self.two, self.cut, self.columns, self.ends[1]),
        ):
            spans = spans_of(low, high, homes)
            found = [(half.array, half.names)] + came
            pieces += [(array, names, spans) for array, names in found if spans]
        return assemble(pieces, [self.widths[o] for o in outputs], self.block, self.shape)


LAYOUT = "cyxwu"


def picker(shape, width):
    block = width // shape.devices
    if block % 16:
        order = jnp.arange(width)
    else:
        names = [dict()]
        for dim in LAYOUT:
            names = [dict(n, **{dim: s}) for n in names for s in range(shape.lines[dim].count)]
        places = jnp.stack([shape.device_of(n) for n in names])
        order = (places[:, None] * block + jnp.arange(block)[None, :]).reshape(width)
    return (jnp.arange(width)[:, None] == order[None, :]).astype(jnp.bfloat16)


def turned_rows(pick, left):
    return dot(pick, left, ((0,), (1,))).astype(jnp.bfloat16)


class Scattering:
    def __init__(self, shape, kept, arrived):
        half, columns = kept.shape
        self.shape, self.dims = shape, LAYOUT[1:]
        form = [shape.lines[d].count for d in self.dims] + [2 * half // shape.devices, columns]
        self.parts = [[kept.reshape(form), arrived.reshape(form)]]

    def beside(self, other):
        self.parts = self.parts + other.parts
        return self

    def term_of(self, step):
        found = []
        for terms in self.parts:
            own = [lax.index_in_dim(t, step, self.axis, False) for t in terms]
            found.append(functools.reduce(jnp.add, [t.astype(jnp.float32) for t in own]))
        return jnp.concatenate(found, axis=-1)

    def start(self, dim, *hold):
        self.line, self.axis, self.step = self.shape.lines[dim], self.dims.index(dim), 1
        self.dims = self.dims.replace(dim, "")
        if hold:
            self.parts = [[after(t, *hold) for t in terms] for terms in self.parts]
        self.sent = self.term_of(1).astype(jnp.bfloat16)
        self.came = self.line.send(self.sent)
        return self

    def advance(self, *hold):
        came = after(self.came, *hold) if hold else self.came
        self.step += 1
        total = self.term_of(self.step % self.line.count) + came.astype(jnp.float32)
        if self.step < self.line.count:
            self.sent = total.astype(jnp.bfloat16)
            self.came = self.line.send(self.sent)
        else:
            self.parts, self.came = [[total]], None
        return self

    def along(self, dim):
        self.start(dim)
        while self.came is not None:
            self.advance()
        return self


def scatter_whole(kept, sent):
    whole = jnp.concatenate([kept, sent], 0).astype(jnp.float32)
    return lax.psum_scatter(whole, ("dp", "seq"), scatter_dimension=0, tiled=True)


FF_TILE = 256


def mlp_kernel(
    block, begins, ends, a_ref, g_ref, at_ref, gt_ref, gate_ref, up_ref, down_ref, *refs
):
    if not begins:
        y_in_ref, da_in_ref, *refs = refs
    if ends:
        x_ref, gain_ref, y_ref, dxo_ref, da_sum, kept_ref, sent_ref, *refs, y_sum = refs
    else:
        y_sum, da_sum, kept_ref, sent_ref, *refs = refs
    hidden_ref, d_gate_ref, d_up_ref = refs
    count = a_ref.shape[0]
    step = pl.program_id(0)

    @pl.when(step == 0)
    def _():
        y_sum[...] = jnp.zeros_like(y_sum) if begins else y_in_ref[...]
        da_sum[...] = jnp.zeros_like(da_sum) if begins else da_in_ref[...]

    for begin in range(0, count, block):
        span = slice(begin, begin + block)
        a, g = a_ref[span, :], g_ref[span, :]
        gate, up = dot(a, gate_ref[...]), dot(a, up_ref[...])
        d_hidden = dot(g, down_ref[...])
        sigma = jax.nn.sigmoid(gate)
        silu = gate * sigma
        hidden = (silu * up).astype(jnp.bfloat16)
        d_gate = (d_hidden * up * (sigma + silu * (1.0 - sigma))).astype(jnp.bfloat16)
        d_up = (d_hidden * silu).astype(jnp.bfloat16)
        hidden_ref[span, :], d_gate_ref[span, :], d_up_ref[span, :] = hidden, d_gate, d_up
        y_sum[span, :] += dot(hidden, down_ref[...], ((1,), (1,)))
        da_sum[span, :] += dot(d_gate, gate_ref[...], ((1,), (1,))) + dot(
            d_up, up_ref[...], ((1,), (1,))
        )
    half = at_ref.shape[0] // 2
    for number, (left, right) in enumerate(
        ((at_ref, d_gate_ref), (at_ref, d_up_ref), (gt_ref, hidden_ref))
    ):
        kept_ref[number] = dot(left[:half, :], right[...]).astype(jnp.bfloat16)
        sent_ref[number] = dot(left[half:, :], right[...]).astype(jnp.bfloat16)
    if not ends:
        return

    @pl.when(step == pl.num_programs(0) - 1)
    def _():
        for begin in range(0, count, block):
            span = slice(begin, begin + block)
            x = x_ref[span, :]
            y_ref[span, :] = (x + y_sum[span, :]).astype(y_ref.dtype)
            scale = lax.rsqrt(jnp.mean(x * x, axis=1, keepdims=True) + epsilon)
            normed = x * scale
            d_normed = da_sum[span, :] * gain_ref[...]
            mean = jnp.mean(d_normed * normed, axis=1, keepdims=True)
            dx = g_ref[span, :].astype(jnp.float32) + scale * (d_normed - normed * mean)
            da_sum[span, :] = dx
            dxo_ref[span, :] = dx.astype(dxo_ref.dtype)


def feed_forward(a, g, a_turned, g_turned, weights, tiles, sums=None, ending=None):
    count, width = a.shape
    half = width // 2

    def held(rows, columns):
        return pl.BlockSpec((rows, columns), lambda j: (0, 0), pipeline_mode=pl.Buffered(1))

    def tile(first):
        return pl.BlockSpec((width, FF_TILE), lambda j: (0, first + j))

    def shape(dtype):
        return jax.ShapeDtypeStruct((count, width), dtype)

    full = held(count, width)
    given = [a, g, a_turned, g_turned] + [array for array, _ in weights]
    specs = [full, full] + [held(width, count)] * 2 + [tile(first) for _, first in weights]
    scratch = [pltpu.VMEM((count, FF_TILE), jnp.bfloat16)] * 3
    if sums is not None:
        given, specs = given + list(sums), specs + [full] * 2
    if ending is not None:
        given, specs = given + list(ending), specs + [full, held(1, width)]
        outs = [shape(jnp.bfloat16), shape(jnp.bfloat16), shape(jnp.float32)]
        scratch = scratch + [pltpu.VMEM((count, width), jnp.float32)]
    else:
        outs = [shape(jnp.float32)] * 2
    hidden = tiles * FF_TILE
    return pl.pallas_call(
        functools.partial(mlp_kernel, min(512, count), sums is None, ending is not None),
        grid=(tiles,),
        in_specs=specs,
        out_specs=[full] * len(outs)
        + [pl.BlockSpec((3, half, FF_TILE), lambda j: (0, 0, j))] * 2,
        out_shape=outs + [jax.ShapeDtypeStruct((3, half, hidden), jnp.bfloat16)] * 2,
        scratch_shapes=scratch,
        compiler_params=pltpu.CompilerParams(
            dimension_semantics=("arbitrary",), vmem_limit_bytes=60 * 2**20
        ),
        cost_estimate=pl.CostEstimate(
            flops=18 * count * width * hidden,
            bytes_accessed=12 * width * hidden + 20 * count * width,
            transcendentals=count * hidden,
        ),
        name="mlp",
    )(*given)


def gain_gradient(weights, gradients, gain):
    products = jnp.sum(weights.astype(jnp.float32) * gradients, axis=1)
    return products / gain.astype(jnp.float32)


def per_device(
    shape,
    layer_input,
    segment_ids,
    gain_attn,
    w_query,
    w_key,
    w_value,
    w_out,
    gain_mlp,
    w_gate,
    w_up,
    w_down,
    grad_output,
):
    rows, shard_len, width = layer_input.shape
    count = rows * shard_len
    narrow, hidden = HEADS * FEAT, w_gate.shape[1]
    attention = Attention(rows, shard_len, width)
    groups, wide, across = attention.groups, attention.wide, attention.across
    gains = jnp.pad(jnp.stack([gain_attn, gain_mlp], axis=1), ((0, 0), (0, LANES - 2)))
    first_parts = [w_query, w_key, w_value, gains]
    homes, grouped = [], []
    for g in range(groups):
        for part, begin, size, place in (
            (w_query, 0, LANES, 0),
            (w_key, narrow, LANES, LANES),
            (w_value, 2 * narrow, wide, 2 * LANES),
        ):
            homes.append((begin + g * size, size, 0, g * across + place))
            grouped.append(part[:, g * size : (g + 1) * size])
    homes.append((groups * across, LANES, 0, groups * across))
    spare = ((0, 0), (0, -hidden % FF_TILE))
    gate_part, up_part, down_part = (
        jnp.pad(part, spare) for part in (w_gate, w_up, w_down.T)
    )
    tiles = gate_part.shape[1] // FF_TILE
    ringed = gains.shape[0] % 16 == 0
    if ringed:
        early = TwoWays(first_parts, shape, homes, [groups * across + LANES])
        rest = TwoWays([gate_part, w_out, up_part], shape)
        early.first()
        early.second()
        early.third()
        begun = [early.one.array, early.two.array]
        rest.first(*begun)
        down = Gathering(shape, down_part).along("x", False, [begun])
        early.last()
        (gathered,) = early.output(0)
    else:
        first_part = jnp.concatenate(grouped + [gains], axis=1)
        gathered, out_w, gate_w, up_w, down_w = (
            lax.all_gather(part, ("dp", "seq"), axis=0, tiled=True)
            for part in (first_part, w_out, gate_part, up_part, down_part)
        )
    qkv_w = gathered[:, : groups * across]
    gain_one = gathered[:, groups * across].astype(jnp.float32)[None, :]
    gain_two = gathered[:, groups * across + 1].astype(jnp.float32)[None, :]

    pick = picker(shape, width)
    cotangent = grad_output.reshape(count, width)
    tokens = layer_input.reshape(count, width).astype(jnp.float32)
    scale_one, normed_one = norm_forward(tokens)
    a_one = (normed_one * gain_one).astype(jnp.bfloat16)
    a_one = after(a_one, rest.held.array, down.array) if ringed else a_one
    qkv = jnp.dot(a_one, qkv_w, preferred_element_type=jnp.float32).astype(jnp.bfloat16)
    place = lax.axis_index("seq")
    own_seg = lax.dynamic_slice_in_dim(segment_ids, place * shard_len, shard_len, 1)
    seg, seg_row = own_seg.reshape(count, 1), own_seg.reshape(rows, 1, shard_len)
    reach = min(shape.seq - 1, -(-(LONGEST - 1) // shard_len))
    states = Passing(segment_ids, shard_len, reach, shape.seq)
    if ringed:
        down = down.along("y", False, [[qkv]])
        tail = attention.tail(after(qkv, down.array), seg)
        rest.second(tail)
        states.start(tail, 1)
        ring = down.ring("z")
        turn = ring.next(tail)
        top, den = attention.near(
            after(qkv, rest.one.array, rest.two.array, turn), seg, seg_row
        )
        turn = ring.next(den)
        earlier = after(states.end(den), turn)
        mixed_cat, inverse = attention.far(qkv, seg, earlier, top, den)
        rest.third(mixed_cat)
        rest.last()
        down = ring.end()
        down_ends = down.pieces("c", [(0, tiles * FF_TILE, 0, 0)])
        (out_w,) = rest.output(1)
    else:
        tail = attention.tail(qkv, seg)
        states.start(tail, 1)
        earlier = states.end()
        top, den = attention.near(qkv, seg, seg_row)
        mixed_cat, inverse = attention.far(qkv, seg, earlier, top, den)
    x_two = tokens + jnp.dot(mixed_cat, out_w, preferred_element_type=jnp.float32)
    scale_two, normed_two = norm_forward(x_two)
    a_two = (normed_two * gain_two).astype(jnp.bfloat16)
    if ringed:
        gate_w, up_w = rest.output(0, 2)
        (down_w,) = assemble(down_ends, [tiles * FF_TILE], down_part.shape[0], shape)
    result, d_branch, d_x_two, kept, sent = feed_forward(
        a_two,
        cotangent,
        turned_rows(pick, a_two),
        turned_rows(pick, cotangent),
        [(gate_w, 0), (up_w, 0), (down_w, 0)],
        tiles,
        None,
        (x_two, gain_two),
    )
    turned_mixed, turned_one = turned_rows(pick, mixed_cat), turned_rows(pick, a_one)
    half = width // 2
    d_mixed = against(d_branch, out_w).astype(jnp.bfloat16)
    ahead, d_top, d_den = attention.head(qkv, d_mixed, mixed_cat, inverse, seg)
    states.start(ahead, -1)
    own = after(d_branch, ahead) if ringed else d_branch
    out_sent, out_kept = (
        dot(t, own).astype(jnp.bfloat16) for t in (turned_mixed[half:], turned_mixed[:half])
    )
    d_qkv, grad_qkv = [], []
    if ringed:
        send_core = shape.lines["c"].send
        arrived, out_arrived = send_core(sent), send_core(out_sent)
        arrived = after(arrived, out_sent, out_kept)
        gate_sum, up_sum, down_sum = (Scattering(shape, kept[i], arrived[i]) for i in range(3))
        gate_sum.beside(Scattering(shape, out_kept, out_arrived)).start("y")
        up_sum.start("x")
        down_sum.start("u")
        d_top = after(d_top, gate_sum.sent, up_sum.sent, down_sum.sent)
        d_near = attention.near_back(qkv, d_top, d_den, seg, seg_row, earlier)
        near = d_near[0]
        gate_sum.advance(near).start("x")
        up_sum.advance(near).start("y")
        down_sum.advance(near).start("w")
        later = after(states.end(near), down_sum.sent, gate_sum.sent, up_sum.sent)

        turned = [turned_one[:half], turned_one[half:]]

        def products(right):
            own_sent = dot(turned[1], right).astype(jnp.bfloat16)
            own_kept = dot(turned[0], right).astype(jnp.bfloat16)
            own_sum = Scattering(shape, own_kept, send_core(own_sent))
            own_sum.sent = own_sent
            return own_sum

        far = attention.far_back(qkv, seg, later, *d_near, range(0, 1))
        d_qkv.append(far)
        qkv_a = products(far)
        later = after(later, qkv_a.sent)
        far = attention.far_back(qkv, seg, later, *d_near, range(1, 2))
        d_qkv.append(far)
        qkv_a.start("y", far)
        qkv_b = products(after(far, qkv_a.sent))
        down_sum.advance(qkv_b.sent).start("x")
        both = gate_sum.advance(qkv_b.sent).beside(up_sum.advance(qkv_b.sent)).start("u")
        qkv_b.start("x", both.sent)
        d_qkv = [after(array, both.sent, qkv_b.sent, down_sum.sent) for array in d_qkv]
        qkv_a.advance(both.sent).start("x")
        down_sum.advance(both.sent).start("y")
        qkv_b.advance().start("y")
        both.advance(qkv_b.sent).start("w")
        qkv_sum = qkv_a.advance(qkv_b.sent).beside(qkv_b.advance()).start("u")
        down_sum.advance(both.sent)
        qkv_sum.advance().start("w")
        both.advance()
        qkv_sum.advance()
        grad_qkv, both, down_sum = (part.parts[0][0] for part in (qkv_sum, both, down_sum))
        grad_qkv = [grad_qkv[:, g * across : (g + 1) * across] for g in range(groups)]
        padded = tiles * FF_TILE
        grad_gate, grad_out = both[:, :hidden], both[:, padded : padded + width]
        grad_up = both[:, padded + width : padded + width + hidden]
        grad_down = down_sum[:, :hidden]
    else:
        later = states.end()
        d_near = attention.near_back(qkv, d_top, d_den, seg, seg_row, earlier)
        grad_gate, grad_up, grad_down = (
            scatter_whole(kept[i], sent[i])[:, :hidden] for i in range(3)
        )
        grad_out = scatter_whole(out_kept, out_sent)
        for g in range(groups):
            only = range(g, g + 1)
            d_qkv.append(attention.far_back(qkv, seg, later, *d_near, only))
            grad_qkv.append(
                scatter_whole(dot(turned_one[:half], d_qkv[g]), dot(turned_one[half:], d_qkv[g]))
            )
    d_a_one = None
    for g in range(groups):
        term = against(d_qkv[g], qkv_w[:, g * across : (g + 1) * across])
        d_a_one = term if d_a_one is None else d_a_one + term
    d_tokens = d_x_two + norm_backward(d_a_one, gain_one, scale_one, normed_one)
    return (
        result.reshape(rows, shard_len, width),
        d_tokens.reshape(rows, shard_len, width),
        gain_gradient(jnp.concatenate(grouped, axis=1), jnp.concatenate(grad_qkv, axis=1), gain_attn),
        jnp.concatenate([part[:, Q] for part in grad_qkv], axis=1),
        jnp.concatenate([part[:, K] for part in grad_qkv], axis=1),
        jnp.concatenate([part[:, V] for part in grad_qkv], axis=1),
        grad_out,
        gain_gradient(
            jnp.concatenate([w_gate, w_up], axis=1),
            jnp.concatenate([grad_gate, grad_up], axis=1),
            gain_mlp,
        ),
        grad_gate,
        grad_up,
        grad_down.T,
    )


def solution(mesh):
    placed = (
        P("dp", "seq", None),
        P("dp", None),
        P(("dp", "seq")),
        P(("dp", "seq"), None),
        P(("dp", "seq"), None),
        P(("dp", "seq"), None),
        P(("dp", "seq"), None),
        P(("dp", "seq")),
        P(("dp", "seq"), None),
        P(("dp", "seq"), None),
        P(None, ("dp", "seq")),
        P("dp", "seq", None),
    )
    return jax.shard_map(
        functools.partial(per_device, Slice(mesh.shape["dp"], mesh.shape["seq"])),
        mesh=mesh,
        in_specs=placed,
        out_specs=(
            P("dp", "seq", None),
            P("dp", "seq", None),
            P(("dp", "seq")),
            P(("dp", "seq"), None),
            P(("dp", "seq"), None),
            P(("dp", "seq"), None),
            P(("dp", "seq"), None),
            P(("dp", "seq")),
            P(("dp", "seq"), None),
            P(("dp", "seq"), None),
            P(None, ("dp", "seq")),
        ),
        check_vma=False,
    )
```

```python
import functools

import jax
import jax.numpy as jnp
import numpy as np
from jax import lax
from jax.experimental import pallas as pl
from jax.experimental.pallas import tpu as pltpu
from jax.sharding import PartitionSpec as P

LONGEST = 1024
HEADS = 16
FEAT = 16
LANES = 128
GROUP = LANES // FEAT
PIECES = FEAT // 2 + 2
WIDE = PIECES * LANES
PACKED = WIDE // 2 + 16


def dot(left, right, dims=((1,), (0,))):
    return lax.dot_general(left, right, (dims, ((), ())), preferred_element_type=jnp.float32)


def rolls(scaled):
    zero = lax.optimization_barrier(jnp.int32(0))
    row = lax.broadcasted_iota(jnp.int32, (LANES, WIDE), 0) + zero
    column = lax.broadcasted_iota(jnp.int32, (LANES, WIDE), 1)
    d, lane = column // LANES - 1, column % LANES
    a = lane % FEAT
    goal = lane - a + (a + d) % FEAT
    found = (row == goal) & (d >= 0) & ((d < FEAT // 2) | (a < FEAT // 2))
    factor = jnp.where(d == 0, 1 / 32, 1 / 16) if scaled else 1.0
    return jnp.where(found, factor, 0.0).astype(jnp.bfloat16)


def features(rows, factors, lin, axis):
    x = rows.astype(jnp.float32)
    pieces = [x * lin]
    for number in range(PIECES - 1):
        span = slice(number * LANES, (number + 1) * LANES)
        piece = x * (factors[:, span] if axis else factors[span, :])
        if number == PIECES - 2:
            place = lax.broadcasted_iota(jnp.int32, piece.shape, axis)
            piece = jnp.where(place % FEAT == FEAT // 2, 1.0, piece)
        pieces.append(piece)
    return jnp.concatenate([piece.astype(jnp.bfloat16) for piece in pieces], axis=axis)


def turned_features(rows, turned_pick_ref, lin):
    turned = rows.astype(jnp.float32).T.astype(jnp.bfloat16)
    return features(turned, dot(turned_pick_ref[LANES:, :], turned), lin, 0)


def upright_features(rows, pick_ref, lin):
    return features(rows, dot(rows, pick_ref[:, LANES:]), lin, 1)


def head_mask(lanes_per_head, first_head):
    row_head = lax.broadcasted_iota(jnp.int32, (LANES, LANES), 0) // FEAT
    lane_head = lax.broadcasted_iota(jnp.int32, (LANES, LANES), 1) // lanes_per_head + first_head
    return row_head == lane_head


def head_masks(value_dim):
    per = LANES // value_dim
    return [head_mask(value_dim, part * per) for part in range(GROUP // per)]


def low_half():
    return lax.broadcasted_iota(jnp.int32, (LANES, LANES), 1) < LANES // 2


def piece_spans():
    return [slice(number * LANES, (number + 1) * LANES) for number in range(PIECES)]


def fold_heads(rows, masks):
    total = None
    for part, mask in enumerate(masks):
        piece = jnp.where(mask, rows[:, part * LANES : (part + 1) * LANES], 0.0)
        total = piece if total is None else total + piece
    return total + pltpu.roll(total, LANES // 2, 1)


def diagonal():
    row = lax.broadcasted_iota(jnp.int32, (LANES, LANES), 0)
    return row == lax.broadcasted_iota(jnp.int32, (LANES, LANES), 1)


def pack_state(out_ref, pieces):
    low, straight = low_half(), diagonal()
    for number in range(0, PIECES, 2):
        rows = slice(number // 2 * LANES, (number // 2 + 1) * LANES)
        values = jnp.where(low, pieces[number][0], pieces[number + 1][0])
        out_ref[0, 0, rows, :] = values.astype(out_ref.dtype)
    sums = [jnp.sum(jnp.where(straight, s, 0.0), axis=0, keepdims=True) for _, s in pieces]
    sums.append(jnp.zeros((PACKED - WIDE // 2 - PIECES, LANES), jnp.float32))
    out_ref[0, 0, WIDE // 2 :, :] = jnp.concatenate(sums, axis=0).astype(out_ref.dtype)


def spread_state(state_ref, wide_ref, value_dim, sums_of):
    masks, low, straight = head_masks(value_dim), low_half(), diagonal()
    all_sums = state_ref[0, 0, WIDE // 2 :, :].astype(jnp.float32)
    for number, span in enumerate(piece_spans()):
        rows = slice(number // 2 * LANES, (number // 2 + 1) * LANES)
        state = state_ref[0, 0, rows, :].astype(jnp.float32)
        turned = pltpu.roll(state, LANES // 2, 1)
        values = jnp.where(low, turned, state) if number % 2 else jnp.where(low, state, turned)
        sums = jnp.where(straight, all_sums[number : number + 1, :], 0.0)
        sums = jnp.broadcast_to(jnp.sum(sums, axis=1, keepdims=True), (LANES, LANES))
        parts = [jnp.where(mask, values, 0.0) for mask in masks] + sums_of(sums, masks)
        for place, part in enumerate(parts):
            wide_ref[span, slice(place * LANES, (place + 1) * LANES)] = part.astype(jnp.bfloat16)


def own_lanes(array, lanes_per_head, head):
    place = lax.broadcasted_iota(jnp.int32, array.shape, 1) // lanes_per_head
    return jnp.where(place == head, array, jnp.zeros_like(array))


Q, K, V = slice(0, LANES), slice(LANES, 2 * LANES), slice(2 * LANES, None)


def tail_kernel(value_dim, x_ref, seg_ref, pick_ref, out_ref):
    seg = seg_ref[...]
    keep = (seg == seg[-1:, :]).astype(jnp.float32)
    values = (x_ref[:, V].astype(jnp.float32) * keep).astype(jnp.bfloat16)
    ones = jnp.broadcast_to(keep, (seg.shape[0], LANES)).astype(jnp.bfloat16)
    phi = turned_features(x_ref[:, K], pick_ref, 1.0)
    full = dot(phi, jnp.concatenate([values, ones], axis=1))
    width, masks = values.shape[1], head_masks(value_dim)
    pack_state(
        out_ref,
        [(fold_heads(full[span, :width], masks), full[span, width:]) for span in piece_spans()],
    )


def masks_of(seg_ref, seg_row_ref, begin, block):
    stop = begin + block
    rows = begin + lax.broadcasted_iota(jnp.int32, (block, stop), 0)
    columns = lax.broadcasted_iota(jnp.int32, (block, stop), 1)
    same = seg_ref[begin:stop, :] == seg_row_ref[0, :, :stop]
    return ((rows >= columns) & same).astype(jnp.float32)


def near_kernel(value_dim, block, x_ref, seg_ref, seg_row_ref, top_ref, den_ref):
    length = x_ref.shape[0]
    low = lax.broadcasted_iota(jnp.int32, (block, LANES), 1) < value_dim
    for begin in range(0, length, block):
        stop = begin + block
        mask = masks_of(seg_ref, seg_row_ref, begin, block)
        queries = x_ref[begin:stop, Q] * jnp.bfloat16(FEAT ** (-0.5))
        keys = x_ref[:stop, K]
        ones = jnp.ones((stop, LANES), jnp.bfloat16)
        for pair in range(GROUP // 2):
            span = slice(pair * LANES, (pair + 1) * LANES)
            first = 2 * LANES + pair * LANES
            values = jnp.concatenate([x_ref[:stop, first : first + LANES], ones], axis=1)
            sides = []
            for head in (2 * pair, 2 * pair + 1):
                scores = dot(own_lanes(queries, FEAT, head), keys, ((1,), (1,)))
                weights = (((0.5 * scores + 1.0) * scores + 1.0) * mask).astype(jnp.bfloat16)
                sides.append(dot(weights, values))
            top_ref[begin:stop, span] = jnp.where(low, sides[0][:, :LANES], sides[1][:, :LANES])
            den_ref[begin:stop, span] = jnp.where(low, sides[0][:, LANES:], sides[1][:, LANES:])


def far_kernel(value_dim, x_ref, seg_ref, state_ref, top_ref, den_ref, pick_ref, *rest):
    y_ref, inverse_ref, state_wide = rest[-3:]
    width = top_ref.shape[1]
    spread_state(
        state_ref, state_wide, value_dim,
        lambda sums, masks: [jnp.where(mask, sums, 0.0) for mask in masks],
    )
    seg = seg_ref[...]
    keep = (seg == seg[:1, :]).astype(jnp.float32)
    far = dot(upright_features(x_ref[:, Q], pick_ref, FEAT ** (-0.5)), state_wide[...])
    top = top_ref[...] + keep * far[:, :width]
    inverse = 1.0 / (den_ref[...] + keep * far[:, width:])
    y_ref[...] = (top * inverse).astype(y_ref.dtype)
    inverse_ref[...] = inverse


def head_kernel(
    value_dim, x_ref, dy_ref, y_ref, inverse_ref, seg_ref, pick_ref, out_ref, dn_ref, dd_ref
):
    width = dy_ref.shape[1]
    d_top = dy_ref[...].astype(jnp.float32) * inverse_ref[...]
    product = d_top * y_ref[...].astype(jnp.float32)
    large = product.astype(jnp.bfloat16)
    small = (product - large.astype(jnp.float32)).astype(jnp.bfloat16)
    row = lax.broadcasted_iota(jnp.int32, (width, LANES), 0) // value_dim
    lane = lax.broadcasted_iota(jnp.int32, (width, LANES), 1) // FEAT
    adder = jnp.where(row == lane, -1.0, 0.0).astype(jnp.bfloat16)
    d_den = dot(large, adder) + dot(small, adder)
    rounded = d_den.astype(jnp.bfloat16).astype(jnp.float32)
    place = lax.broadcasted_iota(jnp.int32, d_den.shape, 1) % FEAT
    d_den = jnp.where(place < FEAT // 2, rounded, d_den - rounded)
    seg = seg_ref[...]
    keep = (seg == seg[:1, :]).astype(jnp.float32)
    dn_ref[...] = d_top.astype(jnp.bfloat16)
    dd_ref[...] = d_den.astype(jnp.bfloat16)
    d_both = [(d_top * keep).astype(jnp.bfloat16), (d_den * keep).astype(jnp.bfloat16)]
    full = dot(
        turned_features(x_ref[:, Q], pick_ref, FEAT ** (-0.5)), jnp.concatenate(d_both, axis=1)
    )
    masks, own, pieces = head_masks(value_dim), head_mask(FEAT, 0), []
    for span in piece_spans():
        sums = jnp.where(own, full[span, width:], 0.0)
        sums = jnp.sum(sums, axis=1, keepdims=True) * (2 / FEAT)
        pieces.append((fold_heads(full[span, :width], masks), sums))
    pack_state(out_ref, pieces)


def from_features(d_phi, rows, pick_ref, lin):
    x = rows.astype(jnp.float32)
    factors = dot(rows, pick_ref[:, LANES:])
    total, scaled = d_phi[:, :LANES] * lin, []
    for number in range(PIECES - 1):
        span = slice(number * LANES, (number + 1) * LANES)
        piece = d_phi[:, (number + 1) * LANES : (number + 2) * LANES]
        total = total + piece * factors[:, span]
        scaled.append((piece * x).astype(jnp.bfloat16))
    return total + dot(jnp.concatenate(scaled, axis=1), pick_ref[:, LANES:], ((1,), (1,)))


def near_back_kernel(
    value_dim, block, x_ref, dn_ref, dd_ref, seg_ref, seg_row_ref, state_ref, pick_ref,
    dq_ref, dk_ref, dv_ref, state_wide, dq_sum,
):
    length, width = dn_ref.shape
    own = head_mask(FEAT, 0)
    spread_state(
        state_ref, state_wide, value_dim,
        lambda sums, masks: [jnp.where(own, sums, 0.0) * (2 / FEAT)],
    )
    keep = seg_ref[...] == seg_ref[:1, :]
    d_both = jnp.concatenate([dn_ref[...], dd_ref[...]], axis=1)
    d_phi = dot(jnp.where(keep, d_both, jnp.zeros_like(d_both)), state_wide[...], ((1,), (1,)))
    dq_sum[...] = from_features(d_phi, x_ref[:, Q], pick_ref, FEAT ** (-0.5))
    scale = jnp.bfloat16(FEAT ** (-0.5))
    low = lax.broadcasted_iota(jnp.int32, (block, LANES), 1) < value_dim
    for begin in range(0, length, block):
        stop, count = begin + block, length - begin
        key_place = lax.broadcasted_iota(jnp.int32, (block, count), 0)
        query_place = lax.broadcasted_iota(jnp.int32, (block, count), 1)
        same = seg_ref[begin:stop, :] == seg_row_ref[0, :, begin:]
        mask = ((query_place >= key_place) & same).astype(jnp.float32)
        queries = x_ref[begin:, Q] * scale
        keys = x_ref[begin:stop, K]
        dd = dd_ref[begin:, :]
        dk = jnp.zeros((block, LANES), jnp.float32)
        for pair in range(GROUP // 2):
            span = slice(pair * LANES, (pair + 1) * LANES)
            first = 2 * LANES + pair * LANES
            values = x_ref[begin:stop, first : first + LANES]
            dn = dn_ref[begin:, span]
            d_both = jnp.concatenate([dn, dd], axis=1)
            sides = []
            for side in range(2):
                head = 2 * pair + side
                own_keys = own_lanes(keys, FEAT, head)
                ones = own_lanes(jnp.full((block, LANES), 2 / FEAT, jnp.bfloat16), FEAT, head)
                own_values = own_lanes(values, value_dim, side)
                scores = dot(own_keys, queries, ((1,), (1,)))
                weights = (((0.5 * scores + 1.0) * scores + 1.0) * mask).astype(jnp.bfloat16)
                d_weights = dot(
                    jnp.concatenate([own_values, ones], axis=1), d_both, ((1,), (1,))
                )
                d_scores = (d_weights * ((scores + 1.0) * mask)).astype(jnp.bfloat16)
                sides.append(dot(weights, dn))
                dk = dk + own_lanes(dot(d_scores, queries), FEAT, head)
                dq_sum[begin:, :] += dot(d_scores, own_keys * scale, ((0,), (0,)))
            dv_ref[begin:stop, span] = jnp.where(low, sides[0], sides[1])
        dk_ref[begin:stop, :] = dk
    dq_ref[...] = dq_sum[...].astype(dq_ref.dtype)


def far_back_kernel(
    value_dim, x_ref, seg_ref, state_ref, dq_ref, dk_ref, dv_ref, pick_ref, out_ref, state_wide
):
    length, width = dv_ref.shape
    spread_state(state_ref, state_wide, value_dim, lambda sums, masks: [sums * (1 / LANES)])
    seg = seg_ref[...]
    keep = (seg == seg[-1:, :]).astype(jnp.float32)
    keys = x_ref[:, K]
    ones = jnp.ones((length, LANES), jnp.bfloat16)
    d_phi = dot(jnp.concatenate([x_ref[:, V], ones], axis=1), state_wide[...], ((1,), (1,)))
    dk = dk_ref[...] + keep * from_features(d_phi, keys, pick_ref, 1.0)
    dv = dv_ref[...] + keep * dot(upright_features(keys, pick_ref, 1.0), state_wide[:, :width])
    out_ref[:, Q] = dq_ref[...]
    out_ref[:, K] = dk.astype(out_ref.dtype)
    out_ref[:, V] = dv.astype(out_ref.dtype)


class Attention:
    def __init__(self, rows, length, width):
        self.rows, self.length = rows, length
        self.value_dim = width // HEADS
        self.groups = HEADS // GROUP
        self.wide = GROUP * self.value_dim
        self.across = 2 * LANES + self.wide
        self.block = min(256, length)
        self.count = rows * length
        self.scaled, self.plain = rolls(True), rolls(False)
        self.all = range(self.groups)

    def specs(self, groups):
        def rows_of(columns):
            return pl.BlockSpec((self.length, columns), lambda r, g: (r, g))

        return dict(
            x=rows_of(self.across),
            values=rows_of(self.wide),
            narrow=rows_of(LANES),
            seg=pl.BlockSpec((self.length, 1), lambda r, g: (r, 0)),
            seg_row=pl.BlockSpec((1, 1, self.length), lambda r, g: (r, 0, 0)),
            state=pl.BlockSpec((1, 1, PACKED, LANES), lambda r, g: (r, g, 0, 0)),
            pick=pl.BlockSpec((LANES, WIDE), lambda r, g: (0, 0)),
            turned_pick=pl.BlockSpec((WIDE, LANES), lambda r, g: (0, 0)),
        )

    def shape(self, columns, dtype, groups):
        return jax.ShapeDtypeStruct((self.count, columns * len(groups)), dtype)

    def state_shape(self, groups):
        return jax.ShapeDtypeStruct((self.rows, len(groups), PACKED, LANES), jnp.bfloat16)

    def wide_state(self, columns):
        return pltpu.VMEM((WIDE, columns), jnp.bfloat16)

    def call(self, kernel, groups, specs, outs, out_specs, scratch, passes, name):
        return pl.pallas_call(
            functools.partial(kernel, self.value_dim),
            grid=(self.rows, len(groups)),
            in_specs=specs,
            out_specs=out_specs,
            out_shape=outs,
            scratch_shapes=scratch,
            compiler_params=pltpu.CompilerParams(
                dimension_semantics=("arbitrary", "arbitrary"), vmem_limit_bytes=56 * 2**20
            ),
            cost_estimate=pl.CostEstimate(
                flops=self.rows * len(groups) * GROUP * passes * 2**26 * self.length // 512,
                bytes_accessed=2**21,
                transcendentals=0,
            ),
            name=name,
        )

    def tail(self, x, seg):
        at = self.specs(self.all)
        return self.call(
            tail_kernel, self.all, [at["x"], at["seg"], at["turned_pick"]],
            self.state_shape(self.all), at["state"], [], 5, "attn_tail",
        )(x, seg, self.plain.T)

    def near(self, x, seg, seg_row):
        def kernel(value_dim, *refs):
            near_kernel(value_dim, self.block, *refs)

        at = self.specs(self.all)
        out = self.shape(self.wide, jnp.float32, self.all)
        return self.call(
            kernel, self.all, [at["x"], at["seg"], at["seg_row"]],
            [out, out], [at["values"]] * 2, [], 8, "attn_near",
        )(x, seg, seg_row)

    def far(self, x, seg, state, top, den):
        at = self.specs(self.all)
        return self.call(
            far_kernel, self.all,
            [at["x"], at["seg"], at["state"], at["values"], at["values"], at["pick"]],
            [self.shape(self.wide, dtype, self.all) for dtype in (jnp.bfloat16, jnp.float32)],
            [at["values"]] * 2, [self.wide_state(2 * self.wide)], 8, "attn_far",
        )(x, seg, state, top, den, self.scaled)

    def head(self, x, dy, y, inverse, seg):
        at = self.specs(self.all)
        return self.call(
            head_kernel, self.all,
            [at["x"], at["values"], at["values"], at["values"], at["seg"], at["turned_pick"]],
            [self.state_shape(self.all), self.shape(self.wide, jnp.bfloat16, self.all),
             self.shape(LANES, jnp.bfloat16, self.all)],
            [at["state"], at["values"], at["narrow"]], [], 5, "attn_head",
        )(x, dy, y, inverse, seg, self.scaled.T)

    def near_back(self, x, dn, dd, seg, seg_row, state):
        def kernel(value_dim, *refs):
            near_back_kernel(value_dim, self.block, *refs)

        at, groups = self.specs(self.all), self.all
        return self.call(
            kernel, groups,
            [at["x"], at["values"], at["narrow"], at["seg"], at["seg_row"], at["state"],
             at["pick"]],
            [self.shape(LANES, jnp.bfloat16, groups), self.shape(LANES, jnp.float32, groups),
             self.shape(self.wide, jnp.float32, groups)],
            [at["narrow"], at["narrow"], at["values"]],
            [self.wide_state(self.wide + LANES), pltpu.VMEM((self.length, LANES), jnp.float32)],
            24, "attn_near_back",
        )(x, dn, dd, seg, seg_row, state, self.scaled)

    def far_back(self, x, seg, state, dq, dk, dv):
        at, groups = self.specs(self.all), self.all
        return self.call(
            far_back_kernel, groups,
            [at["x"], at["seg"], at["state"], at["narrow"], at["narrow"], at["values"],
             at["pick"]],
            self.shape(self.across, jnp.bfloat16, groups), at["x"],
            [self.wide_state(self.wide + LANES)], 9, "attn_far_back",
        )(x, seg, state, dq, dk, dv, self.plain)


class Passing:
    def __init__(self, segment_ids, length, reach, size):
        self.ids, self.length, self.reach, self.size = segment_ids, length, reach, size
        self.place = lax.axis_index("seq")

    def id_at(self, device, last):
        position = jnp.clip(device, 0, self.size - 1) * self.length + last * (self.length - 1)
        return lax.dynamic_index_in_dim(self.ids, position, 1, keepdims=False)

    def start(self, own, shift):
        self.shift, self.came = shift, []
        for k in range(1, self.reach + 1):
            goals = [(i, i + shift * k) for i in range(self.size)]
            pairs = [(i, goal) for i, goal in goals if 0 <= goal < self.size]
            self.came.append(lax.ppermute(own, "seq", pairs))

    def end(self, *hold):
        before = self.shift > 0
        own_id, total = self.id_at(self.place, not before), 0.0
        for k, came in enumerate(self.came, 1):
            linked = self.id_at(self.place - self.shift * k, before) == own_id
            came = after(came, *hold) if hold else came
            total = total + jnp.where(linked[:, None, None, None], came.astype(jnp.float32), 0.0)
        return total.astype(jnp.bfloat16)


epsilon = 1e-05


def against(left, matrix):
    return dot(left, matrix, ((1,), (1,)))


def norm_forward(values):
    scale = lax.rsqrt(jnp.mean(values * values, axis=1, keepdims=True) + epsilon)
    return (scale, values * scale)


def norm_backward(d_scaled, gain, scale, normed):
    d_normed = d_scaled * gain
    return scale * (d_normed - normed * jnp.mean(d_normed * normed, axis=1, keepdims=True))


def fold(count):
    return [0] + list(range(1, count, 2)) + list(range(2, count, 2))[::-1]


class Line:
    def __init__(self, axis, axis_size, stride, count):
        self.axis, self.size, self.stride, self.count = axis, axis_size, stride, count
        self.order = fold(count)

    def send(self, array, steps=1):
        pairs = []
        for index in range(self.size):
            place = (index // self.stride) % self.count
            goal = self.order[(self.order.index(place) + steps) % self.count]
            pairs.append((index, index + (goal - place) * self.stride))
        return lax.ppermute(array, self.axis, pairs)

    def place_back(self, steps):
        own = (lax.axis_index(self.axis) // self.stride) % self.count
        rank = jnp.asarray([self.order.index(p) for p in range(self.count)], jnp.int32)[own]
        return jnp.asarray(self.order, jnp.int32)[(rank - steps) % self.count]


class Slice:
    def __init__(self, dp, seq):
        self.dp, self.seq, self.devices = dp, seq, dp * seq
        self.lines = {
            "z": Line("dp", dp, 2, dp // 2),
            "x": Line("dp", dp, 1, 2),
            "y": Line("seq", seq, 2, seq // 2),
            "c": Line("seq", seq, 1, 2),
        }
        if dp % 4 == 0:
            self.lines["w"] = Line("dp", dp, 4, dp // 4)
            self.lines["u"] = Line("dp", dp, 2, 2)

    def device_of(self, back):
        at = {d: self.lines[d].place_back(back[d]) for d in back}
        z = at["z"] if "z" in at else at["w"] * 2 + at["u"]
        return ((z * 2 + at["x"]) * (self.seq // 2) + at["y"]) * 2 + at["c"]


def after(array, *others):
    return lax.optimization_barrier((array, *others))[0]


def assemble(pieces, widths, block, shape):
    arrays = [array for array, _, _ in pieces]
    dtype = arrays[0].dtype
    places = jnp.stack([shape.device_of(n) for _, names, _ in pieces for n in names])
    copies = sum(len(names) * len(spans) for _, names, spans in pieces)
    windows = [
        (min(span[0] for span in spans), max(span[0] + span[1] for span in spans))
        for _, _, spans in pieces
    ]
    held = [(array.shape[0], high - low) for array, (low, high) in zip(arrays, windows)]

    def kernel(places_ref, *refs):
        piece_refs, refs = refs[: len(pieces)], refs[len(pieces) :]
        out_refs, refs = refs[: len(widths)], refs[len(widths) :]
        buffers, (in_sems, out_sems) = refs[: len(pieces)], refs[len(pieces) :]
        loads = []
        for number, piece_ref in enumerate(piece_refs):
            low, high = windows[number]
            load = pltpu.make_async_copy(
                piece_ref.at[:, pl.ds(low, high - low)], buffers[number], in_sems.at[number]
            )
            load.start()
            loads.append(load)
        stores, begin = [], 0
        for number, (load, (_, names, spans)) in enumerate(zip(loads, pieces)):
            load.wait()
            for i in range(len(names)):
                to = pl.multiple_of(places_ref[begin + i] * block, block)
                for low, width, output, column in spans:
                    store = pltpu.make_async_copy(
                        buffers[number].at[pl.ds(i * block, block), pl.ds(low - windows[number][0], width)],
                        out_refs[output].at[pl.ds(to, block), pl.ds(column, width)],
                        out_sems.at[len(stores)],
                    )
                    store.start()
                    stores.append(store)
            begin += len(names)
        for store in stores:
            store.wait()

    size = sum(tall * wide for tall, wide in held) * dtype.itemsize
    return pl.pallas_call(
        kernel,
        out_shape=[jax.ShapeDtypeStruct((shape.devices * block, w), dtype) for w in widths],
        in_specs=[pl.BlockSpec(memory_space=pltpu.SMEM)]
        + [pl.BlockSpec(memory_space=pl.ANY)] * len(pieces),
        out_specs=[pl.BlockSpec(memory_space=pl.ANY)] * len(widths),
        scratch_shapes=[pltpu.VMEM(size, dtype) for size in held]
        + [
            pltpu.SemaphoreType.DMA((len(pieces),)),
            pltpu.SemaphoreType.DMA((copies,)),
        ],
        cost_estimate=pl.CostEstimate(flops=0, bytes_accessed=2 * size, transcendentals=0),
        name="assemble",
    )(places, *arrays)


class Gathering:
    def __init__(self, shape, array, names=None):
        self.shape, self.array = shape, array
        self.names = names or [dict(z=0, x=0, y=0, c=0)]

    def came(self, dim, direct=False, hold=()):
        line, array, out = self.shape.lines[dim], self.array, []
        for step in range(1, line.count):
            array = line.send(self.array, step) if direct else line.send(array)
            if step <= len(hold):
                array = after(array, *hold[step - 1])
            out.append((array, [dict(n, **{dim: step}) for n in self.names]))
        return out

    def along(self, dim, direct=False, hold=()):
        came = self.came(dim, direct, hold)
        array = jnp.concatenate([self.array] + [a for a, _ in came], 0)
        return Gathering(self.shape, array, self.names + [n for _, names in came for n in names])

    def ring(self, dim):
        return RingGathering(self, dim)

    def columns(self, low, high):
        return Gathering(self.shape, self.array[:, low:high], self.names)

    def pieces(self, dim, spans):
        found = [(self.array, self.names)] + self.came(dim)
        return [(array, names, spans) for array, names in found]


class RingGathering:
    def __init__(self, held, dim):
        self.held, self.dim, self.line = held, dim, held.shape.lines[dim]
        self.arrays = [held.array]
        self.came = self.line.send(held.array)

    def next(self, *hold):
        if len(self.arrays) == self.line.count - 1:
            return self.came
        self.arrays.append(after(self.came, *hold))
        self.came = self.line.send(self.arrays[-1])
        return self.arrays[-1]

    def end(self):
        while len(self.arrays) < self.line.count - 1:
            self.next()
        self.arrays.append(self.came)
        names = [dict(n, **{self.dim: s}) for s in range(self.line.count) for n in self.held.names]
        return Gathering(self.held.shape, jnp.concatenate(self.arrays, 0), names)


def spans_of(low, high, homes):
    spans = []
    for begin, width, output, column in homes:
        first, last = max(low, begin), min(high, begin + width)
        if first < last:
            spans.append((first - low, last - first, output, column + first - begin))
    return spans


def side_by_side(widths):
    return [(sum(widths[:i]), width, i, 0) for i, width in enumerate(widths)]


class TwoWays:
    def __init__(self, parts, shape, homes=None, widths=None):
        own = [part.shape[1] for part in parts]
        self.homes, self.widths = homes or side_by_side(own), widths or own
        self.block, self.shape = parts[0].shape[0], shape
        self.columns = sum(own)
        self.cut = -(-self.columns // 2 // LANES) * LANES
        self.held = Gathering(shape, jnp.concatenate(parts, axis=1))

    def first(self, *hold):
        self.held = self.held.along("z", True, [hold] * 8 if hold else ())

    def second(self, *hold):
        hold = [hold] if hold else ()
        self.one = self.held.columns(0, self.cut).along("x", False, hold)
        self.two = self.held.columns(self.cut, self.columns).along("y", False, hold)

    def third(self, *hold):
        hold = [hold] if hold else ()
        self.one, self.two = self.one.along("y", False, hold), self.two.along("x", False, hold)

    def last(self):
        self.ends = [self.one.came("c"), self.two.came("c")]

    def output(self, *outputs):
        homes = [(b, w, outputs.index(o), c) for b, w, o, c in self.homes if o in outputs]
        pieces = []
        for half, low, high, came in (
            (self.one, 0, self.cut, self.ends[0]),
            (self.two, self.cut, self.columns, self.ends[1]),
        ):
            spans = spans_of(low, high, homes)
            found = [(half.array, half.names)] + came
            pieces += [(array, names, spans) for array, names in found if spans]
        return assemble(pieces, [self.widths[o] for o in outputs], self.block, self.shape)


LAYOUT = "cyxwu"


def picker(shape, width):
    block = width // shape.devices
    if block % 16:
        order = jnp.arange(width)
    else:
        names = [dict()]
        for dim in LAYOUT:
            names = [dict(n, **{dim: s}) for n in names for s in range(shape.lines[dim].count)]
        places = jnp.stack([shape.device_of(n) for n in names])
        order = (places[:, None] * block + jnp.arange(block)[None, :]).reshape(width)
    return (jnp.arange(width)[:, None] == order[None, :]).astype(jnp.bfloat16)


def turned_rows(pick, left):
    return dot(pick, left, ((0,), (1,))).astype(jnp.bfloat16)


class Scattering:
    def __init__(self, shape, kept, arrived):
        half, columns = kept.shape
        self.shape, self.dims = shape, LAYOUT[1:]
        form = [shape.lines[d].count for d in self.dims] + [2 * half // shape.devices, columns]
        self.parts = [[kept.reshape(form), arrived.reshape(form)]]

    def beside(self, other):
        self.parts = self.parts + other.parts
        return self

    def term_of(self, step):
        found = []
        for terms in self.parts:
            own = [lax.index_in_dim(t, step, self.axis, False) for t in terms]
            found.append(functools.reduce(jnp.add, [t.astype(jnp.float32) for t in own]))
        return jnp.concatenate(found, axis=-1)

    def start(self, dim, *hold):
        self.line, self.axis, self.step = self.shape.lines[dim], self.dims.index(dim), 1
        self.dims = self.dims.replace(dim, "")
        if hold:
            self.parts = [[after(t, *hold) for t in terms] for terms in self.parts]
        self.sent = self.term_of(1).astype(jnp.bfloat16)
        self.came = self.line.send(self.sent)
        return self

    def advance(self, *hold):
        flat = [t for terms in self.parts for t in terms]
        came, *flat = lax.optimization_barrier((self.came, *flat, *hold))[: len(flat) + 1]
        self.parts = [[flat.pop(0) for _ in terms] for terms in self.parts]
        self.step += 1
        total = self.term_of(self.step % self.line.count) + came.astype(jnp.float32)
        if self.step < self.line.count:
            self.sent = total.astype(jnp.bfloat16)
            self.came = self.line.send(self.sent)
        else:
            self.parts, self.came = [[total]], None
        return self

    def along(self, dim):
        self.start(dim)
        while self.came is not None:
            self.advance()
        return self


def scatter_whole(kept, sent):
    whole = jnp.concatenate([kept, sent], 0).astype(jnp.float32)
    return lax.psum_scatter(whole, ("dp", "seq"), scatter_dimension=0, tiled=True)


FF_TILE = 256


def mlp_kernel(
    block, begins, ends, a_ref, g_ref, at_ref, gt_ref, gate_ref, up_ref, down_ref, *refs
):
    if not begins:
        y_in_ref, da_in_ref, *refs = refs
    if ends:
        x_ref, gain_ref, y_ref, dxo_ref, da_sum, kept_ref, sent_ref, *refs, y_sum = refs
    else:
        y_sum, da_sum, kept_ref, sent_ref, *refs = refs
    hidden_ref, d_gate_ref, d_up_ref = refs
    count = a_ref.shape[0]
    step = pl.program_id(0)

    @pl.when(step == 0)
    def _():
        y_sum[...] = jnp.zeros_like(y_sum) if begins else y_in_ref[...]
        da_sum[...] = jnp.zeros_like(da_sum) if begins else da_in_ref[...]

    for begin in range(0, count, block):
        span = slice(begin, begin + block)
        a, g = a_ref[span, :], g_ref[span, :]
        gate, up = dot(a, gate_ref[...]), dot(a, up_ref[...])
        d_hidden = dot(g, down_ref[...])
        sigma = jax.nn.sigmoid(gate)
        silu = gate * sigma
        hidden = (silu * up).astype(jnp.bfloat16)
        d_gate = (d_hidden * up * (sigma + silu * (1.0 - sigma))).astype(jnp.bfloat16)
        d_up = (d_hidden * silu).astype(jnp.bfloat16)
        hidden_ref[span, :], d_gate_ref[span, :], d_up_ref[span, :] = hidden, d_gate, d_up
        y_sum[span, :] += dot(hidden, down_ref[...], ((1,), (1,)))
        da_sum[span, :] += dot(d_gate, gate_ref[...], ((1,), (1,))) + dot(
            d_up, up_ref[...], ((1,), (1,))
        )
    half = at_ref.shape[0] // 2
    for number, (left, right) in enumerate(
        ((at_ref, d_gate_ref), (at_ref, d_up_ref), (gt_ref, hidden_ref))
    ):
        kept_ref[number] = dot(left[:half, :], right[...]).astype(jnp.bfloat16)
        sent_ref[number] = dot(left[half:, :], right[...]).astype(jnp.bfloat16)
    if not ends:
        return

    @pl.when(step == pl.num_programs(0) - 1)
    def _():
        for begin in range(0, count, block):
            span = slice(begin, begin + block)
            x = x_ref[span, :]
            y_ref[span, :] = (x + y_sum[span, :]).astype(y_ref.dtype)
            scale = lax.rsqrt(jnp.mean(x * x, axis=1, keepdims=True) + epsilon)
            normed = x * scale
            d_normed = da_sum[span, :] * gain_ref[...]
            mean = jnp.mean(d_normed * normed, axis=1, keepdims=True)
            dx = g_ref[span, :].astype(jnp.float32) + scale * (d_normed - normed * mean)
            da_sum[span, :] = dx
            dxo_ref[span, :] = dx.astype(dxo_ref.dtype)


def feed_forward(a, g, a_turned, g_turned, weights, tiles, sums=None, ending=None):
    count, width = a.shape
    half = width // 2

    def held(rows, columns):
        return pl.BlockSpec((rows, columns), lambda j: (0, 0), pipeline_mode=pl.Buffered(1))

    def tile(first):
        return pl.BlockSpec((width, FF_TILE), lambda j: (0, first + j))

    def shape(dtype):
        return jax.ShapeDtypeStruct((count, width), dtype)

    full = held(count, width)
    given = [a, g, a_turned, g_turned] + [array for array, _ in weights]
    specs = [full, full] + [held(width, count)] * 2 + [tile(first) for _, first in weights]
    scratch = [pltpu.VMEM((count, FF_TILE), jnp.bfloat16)] * 3
    if sums is not None:
        given, specs = given + list(sums), specs + [full] * 2
    if ending is not None:
        given, specs = given + list(ending), specs + [full, held(1, width)]
        outs = [shape(jnp.bfloat16), shape(jnp.bfloat16), shape(jnp.float32)]
        scratch = scratch + [pltpu.VMEM((count, width), jnp.float32)]
    else:
        outs = [shape(jnp.float32)] * 2
    hidden = tiles * FF_TILE
    return pl.pallas_call(
        functools.partial(mlp_kernel, min(512, count), sums is None, ending is not None),
        grid=(tiles,),
        in_specs=specs,
        out_specs=[full] * len(outs)
        + [pl.BlockSpec((3, half, FF_TILE), lambda j: (0, 0, j))] * 2,
        out_shape=outs + [jax.ShapeDtypeStruct((3, half, hidden), jnp.bfloat16)] * 2,
        scratch_shapes=scratch,
        compiler_params=pltpu.CompilerParams(
            dimension_semantics=("arbitrary",), vmem_limit_bytes=60 * 2**20
        ),
        cost_estimate=pl.CostEstimate(
            flops=18 * count * width * hidden,
            bytes_accessed=12 * width * hidden + 20 * count * width,
            transcendentals=count * hidden,
        ),
        name="mlp",
    )(*given)


def gain_gradient(weights, gradients, gain):
    products = jnp.sum(weights.astype(jnp.float32) * gradients, axis=1)
    return products / gain.astype(jnp.float32)


def per_device(
    shape,
    layer_input,
    segment_ids,
    gain_attn,
    w_query,
    w_key,
    w_value,
    w_out,
    gain_mlp,
    w_gate,
    w_up,
    w_down,
    grad_output,
):
    rows, shard_len, width = layer_input.shape
    count = rows * shard_len
    narrow, hidden = HEADS * FEAT, w_gate.shape[1]
    attention = Attention(rows, shard_len, width)
    groups, wide, across = attention.groups, attention.wide, attention.across
    gains = jnp.pad(jnp.stack([gain_attn, gain_mlp], axis=1), ((0, 0), (0, LANES - 2)))
    first_parts = [w_query, w_key, w_value, gains]
    homes, grouped = [], []
    for g in range(groups):
        for part, begin, size, place in (
            (w_query, 0, LANES, 0),
            (w_key, narrow, LANES, LANES),
            (w_value, 2 * narrow, wide, 2 * LANES),
        ):
            homes.append((begin + g * size, size, 0, g * across + place))
            grouped.append(part[:, g * size : (g + 1) * size])
    homes.append((groups * across, LANES, 0, groups * across))
    spare = ((0, 0), (0, -hidden % FF_TILE))
    gate_part, up_part, down_part = (
        jnp.pad(part, spare) for part in (w_gate, w_up, w_down.T)
    )
    tiles = gate_part.shape[1] // FF_TILE
    ringed = gains.shape[0] % 16 == 0
    if ringed:
        early = TwoWays(first_parts, shape, homes, [groups * across + LANES])
        rest = TwoWays([gate_part, w_out, up_part], shape)
        early.first()
        early.second()
        early.third()
        begun = [early.one.array, early.two.array]
        rest.first(*begun)
        down = Gathering(shape, down_part).along("x", False, [begun])
        early.last()
        (gathered,) = early.output(0)
    else:
        first_part = jnp.concatenate(grouped + [gains], axis=1)
        gathered, out_w, gate_w, up_w, down_w = (
            lax.all_gather(part, ("dp", "seq"), axis=0, tiled=True)
            for part in (first_part, w_out, gate_part, up_part, down_part)
        )
    qkv_w = gathered[:, : groups * across]
    gain_one = gathered[:, groups * across].astype(jnp.float32)[None, :]
    gain_two = gathered[:, groups * across + 1].astype(jnp.float32)[None, :]

    pick = picker(shape, width)
    cotangent = grad_output.reshape(count, width)
    tokens = layer_input.reshape(count, width).astype(jnp.float32)
    scale_one, normed_one = norm_forward(tokens)
    a_one = (normed_one * gain_one).astype(jnp.bfloat16)
    a_one = after(a_one, rest.held.array, down.array) if ringed else a_one
    qkv = jnp.dot(a_one, qkv_w, preferred_element_type=jnp.float32).astype(jnp.bfloat16)
    place = lax.axis_index("seq")
    own_seg = lax.dynamic_slice_in_dim(segment_ids, place * shard_len, shard_len, 1)
    seg, seg_row = own_seg.reshape(count, 1), own_seg.reshape(rows, 1, shard_len)
    reach = min(shape.seq - 1, -(-(LONGEST - 1) // shard_len))
    states = Passing(segment_ids, shard_len, reach, shape.seq)
    if ringed:
        down = down.along("y", False, [[qkv]])
        tail = attention.tail(after(qkv, down.array), seg)
        rest.second(tail)
        states.start(tail, 1)
        ring = down.ring("z")
        turn = ring.next(tail)
        top, den = attention.near(
            after(qkv, rest.one.array, rest.two.array, turn), seg, seg_row
        )
        turn = ring.next(den)
        earlier = after(states.end(den), turn)
        mixed_cat, inverse = attention.far(qkv, seg, earlier, top, den)
        rest.third(mixed_cat)
        rest.last()
        down = ring.end()
        down_ends = down.pieces("c", [(0, tiles * FF_TILE, 0, 0)])
        (out_w,) = rest.output(1)
    else:
        tail = attention.tail(qkv, seg)
        states.start(tail, 1)
        earlier = states.end()
        top, den = attention.near(qkv, seg, seg_row)
        mixed_cat, inverse = attention.far(qkv, seg, earlier, top, den)
    x_two = tokens + jnp.dot(mixed_cat, out_w, preferred_element_type=jnp.float32)
    scale_two, normed_two = norm_forward(x_two)
    a_two = (normed_two * gain_two).astype(jnp.bfloat16)
    a_turned = turned_rows(pick, a_two)
    turned_mixed, turned_one = turned_rows(pick, mixed_cat), turned_rows(pick, a_one)
    if ringed:
        gate_w, up_w = rest.output(0, 2)
        a_turned = after(a_turned, turned_mixed, turned_one)
        (down_w,) = assemble(down_ends, [tiles * FF_TILE], down_part.shape[0], shape)
    result, d_branch, d_x_two, kept, sent = feed_forward(
        a_two,
        cotangent,
        a_turned,
        turned_rows(pick, cotangent),
        [(gate_w, 0), (up_w, 0), (down_w, 0)],
        tiles,
        None,
        (x_two, gain_two),
    )
    half = width // 2
    d_mixed = against(d_branch, out_w).astype(jnp.bfloat16)
    ahead, d_top, d_den = attention.head(qkv, d_mixed, mixed_cat, inverse, seg)
    states.start(ahead, -1)
    own = after(d_branch, ahead) if ringed else d_branch
    out_sent, out_kept = (
        dot(t, own).astype(jnp.bfloat16) for t in (turned_mixed[half:], turned_mixed[:half])
    )
    if ringed:
        send_core = shape.lines["c"].send
        arrived, out_arrived = send_core(sent), send_core(out_sent)
        arrived = after(arrived, out_sent, out_kept)
        gate_sum, up_sum, down_sum = (Scattering(shape, kept[i], arrived[i]) for i in range(3))
        gate_sum.beside(Scattering(shape, out_kept, out_arrived)).start("y")
        up_sum.start("x")
        down_sum.start("u")
        d_top = after(d_top, gate_sum.sent, up_sum.sent, down_sum.sent)
        d_near = attention.near_back(qkv, d_top, d_den, seg, seg_row, earlier)
        near = d_near[0]
        gate_sum.advance(near).start("x")
        up_sum.advance(near).start("y")
        down_sum.advance(near).start("w")
        later = after(states.end(near), down_sum.sent, gate_sum.sent, up_sum.sent)

        d_qkv = attention.far_back(qkv, seg, later, *d_near)
        both = gate_sum.advance(d_qkv).beside(up_sum.advance(d_qkv)).start("u")
        right = after(d_qkv, both.sent)
        own_sent = dot(turned_one[half:], right).astype(jnp.bfloat16)
        own_kept = dot(turned_one[:half], right).astype(jnp.bfloat16)
        arrived = after(send_core(own_sent), own_kept)
        down_sum.advance(own_kept).start("x")
        arrived = after(arrived, down_sum.sent)
        qkv_a, qkv_b = (
            Scattering(shape, own_kept[:, low : low + across], arrived[:, low : low + across])
            for low in (0, across)
        )
        qkv_a.start("y")
        qkv_b.start("x")
        d_qkv = after(d_qkv, qkv_a.sent, qkv_b.sent)
        both.advance(qkv_a.sent, qkv_b.sent).start("w")
        qkv_b.advance(both.sent).start("y")
        qkv_a.advance(both.sent).start("x")
        down_sum.advance(qkv_a.sent).start("y")
        qkv_sum = qkv_a.advance(qkv_b.sent).beside(qkv_b.advance()).start("u")
        down_sum.advance(both.sent)
        qkv_sum.advance().start("w")
        both.advance()
        qkv_sum.advance()
        grad_qkv, both, down_sum = (part.parts[0][0] for part in (qkv_sum, both, down_sum))
        grad_qkv = [grad_qkv[:, g * across : (g + 1) * across] for g in range(groups)]
        padded = tiles * FF_TILE
        grad_gate, grad_out = both[:, :hidden], both[:, padded : padded + width]
        grad_up = both[:, padded + width : padded + width + hidden]
        grad_down = down_sum[:, :hidden]
    else:
        later = states.end()
        d_near = attention.near_back(qkv, d_top, d_den, seg, seg_row, earlier)
        grad_gate, grad_up, grad_down = (
            scatter_whole(kept[i], sent[i])[:, :hidden] for i in range(3)
        )
        grad_out = scatter_whole(out_kept, out_sent)
        d_qkv = attention.far_back(qkv, seg, later, *d_near)
        whole = scatter_whole(dot(turned_one[:half], d_qkv), dot(turned_one[half:], d_qkv))
        grad_qkv = [whole[:, g * across : (g + 1) * across] for g in range(groups)]
    d_a_one = against(d_qkv, qkv_w)
    d_tokens = d_x_two + norm_backward(d_a_one, gain_one, scale_one, normed_one)
    return (
        result.reshape(rows, shard_len, width),
        d_tokens.reshape(rows, shard_len, width),
        gain_gradient(jnp.concatenate(grouped, axis=1), jnp.concatenate(grad_qkv, axis=1), gain_attn),
        jnp.concatenate([part[:, Q] for part in grad_qkv], axis=1),
        jnp.concatenate([part[:, K] for part in grad_qkv], axis=1),
        jnp.concatenate([part[:, V] for part in grad_qkv], axis=1),
        grad_out,
        gain_gradient(
            jnp.concatenate([w_gate, w_up], axis=1),
            jnp.concatenate([grad_gate, grad_up], axis=1),
            gain_mlp,
        ),
        grad_gate,
        grad_up,
        grad_down.T,
    )


def solution(mesh):
    placed = (
        P("dp", "seq", None),
        P("dp", None),
        P(("dp", "seq")),
        P(("dp", "seq"), None),
        P(("dp", "seq"), None),
        P(("dp", "seq"), None),
        P(("dp", "seq"), None),
        P(("dp", "seq")),
        P(("dp", "seq"), None),
        P(("dp", "seq"), None),
        P(None, ("dp", "seq")),
        P("dp", "seq", None),
    )
    return jax.shard_map(
        functools.partial(per_device, Slice(mesh.shape["dp"], mesh.shape["seq"])),
        mesh=mesh,
        in_specs=placed,
        out_specs=(
            P("dp", "seq", None),
            P("dp", "seq", None),
            P(("dp", "seq")),
            P(("dp", "seq"), None),
            P(("dp", "seq"), None),
            P(("dp", "seq"), None),
            P(("dp", "seq"), None),
            P(("dp", "seq")),
            P(("dp", "seq"), None),
            P(("dp", "seq"), None),
            P(None, ("dp", "seq")),
        ),
        check_vma=False,
    )
```

```python
import functools

import jax
import jax.numpy as jnp
import numpy as np
from jax import lax
from jax.experimental import pallas as pl
from jax.experimental.pallas import tpu as pltpu
from jax.sharding import PartitionSpec as P

LONGEST = 1024
HEADS = 16
FEAT = 16
LANES = 128
GROUP = LANES // FEAT
PIECES = FEAT // 2 + 2
WIDE = PIECES * LANES
PACKED = WIDE // 2 + 16


def dot(left, right, dims=((1,), (0,))):
    return lax.dot_general(left, right, (dims, ((), ())), preferred_element_type=jnp.float32)


def rolls(scaled):
    zero = lax.optimization_barrier(jnp.int32(0))
    row = lax.broadcasted_iota(jnp.int32, (LANES, WIDE), 0) + zero
    column = lax.broadcasted_iota(jnp.int32, (LANES, WIDE), 1)
    d, lane = column // LANES - 1, column % LANES
    a = lane % FEAT
    goal = lane - a + (a + d) % FEAT
    found = (row == goal) & (d >= 0) & ((d < FEAT // 2) | (a < FEAT // 2))
    factor = jnp.where(d == 0, 1 / 32, 1 / 16) if scaled else 1.0
    return jnp.where(found, factor, 0.0).astype(jnp.bfloat16)


def features(rows, factors, lin, axis):
    x = rows.astype(jnp.float32)
    pieces = [x * lin]
    for number in range(PIECES - 1):
        span = slice(number * LANES, (number + 1) * LANES)
        piece = x * (factors[:, span] if axis else factors[span, :])
        if number == PIECES - 2:
            place = lax.broadcasted_iota(jnp.int32, piece.shape, axis)
            piece = jnp.where(place % FEAT == FEAT // 2, 1.0, piece)
        pieces.append(piece)
    return jnp.concatenate([piece.astype(jnp.bfloat16) for piece in pieces], axis=axis)


def turned_features(rows, turned_pick_ref, lin):
    turned = rows.astype(jnp.float32).T.astype(jnp.bfloat16)
    return features(turned, dot(turned_pick_ref[LANES:, :], turned), lin, 0)


def upright_features(rows, pick_ref, lin):
    return features(rows, dot(rows, pick_ref[:, LANES:]), lin, 1)


def head_mask(lanes_per_head, first_head):
    row_head = lax.broadcasted_iota(jnp.int32, (LANES, LANES), 0) // FEAT
    lane_head = lax.broadcasted_iota(jnp.int32, (LANES, LANES), 1) // lanes_per_head + first_head
    return row_head == lane_head


def head_masks(value_dim):
    per = LANES // value_dim
    return [head_mask(value_dim, part * per) for part in range(GROUP // per)]


def low_half():
    return lax.broadcasted_iota(jnp.int32, (LANES, LANES), 1) < LANES // 2


def piece_spans():
    return [slice(number * LANES, (number + 1) * LANES) for number in range(PIECES)]


def fold_heads(rows, masks):
    total = None
    for part, mask in enumerate(masks):
        piece = jnp.where(mask, rows[:, part * LANES : (part + 1) * LANES], 0.0)
        total = piece if total is None else total + piece
    return total + pltpu.roll(total, LANES // 2, 1)


def diagonal():
    row = lax.broadcasted_iota(jnp.int32, (LANES, LANES), 0)
    return row == lax.broadcasted_iota(jnp.int32, (LANES, LANES), 1)


def pack_state(out_ref, pieces):
    low, straight = low_half(), diagonal()
    for number in range(0, PIECES, 2):
        rows = slice(number // 2 * LANES, (number // 2 + 1) * LANES)
        values = jnp.where(low, pieces[number][0], pieces[number + 1][0])
        out_ref[0, 0, rows, :] = values.astype(out_ref.dtype)
    sums = [jnp.sum(jnp.where(straight, s, 0.0), axis=0, keepdims=True) for _, s in pieces]
    sums.append(jnp.zeros((PACKED - WIDE // 2 - PIECES, LANES), jnp.float32))
    out_ref[0, 0, WIDE // 2 :, :] = jnp.concatenate(sums, axis=0).astype(out_ref.dtype)


def spread_state(state_ref, wide_ref, value_dim, sums_of):
    masks, low, straight = head_masks(value_dim), low_half(), diagonal()
    all_sums = state_ref[0, 0, WIDE // 2 :, :].astype(jnp.float32)
    for number, span in enumerate(piece_spans()):
        rows = slice(number // 2 * LANES, (number // 2 + 1) * LANES)
        state = state_ref[0, 0, rows, :].astype(jnp.float32)
        turned = pltpu.roll(state, LANES // 2, 1)
        values = jnp.where(low, turned, state) if number % 2 else jnp.where(low, state, turned)
        sums = jnp.where(straight, all_sums[number : number + 1, :], 0.0)
        sums = jnp.broadcast_to(jnp.sum(sums, axis=1, keepdims=True), (LANES, LANES))
        parts = [jnp.where(mask, values, 0.0) for mask in masks] + sums_of(sums, masks)
        for place, part in enumerate(parts):
            wide_ref[span, slice(place * LANES, (place + 1) * LANES)] = part.astype(jnp.bfloat16)


def own_lanes(array, lanes_per_head, head):
    place = lax.broadcasted_iota(jnp.int32, array.shape, 1) // lanes_per_head
    return jnp.where(place == head, array, jnp.zeros_like(array))


Q, K, V = slice(0, LANES), slice(LANES, 2 * LANES), slice(2 * LANES, None)


def tail_kernel(value_dim, x_ref, seg_ref, pick_ref, out_ref):
    seg = seg_ref[...]
    keep = (seg == seg[-1:, :]).astype(jnp.float32)
    values = (x_ref[:, V].astype(jnp.float32) * keep).astype(jnp.bfloat16)
    ones = jnp.broadcast_to(keep, (seg.shape[0], LANES)).astype(jnp.bfloat16)
    phi = turned_features(x_ref[:, K], pick_ref, 1.0)
    full = dot(phi, jnp.concatenate([values, ones], axis=1))
    width, masks = values.shape[1], head_masks(value_dim)
    pack_state(
        out_ref,
        [(fold_heads(full[span, :width], masks), full[span, width:]) for span in piece_spans()],
    )


def masks_of(seg_ref, seg_row_ref, begin, block):
    stop = begin + block
    rows = begin + lax.broadcasted_iota(jnp.int32, (block, stop), 0)
    columns = lax.broadcasted_iota(jnp.int32, (block, stop), 1)
    same = seg_ref[begin:stop, :] == seg_row_ref[0, :, :stop]
    return ((rows >= columns) & same).astype(jnp.float32)


def near_kernel(value_dim, block, x_ref, seg_ref, seg_row_ref, top_ref, den_ref):
    length = x_ref.shape[0]
    low = lax.broadcasted_iota(jnp.int32, (block, LANES), 1) < value_dim
    for begin in range(0, length, block):
        stop = begin + block
        mask = masks_of(seg_ref, seg_row_ref, begin, block)
        queries = x_ref[begin:stop, Q] * jnp.bfloat16(FEAT ** (-0.5))
        keys = x_ref[:stop, K]
        ones = jnp.ones((stop, LANES), jnp.bfloat16)
        for pair in range(GROUP // 2):
            span = slice(pair * LANES, (pair + 1) * LANES)
            first = 2 * LANES + pair * LANES
            values = jnp.concatenate([x_ref[:stop, first : first + LANES], ones], axis=1)
            sides = []
            for head in (2 * pair, 2 * pair + 1):
                scores = dot(own_lanes(queries, FEAT, head), keys, ((1,), (1,)))
                weights = (((0.5 * scores + 1.0) * scores + 1.0) * mask).astype(jnp.bfloat16)
                sides.append(dot(weights, values))
            top_ref[begin:stop, span] = jnp.where(low, sides[0][:, :LANES], sides[1][:, :LANES])
            den_ref[begin:stop, span] = jnp.where(low, sides[0][:, LANES:], sides[1][:, LANES:])


def far_kernel(value_dim, x_ref, seg_ref, state_ref, top_ref, den_ref, pick_ref, *rest):
    y_ref, inverse_ref, state_wide = rest[-3:]
    width = top_ref.shape[1]
    spread_state(
        state_ref, state_wide, value_dim,
        lambda sums, masks: [jnp.where(mask, sums, 0.0) for mask in masks],
    )
    seg = seg_ref[...]
    keep = (seg == seg[:1, :]).astype(jnp.float32)
    far = dot(upright_features(x_ref[:, Q], pick_ref, FEAT ** (-0.5)), state_wide[...])
    top = top_ref[...] + keep * far[:, :width]
    inverse = 1.0 / (den_ref[...] + keep * far[:, width:])
    y_ref[...] = (top * inverse).astype(y_ref.dtype)
    inverse_ref[...] = inverse


def head_kernel(
    value_dim, x_ref, dy_ref, y_ref, inverse_ref, seg_ref, pick_ref, out_ref, dn_ref, dd_ref
):
    width = dy_ref.shape[1]
    d_top = dy_ref[...].astype(jnp.float32) * inverse_ref[...]
    product = d_top * y_ref[...].astype(jnp.float32)
    large = product.astype(jnp.bfloat16)
    small = (product - large.astype(jnp.float32)).astype(jnp.bfloat16)
    row = lax.broadcasted_iota(jnp.int32, (width, LANES), 0) // value_dim
    lane = lax.broadcasted_iota(jnp.int32, (width, LANES), 1) // FEAT
    adder = jnp.where(row == lane, -1.0, 0.0).astype(jnp.bfloat16)
    d_den = dot(large, adder) + dot(small, adder)
    rounded = d_den.astype(jnp.bfloat16).astype(jnp.float32)
    place = lax.broadcasted_iota(jnp.int32, d_den.shape, 1) % FEAT
    d_den = jnp.where(place < FEAT // 2, rounded, d_den - rounded)
    seg = seg_ref[...]
    keep = (seg == seg[:1, :]).astype(jnp.float32)
    dn_ref[...] = d_top.astype(jnp.bfloat16)
    dd_ref[...] = d_den.astype(jnp.bfloat16)
    d_both = [(d_top * keep).astype(jnp.bfloat16), (d_den * keep).astype(jnp.bfloat16)]
    full = dot(
        turned_features(x_ref[:, Q], pick_ref, FEAT ** (-0.5)), jnp.concatenate(d_both, axis=1)
    )
    masks, own, pieces = head_masks(value_dim), head_mask(FEAT, 0), []
    for span in piece_spans():
        sums = jnp.where(own, full[span, width:], 0.0)
        sums = jnp.sum(sums, axis=1, keepdims=True) * (2 / FEAT)
        pieces.append((fold_heads(full[span, :width], masks), sums))
    pack_state(out_ref, pieces)


def from_features(d_phi, rows, pick_ref, lin):
    x = rows.astype(jnp.float32)
    factors = dot(rows, pick_ref[:, LANES:])
    total, scaled = d_phi[:, :LANES] * lin, []
    for number in range(PIECES - 1):
        span = slice(number * LANES, (number + 1) * LANES)
        piece = d_phi[:, (number + 1) * LANES : (number + 2) * LANES]
        total = total + piece * factors[:, span]
        scaled.append((piece * x).astype(jnp.bfloat16))
    return total + dot(jnp.concatenate(scaled, axis=1), pick_ref[:, LANES:], ((1,), (1,)))


def near_back_kernel(
    value_dim, block, x_ref, dn_ref, dd_ref, seg_ref, seg_row_ref, state_ref, pick_ref,
    dq_ref, dk_ref, dv_ref, state_wide, dq_sum,
):
    length, width = dn_ref.shape
    own = head_mask(FEAT, 0)
    spread_state(
        state_ref, state_wide, value_dim,
        lambda sums, masks: [jnp.where(own, sums, 0.0) * (2 / FEAT)],
    )
    keep = seg_ref[...] == seg_ref[:1, :]
    d_both = jnp.concatenate([dn_ref[...], dd_ref[...]], axis=1)
    d_phi = dot(jnp.where(keep, d_both, jnp.zeros_like(d_both)), state_wide[...], ((1,), (1,)))
    dq_sum[...] = from_features(d_phi, x_ref[:, Q], pick_ref, FEAT ** (-0.5))
    scale = jnp.bfloat16(FEAT ** (-0.5))
    low = lax.broadcasted_iota(jnp.int32, (block, LANES), 1) < value_dim
    for begin in range(0, length, block):
        stop, count = begin + block, length - begin
        key_place = lax.broadcasted_iota(jnp.int32, (block, count), 0)
        query_place = lax.broadcasted_iota(jnp.int32, (block, count), 1)
        same = seg_ref[begin:stop, :] == seg_row_ref[0, :, begin:]
        mask = ((query_place >= key_place) & same).astype(jnp.float32)
        queries = x_ref[begin:, Q] * scale
        keys = x_ref[begin:stop, K]
        dd = dd_ref[begin:, :]
        dk = jnp.zeros((block, LANES), jnp.float32)
        for pair in range(GROUP // 2):
            span = slice(pair * LANES, (pair + 1) * LANES)
            first = 2 * LANES + pair * LANES
            values = x_ref[begin:stop, first : first + LANES]
            dn = dn_ref[begin:, span]
            d_both = jnp.concatenate([dn, dd], axis=1)
            sides = []
            for side in range(2):
                head = 2 * pair + side
                own_keys = own_lanes(keys, FEAT, head)
                ones = own_lanes(jnp.full((block, LANES), 2 / FEAT, jnp.bfloat16), FEAT, head)
                own_values = own_lanes(values, value_dim, side)
                scores = dot(own_keys, queries, ((1,), (1,)))
                weights = (((0.5 * scores + 1.0) * scores + 1.0) * mask).astype(jnp.bfloat16)
                d_weights = dot(
                    jnp.concatenate([own_values, ones], axis=1), d_both, ((1,), (1,))
                )
                d_scores = (d_weights * ((scores + 1.0) * mask)).astype(jnp.bfloat16)
                sides.append(dot(weights, dn))
                dk = dk + own_lanes(dot(d_scores, queries), FEAT, head)
                dq_sum[begin:, :] += dot(d_scores, own_keys * scale, ((0,), (0,)))
            dv_ref[begin:stop, span] = jnp.where(low, sides[0], sides[1])
        dk_ref[begin:stop, :] = dk
    dq_ref[...] = dq_sum[...].astype(dq_ref.dtype)


def far_back_kernel(
    value_dim, x_ref, seg_ref, state_ref, dq_ref, dk_ref, dv_ref, pick_ref, out_ref, state_wide
):
    length, width = dv_ref.shape
    spread_state(state_ref, state_wide, value_dim, lambda sums, masks: [sums * (1 / LANES)])
    seg = seg_ref[...]
    keep = (seg == seg[-1:, :]).astype(jnp.float32)
    keys = x_ref[:, K]
    ones = jnp.ones((length, LANES), jnp.bfloat16)
    d_phi = dot(jnp.concatenate([x_ref[:, V], ones], axis=1), state_wide[...], ((1,), (1,)))
    dk = dk_ref[...] + keep * from_features(d_phi, keys, pick_ref, 1.0)
    dv = dv_ref[...] + keep * dot(upright_features(keys, pick_ref, 1.0), state_wide[:, :width])
    out_ref[:, Q] = dq_ref[...]
    out_ref[:, K] = dk.astype(out_ref.dtype)
    out_ref[:, V] = dv.astype(out_ref.dtype)


class Attention:
    def __init__(self, rows, length, width):
        self.rows, self.length = rows, length
        self.value_dim = width // HEADS
        self.groups = HEADS // GROUP
        self.wide = GROUP * self.value_dim
        self.across = 2 * LANES + self.wide
        self.block = min(256, length)
        self.count = rows * length
        self.scaled, self.plain = rolls(True), rolls(False)
        self.all = range(self.groups)

    def specs(self, groups):
        def rows_of(columns):
            return pl.BlockSpec((self.length, columns), lambda r, g: (r, g))

        return dict(
            x=rows_of(self.across),
            values=rows_of(self.wide),
            narrow=rows_of(LANES),
            seg=pl.BlockSpec((self.length, 1), lambda r, g: (r, 0)),
            seg_row=pl.BlockSpec((1, 1, self.length), lambda r, g: (r, 0, 0)),
            state=pl.BlockSpec((1, 1, PACKED, LANES), lambda r, g: (r, g, 0, 0)),
            pick=pl.BlockSpec((LANES, WIDE), lambda r, g: (0, 0)),
            turned_pick=pl.BlockSpec((WIDE, LANES), lambda r, g: (0, 0)),
        )

    def shape(self, columns, dtype, groups):
        return jax.ShapeDtypeStruct((self.count, columns * len(groups)), dtype)

    def state_shape(self, groups):
        return jax.ShapeDtypeStruct((self.rows, len(groups), PACKED, LANES), jnp.bfloat16)

    def wide_state(self, columns):
        return pltpu.VMEM((WIDE, columns), jnp.bfloat16)

    def call(self, kernel, groups, specs, outs, out_specs, scratch, passes, name):
        return pl.pallas_call(
            functools.partial(kernel, self.value_dim),
            grid=(self.rows, len(groups)),
            in_specs=specs,
            out_specs=out_specs,
            out_shape=outs,
            scratch_shapes=scratch,
            compiler_params=pltpu.CompilerParams(
                dimension_semantics=("arbitrary", "arbitrary"), vmem_limit_bytes=56 * 2**20
            ),
            cost_estimate=pl.CostEstimate(
                flops=self.rows * len(groups) * GROUP * passes * 2**26 * self.length // 512,
                bytes_accessed=2**21,
                transcendentals=0,
            ),
            name=name,
        )

    def tail(self, x, seg):
        at = self.specs(self.all)
        return self.call(
            tail_kernel, self.all, [at["x"], at["seg"], at["turned_pick"]],
            self.state_shape(self.all), at["state"], [], 5, "attn_tail",
        )(x, seg, self.plain.T)

    def near(self, x, seg, seg_row):
        def kernel(value_dim, *refs):
            near_kernel(value_dim, self.block, *refs)

        at = self.specs(self.all)
        out = self.shape(self.wide, jnp.float32, self.all)
        return self.call(
            kernel, self.all, [at["x"], at["seg"], at["seg_row"]],
            [out, out], [at["values"]] * 2, [], 8, "attn_near",
        )(x, seg, seg_row)

    def far(self, x, seg, state, top, den):
        at = self.specs(self.all)
        return self.call(
            far_kernel, self.all,
            [at["x"], at["seg"], at["state"], at["values"], at["values"], at["pick"]],
            [self.shape(self.wide, dtype, self.all) for dtype in (jnp.bfloat16, jnp.float32)],
            [at["values"]] * 2, [self.wide_state(2 * self.wide)], 8, "attn_far",
        )(x, seg, state, top, den, self.scaled)

    def head(self, x, dy, y, inverse, seg):
        at = self.specs(self.all)
        return self.call(
            head_kernel, self.all,
            [at["x"], at["values"], at["values"], at["values"], at["seg"], at["turned_pick"]],
            [self.state_shape(self.all), self.shape(self.wide, jnp.bfloat16, self.all),
             self.shape(LANES, jnp.bfloat16, self.all)],
            [at["state"], at["values"], at["narrow"]], [], 5, "attn_head",
        )(x, dy, y, inverse, seg, self.scaled.T)

    def near_back(self, x, dn, dd, seg, seg_row, state):
        def kernel(value_dim, *refs):
            near_back_kernel(value_dim, self.block, *refs)

        at, groups = self.specs(self.all), self.all
        return self.call(
            kernel, groups,
            [at["x"], at["values"], at["narrow"], at["seg"], at["seg_row"], at["state"],
             at["pick"]],
            [self.shape(LANES, jnp.bfloat16, groups), self.shape(LANES, jnp.float32, groups),
             self.shape(self.wide, jnp.float32, groups)],
            [at["narrow"], at["narrow"], at["values"]],
            [self.wide_state(self.wide + LANES), pltpu.VMEM((self.length, LANES), jnp.float32)],
            24, "attn_near_back",
        )(x, dn, dd, seg, seg_row, state, self.scaled)

    def far_back(self, x, seg, state, dq, dk, dv):
        at, groups = self.specs(self.all), self.all
        return self.call(
            far_back_kernel, groups,
            [at["x"], at["seg"], at["state"], at["narrow"], at["narrow"], at["values"],
             at["pick"]],
            self.shape(self.across, jnp.bfloat16, groups), at["x"],
            [self.wide_state(self.wide + LANES)], 9, "attn_far_back",
        )(x, seg, state, dq, dk, dv, self.plain)


class Passing:
    def __init__(self, segment_ids, length, reach, size):
        self.ids, self.length, self.reach, self.size = segment_ids, length, reach, size
        self.place = lax.axis_index("seq")

    def id_at(self, device, last):
        position = jnp.clip(device, 0, self.size - 1) * self.length + last * (self.length - 1)
        return lax.dynamic_index_in_dim(self.ids, position, 1, keepdims=False)

    def start(self, own, shift):
        self.shift, self.came = shift, []
        for k in range(1, self.reach + 1):
            goals = [(i, i + shift * k) for i in range(self.size)]
            pairs = [(i, goal) for i, goal in goals if 0 <= goal < self.size]
            self.came.append(lax.ppermute(own, "seq", pairs))

    def end(self, *hold):
        before = self.shift > 0
        own_id, total = self.id_at(self.place, not before), 0.0
        for k, came in enumerate(self.came, 1):
            linked = self.id_at(self.place - self.shift * k, before) == own_id
            came = after(came, *hold) if hold else came
            total = total + jnp.where(linked[:, None, None, None], came.astype(jnp.float32), 0.0)
        return total.astype(jnp.bfloat16)


epsilon = 1e-05


def against(left, matrix):
    return dot(left, matrix, ((1,), (1,)))


def norm_forward(values):
    scale = lax.rsqrt(jnp.mean(values * values, axis=1, keepdims=True) + epsilon)
    return (scale, values * scale)


def norm_backward(d_scaled, gain, scale, normed):
    d_normed = d_scaled * gain
    return scale * (d_normed - normed * jnp.mean(d_normed * normed, axis=1, keepdims=True))


def fold(count):
    return [0] + list(range(1, count, 2)) + list(range(2, count, 2))[::-1]


class Line:
    def __init__(self, axis, axis_size, stride, count):
        self.axis, self.size, self.stride, self.count = axis, axis_size, stride, count
        self.order = fold(count)

    def send(self, array, steps=1):
        pairs = []
        for index in range(self.size):
            place = (index // self.stride) % self.count
            goal = self.order[(self.order.index(place) + steps) % self.count]
            pairs.append((index, index + (goal - place) * self.stride))
        return lax.ppermute(array, self.axis, pairs)

    def place_back(self, steps):
        own = (lax.axis_index(self.axis) // self.stride) % self.count
        rank = jnp.asarray([self.order.index(p) for p in range(self.count)], jnp.int32)[own]
        return jnp.asarray(self.order, jnp.int32)[(rank - steps) % self.count]


class Slice:
    def __init__(self, dp, seq):
        self.dp, self.seq, self.devices = dp, seq, dp * seq
        self.lines = {
            "z": Line("dp", dp, 2, dp // 2),
            "x": Line("dp", dp, 1, 2),
            "y": Line("seq", seq, 2, seq // 2),
            "c": Line("seq", seq, 1, 2),
        }
        if dp % 4 == 0:
            self.lines["w"] = Line("dp", dp, 4, dp // 4)
            self.lines["u"] = Line("dp", dp, 2, 2)

    def device_of(self, back):
        at = {d: self.lines[d].place_back(back[d]) for d in back}
        z = at["z"] if "z" in at else at["w"] * 2 + at["u"]
        return ((z * 2 + at["x"]) * (self.seq // 2) + at["y"]) * 2 + at["c"]


def after(array, *others):
    return lax.optimization_barrier((array, *others))[0]


def assemble(pieces, widths, block, shape):
    arrays = [array for array, _, _ in pieces]
    dtype = arrays[0].dtype
    places = jnp.stack([shape.device_of(n) for _, names, _ in pieces for n in names])
    copies = sum(len(names) * len(spans) for _, names, spans in pieces)
    windows = [
        (min(span[0] for span in spans), max(span[0] + span[1] for span in spans))
        for _, _, spans in pieces
    ]
    held = [(array.shape[0], high - low) for array, (low, high) in zip(arrays, windows)]

    def kernel(places_ref, *refs):
        piece_refs, refs = refs[: len(pieces)], refs[len(pieces) :]
        out_refs, refs = refs[: len(widths)], refs[len(widths) :]
        buffers, (in_sems, out_sems) = refs[: len(pieces)], refs[len(pieces) :]
        loads = []
        for number, piece_ref in enumerate(piece_refs):
            low, high = windows[number]
            load = pltpu.make_async_copy(
                piece_ref.at[:, pl.ds(low, high - low)], buffers[number], in_sems.at[number]
            )
            load.start()
            loads.append(load)
        stores, begin = [], 0
        for number, (load, (_, names, spans)) in enumerate(zip(loads, pieces)):
            load.wait()
            for i in range(len(names)):
                to = pl.multiple_of(places_ref[begin + i] * block, block)
                for low, width, output, column in spans:
                    store = pltpu.make_async_copy(
                        buffers[number].at[pl.ds(i * block, block), pl.ds(low - windows[number][0], width)],
                        out_refs[output].at[pl.ds(to, block), pl.ds(column, width)],
                        out_sems.at[len(stores)],
                    )
                    store.start()
                    stores.append(store)
            begin += len(names)
        for store in stores:
            store.wait()

    size = sum(tall * wide for tall, wide in held) * dtype.itemsize
    return pl.pallas_call(
        kernel,
        out_shape=[jax.ShapeDtypeStruct((shape.devices * block, w), dtype) for w in widths],
        in_specs=[pl.BlockSpec(memory_space=pltpu.SMEM)]
        + [pl.BlockSpec(memory_space=pl.ANY)] * len(pieces),
        out_specs=[pl.BlockSpec(memory_space=pl.ANY)] * len(widths),
        scratch_shapes=[pltpu.VMEM(size, dtype) for size in held]
        + [
            pltpu.SemaphoreType.DMA((len(pieces),)),
            pltpu.SemaphoreType.DMA((copies,)),
        ],
        cost_estimate=pl.CostEstimate(flops=0, bytes_accessed=2 * size, transcendentals=0),
        name="assemble",
    )(places, *arrays)


class Gathering:
    def __init__(self, shape, array, names=None):
        self.shape, self.array = shape, array
        self.names = names or [dict(z=0, x=0, y=0, c=0)]

    def came(self, dim, direct=False, hold=()):
        line, array, out = self.shape.lines[dim], self.array, []
        for step in range(1, line.count):
            array = line.send(self.array, step) if direct else line.send(array)
            if step <= len(hold):
                array = after(array, *hold[step - 1])
            out.append((array, [dict(n, **{dim: step}) for n in self.names]))
        return out

    def along(self, dim, direct=False, hold=()):
        came = self.came(dim, direct, hold)
        array = jnp.concatenate([self.array] + [a for a, _ in came], 0)
        return Gathering(self.shape, array, self.names + [n for _, names in came for n in names])

    def ring(self, dim):
        return RingGathering(self, dim)

    def columns(self, low, high):
        return Gathering(self.shape, self.array[:, low:high], self.names)

    def pieces(self, dim, spans):
        found = [(self.array, self.names)] + self.came(dim)
        return [(array, names, spans) for array, names in found]


class RingGathering:
    def __init__(self, held, dim):
        self.held, self.dim, self.line = held, dim, held.shape.lines[dim]
        self.arrays = [held.array]
        self.came = self.line.send(held.array)

    def next(self, *hold):
        if len(self.arrays) == self.line.count - 1:
            return self.came
        self.arrays.append(after(self.came, *hold))
        self.came = self.line.send(self.arrays[-1])
        return self.arrays[-1]

    def end(self):
        while len(self.arrays) < self.line.count - 1:
            self.next()
        self.arrays.append(self.came)
        names = [dict(n, **{self.dim: s}) for s in range(self.line.count) for n in self.held.names]
        return Gathering(self.held.shape, jnp.concatenate(self.arrays, 0), names)


def spans_of(low, high, homes):
    spans = []
    for begin, width, output, column in homes:
        first, last = max(low, begin), min(high, begin + width)
        if first < last:
            spans.append((first - low, last - first, output, column + first - begin))
    return spans


def side_by_side(widths):
    return [(sum(widths[:i]), width, i, 0) for i, width in enumerate(widths)]


class TwoWays:
    def __init__(self, parts, shape, homes=None, widths=None):
        own = [part.shape[1] for part in parts]
        self.homes, self.widths = homes or side_by_side(own), widths or own
        self.block, self.shape = parts[0].shape[0], shape
        self.columns = sum(own)
        self.cut = -(-self.columns // 2 // LANES) * LANES
        self.held = Gathering(shape, jnp.concatenate(parts, axis=1))

    def first(self, *hold):
        self.held = self.held.along("z", True, [hold] * 8 if hold else ())

    def second(self, *hold):
        hold = [hold] if hold else ()
        self.one = self.held.columns(0, self.cut).along("x", False, hold)
        self.two = self.held.columns(self.cut, self.columns).along("y", False, hold)

    def third(self, *hold):
        hold = [hold] if hold else ()
        self.one, self.two = self.one.along("y", False, hold), self.two.along("x", False, hold)

    def last(self):
        self.ends = [self.one.came("c"), self.two.came("c")]

    def output(self, *outputs):
        homes = [(b, w, outputs.index(o), c) for b, w, o, c in self.homes if o in outputs]
        pieces = []
        for half, low, high, came in (
            (self.one, 0, self.cut, self.ends[0]),
            (self.two, self.cut, self.columns, self.ends[1]),
        ):
            spans = spans_of(low, high, homes)
            found = [(half.array, half.names)] + came
            pieces += [(array, names, spans) for array, names in found if spans]
        return assemble(pieces, [self.widths[o] for o in outputs], self.block, self.shape)


LAYOUT = "cyxwu"


def picker(shape, width):
    block = width // shape.devices
    if block % 16:
        order = jnp.arange(width)
    else:
        names = [dict()]
        for dim in LAYOUT:
            names = [dict(n, **{dim: s}) for n in names for s in range(shape.lines[dim].count)]
        places = jnp.stack([shape.device_of(n) for n in names])
        order = (places[:, None] * block + jnp.arange(block)[None, :]).reshape(width)
    return (jnp.arange(width)[:, None] == order[None, :]).astype(jnp.bfloat16)


def turned_rows(pick, left):
    return dot(pick, left, ((0,), (1,))).astype(jnp.bfloat16)


class Scattering:
    def __init__(self, shape, kept, arrived, number=0):
        count, half, columns = kept.shape
        self.shape, self.dims = shape, LAYOUT[1:]
        form = [shape.lines[d].count for d in self.dims] + [2 * half // shape.devices, columns]
        self.parts = [[(t.reshape([count] + form), number) for t in (kept, arrived)]]

    def beside(self, other):
        self.parts = self.parts + other.parts
        return self

    def term_of(self, step):
        found = []
        for terms in self.parts:
            own = [lax.index_in_dim(t[i], step, self.axis, False) for t, i in terms]
            found.append(functools.reduce(jnp.add, [t.astype(jnp.float32) for t in own]))
        return jnp.concatenate(found, axis=-1)

    def start(self, dim, *hold):
        self.line, self.axis, self.step = self.shape.lines[dim], self.dims.index(dim), 1
        self.dims = self.dims.replace(dim, "")
        if hold:
            self.parts = [[(after(t, *hold), i) for t, i in terms] for terms in self.parts]
        self.sent = self.term_of(1).astype(jnp.bfloat16)
        self.came = self.line.send(self.sent)
        return self

    def advance(self, *hold):
        flat = [t for terms in self.parts for t, _ in terms]
        came, *flat = lax.optimization_barrier((self.came, *flat, *hold))[: len(flat) + 1]
        self.parts = [[(flat.pop(0), i) for _, i in terms] for terms in self.parts]
        self.step += 1
        total = self.term_of(self.step % self.line.count) + came.astype(jnp.float32)
        if self.step < self.line.count:
            self.sent = total.astype(jnp.bfloat16)
            self.came = self.line.send(self.sent)
        else:
            self.parts, self.came = [[(total[None], 0)]], None
        return self

    def along(self, dim):
        self.start(dim)
        while self.came is not None:
            self.advance()
        return self


def scatter_whole(kept, sent):
    whole = jnp.concatenate([kept, sent], 0).astype(jnp.float32)
    return lax.psum_scatter(whole, ("dp", "seq"), scatter_dimension=0, tiled=True)


FF_TILE = 256


def mlp_kernel(
    block, begins, ends, a_ref, g_ref, at_ref, gt_ref, gate_ref, up_ref, down_ref, *refs
):
    if not begins:
        y_in_ref, da_in_ref, *refs = refs
    if ends:
        x_ref, gain_ref, y_ref, dxo_ref, da_sum, kept_ref, sent_ref, *refs, y_sum = refs
    else:
        y_sum, da_sum, kept_ref, sent_ref, *refs = refs
    hidden_ref, d_gate_ref, d_up_ref = refs
    count = a_ref.shape[0]
    step = pl.program_id(0)

    @pl.when(step == 0)
    def _():
        y_sum[...] = jnp.zeros_like(y_sum) if begins else y_in_ref[...]
        da_sum[...] = jnp.zeros_like(da_sum) if begins else da_in_ref[...]

    for begin in range(0, count, block):
        span = slice(begin, begin + block)
        a, g = a_ref[span, :], g_ref[span, :]
        gate, up = dot(a, gate_ref[...]), dot(a, up_ref[...])
        d_hidden = dot(g, down_ref[...])
        sigma = jax.nn.sigmoid(gate)
        silu = gate * sigma
        hidden = (silu * up).astype(jnp.bfloat16)
        d_gate = (d_hidden * up * (sigma + silu * (1.0 - sigma))).astype(jnp.bfloat16)
        d_up = (d_hidden * silu).astype(jnp.bfloat16)
        hidden_ref[span, :], d_gate_ref[span, :], d_up_ref[span, :] = hidden, d_gate, d_up
        y_sum[span, :] += dot(hidden, down_ref[...], ((1,), (1,)))
        da_sum[span, :] += dot(d_gate, gate_ref[...], ((1,), (1,))) + dot(
            d_up, up_ref[...], ((1,), (1,))
        )
    half = at_ref.shape[0] // 2
    for number, (left, right) in enumerate(
        ((at_ref, d_gate_ref), (at_ref, d_up_ref), (gt_ref, hidden_ref))
    ):
        kept_ref[number] = dot(left[:half, :], right[...]).astype(jnp.bfloat16)
        sent_ref[number] = dot(left[half:, :], right[...]).astype(jnp.bfloat16)
    if not ends:
        return

    @pl.when(step == pl.num_programs(0) - 1)
    def _():
        for begin in range(0, count, block):
            span = slice(begin, begin + block)
            x = x_ref[span, :]
            y_ref[span, :] = (x + y_sum[span, :]).astype(y_ref.dtype)
            scale = lax.rsqrt(jnp.mean(x * x, axis=1, keepdims=True) + epsilon)
            normed = x * scale
            d_normed = da_sum[span, :] * gain_ref[...]
            mean = jnp.mean(d_normed * normed, axis=1, keepdims=True)
            dx = g_ref[span, :].astype(jnp.float32) + scale * (d_normed - normed * mean)
            da_sum[span, :] = dx
            dxo_ref[span, :] = dx.astype(dxo_ref.dtype)


def feed_forward(a, g, a_turned, g_turned, weights, tiles, sums=None, ending=None):
    count, width = a.shape
    half = width // 2

    def held(rows, columns):
        return pl.BlockSpec((rows, columns), lambda j: (0, 0), pipeline_mode=pl.Buffered(1))

    def tile(first):
        return pl.BlockSpec((width, FF_TILE), lambda j: (0, first + j))

    def shape(dtype):
        return jax.ShapeDtypeStruct((count, width), dtype)

    full = held(count, width)
    given = [a, g, a_turned, g_turned] + [array for array, _ in weights]
    specs = [full, full] + [held(width, count)] * 2 + [tile(first) for _, first in weights]
    scratch = [pltpu.VMEM((count, FF_TILE), jnp.bfloat16)] * 3
    if sums is not None:
        given, specs = given + list(sums), specs + [full] * 2
    if ending is not None:
        given, specs = given + list(ending), specs + [full, held(1, width)]
        outs = [shape(jnp.bfloat16), shape(jnp.bfloat16), shape(jnp.float32)]
        scratch = scratch + [pltpu.VMEM((count, width), jnp.float32)]
    else:
        outs = [shape(jnp.float32)] * 2
    hidden = tiles * FF_TILE
    return pl.pallas_call(
        functools.partial(mlp_kernel, min(512, count), sums is None, ending is not None),
        grid=(tiles,),
        in_specs=specs,
        out_specs=[full] * len(outs)
        + [pl.BlockSpec((3, half, FF_TILE), lambda j: (0, 0, j))] * 2,
        out_shape=outs + [jax.ShapeDtypeStruct((3, half, hidden), jnp.bfloat16)] * 2,
        scratch_shapes=scratch,
        compiler_params=pltpu.CompilerParams(
            dimension_semantics=("arbitrary",), vmem_limit_bytes=60 * 2**20
        ),
        cost_estimate=pl.CostEstimate(
            flops=18 * count * width * hidden,
            bytes_accessed=12 * width * hidden + 20 * count * width,
            transcendentals=count * hidden,
        ),
        name="mlp",
    )(*given)


def gain_gradient(weights, gradients, gain):
    products = jnp.sum(weights.astype(jnp.float32) * gradients, axis=1)
    return products / gain.astype(jnp.float32)


def per_device(
    shape,
    layer_input,
    segment_ids,
    gain_attn,
    w_query,
    w_key,
    w_value,
    w_out,
    gain_mlp,
    w_gate,
    w_up,
    w_down,
    grad_output,
):
    rows, shard_len, width = layer_input.shape
    count = rows * shard_len
    narrow, hidden = HEADS * FEAT, w_gate.shape[1]
    attention = Attention(rows, shard_len, width)
    groups, wide, across = attention.groups, attention.wide, attention.across
    gains = jnp.pad(jnp.stack([gain_attn, gain_mlp], axis=1), ((0, 0), (0, LANES - 2)))
    first_parts = [w_query, w_key, w_value, gains]
    homes, grouped = [], []
    for g in range(groups):
        for part, begin, size, place in (
            (w_query, 0, LANES, 0),
            (w_key, narrow, LANES, LANES),
            (w_value, 2 * narrow, wide, 2 * LANES),
        ):
            homes.append((begin + g * size, size, 0, g * across + place))
            grouped.append(part[:, g * size : (g + 1) * size])
    homes.append((groups * across, LANES, 0, groups * across))
    spare = ((0, 0), (0, -hidden % FF_TILE))
    gate_part, up_part, down_part = (
        jnp.pad(part, spare) for part in (w_gate, w_up, w_down.T)
    )
    tiles = gate_part.shape[1] // FF_TILE
    ringed = gains.shape[0] % 16 == 0
    if ringed:
        early = TwoWays(first_parts, shape, homes, [groups * across + LANES])
        rest = TwoWays([gate_part, w_out, up_part], shape)
        early.first()
        early.second()
        early.third()
        begun = [early.one.array, early.two.array]
        rest.first(*begun)
        down = Gathering(shape, down_part).along("x", False, [begun])
        early.last()
        (gathered,) = early.output(0)
    else:
        first_part = jnp.concatenate(grouped + [gains], axis=1)
        gathered, out_w, gate_w, up_w, down_w = (
            lax.all_gather(part, ("dp", "seq"), axis=0, tiled=True)
            for part in (first_part, w_out, gate_part, up_part, down_part)
        )
    qkv_w = gathered[:, : groups * across]
    gain_one = gathered[:, groups * across].astype(jnp.float32)[None, :]
    gain_two = gathered[:, groups * across + 1].astype(jnp.float32)[None, :]

    pick = picker(shape, width)
    cotangent = grad_output.reshape(count, width)
    tokens = layer_input.reshape(count, width).astype(jnp.float32)
    scale_one, normed_one = norm_forward(tokens)
    a_one = (normed_one * gain_one).astype(jnp.bfloat16)
    a_one = after(a_one, rest.held.array, down.array) if ringed else a_one
    qkv = jnp.dot(a_one, qkv_w, preferred_element_type=jnp.float32).astype(jnp.bfloat16)
    place = lax.axis_index("seq")
    own_seg = lax.dynamic_slice_in_dim(segment_ids, place * shard_len, shard_len, 1)
    seg, seg_row = own_seg.reshape(count, 1), own_seg.reshape(rows, 1, shard_len)
    reach = min(shape.seq - 1, -(-(LONGEST - 1) // shard_len))
    states = Passing(segment_ids, shard_len, reach, shape.seq)
    if ringed:
        down = down.along("y", False, [[qkv]])
        tail = attention.tail(after(qkv, down.array), seg)
        rest.second(tail)
        states.start(tail, 1)
        ring = down.ring("z")
        turn = ring.next(tail)
        top, den = attention.near(
            after(qkv, rest.one.array, rest.two.array, turn), seg, seg_row
        )
        turn = ring.next(den)
        earlier = after(states.end(den), turn)
        mixed_cat, inverse = attention.far(qkv, seg, earlier, top, den)
        turned_mixed, turned_one = turned_rows(pick, mixed_cat), turned_rows(pick, a_one)
        rest.third(turned_mixed, turned_one)
        rest.last()
        down = ring.end()
        down_ends = down.pieces("c", [(0, tiles * FF_TILE, 0, 0)])
        (out_w,) = rest.output(1)
    else:
        tail = attention.tail(qkv, seg)
        states.start(tail, 1)
        earlier = states.end()
        top, den = attention.near(qkv, seg, seg_row)
        mixed_cat, inverse = attention.far(qkv, seg, earlier, top, den)
        turned_mixed, turned_one = turned_rows(pick, mixed_cat), turned_rows(pick, a_one)
    x_two = tokens + jnp.dot(mixed_cat, out_w, preferred_element_type=jnp.float32)
    scale_two, normed_two = norm_forward(x_two)
    a_two = (normed_two * gain_two).astype(jnp.bfloat16)
    a_turned = turned_rows(pick, a_two)
    if ringed:
        gate_w, up_w = rest.output(0, 2)
        (down_w,) = assemble(down_ends, [tiles * FF_TILE], down_part.shape[0], shape)
    result, d_branch, d_x_two, kept, sent = feed_forward(
        a_two,
        cotangent,
        a_turned,
        turned_rows(pick, cotangent),
        [(gate_w, 0), (up_w, 0), (down_w, 0)],
        tiles,
        None,
        (x_two, gain_two),
    )
    half = width // 2
    d_mixed = against(d_branch, out_w).astype(jnp.bfloat16)
    ahead, d_top, d_den = attention.head(qkv, d_mixed, mixed_cat, inverse, seg)
    states.start(ahead, -1)
    own = after(d_branch, ahead) if ringed else d_branch
    out_sent, out_kept = (
        dot(t, own).astype(jnp.bfloat16) for t in (turned_mixed[half:], turned_mixed[:half])
    )
    if ringed:
        send_core = shape.lines["c"].send
        arrived, out_arrived = send_core(sent), send_core(out_sent)
        arrived = after(arrived, out_sent, out_kept)
        gate_sum, up_sum, down_sum = (Scattering(shape, kept, arrived, i) for i in range(3))
        gate_sum.beside(Scattering(shape, out_kept[None], out_arrived[None])).start("y")
        up_sum.start("x")
        down_sum.start("u")
        d_top = after(d_top, gate_sum.sent, up_sum.sent, down_sum.sent)
        d_near = attention.near_back(qkv, d_top, d_den, seg, seg_row, earlier)
        near = d_near[0]
        gate_sum.advance(near).start("x")
        up_sum.advance(near).start("y")
        down_sum.advance(near).start("w")
        later = after(states.end(near), down_sum.sent, gate_sum.sent, up_sum.sent)

        d_qkv = attention.far_back(qkv, seg, later, *d_near)
        own_sent = dot(turned_one[half:], d_qkv).astype(jnp.bfloat16)
        own_kept = dot(turned_one[:half], d_qkv).astype(jnp.bfloat16)
        both = gate_sum.advance(own_kept).beside(up_sum.advance(own_kept)).start("u")
        arrived = after(send_core(own_sent), own_kept)
        down_sum.advance(both.sent).start("x")
        arrived = after(arrived, down_sum.sent)
        qkv_a, qkv_b = (
            Scattering(shape, own_kept[None, :, low : low + across], arrived[None, :, low : low + across])
            for low in (0, across)
        )
        qkv_a.start("y")
        qkv_b.start("x")
        d_qkv = after(d_qkv, qkv_a.sent, qkv_b.sent)
        d_a_one = against(d_qkv, qkv_w)
        both.advance(d_a_one).start("w")
        qkv_b.advance(both.sent).start("y")
        qkv_a.advance(both.sent).start("x")
        down_sum.advance(qkv_a.sent).start("y")
        qkv_sum = qkv_a.advance(qkv_b.sent).beside(qkv_b.advance()).start("u")
        down_sum.advance(both.sent)
        qkv_sum.advance().start("w")
        both.advance()
        qkv_sum.advance()
        grad_qkv, both, down_sum = (part.parts[0][0][0][0] for part in (qkv_sum, both, down_sum))
        grad_qkv = [grad_qkv[:, g * across : (g + 1) * across] for g in range(groups)]
        padded = tiles * FF_TILE
        grad_gate, grad_out = both[:, :hidden], both[:, padded : padded + width]
        grad_up = both[:, padded + width : padded + width + hidden]
        grad_down = down_sum[:, :hidden]
    else:
        later = states.end()
        d_near = attention.near_back(qkv, d_top, d_den, seg, seg_row, earlier)
        grad_gate, grad_up, grad_down = (
            scatter_whole(kept[i], sent[i])[:, :hidden] for i in range(3)
        )
        grad_out = scatter_whole(out_kept, out_sent)
        d_qkv = attention.far_back(qkv, seg, later, *d_near)
        whole = scatter_whole(dot(turned_one[:half], d_qkv), dot(turned_one[half:], d_qkv))
        grad_qkv = [whole[:, g * across : (g + 1) * across] for g in range(groups)]
        d_a_one = against(d_qkv, qkv_w)
    d_tokens = d_x_two + norm_backward(d_a_one, gain_one, scale_one, normed_one)
    return (
        result.reshape(rows, shard_len, width),
        d_tokens.reshape(rows, shard_len, width),
        gain_gradient(jnp.concatenate(grouped, axis=1), jnp.concatenate(grad_qkv, axis=1), gain_attn),
        jnp.concatenate([part[:, Q] for part in grad_qkv], axis=1),
        jnp.concatenate([part[:, K] for part in grad_qkv], axis=1),
        jnp.concatenate([part[:, V] for part in grad_qkv], axis=1),
        grad_out,
        gain_gradient(
            jnp.concatenate([w_gate, w_up], axis=1),
            jnp.concatenate([grad_gate, grad_up], axis=1),
            gain_mlp,
        ),
        grad_gate,
        grad_up,
        grad_down.T,
    )


def solution(mesh):
    placed = (
        P("dp", "seq", None),
        P("dp", None),
        P(("dp", "seq")),
        P(("dp", "seq"), None),
        P(("dp", "seq"), None),
        P(("dp", "seq"), None),
        P(("dp", "seq"), None),
        P(("dp", "seq")),
        P(("dp", "seq"), None),
        P(("dp", "seq"), None),
        P(None, ("dp", "seq")),
        P("dp", "seq", None),
    )
    return jax.shard_map(
        functools.partial(per_device, Slice(mesh.shape["dp"], mesh.shape["seq"])),
        mesh=mesh,
        in_specs=placed,
        out_specs=(
            P("dp", "seq", None),
            P("dp", "seq", None),
            P(("dp", "seq")),
            P(("dp", "seq"), None),
            P(("dp", "seq"), None),
            P(("dp", "seq"), None),
            P(("dp", "seq"), None),
            P(("dp", "seq")),
            P(("dp", "seq"), None),
            P(("dp", "seq"), None),
            P(None, ("dp", "seq")),
        ),
        check_vma=False,
    )
```

```python
import functools

import jax
import jax.numpy as jnp
import numpy as np
from jax import lax
from jax.experimental import pallas as pl
from jax.experimental.pallas import tpu as pltpu
from jax.sharding import PartitionSpec as P

LONGEST = 1024
HEADS = 16
FEAT = 16
LANES = 128
GROUP = LANES // FEAT
PIECES = FEAT // 2 + 2
WIDE = PIECES * LANES
PACKED = WIDE // 2 + 16


def dot(left, right, dims=((1,), (0,))):
    return lax.dot_general(left, right, (dims, ((), ())), preferred_element_type=jnp.float32)


def rolls(scaled):
    zero = lax.optimization_barrier(jnp.int32(0))
    row = lax.broadcasted_iota(jnp.int32, (LANES, WIDE), 0) + zero
    column = lax.broadcasted_iota(jnp.int32, (LANES, WIDE), 1)
    d, lane = column // LANES - 1, column % LANES
    a = lane % FEAT
    goal = lane - a + (a + d) % FEAT
    found = (row == goal) & (d >= 0) & ((d < FEAT // 2) | (a < FEAT // 2))
    factor = jnp.where(d == 0, 1 / 32, 1 / 16) if scaled else 1.0
    return jnp.where(found, factor, 0.0).astype(jnp.bfloat16)


def features(rows, factors, lin, axis):
    x = rows.astype(jnp.float32)
    pieces = [x * lin]
    for number in range(PIECES - 1):
        span = slice(number * LANES, (number + 1) * LANES)
        piece = x * (factors[:, span] if axis else factors[span, :])
        if number == PIECES - 2:
            place = lax.broadcasted_iota(jnp.int32, piece.shape, axis)
            piece = jnp.where(place % FEAT == FEAT // 2, 1.0, piece)
        pieces.append(piece)
    return jnp.concatenate([piece.astype(jnp.bfloat16) for piece in pieces], axis=axis)


def turned_features(rows, turned_pick_ref, lin):
    turned = rows.astype(jnp.float32).T.astype(jnp.bfloat16)
    return features(turned, dot(turned_pick_ref[LANES:, :], turned), lin, 0)


def upright_features(rows, pick_ref, lin):
    return features(rows, dot(rows, pick_ref[:, LANES:]), lin, 1)


def head_mask(lanes_per_head, first_head):
    row_head = lax.broadcasted_iota(jnp.int32, (LANES, LANES), 0) // FEAT
    lane_head = lax.broadcasted_iota(jnp.int32, (LANES, LANES), 1) // lanes_per_head + first_head
    return row_head == lane_head


def head_masks(value_dim):
    per = LANES // value_dim
    return [head_mask(value_dim, part * per) for part in range(GROUP // per)]


def low_half():
    return lax.broadcasted_iota(jnp.int32, (LANES, LANES), 1) < LANES // 2


def piece_spans():
    return [slice(number * LANES, (number + 1) * LANES) for number in range(PIECES)]


def fold_heads(rows, masks):
    total = None
    for part, mask in enumerate(masks):
        piece = jnp.where(mask, rows[:, part * LANES : (part + 1) * LANES], 0.0)
        total = piece if total is None else total + piece
    return total + pltpu.roll(total, LANES // 2, 1)


def diagonal():
    row = lax.broadcasted_iota(jnp.int32, (LANES, LANES), 0)
    return row == lax.broadcasted_iota(jnp.int32, (LANES, LANES), 1)


def pack_state(out_ref, pieces):
    low, straight = low_half(), diagonal()
    for number in range(0, PIECES, 2):
        rows = slice(number // 2 * LANES, (number // 2 + 1) * LANES)
        values = jnp.where(low, pieces[number][0], pieces[number + 1][0])
        out_ref[0, 0, rows, :] = values.astype(out_ref.dtype)
    sums = [jnp.sum(jnp.where(straight, s, 0.0), axis=0, keepdims=True) for _, s in pieces]
    sums.append(jnp.zeros((PACKED - WIDE // 2 - PIECES, LANES), jnp.float32))
    out_ref[0, 0, WIDE // 2 :, :] = jnp.concatenate(sums, axis=0).astype(out_ref.dtype)


def spread_state(state_ref, wide_ref, value_dim, sums_of):
    masks, low, straight = head_masks(value_dim), low_half(), diagonal()
    all_sums = state_ref[0, 0, WIDE // 2 :, :].astype(jnp.float32)
    for number, span in enumerate(piece_spans()):
        rows = slice(number // 2 * LANES, (number // 2 + 1) * LANES)
        state = state_ref[0, 0, rows, :].astype(jnp.float32)
        turned = pltpu.roll(state, LANES // 2, 1)
        values = jnp.where(low, turned, state) if number % 2 else jnp.where(low, state, turned)
        sums = jnp.where(straight, all_sums[number : number + 1, :], 0.0)
        sums = jnp.broadcast_to(jnp.sum(sums, axis=1, keepdims=True), (LANES, LANES))
        parts = [jnp.where(mask, values, 0.0) for mask in masks] + sums_of(sums, masks)
        for place, part in enumerate(parts):
            wide_ref[span, slice(place * LANES, (place + 1) * LANES)] = part.astype(jnp.bfloat16)


def own_lanes(array, lanes_per_head, head):
    place = lax.broadcasted_iota(jnp.int32, array.shape, 1) // lanes_per_head
    return jnp.where(place == head, array, jnp.zeros_like(array))


Q, K, V = slice(0, LANES), slice(LANES, 2 * LANES), slice(2 * LANES, None)


def tail_kernel(value_dim, x_ref, seg_ref, pick_ref, out_ref):
    seg = seg_ref[...]
    keep = (seg == seg[-1:, :]).astype(jnp.float32)
    values = (x_ref[:, V].astype(jnp.float32) * keep).astype(jnp.bfloat16)
    ones = jnp.broadcast_to(keep, (seg.shape[0], LANES)).astype(jnp.bfloat16)
    phi = turned_features(x_ref[:, K], pick_ref, 1.0)
    full = dot(phi, jnp.concatenate([values, ones], axis=1))
    width, masks = values.shape[1], head_masks(value_dim)
    pack_state(
        out_ref,
        [(fold_heads(full[span, :width], masks), full[span, width:]) for span in piece_spans()],
    )


def masks_of(seg_ref, seg_row_ref, begin, block):
    stop = begin + block
    rows = begin + lax.broadcasted_iota(jnp.int32, (block, stop), 0)
    columns = lax.broadcasted_iota(jnp.int32, (block, stop), 1)
    same = seg_ref[begin:stop, :] == seg_row_ref[0, :, :stop]
    return ((rows >= columns) & same).astype(jnp.float32)


def near_kernel(value_dim, block, x_ref, seg_ref, seg_row_ref, top_ref, den_ref):
    length = x_ref.shape[0]
    low = lax.broadcasted_iota(jnp.int32, (block, LANES), 1) < value_dim
    for begin in range(0, length, block):
        stop = begin + block
        mask = masks_of(seg_ref, seg_row_ref, begin, block)
        queries = x_ref[begin:stop, Q] * jnp.bfloat16(FEAT ** (-0.5))
        keys = x_ref[:stop, K]
        ones = jnp.ones((stop, LANES), jnp.bfloat16)
        for pair in range(GROUP // 2):
            span = slice(pair * LANES, (pair + 1) * LANES)
            first = 2 * LANES + pair * LANES
            values = jnp.concatenate([x_ref[:stop, first : first + LANES], ones], axis=1)
            sides = []
            for head in (2 * pair, 2 * pair + 1):
                scores = dot(own_lanes(queries, FEAT, head), keys, ((1,), (1,)))
                weights = (((0.5 * scores + 1.0) * scores + 1.0) * mask).astype(jnp.bfloat16)
                sides.append(dot(weights, values))
            top_ref[begin:stop, span] = jnp.where(low, sides[0][:, :LANES], sides[1][:, :LANES])
            den_ref[begin:stop, span] = jnp.where(low, sides[0][:, LANES:], sides[1][:, LANES:])


def far_kernel(value_dim, x_ref, seg_ref, state_ref, top_ref, den_ref, pick_ref, *rest):
    y_ref, inverse_ref, state_wide = rest[-3:]
    width = top_ref.shape[1]
    spread_state(
        state_ref, state_wide, value_dim,
        lambda sums, masks: [jnp.where(mask, sums, 0.0) for mask in masks],
    )
    seg = seg_ref[...]
    keep = (seg == seg[:1, :]).astype(jnp.float32)
    far = dot(upright_features(x_ref[:, Q], pick_ref, FEAT ** (-0.5)), state_wide[...])
    top = top_ref[...] + keep * far[:, :width]
    inverse = 1.0 / (den_ref[...] + keep * far[:, width:])
    y_ref[...] = (top * inverse).astype(y_ref.dtype)
    inverse_ref[...] = inverse


def head_kernel(
    value_dim, x_ref, dy_ref, y_ref, inverse_ref, seg_ref, pick_ref, out_ref, dn_ref, dd_ref
):
    width = dy_ref.shape[1]
    d_top = dy_ref[...].astype(jnp.float32) * inverse_ref[...]
    product = d_top * y_ref[...].astype(jnp.float32)
    large = product.astype(jnp.bfloat16)
    small = (product - large.astype(jnp.float32)).astype(jnp.bfloat16)
    row = lax.broadcasted_iota(jnp.int32, (width, LANES), 0) // value_dim
    lane = lax.broadcasted_iota(jnp.int32, (width, LANES), 1) // FEAT
    adder = jnp.where(row == lane, -1.0, 0.0).astype(jnp.bfloat16)
    d_den = dot(large, adder) + dot(small, adder)
    rounded = d_den.astype(jnp.bfloat16).astype(jnp.float32)
    place = lax.broadcasted_iota(jnp.int32, d_den.shape, 1) % FEAT
    d_den = jnp.where(place < FEAT // 2, rounded, d_den - rounded)
    seg = seg_ref[...]
    keep = (seg == seg[:1, :]).astype(jnp.float32)
    dn_ref[...] = d_top.astype(jnp.bfloat16)
    dd_ref[...] = d_den.astype(jnp.bfloat16)
    d_both = [(d_top * keep).astype(jnp.bfloat16), (d_den * keep).astype(jnp.bfloat16)]
    full = dot(
        turned_features(x_ref[:, Q], pick_ref, FEAT ** (-0.5)), jnp.concatenate(d_both, axis=1)
    )
    masks, own, pieces = head_masks(value_dim), head_mask(FEAT, 0), []
    for span in piece_spans():
        sums = jnp.where(own, full[span, width:], 0.0)
        sums = jnp.sum(sums, axis=1, keepdims=True) * (2 / FEAT)
        pieces.append((fold_heads(full[span, :width], masks), sums))
    pack_state(out_ref, pieces)


def from_features(d_phi, rows, pick_ref, lin):
    x = rows.astype(jnp.float32)
    factors = dot(rows, pick_ref[:, LANES:])
    total, scaled = d_phi[:, :LANES] * lin, []
    for number in range(PIECES - 1):
        span = slice(number * LANES, (number + 1) * LANES)
        piece = d_phi[:, (number + 1) * LANES : (number + 2) * LANES]
        total = total + piece * factors[:, span]
        scaled.append((piece * x).astype(jnp.bfloat16))
    return total + dot(jnp.concatenate(scaled, axis=1), pick_ref[:, LANES:], ((1,), (1,)))


def near_back_kernel(
    value_dim, block, x_ref, dn_ref, dd_ref, seg_ref, seg_row_ref, state_ref, pick_ref,
    dq_ref, dk_ref, dv_ref, state_wide, dq_sum,
):
    length, width = dn_ref.shape
    own = head_mask(FEAT, 0)
    spread_state(
        state_ref, state_wide, value_dim,
        lambda sums, masks: [jnp.where(own, sums, 0.0) * (2 / FEAT)],
    )
    keep = seg_ref[...] == seg_ref[:1, :]
    d_both = jnp.concatenate([dn_ref[...], dd_ref[...]], axis=1)
    d_phi = dot(jnp.where(keep, d_both, jnp.zeros_like(d_both)), state_wide[...], ((1,), (1,)))
    dq_sum[...] = from_features(d_phi, x_ref[:, Q], pick_ref, FEAT ** (-0.5))
    scale = jnp.bfloat16(FEAT ** (-0.5))
    low = lax.broadcasted_iota(jnp.int32, (block, LANES), 1) < value_dim
    for begin in range(0, length, block):
        stop, count = begin + block, length - begin
        key_place = lax.broadcasted_iota(jnp.int32, (block, count), 0)
        query_place = lax.broadcasted_iota(jnp.int32, (block, count), 1)
        same = seg_ref[begin:stop, :] == seg_row_ref[0, :, begin:]
        mask = ((query_place >= key_place) & same).astype(jnp.float32)
        queries = x_ref[begin:, Q] * scale
        keys = x_ref[begin:stop, K]
        dd = dd_ref[begin:, :]
        dk = jnp.zeros((block, LANES), jnp.float32)
        for pair in range(GROUP // 2):
            span = slice(pair * LANES, (pair + 1) * LANES)
            first = 2 * LANES + pair * LANES
            values = x_ref[begin:stop, first : first + LANES]
            dn = dn_ref[begin:, span]
            d_both = jnp.concatenate([dn, dd], axis=1)
            sides = []
            for side in range(2):
                head = 2 * pair + side
                own_keys = own_lanes(keys, FEAT, head)
                ones = own_lanes(jnp.full((block, LANES), 2 / FEAT, jnp.bfloat16), FEAT, head)
                own_values = own_lanes(values, value_dim, side)
                scores = dot(own_keys, queries, ((1,), (1,)))
                weights = (((0.5 * scores + 1.0) * scores + 1.0) * mask).astype(jnp.bfloat16)
                d_weights = dot(
                    jnp.concatenate([own_values, ones], axis=1), d_both, ((1,), (1,))
                )
                d_scores = (d_weights * ((scores + 1.0) * mask)).astype(jnp.bfloat16)
                sides.append(dot(weights, dn))
                dk = dk + own_lanes(dot(d_scores, queries), FEAT, head)
                dq_sum[begin:, :] += dot(d_scores, own_keys * scale, ((0,), (0,)))
            dv_ref[begin:stop, span] = jnp.where(low, sides[0], sides[1])
        dk_ref[begin:stop, :] = dk
    dq_ref[...] = dq_sum[...].astype(dq_ref.dtype)


def far_back_kernel(
    value_dim, x_ref, seg_ref, state_ref, dq_ref, dk_ref, dv_ref, pick_ref, out_ref, state_wide
):
    length, width = dv_ref.shape
    spread_state(state_ref, state_wide, value_dim, lambda sums, masks: [sums * (1 / LANES)])
    seg = seg_ref[...]
    keep = (seg == seg[-1:, :]).astype(jnp.float32)
    keys = x_ref[:, K]
    ones = jnp.ones((length, LANES), jnp.bfloat16)
    d_phi = dot(jnp.concatenate([x_ref[:, V], ones], axis=1), state_wide[...], ((1,), (1,)))
    dk = dk_ref[...] + keep * from_features(d_phi, keys, pick_ref, 1.0)
    dv = dv_ref[...] + keep * dot(upright_features(keys, pick_ref, 1.0), state_wide[:, :width])
    out_ref[:, Q] = dq_ref[...]
    out_ref[:, K] = dk.astype(out_ref.dtype)
    out_ref[:, V] = dv.astype(out_ref.dtype)


class Attention:
    def __init__(self, rows, length, width):
        self.rows, self.length = rows, length
        self.value_dim = width // HEADS
        self.groups = HEADS // GROUP
        self.wide = GROUP * self.value_dim
        self.across = 2 * LANES + self.wide
        self.block = min(256, length)
        self.count = rows * length
        self.scaled, self.plain = rolls(True), rolls(False)
        self.all = range(self.groups)

    def specs(self, groups):
        def rows_of(columns):
            return pl.BlockSpec((self.length, columns), lambda r, g: (r, g))

        return dict(
            x=rows_of(self.across),
            values=rows_of(self.wide),
            narrow=rows_of(LANES),
            seg=pl.BlockSpec((self.length, 1), lambda r, g: (r, 0)),
            seg_row=pl.BlockSpec((1, 1, self.length), lambda r, g: (r, 0, 0)),
            state=pl.BlockSpec((1, 1, PACKED, LANES), lambda r, g: (r, g, 0, 0)),
            pick=pl.BlockSpec((LANES, WIDE), lambda r, g: (0, 0)),
            turned_pick=pl.BlockSpec((WIDE, LANES), lambda r, g: (0, 0)),
        )

    def shape(self, columns, dtype, groups):
        return jax.ShapeDtypeStruct((self.count, columns * len(groups)), dtype)

    def state_shape(self, groups):
        return jax.ShapeDtypeStruct((self.rows, len(groups), PACKED, LANES), jnp.bfloat16)

    def wide_state(self, columns):
        return pltpu.VMEM((WIDE, columns), jnp.bfloat16)

    def call(self, kernel, groups, specs, outs, out_specs, scratch, passes, name):
        return pl.pallas_call(
            functools.partial(kernel, self.value_dim),
            grid=(self.rows, len(groups)),
            in_specs=specs,
            out_specs=out_specs,
            out_shape=outs,
            scratch_shapes=scratch,
            compiler_params=pltpu.CompilerParams(
                dimension_semantics=("arbitrary", "arbitrary"), vmem_limit_bytes=56 * 2**20
            ),
            cost_estimate=pl.CostEstimate(
                flops=self.rows * len(groups) * GROUP * passes * 2**26 * self.length // 512,
                bytes_accessed=2**21,
                transcendentals=0,
            ),
            name=name,
        )

    def tail(self, x, seg):
        at = self.specs(self.all)
        return self.call(
            tail_kernel, self.all, [at["x"], at["seg"], at["turned_pick"]],
            self.state_shape(self.all), at["state"], [], 5, "attn_tail",
        )(x, seg, self.plain.T)

    def near(self, x, seg, seg_row):
        def kernel(value_dim, *refs):
            near_kernel(value_dim, self.block, *refs)

        at = self.specs(self.all)
        out = self.shape(self.wide, jnp.float32, self.all)
        return self.call(
            kernel, self.all, [at["x"], at["seg"], at["seg_row"]],
            [out, out], [at["values"]] * 2, [], 8, "attn_near",
        )(x, seg, seg_row)

    def far(self, x, seg, state, top, den):
        at = self.specs(self.all)
        return self.call(
            far_kernel, self.all,
            [at["x"], at["seg"], at["state"], at["values"], at["values"], at["pick"]],
            [self.shape(self.wide, dtype, self.all) for dtype in (jnp.bfloat16, jnp.float32)],
            [at["values"]] * 2, [self.wide_state(2 * self.wide)], 8, "attn_far",
        )(x, seg, state, top, den, self.scaled)

    def head(self, x, dy, y, inverse, seg):
        at = self.specs(self.all)
        return self.call(
            head_kernel, self.all,
            [at["x"], at["values"], at["values"], at["values"], at["seg"], at["turned_pick"]],
            [self.state_shape(self.all), self.shape(self.wide, jnp.bfloat16, self.all),
             self.shape(LANES, jnp.bfloat16, self.all)],
            [at["state"], at["values"], at["narrow"]], [], 5, "attn_head",
        )(x, dy, y, inverse, seg, self.scaled.T)

    def near_back(self, x, dn, dd, seg, seg_row, state):
        def kernel(value_dim, *refs):
            near_back_kernel(value_dim, self.block, *refs)

        at, groups = self.specs(self.all), self.all
        return self.call(
            kernel, groups,
            [at["x"], at["values"], at["narrow"], at["seg"], at["seg_row"], at["state"],
             at["pick"]],
            [self.shape(LANES, jnp.bfloat16, groups), self.shape(LANES, jnp.float32, groups),
             self.shape(self.wide, jnp.float32, groups)],
            [at["narrow"], at["narrow"], at["values"]],
            [self.wide_state(self.wide + LANES), pltpu.VMEM((self.length, LANES), jnp.float32)],
            24, "attn_near_back",
        )(x, dn, dd, seg, seg_row, state, self.scaled)

    def far_back(self, x, seg, state, dq, dk, dv):
        at, groups = self.specs(self.all), self.all
        return self.call(
            far_back_kernel, groups,
            [at["x"], at["seg"], at["state"], at["narrow"], at["narrow"], at["values"],
             at["pick"]],
            self.shape(self.across, jnp.bfloat16, groups), at["x"],
            [self.wide_state(self.wide + LANES)], 9, "attn_far_back",
        )(x, seg, state, dq, dk, dv, self.plain)


class Passing:
    def __init__(self, segment_ids, length, reach, size):
        self.ids, self.length, self.reach, self.size = segment_ids, length, reach, size
        self.place = lax.axis_index("seq")

    def id_at(self, device, last):
        position = jnp.clip(device, 0, self.size - 1) * self.length + last * (self.length - 1)
        return lax.dynamic_index_in_dim(self.ids, position, 1, keepdims=False)

    def start(self, own, shift):
        self.shift, self.came = shift, []
        for k in range(1, self.reach + 1):
            goals = [(i, i + shift * k) for i in range(self.size)]
            pairs = [(i, goal) for i, goal in goals if 0 <= goal < self.size]
            self.came.append(lax.ppermute(own, "seq", pairs))

    def end(self, *hold):
        before = self.shift > 0
        own_id, total = self.id_at(self.place, not before), 0.0
        for k, came in enumerate(self.came, 1):
            linked = self.id_at(self.place - self.shift * k, before) == own_id
            came = after(came, *hold) if hold else came
            total = total + jnp.where(linked[:, None, None, None], came.astype(jnp.float32), 0.0)
        return total.astype(jnp.bfloat16)


epsilon = 1e-05


def against(left, matrix):
    return dot(left, matrix, ((1,), (1,)))


def norm_forward(values):
    scale = lax.rsqrt(jnp.mean(values * values, axis=1, keepdims=True) + epsilon)
    return (scale, values * scale)


def norm_backward(d_scaled, gain, scale, normed):
    d_normed = d_scaled * gain
    return scale * (d_normed - normed * jnp.mean(d_normed * normed, axis=1, keepdims=True))


def fold(count):
    return [0] + list(range(1, count, 2)) + list(range(2, count, 2))[::-1]


class Line:
    def __init__(self, axis, axis_size, stride, count):
        self.axis, self.size, self.stride, self.count = axis, axis_size, stride, count
        self.order = fold(count)

    def send(self, array, steps=1):
        pairs = []
        for index in range(self.size):
            place = (index // self.stride) % self.count
            goal = self.order[(self.order.index(place) + steps) % self.count]
            pairs.append((index, index + (goal - place) * self.stride))
        return lax.ppermute(array, self.axis, pairs)

    def place_back(self, steps):
        own = (lax.axis_index(self.axis) // self.stride) % self.count
        rank = jnp.asarray([self.order.index(p) for p in range(self.count)], jnp.int32)[own]
        return jnp.asarray(self.order, jnp.int32)[(rank - steps) % self.count]


class Slice:
    def __init__(self, dp, seq):
        self.dp, self.seq, self.devices = dp, seq, dp * seq
        self.lines = {
            "z": Line("dp", dp, 2, dp // 2),
            "x": Line("dp", dp, 1, 2),
            "y": Line("seq", seq, 2, seq // 2),
            "c": Line("seq", seq, 1, 2),
        }
        if dp % 4 == 0:
            self.lines["w"] = Line("dp", dp, 4, dp // 4)
            self.lines["u"] = Line("dp", dp, 2, 2)

    def device_of(self, back):
        at = {d: self.lines[d].place_back(back[d]) for d in back}
        z = at["z"] if "z" in at else at["w"] * 2 + at["u"]
        return ((z * 2 + at["x"]) * (self.seq // 2) + at["y"]) * 2 + at["c"]


def after(array, *others):
    return lax.optimization_barrier((array, *others))[0]


def assemble(pieces, widths, block, shape):
    arrays = [array for array, _, _ in pieces]
    dtype = arrays[0].dtype
    places = jnp.stack([shape.device_of(n) for _, names, _ in pieces for n in names])
    copies = sum(len(names) * len(spans) for _, names, spans in pieces)
    windows = [
        (min(span[0] for span in spans), max(span[0] + span[1] for span in spans))
        for _, _, spans in pieces
    ]
    held = [(array.shape[0], high - low) for array, (low, high) in zip(arrays, windows)]

    def kernel(places_ref, *refs):
        piece_refs, refs = refs[: len(pieces)], refs[len(pieces) :]
        out_refs, refs = refs[: len(widths)], refs[len(widths) :]
        buffers, (in_sems, out_sems) = refs[: len(pieces)], refs[len(pieces) :]
        loads = []
        for number, piece_ref in enumerate(piece_refs):
            low, high = windows[number]
            load = pltpu.make_async_copy(
                piece_ref.at[:, pl.ds(low, high - low)], buffers[number], in_sems.at[number]
            )
            load.start()
            loads.append(load)
        stores, begin = [], 0
        for number, (load, (_, names, spans)) in enumerate(zip(loads, pieces)):
            load.wait()
            for i in range(len(names)):
                to = pl.multiple_of(places_ref[begin + i] * block, block)
                for low, width, output, column in spans:
                    store = pltpu.make_async_copy(
                        buffers[number].at[pl.ds(i * block, block), pl.ds(low - windows[number][0], width)],
                        out_refs[output].at[pl.ds(to, block), pl.ds(column, width)],
                        out_sems.at[len(stores)],
                    )
                    store.start()
                    stores.append(store)
            begin += len(names)
        for store in stores:
            store.wait()

    size = sum(tall * wide for tall, wide in held) * dtype.itemsize
    return pl.pallas_call(
        kernel,
        out_shape=[jax.ShapeDtypeStruct((shape.devices * block, w), dtype) for w in widths],
        in_specs=[pl.BlockSpec(memory_space=pltpu.SMEM)]
        + [pl.BlockSpec(memory_space=pl.ANY)] * len(pieces),
        out_specs=[pl.BlockSpec(memory_space=pl.ANY)] * len(widths),
        scratch_shapes=[pltpu.VMEM(size, dtype) for size in held]
        + [
            pltpu.SemaphoreType.DMA((len(pieces),)),
            pltpu.SemaphoreType.DMA((copies,)),
        ],
        cost_estimate=pl.CostEstimate(flops=0, bytes_accessed=2 * size, transcendentals=0),
        name="assemble",
    )(places, *arrays)


class Gathering:
    def __init__(self, shape, array, names=None):
        self.shape, self.array = shape, array
        self.names = names or [dict(z=0, x=0, y=0, c=0)]

    def came(self, dim, direct=False, hold=()):
        line, array, out = self.shape.lines[dim], self.array, []
        for step in range(1, line.count):
            array = line.send(self.array, step) if direct else line.send(array)
            if step <= len(hold):
                array = after(array, *hold[step - 1])
            out.append((array, [dict(n, **{dim: step}) for n in self.names]))
        return out

    def along(self, dim, direct=False, hold=()):
        came = self.came(dim, direct, hold)
        array = jnp.concatenate([self.array] + [a for a, _ in came], 0)
        return Gathering(self.shape, array, self.names + [n for _, names in came for n in names])

    def ring(self, dim):
        return RingGathering(self, dim)

    def columns(self, low, high):
        return Gathering(self.shape, self.array[:, low:high], self.names)

    def pieces(self, dim, spans):
        found = [(self.array, self.names)] + self.came(dim)
        return [(array, names, spans) for array, names in found]


class RingGathering:
    def __init__(self, held, dim):
        self.held, self.dim, self.line = held, dim, held.shape.lines[dim]
        self.arrays = [held.array]
        self.came = self.line.send(held.array)

    def next(self, *hold):
        if len(self.arrays) == self.line.count - 1:
            return self.came
        self.arrays.append(after(self.came, *hold))
        self.came = self.line.send(self.arrays[-1])
        return self.arrays[-1]

    def end(self):
        while len(self.arrays) < self.line.count - 1:
            self.next()
        self.arrays.append(self.came)
        names = [dict(n, **{self.dim: s}) for s in range(self.line.count) for n in self.held.names]
        return Gathering(self.held.shape, jnp.concatenate(self.arrays, 0), names)


def spans_of(low, high, homes):
    spans = []
    for begin, width, output, column in homes:
        first, last = max(low, begin), min(high, begin + width)
        if first < last:
            spans.append((first - low, last - first, output, column + first - begin))
    return spans


def side_by_side(widths):
    return [(sum(widths[:i]), width, i, 0) for i, width in enumerate(widths)]


class TwoWays:
    def __init__(self, parts, shape, homes=None, widths=None):
        own = [part.shape[1] for part in parts]
        self.homes, self.widths = homes or side_by_side(own), widths or own
        self.block, self.shape = parts[0].shape[0], shape
        self.columns = sum(own)
        self.cut = -(-self.columns // 2 // LANES) * LANES
        self.held = Gathering(shape, jnp.concatenate(parts, axis=1))

    def first(self, *hold):
        self.held = self.held.along("z", True, [hold] * 8 if hold else ())

    def second(self, *hold):
        hold = [hold] if hold else ()
        self.one = self.held.columns(0, self.cut).along("x", False, hold)
        self.two = self.held.columns(self.cut, self.columns).along("y", False, hold)

    def third(self, *hold):
        hold = [hold] if hold else ()
        self.one, self.two = self.one.along("y", False, hold), self.two.along("x", False, hold)

    def last(self):
        self.ends = [self.one.came("c"), self.two.came("c")]

    def output(self, *outputs):
        homes = [(b, w, outputs.index(o), c) for b, w, o, c in self.homes if o in outputs]
        pieces = []
        for half, low, high, came in (
            (self.one, 0, self.cut, self.ends[0]),
            (self.two, self.cut, self.columns, self.ends[1]),
        ):
            spans = spans_of(low, high, homes)
            found = [(half.array, half.names)] + came
            pieces += [(array, names, spans) for array, names in found if spans]
        return assemble(pieces, [self.widths[o] for o in outputs], self.block, self.shape)


LAYOUT = "cyxwu"


def picker(shape, width):
    block = width // shape.devices
    if block % 16:
        order = jnp.arange(width)
    else:
        names = [dict()]
        for dim in LAYOUT:
            names = [dict(n, **{dim: s}) for n in names for s in range(shape.lines[dim].count)]
        places = jnp.stack([shape.device_of(n) for n in names])
        order = (places[:, None] * block + jnp.arange(block)[None, :]).reshape(width)
    return (jnp.arange(width)[:, None] == order[None, :]).astype(jnp.bfloat16)


def turned_rows(pick, left):
    return dot(pick, left, ((0,), (1,))).astype(jnp.bfloat16)


class Scattering:
    def __init__(self, shape, kept, arrived, number=0):
        count, half, columns = kept.shape
        self.shape, self.dims = shape, LAYOUT[1:]
        form = [shape.lines[d].count for d in self.dims] + [2 * half // shape.devices, columns]
        self.parts = [[(t.reshape([count] + form), number) for t in (kept, arrived)]]

    def beside(self, other):
        self.parts = self.parts + other.parts
        return self

    def term_of(self, step):
        found = []
        for terms in self.parts:
            own = [lax.index_in_dim(t[i], step, self.axis, False) for t, i in terms]
            found.append(functools.reduce(jnp.add, [t.astype(jnp.float32) for t in own]))
        return jnp.concatenate(found, axis=-1)

    def start(self, dim, *hold):
        self.line, self.axis, self.step = self.shape.lines[dim], self.dims.index(dim), 1
        self.dims = self.dims.replace(dim, "")
        if hold:
            self.parts = [[(after(t, *hold), i) for t, i in terms] for terms in self.parts]
        self.sent = self.term_of(1).astype(jnp.bfloat16)
        self.came = self.line.send(self.sent)
        return self

    def advance(self, *hold):
        flat = [t for terms in self.parts for t, _ in terms]
        came, *flat = lax.optimization_barrier((self.came, *flat, *hold))[: len(flat) + 1]
        self.parts = [[(flat.pop(0), i) for _, i in terms] for terms in self.parts]
        self.step += 1
        total = self.term_of(self.step % self.line.count) + came.astype(jnp.float32)
        if self.step < self.line.count:
            self.sent = total.astype(jnp.bfloat16)
            self.came = self.line.send(self.sent)
        else:
            self.parts, self.came = [[(total[None], 0)]], None
        return self

    def along(self, dim):
        self.start(dim)
        while self.came is not None:
            self.advance()
        return self


def scatter_whole(kept, sent):
    whole = jnp.concatenate([kept, sent], 0).astype(jnp.float32)
    return lax.psum_scatter(whole, ("dp", "seq"), scatter_dimension=0, tiled=True)


FF_TILE = 256


def mlp_kernel(
    block, begins, ends, a_ref, g_ref, at_ref, gt_ref, gate_ref, up_ref, down_ref, *refs
):
    if not begins:
        y_in_ref, da_in_ref, *refs = refs
    if ends:
        x_ref, gain_ref, y_ref, dxo_ref, da_sum, kept_ref, sent_ref, *refs, y_sum = refs
    else:
        y_sum, da_sum, kept_ref, sent_ref, *refs = refs
    hidden_ref, d_gate_ref, d_up_ref = refs
    count = a_ref.shape[0]
    step = pl.program_id(0)

    @pl.when(step == 0)
    def _():
        y_sum[...] = jnp.zeros_like(y_sum) if begins else y_in_ref[...]
        da_sum[...] = jnp.zeros_like(da_sum) if begins else da_in_ref[...]

    for begin in range(0, count, block):
        span = slice(begin, begin + block)
        a, g = a_ref[span, :], g_ref[span, :]
        gate, up = dot(a, gate_ref[...]), dot(a, up_ref[...])
        d_hidden = dot(g, down_ref[...])
        sigma = jax.nn.sigmoid(gate)
        silu = gate * sigma
        hidden = (silu * up).astype(jnp.bfloat16)
        d_gate = (d_hidden * up * (sigma + silu * (1.0 - sigma))).astype(jnp.bfloat16)
        d_up = (d_hidden * silu).astype(jnp.bfloat16)
        hidden_ref[span, :], d_gate_ref[span, :], d_up_ref[span, :] = hidden, d_gate, d_up
        y_sum[span, :] += dot(hidden, down_ref[...], ((1,), (1,)))
        da_sum[span, :] += dot(d_gate, gate_ref[...], ((1,), (1,))) + dot(
            d_up, up_ref[...], ((1,), (1,))
        )
    half = at_ref.shape[0] // 2
    for number, (left, right) in enumerate(
        ((at_ref, d_gate_ref), (at_ref, d_up_ref), (gt_ref, hidden_ref))
    ):
        kept_ref[number] = dot(left[:half, :], right[...]).astype(jnp.bfloat16)
        sent_ref[number] = dot(left[half:, :], right[...]).astype(jnp.bfloat16)
    if not ends:
        return

    @pl.when(step == pl.num_programs(0) - 1)
    def _():
        for begin in range(0, count, block):
            span = slice(begin, begin + block)
            x = x_ref[span, :]
            y_ref[span, :] = (x + y_sum[span, :]).astype(y_ref.dtype)
            scale = lax.rsqrt(jnp.mean(x * x, axis=1, keepdims=True) + epsilon)
            normed = x * scale
            d_normed = da_sum[span, :] * gain_ref[...]
            mean = jnp.mean(d_normed * normed, axis=1, keepdims=True)
            dx = g_ref[span, :].astype(jnp.float32) + scale * (d_normed - normed * mean)
            da_sum[span, :] = dx
            dxo_ref[span, :] = dx.astype(dxo_ref.dtype)


def feed_forward(a, g, a_turned, g_turned, weights, tiles, sums=None, ending=None):
    count, width = a.shape
    half = width // 2

    def held(rows, columns):
        return pl.BlockSpec((rows, columns), lambda j: (0, 0), pipeline_mode=pl.Buffered(1))

    def tile(first):
        return pl.BlockSpec((width, FF_TILE), lambda j: (0, first + j))

    def shape(dtype):
        return jax.ShapeDtypeStruct((count, width), dtype)

    full = held(count, width)
    given = [a, g, a_turned, g_turned] + [array for array, _ in weights]
    specs = [full, full] + [held(width, count)] * 2 + [tile(first) for _, first in weights]
    scratch = [pltpu.VMEM((count, FF_TILE), jnp.bfloat16)] * 3
    if sums is not None:
        given, specs = given + list(sums), specs + [full] * 2
    if ending is not None:
        given, specs = given + list(ending), specs + [full, held(1, width)]
        outs = [shape(jnp.bfloat16), shape(jnp.bfloat16), shape(jnp.float32)]
        scratch = scratch + [pltpu.VMEM((count, width), jnp.float32)]
    else:
        outs = [shape(jnp.float32)] * 2
    hidden = tiles * FF_TILE
    return pl.pallas_call(
        functools.partial(mlp_kernel, min(512, count), sums is None, ending is not None),
        grid=(tiles,),
        in_specs=specs,
        out_specs=[full] * len(outs)
        + [pl.BlockSpec((3, half, FF_TILE), lambda j: (0, 0, j))] * 2,
        out_shape=outs + [jax.ShapeDtypeStruct((3, half, hidden), jnp.bfloat16)] * 2,
        scratch_shapes=scratch,
        compiler_params=pltpu.CompilerParams(
            dimension_semantics=("arbitrary",), vmem_limit_bytes=60 * 2**20
        ),
        cost_estimate=pl.CostEstimate(
            flops=18 * count * width * hidden,
            bytes_accessed=12 * width * hidden + 20 * count * width,
            transcendentals=count * hidden,
        ),
        name="mlp",
    )(*given)


def gain_gradient(weights, gradients, gain):
    products = jnp.sum(weights.astype(jnp.float32) * gradients, axis=1)
    return products / gain.astype(jnp.float32)


def per_device(
    shape,
    layer_input,
    segment_ids,
    gain_attn,
    w_query,
    w_key,
    w_value,
    w_out,
    gain_mlp,
    w_gate,
    w_up,
    w_down,
    grad_output,
):
    rows, shard_len, width = layer_input.shape
    count = rows * shard_len
    narrow, hidden = HEADS * FEAT, w_gate.shape[1]
    attention = Attention(rows, shard_len, width)
    groups, wide, across = attention.groups, attention.wide, attention.across
    gains = jnp.pad(jnp.stack([gain_attn, gain_mlp], axis=1), ((0, 0), (0, LANES - 2)))
    first_parts = [w_query, w_key, w_value, gains]
    homes, grouped = [], []
    for g in range(groups):
        for part, begin, size, place in (
            (w_query, 0, LANES, 0),
            (w_key, narrow, LANES, LANES),
            (w_value, 2 * narrow, wide, 2 * LANES),
        ):
            homes.append((begin + g * size, size, 0, g * across + place))
            grouped.append(part[:, g * size : (g + 1) * size])
    homes.append((groups * across, LANES, 0, groups * across))
    spare = ((0, 0), (0, -hidden % FF_TILE))
    gate_part, up_part, down_part = (
        jnp.pad(part, spare) for part in (w_gate, w_up, w_down.T)
    )
    tiles = gate_part.shape[1] // FF_TILE
    ringed = gains.shape[0] % 16 == 0
    if ringed:
        early = TwoWays(first_parts, shape, homes, [groups * across + LANES])
        rest = TwoWays([gate_part, w_out, up_part], shape)
        early.first()
        early.second()
        early.third()
        begun = [early.one.array, early.two.array]
        rest.first(*begun)
        down = Gathering(shape, down_part).along("x", False, [begun])
        early.last()
        (gathered,) = early.output(0)
    else:
        first_part = jnp.concatenate(grouped + [gains], axis=1)
        gathered, out_w, gate_w, up_w, down_w = (
            lax.all_gather(part, ("dp", "seq"), axis=0, tiled=True)
            for part in (first_part, w_out, gate_part, up_part, down_part)
        )
    qkv_w = gathered[:, : groups * across]
    gain_one = gathered[:, groups * across].astype(jnp.float32)[None, :]
    gain_two = gathered[:, groups * across + 1].astype(jnp.float32)[None, :]

    pick = picker(shape, width)
    cotangent = grad_output.reshape(count, width)
    tokens = layer_input.reshape(count, width).astype(jnp.float32)
    scale_one, normed_one = norm_forward(tokens)
    a_one = (normed_one * gain_one).astype(jnp.bfloat16)
    a_one = after(a_one, rest.held.array, down.array) if ringed else a_one
    qkv = jnp.dot(a_one, qkv_w, preferred_element_type=jnp.float32).astype(jnp.bfloat16)
    place = lax.axis_index("seq")
    own_seg = lax.dynamic_slice_in_dim(segment_ids, place * shard_len, shard_len, 1)
    seg, seg_row = own_seg.reshape(count, 1), own_seg.reshape(rows, 1, shard_len)
    reach = min(shape.seq - 1, -(-(LONGEST - 1) // shard_len))
    states = Passing(segment_ids, shard_len, reach, shape.seq)
    if ringed:
        down = down.along("y", False, [[qkv]])
        tail = attention.tail(after(qkv, down.array), seg)
        rest.second(tail)
        states.start(tail, 1)
        ring = down.ring("z")
        turn = ring.next(tail)
        top, den = attention.near(
            after(qkv, rest.one.array, rest.two.array, turn), seg, seg_row
        )
        turn = ring.next(den)
        earlier = after(states.end(den), turn)
        mixed_cat, inverse = attention.far(qkv, seg, earlier, top, den)
        turned_mixed, turned_one = turned_rows(pick, mixed_cat), turned_rows(pick, a_one)
        rest.third(turned_mixed, turned_one)
        rest.last()
        down = ring.end()
        down_ends = down.pieces("c", [(0, tiles * FF_TILE, 0, 0)])
        (out_w,) = rest.output(1)
    else:
        tail = attention.tail(qkv, seg)
        states.start(tail, 1)
        earlier = states.end()
        top, den = attention.near(qkv, seg, seg_row)
        mixed_cat, inverse = attention.far(qkv, seg, earlier, top, den)
        turned_mixed, turned_one = turned_rows(pick, mixed_cat), turned_rows(pick, a_one)
    x_two = tokens + jnp.dot(mixed_cat, out_w, preferred_element_type=jnp.float32)
    scale_two, normed_two = norm_forward(x_two)
    a_two = (normed_two * gain_two).astype(jnp.bfloat16)
    a_turned = turned_rows(pick, a_two)
    if ringed:
        gate_w, up_w = rest.output(0, 2)
        (down_w,) = assemble(down_ends, [tiles * FF_TILE], down_part.shape[0], shape)
    result, d_branch, d_x_two, kept, sent = feed_forward(
        a_two,
        cotangent,
        a_turned,
        turned_rows(pick, cotangent),
        [(gate_w, 0), (up_w, 0), (down_w, 0)],
        tiles,
        None,
        (x_two, gain_two),
    )
    half = width // 2
    d_mixed = against(d_branch, out_w).astype(jnp.bfloat16)
    ahead, d_top, d_den = attention.head(qkv, d_mixed, mixed_cat, inverse, seg)
    states.start(ahead, -1)
    own = after(d_branch, ahead) if ringed else d_branch
    out_sent, out_kept = (
        dot(t, own).astype(jnp.bfloat16) for t in (turned_mixed[half:], turned_mixed[:half])
    )
    if ringed:
        send_core = shape.lines["c"].send
        arrived, out_arrived = send_core(sent), send_core(out_sent)
        arrived = after(arrived, out_sent, out_kept)
        gate_sum, up_sum, down_sum = (Scattering(shape, kept, arrived, i) for i in range(3))
        gate_sum.beside(Scattering(shape, out_kept[None], out_arrived[None])).start("y")
        up_sum.start("x")
        down_sum.start("u")
        d_top = after(d_top, gate_sum.sent, up_sum.sent, down_sum.sent)
        d_near = attention.near_back(qkv, d_top, d_den, seg, seg_row, earlier)
        near = d_near[0]
        gate_sum.advance(near).start("x")
        up_sum.advance(near).start("y")
        down_sum.advance(near).start("w")
        later = after(states.end(near), down_sum.sent, gate_sum.sent, up_sum.sent)

        d_qkv = attention.far_back(qkv, seg, later, *d_near)
        own_sent = dot(turned_one[half:], d_qkv).astype(jnp.bfloat16)
        own_kept = dot(turned_one[:half], d_qkv).astype(jnp.bfloat16)
        both = gate_sum.advance(own_kept).beside(up_sum.advance(own_kept)).start("u")
        arrived = after(send_core(own_sent), own_kept)
        down_sum.advance(both.sent).start("x")
        arrived = after(arrived, down_sum.sent)
        qkv_a, qkv_b = (
            Scattering(shape, own_kept[None, :, low : low + across], arrived[None, :, low : low + across])
            for low in (0, across)
        )
        qkv_a.start("y")
        qkv_b.start("x")
        d_qkv = after(d_qkv, qkv_a.sent, qkv_b.sent)
        d_a_one = against(d_qkv[:, :across], qkv_w[:, :across])
        qkv_b.advance(d_a_one).start("y")
        qkv_a.advance(d_a_one).start("x")
        d_qkv = after(d_qkv, qkv_b.sent, qkv_a.sent)
        d_a_one = d_a_one + against(d_qkv[:, across:], qkv_w[:, across:])
        both.advance(d_a_one).start("w")
        down_sum.advance(both.sent).start("y")
        qkv_sum = qkv_a.advance(both.sent).beside(qkv_b.advance(both.sent)).start("u")
        down_sum.advance(both.sent)
        qkv_sum.advance().start("w")
        both.advance()
        qkv_sum.advance()
        grad_qkv, both, down_sum = (part.parts[0][0][0][0] for part in (qkv_sum, both, down_sum))
        grad_qkv = [grad_qkv[:, g * across : (g + 1) * across] for g in range(groups)]
        padded = tiles * FF_TILE
        grad_gate, grad_out = both[:, :hidden], both[:, padded : padded + width]
        grad_up = both[:, padded + width : padded + width + hidden]
        grad_down = down_sum[:, :hidden]
    else:
        later = states.end()
        d_near = attention.near_back(qkv, d_top, d_den, seg, seg_row, earlier)
        grad_gate, grad_up, grad_down = (
            scatter_whole(kept[i], sent[i])[:, :hidden] for i in range(3)
        )
        grad_out = scatter_whole(out_kept, out_sent)
        d_qkv = attention.far_back(qkv, seg, later, *d_near)
        whole = scatter_whole(dot(turned_one[:half], d_qkv), dot(turned_one[half:], d_qkv))
        grad_qkv = [whole[:, g * across : (g + 1) * across] for g in range(groups)]
        d_a_one = against(d_qkv, qkv_w)
    d_tokens = d_x_two + norm_backward(d_a_one, gain_one, scale_one, normed_one)
    return (
        result.reshape(rows, shard_len, width),
        d_tokens.reshape(rows, shard_len, width),
        gain_gradient(jnp.concatenate(grouped, axis=1), jnp.concatenate(grad_qkv, axis=1), gain_attn),
        jnp.concatenate([part[:, Q] for part in grad_qkv], axis=1),
        jnp.concatenate([part[:, K] for part in grad_qkv], axis=1),
        jnp.concatenate([part[:, V] for part in grad_qkv], axis=1),
        grad_out,
        gain_gradient(
            jnp.concatenate([w_gate, w_up], axis=1),
            jnp.concatenate([grad_gate, grad_up], axis=1),
            gain_mlp,
        ),
        grad_gate,
        grad_up,
        grad_down.T,
    )


def solution(mesh):
    placed = (
        P("dp", "seq", None),
        P("dp", None),
        P(("dp", "seq")),
        P(("dp", "seq"), None),
        P(("dp", "seq"), None),
        P(("dp", "seq"), None),
        P(("dp", "seq"), None),
        P(("dp", "seq")),
        P(("dp", "seq"), None),
        P(("dp", "seq"), None),
        P(None, ("dp", "seq")),
        P("dp", "seq", None),
    )
    return jax.shard_map(
        functools.partial(per_device, Slice(mesh.shape["dp"], mesh.shape["seq"])),
        mesh=mesh,
        in_specs=placed,
        out_specs=(
            P("dp", "seq", None),
            P("dp", "seq", None),
            P(("dp", "seq")),
            P(("dp", "seq"), None),
            P(("dp", "seq"), None),
            P(("dp", "seq"), None),
            P(("dp", "seq"), None),
            P(("dp", "seq")),
            P(("dp", "seq"), None),
            P(("dp", "seq"), None),
            P(None, ("dp", "seq")),
        ),
        check_vma=False,
    )
```

```python
import functools

import jax
import jax.numpy as jnp
import numpy as np
from jax import lax
from jax.experimental import pallas as pl
from jax.experimental.pallas import tpu as pltpu
from jax.sharding import PartitionSpec as P

LONGEST = 1024
HEADS = 16
FEAT = 16
LANES = 128
GROUP = LANES // FEAT
PIECES = FEAT // 2 + 2
WIDE = PIECES * LANES
PACKED = WIDE // 2 + 16


def dot(left, right, dims=((1,), (0,))):
    return lax.dot_general(left, right, (dims, ((), ())), preferred_element_type=jnp.float32)


def rolls(scaled):
    zero = lax.optimization_barrier(jnp.int32(0))
    row = lax.broadcasted_iota(jnp.int32, (LANES, WIDE), 0) + zero
    column = lax.broadcasted_iota(jnp.int32, (LANES, WIDE), 1)
    d, lane = column // LANES - 1, column % LANES
    a = lane % FEAT
    goal = lane - a + (a + d) % FEAT
    found = (row == goal) & (d >= 0) & ((d < FEAT // 2) | (a < FEAT // 2))
    factor = jnp.where(d == 0, 1 / 32, 1 / 16) if scaled else 1.0
    return jnp.where(found, factor, 0.0).astype(jnp.bfloat16)


def features(rows, factors, lin, axis):
    x = rows.astype(jnp.float32)
    pieces = [x * lin]
    for number in range(PIECES - 1):
        span = slice(number * LANES, (number + 1) * LANES)
        piece = x * (factors[:, span] if axis else factors[span, :])
        if number == PIECES - 2:
            place = lax.broadcasted_iota(jnp.int32, piece.shape, axis)
            piece = jnp.where(place % FEAT == FEAT // 2, 1.0, piece)
        pieces.append(piece)
    return jnp.concatenate([piece.astype(jnp.bfloat16) for piece in pieces], axis=axis)


def turned_features(rows, turned_pick_ref, lin):
    turned = rows.astype(jnp.float32).T.astype(jnp.bfloat16)
    return features(turned, dot(turned_pick_ref[LANES:, :], turned), lin, 0)


def upright_features(rows, pick_ref, lin):
    return features(rows, dot(rows, pick_ref[:, LANES:]), lin, 1)


def head_mask(lanes_per_head, first_head):
    row_head = lax.broadcasted_iota(jnp.int32, (LANES, LANES), 0) // FEAT
    lane_head = lax.broadcasted_iota(jnp.int32, (LANES, LANES), 1) // lanes_per_head + first_head
    return row_head == lane_head


def head_masks(value_dim):
    per = LANES // value_dim
    return [head_mask(value_dim, part * per) for part in range(GROUP // per)]


def low_half():
    return lax.broadcasted_iota(jnp.int32, (LANES, LANES), 1) < LANES // 2


def piece_spans():
    return [slice(number * LANES, (number + 1) * LANES) for number in range(PIECES)]


def fold_heads(rows, masks):
    total = None
    for part, mask in enumerate(masks):
        piece = jnp.where(mask, rows[:, part * LANES : (part + 1) * LANES], 0.0)
        total = piece if total is None else total + piece
    return total + pltpu.roll(total, LANES // 2, 1)


def diagonal():
    row = lax.broadcasted_iota(jnp.int32, (LANES, LANES), 0)
    return row == lax.broadcasted_iota(jnp.int32, (LANES, LANES), 1)


def pack_state(out_ref, pieces):
    low, straight = low_half(), diagonal()
    for number in range(0, PIECES, 2):
        rows = slice(number // 2 * LANES, (number // 2 + 1) * LANES)
        values = jnp.where(low, pieces[number][0], pieces[number + 1][0])
        out_ref[0, 0, rows, :] = values.astype(out_ref.dtype)
    sums = [jnp.sum(jnp.where(straight, s, 0.0), axis=0, keepdims=True) for _, s in pieces]
    sums.append(jnp.zeros((PACKED - WIDE // 2 - PIECES, LANES), jnp.float32))
    out_ref[0, 0, WIDE // 2 :, :] = jnp.concatenate(sums, axis=0).astype(out_ref.dtype)


def spread_state(state_ref, wide_ref, value_dim, sums_of):
    masks, low, straight = head_masks(value_dim), low_half(), diagonal()
    all_sums = state_ref[0, 0, WIDE // 2 :, :].astype(jnp.float32)
    for number, span in enumerate(piece_spans()):
        rows = slice(number // 2 * LANES, (number // 2 + 1) * LANES)
        state = state_ref[0, 0, rows, :].astype(jnp.float32)
        turned = pltpu.roll(state, LANES // 2, 1)
        values = jnp.where(low, turned, state) if number % 2 else jnp.where(low, state, turned)
        sums = jnp.where(straight, all_sums[number : number + 1, :], 0.0)
        sums = jnp.broadcast_to(jnp.sum(sums, axis=1, keepdims=True), (LANES, LANES))
        parts = [jnp.where(mask, values, 0.0) for mask in masks] + sums_of(sums, masks)
        for place, part in enumerate(parts):
            wide_ref[span, slice(place * LANES, (place + 1) * LANES)] = part.astype(jnp.bfloat16)


def own_lanes(array, lanes_per_head, head):
    place = lax.broadcasted_iota(jnp.int32, array.shape, 1) // lanes_per_head
    return jnp.where(place == head, array, jnp.zeros_like(array))


Q, K, V = slice(0, LANES), slice(LANES, 2 * LANES), slice(2 * LANES, None)


def tail_kernel(value_dim, x_ref, seg_ref, pick_ref, out_ref):
    seg = seg_ref[...]
    keep = (seg == seg[-1:, :]).astype(jnp.float32)
    values = (x_ref[:, V].astype(jnp.float32) * keep).astype(jnp.bfloat16)
    ones = jnp.broadcast_to(keep, (seg.shape[0], LANES)).astype(jnp.bfloat16)
    phi = turned_features(x_ref[:, K], pick_ref, 1.0)
    full = dot(phi, jnp.concatenate([values, ones], axis=1))
    width, masks = values.shape[1], head_masks(value_dim)
    pack_state(
        out_ref,
        [(fold_heads(full[span, :width], masks), full[span, width:]) for span in piece_spans()],
    )


def masks_of(seg_ref, seg_row_ref, begin, block):
    stop = begin + block
    rows = begin + lax.broadcasted_iota(jnp.int32, (block, stop), 0)
    columns = lax.broadcasted_iota(jnp.int32, (block, stop), 1)
    same = seg_ref[begin:stop, :] == seg_row_ref[0, :, :stop]
    return ((rows >= columns) & same).astype(jnp.float32)


def near_kernel(value_dim, block, x_ref, seg_ref, seg_row_ref, top_ref, den_ref):
    length = x_ref.shape[0]
    low = lax.broadcasted_iota(jnp.int32, (block, LANES), 1) < value_dim
    for begin in range(0, length, block):
        stop = begin + block
        mask = masks_of(seg_ref, seg_row_ref, begin, block)
        queries = x_ref[begin:stop, Q] * jnp.bfloat16(FEAT ** (-0.5))
        keys = x_ref[:stop, K]
        ones = jnp.ones((stop, LANES), jnp.bfloat16)
        for pair in range(GROUP // 2):
            span = slice(pair * LANES, (pair + 1) * LANES)
            first = 2 * LANES + pair * LANES
            values = jnp.concatenate([x_ref[:stop, first : first + LANES], ones], axis=1)
            sides = []
            for head in (2 * pair, 2 * pair + 1):
                scores = dot(own_lanes(queries, FEAT, head), keys, ((1,), (1,)))
                weights = (((0.5 * scores + 1.0) * scores + 1.0) * mask).astype(jnp.bfloat16)
                sides.append(dot(weights, values))
            top_ref[begin:stop, span] = jnp.where(low, sides[0][:, :LANES], sides[1][:, :LANES])
            den_ref[begin:stop, span] = jnp.where(low, sides[0][:, LANES:], sides[1][:, LANES:])


def far_kernel(value_dim, x_ref, seg_ref, state_ref, top_ref, den_ref, pick_ref, *rest):
    y_ref, inverse_ref, state_wide = rest[-3:]
    width = top_ref.shape[1]
    spread_state(
        state_ref, state_wide, value_dim,
        lambda sums, masks: [jnp.where(mask, sums, 0.0) for mask in masks],
    )
    seg = seg_ref[...]
    keep = (seg == seg[:1, :]).astype(jnp.float32)
    far = dot(upright_features(x_ref[:, Q], pick_ref, FEAT ** (-0.5)), state_wide[...])
    top = top_ref[...] + keep * far[:, :width]
    inverse = 1.0 / (den_ref[...] + keep * far[:, width:])
    y_ref[...] = (top * inverse).astype(y_ref.dtype)
    inverse_ref[...] = inverse


def head_kernel(
    value_dim, x_ref, dy_ref, y_ref, inverse_ref, seg_ref, pick_ref, out_ref, dn_ref, dd_ref
):
    width = dy_ref.shape[1]
    d_top = dy_ref[...].astype(jnp.float32) * inverse_ref[...]
    product = d_top * y_ref[...].astype(jnp.float32)
    large = product.astype(jnp.bfloat16)
    small = (product - large.astype(jnp.float32)).astype(jnp.bfloat16)
    row = lax.broadcasted_iota(jnp.int32, (width, LANES), 0) // value_dim
    lane = lax.broadcasted_iota(jnp.int32, (width, LANES), 1) // FEAT
    adder = jnp.where(row == lane, -1.0, 0.0).astype(jnp.bfloat16)
    d_den = dot(large, adder) + dot(small, adder)
    rounded = d_den.astype(jnp.bfloat16).astype(jnp.float32)
    place = lax.broadcasted_iota(jnp.int32, d_den.shape, 1) % FEAT
    d_den = jnp.where(place < FEAT // 2, rounded, d_den - rounded)
    seg = seg_ref[...]
    keep = (seg == seg[:1, :]).astype(jnp.float32)
    dn_ref[...] = d_top.astype(jnp.bfloat16)
    dd_ref[...] = d_den.astype(jnp.bfloat16)
    d_both = [(d_top * keep).astype(jnp.bfloat16), (d_den * keep).astype(jnp.bfloat16)]
    full = dot(
        turned_features(x_ref[:, Q], pick_ref, FEAT ** (-0.5)), jnp.concatenate(d_both, axis=1)
    )
    masks, own, pieces = head_masks(value_dim), head_mask(FEAT, 0), []
    for span in piece_spans():
        sums = jnp.where(own, full[span, width:], 0.0)
        sums = jnp.sum(sums, axis=1, keepdims=True) * (2 / FEAT)
        pieces.append((fold_heads(full[span, :width], masks), sums))
    pack_state(out_ref, pieces)


def from_features(d_phi, rows, pick_ref, lin):
    x = rows.astype(jnp.float32)
    factors = dot(rows, pick_ref[:, LANES:])
    total, scaled = d_phi[:, :LANES] * lin, []
    for number in range(PIECES - 1):
        span = slice(number * LANES, (number + 1) * LANES)
        piece = d_phi[:, (number + 1) * LANES : (number + 2) * LANES]
        total = total + piece * factors[:, span]
        scaled.append((piece * x).astype(jnp.bfloat16))
    return total + dot(jnp.concatenate(scaled, axis=1), pick_ref[:, LANES:], ((1,), (1,)))


def near_back_kernel(
    value_dim, block, x_ref, dn_ref, dd_ref, seg_ref, seg_row_ref, state_ref, pick_ref,
    dq_ref, dk_ref, dv_ref, state_wide, dq_sum,
):
    length, width = dn_ref.shape
    own = head_mask(FEAT, 0)
    spread_state(
        state_ref, state_wide, value_dim,
        lambda sums, masks: [jnp.where(own, sums, 0.0) * (2 / FEAT)],
    )
    keep = seg_ref[...] == seg_ref[:1, :]
    d_both = jnp.concatenate([dn_ref[...], dd_ref[...]], axis=1)
    d_phi = dot(jnp.where(keep, d_both, jnp.zeros_like(d_both)), state_wide[...], ((1,), (1,)))
    dq_sum[...] = from_features(d_phi, x_ref[:, Q], pick_ref, FEAT ** (-0.5))
    scale = jnp.bfloat16(FEAT ** (-0.5))
    low = lax.broadcasted_iota(jnp.int32, (block, LANES), 1) < value_dim
    for begin in range(0, length, block):
        stop, count = begin + block, length - begin
        key_place = lax.broadcasted_iota(jnp.int32, (block, count), 0)
        query_place = lax.broadcasted_iota(jnp.int32, (block, count), 1)
        same = seg_ref[begin:stop, :] == seg_row_ref[0, :, begin:]
        mask = ((query_place >= key_place) & same).astype(jnp.float32)
        queries = x_ref[begin:, Q] * scale
        keys = x_ref[begin:stop, K]
        dd = dd_ref[begin:, :]
        dk = jnp.zeros((block, LANES), jnp.float32)
        for pair in range(GROUP // 2):
            span = slice(pair * LANES, (pair + 1) * LANES)
            first = 2 * LANES + pair * LANES
            values = x_ref[begin:stop, first : first + LANES]
            dn = dn_ref[begin:, span]
            d_both = jnp.concatenate([dn, dd], axis=1)
            sides = []
            for side in range(2):
                head = 2 * pair + side
                own_keys = own_lanes(keys, FEAT, head)
                ones = own_lanes(jnp.full((block, LANES), 2 / FEAT, jnp.bfloat16), FEAT, head)
                own_values = own_lanes(values, value_dim, side)
                scores = dot(own_keys, queries, ((1,), (1,)))
                weights = (((0.5 * scores + 1.0) * scores + 1.0) * mask).astype(jnp.bfloat16)
                d_weights = dot(
                    jnp.concatenate([own_values, ones], axis=1), d_both, ((1,), (1,))
                )
                d_scores = (d_weights * ((scores + 1.0) * mask)).astype(jnp.bfloat16)
                sides.append(dot(weights, dn))
                dk = dk + own_lanes(dot(d_scores, queries), FEAT, head)
                dq_sum[begin:, :] += dot(d_scores, own_keys * scale, ((0,), (0,)))
            dv_ref[begin:stop, span] = jnp.where(low, sides[0], sides[1])
        dk_ref[begin:stop, :] = dk
    dq_ref[...] = dq_sum[...].astype(dq_ref.dtype)


def far_back_kernel(
    value_dim, x_ref, seg_ref, state_ref, dq_ref, dk_ref, dv_ref, pick_ref, out_ref, state_wide
):
    length, width = dv_ref.shape
    spread_state(state_ref, state_wide, value_dim, lambda sums, masks: [sums * (1 / LANES)])
    seg = seg_ref[...]
    keep = (seg == seg[-1:, :]).astype(jnp.float32)
    keys = x_ref[:, K]
    ones = jnp.ones((length, LANES), jnp.bfloat16)
    d_phi = dot(jnp.concatenate([x_ref[:, V], ones], axis=1), state_wide[...], ((1,), (1,)))
    dk = dk_ref[...] + keep * from_features(d_phi, keys, pick_ref, 1.0)
    dv = dv_ref[...] + keep * dot(upright_features(keys, pick_ref, 1.0), state_wide[:, :width])
    out_ref[:, Q] = dq_ref[...]
    out_ref[:, K] = dk.astype(out_ref.dtype)
    out_ref[:, V] = dv.astype(out_ref.dtype)


class Attention:
    def __init__(self, rows, length, width):
        self.rows, self.length = rows, length
        self.value_dim = width // HEADS
        self.groups = HEADS // GROUP
        self.wide = GROUP * self.value_dim
        self.across = 2 * LANES + self.wide
        self.block = min(256, length)
        self.count = rows * length
        self.scaled, self.plain = rolls(True), rolls(False)
        self.all = range(self.groups)

    def specs(self, groups):
        def rows_of(columns):
            return pl.BlockSpec((self.length, columns), lambda r, g: (r, g))

        return dict(
            x=rows_of(self.across),
            values=rows_of(self.wide),
            narrow=rows_of(LANES),
            seg=pl.BlockSpec((self.length, 1), lambda r, g: (r, 0)),
            seg_row=pl.BlockSpec((1, 1, self.length), lambda r, g: (r, 0, 0)),
            state=pl.BlockSpec((1, 1, PACKED, LANES), lambda r, g: (r, g, 0, 0)),
            pick=pl.BlockSpec((LANES, WIDE), lambda r, g: (0, 0)),
            turned_pick=pl.BlockSpec((WIDE, LANES), lambda r, g: (0, 0)),
        )

    def shape(self, columns, dtype, groups):
        return jax.ShapeDtypeStruct((self.count, columns * len(groups)), dtype)

    def state_shape(self, groups):
        return jax.ShapeDtypeStruct((self.rows, len(groups), PACKED, LANES), jnp.bfloat16)

    def wide_state(self, columns):
        return pltpu.VMEM((WIDE, columns), jnp.bfloat16)

    def call(self, kernel, groups, specs, outs, out_specs, scratch, passes, name):
        return pl.pallas_call(
            functools.partial(kernel, self.value_dim),
            grid=(self.rows, len(groups)),
            in_specs=specs,
            out_specs=out_specs,
            out_shape=outs,
            scratch_shapes=scratch,
            compiler_params=pltpu.CompilerParams(
                dimension_semantics=("arbitrary", "arbitrary"), vmem_limit_bytes=56 * 2**20
            ),
            cost_estimate=pl.CostEstimate(
                flops=self.rows * len(groups) * GROUP * passes * 2**26 * self.length // 512,
                bytes_accessed=2**21,
                transcendentals=0,
            ),
            name=name,
        )

    def tail(self, x, seg):
        at = self.specs(self.all)
        return self.call(
            tail_kernel, self.all, [at["x"], at["seg"], at["turned_pick"]],
            self.state_shape(self.all), at["state"], [], 5, "attn_tail",
        )(x, seg, self.plain.T)

    def near(self, x, seg, seg_row):
        def kernel(value_dim, *refs):
            near_kernel(value_dim, self.block, *refs)

        at = self.specs(self.all)
        out = self.shape(self.wide, jnp.float32, self.all)
        return self.call(
            kernel, self.all, [at["x"], at["seg"], at["seg_row"]],
            [out, out], [at["values"]] * 2, [], 8, "attn_near",
        )(x, seg, seg_row)

    def far(self, x, seg, state, top, den):
        at = self.specs(self.all)
        return self.call(
            far_kernel, self.all,
            [at["x"], at["seg"], at["state"], at["values"], at["values"], at["pick"]],
            [self.shape(self.wide, dtype, self.all) for dtype in (jnp.bfloat16, jnp.float32)],
            [at["values"]] * 2, [self.wide_state(2 * self.wide)], 8, "attn_far",
        )(x, seg, state, top, den, self.scaled)

    def head(self, x, dy, y, inverse, seg):
        at = self.specs(self.all)
        return self.call(
            head_kernel, self.all,
            [at["x"], at["values"], at["values"], at["values"], at["seg"], at["turned_pick"]],
            [self.state_shape(self.all), self.shape(self.wide, jnp.bfloat16, self.all),
             self.shape(LANES, jnp.bfloat16, self.all)],
            [at["state"], at["values"], at["narrow"]], [], 5, "attn_head",
        )(x, dy, y, inverse, seg, self.scaled.T)

    def near_back(self, x, dn, dd, seg, seg_row, state):
        def kernel(value_dim, *refs):
            near_back_kernel(value_dim, self.block, *refs)

        at, groups = self.specs(self.all), self.all
        return self.call(
            kernel, groups,
            [at["x"], at["values"], at["narrow"], at["seg"], at["seg_row"], at["state"],
             at["pick"]],
            [self.shape(LANES, jnp.bfloat16, groups), self.shape(LANES, jnp.float32, groups),
             self.shape(self.wide, jnp.float32, groups)],
            [at["narrow"], at["narrow"], at["values"]],
            [self.wide_state(self.wide + LANES), pltpu.VMEM((self.length, LANES), jnp.float32)],
            24, "attn_near_back",
        )(x, dn, dd, seg, seg_row, state, self.scaled)

    def far_back(self, x, seg, state, dq, dk, dv):
        at, groups = self.specs(self.all), self.all
        return self.call(
            far_back_kernel, groups,
            [at["x"], at["seg"], at["state"], at["narrow"], at["narrow"], at["values"],
             at["pick"]],
            self.shape(self.across, jnp.bfloat16, groups), at["x"],
            [self.wide_state(self.wide + LANES)], 9, "attn_far_back",
        )(x, seg, state, dq, dk, dv, self.plain)


class Passing:
    def __init__(self, segment_ids, length, reach, size):
        self.ids, self.length, self.reach, self.size = segment_ids, length, reach, size
        self.place = lax.axis_index("seq")

    def id_at(self, device, last):
        position = jnp.clip(device, 0, self.size - 1) * self.length + last * (self.length - 1)
        return lax.dynamic_index_in_dim(self.ids, position, 1, keepdims=False)

    def start(self, own, shift):
        self.shift, self.came = shift, []
        for k in range(1, self.reach + 1):
            goals = [(i, i + shift * k) for i in range(self.size)]
            pairs = [(i, goal) for i, goal in goals if 0 <= goal < self.size]
            self.came.append(lax.ppermute(own, "seq", pairs))

    def end(self, *hold):
        before = self.shift > 0
        own_id, total = self.id_at(self.place, not before), 0.0
        for k, came in enumerate(self.came, 1):
            linked = self.id_at(self.place - self.shift * k, before) == own_id
            came = after(came, *hold) if hold else came
            total = total + jnp.where(linked[:, None, None, None], came.astype(jnp.float32), 0.0)
        return total.astype(jnp.bfloat16)


epsilon = 1e-05


def against(left, matrix):
    return dot(left, matrix, ((1,), (1,)))


def norm_forward(values):
    scale = lax.rsqrt(jnp.mean(values * values, axis=1, keepdims=True) + epsilon)
    return (scale, values * scale)


def norm_backward(d_scaled, gain, scale, normed):
    d_normed = d_scaled * gain
    return scale * (d_normed - normed * jnp.mean(d_normed * normed, axis=1, keepdims=True))


def fold(count):
    return [0] + list(range(1, count, 2)) + list(range(2, count, 2))[::-1]


class Line:
    def __init__(self, axis, axis_size, stride, count):
        self.axis, self.size, self.stride, self.count = axis, axis_size, stride, count
        self.order = fold(count)

    def send(self, array, steps=1):
        pairs = []
        for index in range(self.size):
            place = (index // self.stride) % self.count
            goal = self.order[(self.order.index(place) + steps) % self.count]
            pairs.append((index, index + (goal - place) * self.stride))
        return lax.ppermute(array, self.axis, pairs)

    def place_back(self, steps):
        own = (lax.axis_index(self.axis) // self.stride) % self.count
        rank = jnp.asarray([self.order.index(p) for p in range(self.count)], jnp.int32)[own]
        return jnp.asarray(self.order, jnp.int32)[(rank - steps) % self.count]


class Slice:
    def __init__(self, dp, seq):
        self.dp, self.seq, self.devices = dp, seq, dp * seq
        self.lines = {
            "z": Line("dp", dp, 2, dp // 2),
            "x": Line("dp", dp, 1, 2),
            "y": Line("seq", seq, 2, seq // 2),
            "c": Line("seq", seq, 1, 2),
        }
        if dp % 4 == 0:
            self.lines["w"] = Line("dp", dp, 4, dp // 4)
            self.lines["u"] = Line("dp", dp, 2, 2)

    def device_of(self, back):
        at = {d: self.lines[d].place_back(back[d]) for d in back}
        z = at["z"] if "z" in at else at["w"] * 2 + at["u"]
        return ((z * 2 + at["x"]) * (self.seq // 2) + at["y"]) * 2 + at["c"]


def after(array, *others):
    return lax.optimization_barrier((array, *others))[0]


def assemble(pieces, widths, block, shape):
    arrays = [array for array, _, _ in pieces]
    dtype = arrays[0].dtype
    places = jnp.stack([shape.device_of(n) for _, names, _ in pieces for n in names])
    copies = sum(len(names) * len(spans) for _, names, spans in pieces)
    windows = [
        (min(span[0] for span in spans), max(span[0] + span[1] for span in spans))
        for _, _, spans in pieces
    ]
    held = [(array.shape[0], high - low) for array, (low, high) in zip(arrays, windows)]

    def kernel(places_ref, *refs):
        piece_refs, refs = refs[: len(pieces)], refs[len(pieces) :]
        out_refs, refs = refs[: len(widths)], refs[len(widths) :]
        buffers, (in_sems, out_sems) = refs[: len(pieces)], refs[len(pieces) :]
        loads = []
        for number, piece_ref in enumerate(piece_refs):
            low, high = windows[number]
            load = pltpu.make_async_copy(
                piece_ref.at[:, pl.ds(low, high - low)], buffers[number], in_sems.at[number]
            )
            load.start()
            loads.append(load)
        stores, begin = [], 0
        for number, (load, (_, names, spans)) in enumerate(zip(loads, pieces)):
            load.wait()
            for i in range(len(names)):
                to = pl.multiple_of(places_ref[begin + i] * block, block)
                for low, width, output, column in spans:
                    store = pltpu.make_async_copy(
                        buffers[number].at[pl.ds(i * block, block), pl.ds(low - windows[number][0], width)],
                        out_refs[output].at[pl.ds(to, block), pl.ds(column, width)],
                        out_sems.at[len(stores)],
                    )
                    store.start()
                    stores.append(store)
            begin += len(names)
        for store in stores:
            store.wait()

    size = sum(tall * wide for tall, wide in held) * dtype.itemsize
    return pl.pallas_call(
        kernel,
        out_shape=[jax.ShapeDtypeStruct((shape.devices * block, w), dtype) for w in widths],
        in_specs=[pl.BlockSpec(memory_space=pltpu.SMEM)]
        + [pl.BlockSpec(memory_space=pl.ANY)] * len(pieces),
        out_specs=[pl.BlockSpec(memory_space=pl.ANY)] * len(widths),
        scratch_shapes=[pltpu.VMEM(size, dtype) for size in held]
        + [
            pltpu.SemaphoreType.DMA((len(pieces),)),
            pltpu.SemaphoreType.DMA((copies,)),
        ],
        cost_estimate=pl.CostEstimate(flops=0, bytes_accessed=2 * size, transcendentals=0),
        name="assemble",
    )(places, *arrays)


class Gathering:
    def __init__(self, shape, array, names=None):
        self.shape, self.array = shape, array
        self.names = names or [dict(z=0, x=0, y=0, c=0)]

    def came(self, dim, direct=False, hold=()):
        line, array, out = self.shape.lines[dim], self.array, []
        for step in range(1, line.count):
            array = line.send(self.array, step) if direct else line.send(array)
            if step <= len(hold):
                array = after(array, *hold[step - 1])
            out.append((array, [dict(n, **{dim: step}) for n in self.names]))
        return out

    def along(self, dim, direct=False, hold=()):
        came = self.came(dim, direct, hold)
        array = jnp.concatenate([self.array] + [a for a, _ in came], 0)
        return Gathering(self.shape, array, self.names + [n for _, names in came for n in names])

    def ring(self, dim):
        return RingGathering(self, dim)

    def columns(self, low, high):
        return Gathering(self.shape, self.array[:, low:high], self.names)

    def pieces(self, dim, spans):
        found = [(self.array, self.names)] + self.came(dim)
        return [(array, names, spans) for array, names in found]


class RingGathering:
    def __init__(self, held, dim):
        self.held, self.dim, self.line = held, dim, held.shape.lines[dim]
        self.arrays = [held.array]
        self.came = self.line.send(held.array)

    def next(self, *hold):
        if len(self.arrays) == self.line.count - 1:
            return self.came
        self.arrays.append(after(self.came, *hold))
        self.came = self.line.send(self.arrays[-1])
        return self.arrays[-1]

    def end(self):
        while len(self.arrays) < self.line.count - 1:
            self.next()
        self.arrays.append(self.came)
        names = [dict(n, **{self.dim: s}) for s in range(self.line.count) for n in self.held.names]
        return Gathering(self.held.shape, jnp.concatenate(self.arrays, 0), names)


def spans_of(low, high, homes):
    spans = []
    for begin, width, output, column in homes:
        first, last = max(low, begin), min(high, begin + width)
        if first < last:
            spans.append((first - low, last - first, output, column + first - begin))
    return spans


def side_by_side(widths):
    return [(sum(widths[:i]), width, i, 0) for i, width in enumerate(widths)]


class TwoWays:
    def __init__(self, parts, shape, homes=None, widths=None):
        own = [part.shape[1] for part in parts]
        self.homes, self.widths = homes or side_by_side(own), widths or own
        self.block, self.shape = parts[0].shape[0], shape
        self.columns = sum(own)
        self.cut = -(-self.columns // 2 // LANES) * LANES
        self.held = Gathering(shape, jnp.concatenate(parts, axis=1))

    def first(self, *hold):
        self.held = self.held.along("z", True, [hold] * 8 if hold else ())

    def second(self, *hold):
        hold = [hold] if hold else ()
        self.one = self.held.columns(0, self.cut).along("x", False, hold)
        self.two = self.held.columns(self.cut, self.columns).along("y", False, hold)

    def third(self, *hold):
        hold = [hold] if hold else ()
        self.one, self.two = self.one.along("y", False, hold), self.two.along("x", False, hold)

    def last(self):
        self.ends = [self.one.came("c"), self.two.came("c")]

    def output(self, *outputs):
        homes = [(b, w, outputs.index(o), c) for b, w, o, c in self.homes if o in outputs]
        pieces = []
        for half, low, high, came in (
            (self.one, 0, self.cut, self.ends[0]),
            (self.two, self.cut, self.columns, self.ends[1]),
        ):
            spans = spans_of(low, high, homes)
            found = [(half.array, half.names)] + came
            pieces += [(array, names, spans) for array, names in found if spans]
        return assemble(pieces, [self.widths[o] for o in outputs], self.block, self.shape)


LAYOUT = "cyxwu"


def picker(shape, width):
    block = width // shape.devices
    if block % 16:
        order = jnp.arange(width)
    else:
        names = [dict()]
        for dim in LAYOUT:
            names = [dict(n, **{dim: s}) for n in names for s in range(shape.lines[dim].count)]
        places = jnp.stack([shape.device_of(n) for n in names])
        order = (places[:, None] * block + jnp.arange(block)[None, :]).reshape(width)
    return (jnp.arange(width)[:, None] == order[None, :]).astype(jnp.bfloat16)


def turned_rows(pick, left):
    return dot(pick, left, ((0,), (1,))).astype(jnp.bfloat16)


class Scattering:
    def __init__(self, shape, kept, arrived, number=0):
        count, half, columns = kept.shape
        self.shape, self.dims = shape, LAYOUT[1:]
        form = [shape.lines[d].count for d in self.dims] + [2 * half // shape.devices, columns]
        self.parts = [[(t.reshape([count] + form), number) for t in (kept, arrived)]]

    def beside(self, other):
        self.parts = self.parts + other.parts
        return self

    def piece(self, array, number, step):
        low, high = [0] * array.ndim, list(array.shape)
        for axis, place in ((0, number), (self.axis + 1, step)):
            low[axis], high[axis] = place, place + 1
        rest = array.shape[1 : self.axis + 1] + array.shape[self.axis + 2 :]
        return lax.slice(array, low, high).reshape(rest)

    def terms_of(self, step, came=None):
        found, begin = [], 0
        for terms in self.parts:
            own = [self.piece(t, i, step) for t, i in terms]
            end = begin + own[0].shape[-1]
            own += [] if came is None else [came[..., begin:end]]
            found.append(functools.reduce(jnp.add, [t.astype(jnp.float32) for t in own]))
            begin = end
        return found

    def go(self, terms):
        self.sent = jnp.concatenate([t.astype(jnp.bfloat16) for t in terms], axis=-1)
        self.came = self.line.send(self.sent)

    def start(self, dim, *hold):
        self.line, self.axis, self.step = self.shape.lines[dim], self.dims.index(dim), 1
        self.dims = self.dims.replace(dim, "")
        if hold:
            self.parts = [[(after(t, *hold), i) for t, i in terms] for terms in self.parts]
        self.go(self.terms_of(1))
        return self

    def advance(self, *hold):
        flat = [t for terms in self.parts for t, _ in terms]
        came, *flat = lax.optimization_barrier((self.came, *flat, *hold))[: len(flat) + 1]
        self.parts = [[(flat.pop(0), i) for _, i in terms] for terms in self.parts]
        self.step += 1
        totals = self.terms_of(self.step % self.line.count, came)
        if self.step < self.line.count:
            self.go(totals)
        else:
            self.parts, self.came = [[(total[None], 0)] for total in totals], None
        return self

    def along(self, dim):
        self.start(dim)
        while self.came is not None:
            self.advance()
        return self


def scatter_whole(kept, sent):
    whole = jnp.concatenate([kept, sent], 0).astype(jnp.float32)
    return lax.psum_scatter(whole, ("dp", "seq"), scatter_dimension=0, tiled=True)


FF_TILE = 256


def mlp_kernel(
    block, begins, ends, a_ref, g_ref, at_ref, gt_ref, gate_ref, up_ref, down_ref, *refs
):
    if not begins:
        y_in_ref, da_in_ref, *refs = refs
    if ends:
        x_ref, gain_ref, y_ref, dxo_ref, da_sum, kept_ref, sent_ref, *refs, y_sum = refs
    else:
        y_sum, da_sum, kept_ref, sent_ref, *refs = refs
    hidden_ref, d_gate_ref, d_up_ref = refs
    count = a_ref.shape[0]
    step = pl.program_id(0)

    @pl.when(step == 0)
    def _():
        y_sum[...] = jnp.zeros_like(y_sum) if begins else y_in_ref[...]
        da_sum[...] = jnp.zeros_like(da_sum) if begins else da_in_ref[...]

    for begin in range(0, count, block):
        span = slice(begin, begin + block)
        a, g = a_ref[span, :], g_ref[span, :]
        gate, up = dot(a, gate_ref[...]), dot(a, up_ref[...])
        d_hidden = dot(g, down_ref[...])
        sigma = jax.nn.sigmoid(gate)
        silu = gate * sigma
        hidden = (silu * up).astype(jnp.bfloat16)
        d_gate = (d_hidden * up * (sigma + silu * (1.0 - sigma))).astype(jnp.bfloat16)
        d_up = (d_hidden * silu).astype(jnp.bfloat16)
        hidden_ref[span, :], d_gate_ref[span, :], d_up_ref[span, :] = hidden, d_gate, d_up
        y_sum[span, :] += dot(hidden, down_ref[...], ((1,), (1,)))
        da_sum[span, :] += dot(d_gate, gate_ref[...], ((1,), (1,))) + dot(
            d_up, up_ref[...], ((1,), (1,))
        )
    half = at_ref.shape[0] // 2
    for number, (left, right) in enumerate(
        ((at_ref, d_gate_ref), (at_ref, d_up_ref), (gt_ref, hidden_ref))
    ):
        kept_ref[number] = dot(left[:half, :], right[...]).astype(jnp.bfloat16)
        sent_ref[number] = dot(left[half:, :], right[...]).astype(jnp.bfloat16)
    if not ends:
        return

    @pl.when(step == pl.num_programs(0) - 1)
    def _():
        for begin in range(0, count, block):
            span = slice(begin, begin + block)
            x = x_ref[span, :]
            y_ref[span, :] = (x + y_sum[span, :]).astype(y_ref.dtype)
            scale = lax.rsqrt(jnp.mean(x * x, axis=1, keepdims=True) + epsilon)
            normed = x * scale
            d_normed = da_sum[span, :] * gain_ref[...]
            mean = jnp.mean(d_normed * normed, axis=1, keepdims=True)
            dx = g_ref[span, :].astype(jnp.float32) + scale * (d_normed - normed * mean)
            da_sum[span, :] = dx
            dxo_ref[span, :] = dx.astype(dxo_ref.dtype)


def feed_forward(a, g, a_turned, g_turned, weights, tiles, sums=None, ending=None):
    count, width = a.shape
    half = width // 2

    def held(rows, columns):
        return pl.BlockSpec((rows, columns), lambda j: (0, 0), pipeline_mode=pl.Buffered(1))

    def tile(first):
        return pl.BlockSpec((width, FF_TILE), lambda j: (0, first + j))

    def shape(dtype):
        return jax.ShapeDtypeStruct((count, width), dtype)

    full = held(count, width)
    given = [a, g, a_turned, g_turned] + [array for array, _ in weights]
    specs = [full, full] + [held(width, count)] * 2 + [tile(first) for _, first in weights]
    scratch = [pltpu.VMEM((count, FF_TILE), jnp.bfloat16)] * 3
    if sums is not None:
        given, specs = given + list(sums), specs + [full] * 2
    if ending is not None:
        given, specs = given + list(ending), specs + [full, held(1, width)]
        outs = [shape(jnp.bfloat16), shape(jnp.bfloat16), shape(jnp.float32)]
        scratch = scratch + [pltpu.VMEM((count, width), jnp.float32)]
    else:
        outs = [shape(jnp.float32)] * 2
    hidden = tiles * FF_TILE
    return pl.pallas_call(
        functools.partial(mlp_kernel, min(512, count), sums is None, ending is not None),
        grid=(tiles,),
        in_specs=specs,
        out_specs=[full] * len(outs)
        + [pl.BlockSpec((3, half, FF_TILE), lambda j: (0, 0, j))] * 2,
        out_shape=outs + [jax.ShapeDtypeStruct((3, half, hidden), jnp.bfloat16)] * 2,
        scratch_shapes=scratch,
        compiler_params=pltpu.CompilerParams(
            dimension_semantics=("arbitrary",), vmem_limit_bytes=60 * 2**20
        ),
        cost_estimate=pl.CostEstimate(
            flops=18 * count * width * hidden,
            bytes_accessed=12 * width * hidden + 20 * count * width,
            transcendentals=count * hidden,
        ),
        name="mlp",
    )(*given)


def gain_gradient(weights, gradients, gain):
    products = jnp.sum(weights.astype(jnp.float32) * gradients, axis=1)
    return products / gain.astype(jnp.float32)


def per_device(
    shape,
    layer_input,
    segment_ids,
    gain_attn,
    w_query,
    w_key,
    w_value,
    w_out,
    gain_mlp,
    w_gate,
    w_up,
    w_down,
    grad_output,
):
    rows, shard_len, width = layer_input.shape
    count = rows * shard_len
    narrow, hidden = HEADS * FEAT, w_gate.shape[1]
    attention = Attention(rows, shard_len, width)
    groups, wide, across = attention.groups, attention.wide, attention.across
    gains = jnp.pad(jnp.stack([gain_attn, gain_mlp], axis=1), ((0, 0), (0, LANES - 2)))
    first_parts = [w_query, w_key, w_value, gains]
    homes, grouped = [], []
    for g in range(groups):
        for part, begin, size, place in (
            (w_query, 0, LANES, 0),
            (w_key, narrow, LANES, LANES),
            (w_value, 2 * narrow, wide, 2 * LANES),
        ):
            homes.append((begin + g * size, size, 0, g * across + place))
            grouped.append(part[:, g * size : (g + 1) * size])
    homes.append((groups * across, LANES, 0, groups * across))
    spare = ((0, 0), (0, -hidden % FF_TILE))
    gate_part, up_part, down_part = (
        jnp.pad(part, spare) for part in (w_gate, w_up, w_down.T)
    )
    tiles = gate_part.shape[1] // FF_TILE
    ringed = gains.shape[0] % 16 == 0
    if ringed:
        early = TwoWays(first_parts, shape, homes, [groups * across + LANES])
        rest = TwoWays([gate_part, w_out, up_part], shape)
        early.first()
        early.second()
        early.third()
        begun = [early.one.array, early.two.array]
        rest.first(*begun)
        down = Gathering(shape, down_part).along("x", False, [begun])
        early.last()
        (gathered,) = early.output(0)
    else:
        first_part = jnp.concatenate(grouped + [gains], axis=1)
        gathered, out_w, gate_w, up_w, down_w = (
            lax.all_gather(part, ("dp", "seq"), axis=0, tiled=True)
            for part in (first_part, w_out, gate_part, up_part, down_part)
        )
    qkv_w = gathered[:, : groups * across]
    gain_one = gathered[:, groups * across].astype(jnp.float32)[None, :]
    gain_two = gathered[:, groups * across + 1].astype(jnp.float32)[None, :]

    pick = picker(shape, width)
    cotangent = grad_output.reshape(count, width)
    tokens = layer_input.reshape(count, width).astype(jnp.float32)
    scale_one, normed_one = norm_forward(tokens)
    a_one = (normed_one * gain_one).astype(jnp.bfloat16)
    a_one = after(a_one, rest.held.array, down.array) if ringed else a_one
    qkv = jnp.dot(a_one, qkv_w, preferred_element_type=jnp.float32).astype(jnp.bfloat16)
    place = lax.axis_index("seq")
    own_seg = lax.dynamic_slice_in_dim(segment_ids, place * shard_len, shard_len, 1)
    seg, seg_row = own_seg.reshape(count, 1), own_seg.reshape(rows, 1, shard_len)
    reach = min(shape.seq - 1, -(-(LONGEST - 1) // shard_len))
    states = Passing(segment_ids, shard_len, reach, shape.seq)
    if ringed:
        down = down.along("y", False, [[qkv]])
        tail = attention.tail(after(qkv, down.array), seg)
        rest.second(tail)
        states.start(tail, 1)
        ring = down.ring("z")
        turn = ring.next(tail)
        top, den = attention.near(
            after(qkv, rest.one.array, rest.two.array, turn), seg, seg_row
        )
        turn = ring.next(den)
        earlier = after(states.end(den), turn)
        mixed_cat, inverse = attention.far(qkv, seg, earlier, top, den)
        turned_mixed, turned_one = turned_rows(pick, mixed_cat), turned_rows(pick, a_one)
        rest.third(turned_mixed, turned_one)
        rest.last()
        down = ring.end()
        down_ends = down.pieces("c", [(0, tiles * FF_TILE, 0, 0)])
        (out_w,) = rest.output(1)
    else:
        tail = attention.tail(qkv, seg)
        states.start(tail, 1)
        earlier = states.end()
        top, den = attention.near(qkv, seg, seg_row)
        mixed_cat, inverse = attention.far(qkv, seg, earlier, top, den)
        turned_mixed, turned_one = turned_rows(pick, mixed_cat), turned_rows(pick, a_one)
    x_two = tokens + jnp.dot(mixed_cat, out_w, preferred_element_type=jnp.float32)
    scale_two, normed_two = norm_forward(x_two)
    a_two = (normed_two * gain_two).astype(jnp.bfloat16)
    a_turned = turned_rows(pick, a_two)
    if ringed:
        gate_w, up_w = rest.output(0, 2)
        (down_w,) = assemble(down_ends, [tiles * FF_TILE], down_part.shape[0], shape)
    result, d_branch, d_x_two, kept, sent = feed_forward(
        a_two,
        cotangent,
        a_turned,
        turned_rows(pick, cotangent),
        [(gate_w, 0), (up_w, 0), (down_w, 0)],
        tiles,
        None,
        (x_two, gain_two),
    )
    half = width // 2
    d_mixed = against(d_branch, out_w).astype(jnp.bfloat16)
    ahead, d_top, d_den = attention.head(qkv, d_mixed, mixed_cat, inverse, seg)
    states.start(ahead, -1)
    own = after(d_branch, ahead) if ringed else d_branch
    out_sent, out_kept = (
        dot(t, own).astype(jnp.bfloat16) for t in (turned_mixed[half:], turned_mixed[:half])
    )
    if ringed:
        send_core = shape.lines["c"].send
        arrived, out_arrived = send_core(sent), send_core(out_sent)
        arrived = after(arrived, out_sent, out_kept)
        gate_sum, up_sum, down_sum = (Scattering(shape, kept, arrived, i) for i in range(3))
        gate_sum.beside(Scattering(shape, out_kept[None], out_arrived[None])).start("y")
        up_sum.start("x")
        down_sum.start("u")
        d_top = after(d_top, gate_sum.sent, up_sum.sent, down_sum.sent)
        d_near = attention.near_back(qkv, d_top, d_den, seg, seg_row, earlier)
        near = d_near[0]
        gate_sum.advance(near).start("x")
        up_sum.advance(near).start("y")
        down_sum.advance(near).start("w")
        later = after(states.end(near), down_sum.sent, gate_sum.sent, up_sum.sent)

        d_qkv = attention.far_back(qkv, seg, later, *d_near)
        own_sent = dot(turned_one[half:], d_qkv).astype(jnp.bfloat16)
        own_kept = dot(turned_one[:half], d_qkv).astype(jnp.bfloat16)
        both = gate_sum.advance(own_kept).beside(up_sum.advance(own_kept)).start("u")
        arrived = after(send_core(own_sent), own_kept)
        down_sum.advance(both.sent).start("x")
        arrived = after(arrived, down_sum.sent)
        qkv_a, qkv_b = (
            Scattering(shape, own_kept[None, :, low : low + across], arrived[None, :, low : low + across])
            for low in (0, across)
        )
        qkv_a.start("y")
        qkv_b.start("x")
        d_qkv = after(d_qkv, qkv_a.sent, qkv_b.sent)
        d_a_one = against(d_qkv[:, :across], qkv_w[:, :across])
        qkv_b.advance(d_a_one).start("y")
        qkv_a.advance(d_a_one).start("x")
        d_qkv = after(d_qkv, qkv_b.sent, qkv_a.sent)
        d_a_one = d_a_one + against(d_qkv[:, across:], qkv_w[:, across:])
        both.advance(d_a_one).start("w")
        down_sum.advance(both.sent).start("y")
        qkv_sum = qkv_a.advance(both.sent).beside(qkv_b.advance(both.sent)).start("u")
        down_sum.advance(both.sent)
        qkv_sum.advance().start("w")
        both.advance()
        qkv_sum.advance()
        grad_qkv = [terms[0][0][0] for terms in qkv_sum.parts]
        grad_gate, grad_out, grad_up = (terms[0][0][0] for terms in both.parts)
        grad_down = down_sum.parts[0][0][0][0][:, :hidden]
        grad_gate, grad_up = grad_gate[:, :hidden], grad_up[:, :hidden]
    else:
        later = states.end()
        d_near = attention.near_back(qkv, d_top, d_den, seg, seg_row, earlier)
        grad_gate, grad_up, grad_down = (
            scatter_whole(kept[i], sent[i])[:, :hidden] for i in range(3)
        )
        grad_out = scatter_whole(out_kept, out_sent)
        d_qkv = attention.far_back(qkv, seg, later, *d_near)
        whole = scatter_whole(dot(turned_one[:half], d_qkv), dot(turned_one[half:], d_qkv))
        grad_qkv = [whole[:, g * across : (g + 1) * across] for g in range(groups)]
        d_a_one = against(d_qkv, qkv_w)
    d_tokens = d_x_two + norm_backward(d_a_one, gain_one, scale_one, normed_one)
    return (
        result.reshape(rows, shard_len, width),
        d_tokens.reshape(rows, shard_len, width),
        gain_gradient(jnp.concatenate(grouped, axis=1), jnp.concatenate(grad_qkv, axis=1), gain_attn),
        jnp.concatenate([part[:, Q] for part in grad_qkv], axis=1),
        jnp.concatenate([part[:, K] for part in grad_qkv], axis=1),
        jnp.concatenate([part[:, V] for part in grad_qkv], axis=1),
        grad_out,
        gain_gradient(
            jnp.concatenate([w_gate, w_up], axis=1),
            jnp.concatenate([grad_gate, grad_up], axis=1),
            gain_mlp,
        ),
        grad_gate,
        grad_up,
        grad_down.T,
    )


def solution(mesh):
    placed = (
        P("dp", "seq", None),
        P("dp", None),
        P(("dp", "seq")),
        P(("dp", "seq"), None),
        P(("dp", "seq"), None),
        P(("dp", "seq"), None),
        P(("dp", "seq"), None),
        P(("dp", "seq")),
        P(("dp", "seq"), None),
        P(("dp", "seq"), None),
        P(None, ("dp", "seq")),
        P("dp", "seq", None),
    )
    return jax.shard_map(
        functools.partial(per_device, Slice(mesh.shape["dp"], mesh.shape["seq"])),
        mesh=mesh,
        in_specs=placed,
        out_specs=(
            P("dp", "seq", None),
            P("dp", "seq", None),
            P(("dp", "seq")),
            P(("dp", "seq"), None),
            P(("dp", "seq"), None),
            P(("dp", "seq"), None),
            P(("dp", "seq"), None),
            P(("dp", "seq")),
            P(("dp", "seq"), None),
            P(("dp", "seq"), None),
            P(None, ("dp", "seq")),
        ),
        check_vma=False,
    )
```

```python
import functools

import jax
import jax.numpy as jnp
import numpy as np
from jax import lax
from jax.experimental import pallas as pl
from jax.experimental.pallas import tpu as pltpu
from jax.sharding import PartitionSpec as P

LONGEST = 1024
HEADS = 16
FEAT = 16
LANES = 128
GROUP = LANES // FEAT
PIECES = FEAT // 2 + 2
WIDE = PIECES * LANES
PACKED = WIDE // 2 + 16


def dot(left, right, dims=((1,), (0,))):
    return lax.dot_general(left, right, (dims, ((), ())), preferred_element_type=jnp.float32)


def rolls(scaled):
    zero = lax.optimization_barrier(jnp.int32(0))
    row = lax.broadcasted_iota(jnp.int32, (LANES, WIDE), 0) + zero
    column = lax.broadcasted_iota(jnp.int32, (LANES, WIDE), 1)
    d, lane = column // LANES - 1, column % LANES
    a = lane % FEAT
    goal = lane - a + (a + d) % FEAT
    found = (row == goal) & (d >= 0) & ((d < FEAT // 2) | (a < FEAT // 2))
    factor = jnp.where(d == 0, 1 / 32, 1 / 16) if scaled else 1.0
    return jnp.where(found, factor, 0.0).astype(jnp.bfloat16)


def features(rows, factors, lin, axis):
    x = rows.astype(jnp.float32)
    pieces = [x * lin]
    for number in range(PIECES - 1):
        span = slice(number * LANES, (number + 1) * LANES)
        piece = x * (factors[:, span] if axis else factors[span, :])
        if number == PIECES - 2:
            place = lax.broadcasted_iota(jnp.int32, piece.shape, axis)
            piece = jnp.where(place % FEAT == FEAT // 2, 1.0, piece)
        pieces.append(piece)
    return jnp.concatenate([piece.astype(jnp.bfloat16) for piece in pieces], axis=axis)


def turned_features(rows, turned_pick_ref, lin):
    turned = rows.astype(jnp.float32).T.astype(jnp.bfloat16)
    return features(turned, dot(turned_pick_ref[LANES:, :], turned), lin, 0)


def upright_features(rows, pick_ref, lin):
    return features(rows, dot(rows, pick_ref[:, LANES:]), lin, 1)


def head_mask(lanes_per_head, first_head):
    row_head = lax.broadcasted_iota(jnp.int32, (LANES, LANES), 0) // FEAT
    lane_head = lax.broadcasted_iota(jnp.int32, (LANES, LANES), 1) // lanes_per_head + first_head
    return row_head == lane_head


def head_masks(value_dim):
    per = LANES // value_dim
    return [head_mask(value_dim, part * per) for part in range(GROUP // per)]


def low_half():
    return lax.broadcasted_iota(jnp.int32, (LANES, LANES), 1) < LANES // 2


def piece_spans():
    return [slice(number * LANES, (number + 1) * LANES) for number in range(PIECES)]


def fold_heads(rows, masks):
    total = None
    for part, mask in enumerate(masks):
        piece = jnp.where(mask, rows[:, part * LANES : (part + 1) * LANES], 0.0)
        total = piece if total is None else total + piece
    return total + pltpu.roll(total, LANES // 2, 1)


def diagonal():
    row = lax.broadcasted_iota(jnp.int32, (LANES, LANES), 0)
    return row == lax.broadcasted_iota(jnp.int32, (LANES, LANES), 1)


def pack_state(out_ref, pieces):
    low, straight = low_half(), diagonal()
    for number in range(0, PIECES, 2):
        rows = slice(number // 2 * LANES, (number // 2 + 1) * LANES)
        values = jnp.where(low, pieces[number][0], pieces[number + 1][0])
        out_ref[0, 0, rows, :] = values.astype(out_ref.dtype)
    sums = [jnp.sum(jnp.where(straight, s, 0.0), axis=0, keepdims=True) for _, s in pieces]
    sums.append(jnp.zeros((PACKED - WIDE // 2 - PIECES, LANES), jnp.float32))
    out_ref[0, 0, WIDE // 2 :, :] = jnp.concatenate(sums, axis=0).astype(out_ref.dtype)


def spread_state(state_ref, wide_ref, value_dim, sums_of):
    masks, low, straight = head_masks(value_dim), low_half(), diagonal()
    all_sums = state_ref[0, 0, WIDE // 2 :, :].astype(jnp.float32)
    for number, span in enumerate(piece_spans()):
        rows = slice(number // 2 * LANES, (number // 2 + 1) * LANES)
        state = state_ref[0, 0, rows, :].astype(jnp.float32)
        turned = pltpu.roll(state, LANES // 2, 1)
        values = jnp.where(low, turned, state) if number % 2 else jnp.where(low, state, turned)
        sums = jnp.where(straight, all_sums[number : number + 1, :], 0.0)
        sums = jnp.broadcast_to(jnp.sum(sums, axis=1, keepdims=True), (LANES, LANES))
        parts = [jnp.where(mask, values, 0.0) for mask in masks] + sums_of(sums, masks)
        for place, part in enumerate(parts):
            wide_ref[span, slice(place * LANES, (place + 1) * LANES)] = part.astype(jnp.bfloat16)


def own_lanes(array, lanes_per_head, head):
    place = lax.broadcasted_iota(jnp.int32, array.shape, 1) // lanes_per_head
    return jnp.where(place == head, array, jnp.zeros_like(array))


Q, K, V = slice(0, LANES), slice(LANES, 2 * LANES), slice(2 * LANES, None)


def tail_kernel(value_dim, x_ref, seg_ref, pick_ref, out_ref):
    seg = seg_ref[...]
    keep = (seg == seg[-1:, :]).astype(jnp.float32)
    values = (x_ref[:, V].astype(jnp.float32) * keep).astype(jnp.bfloat16)
    ones = jnp.broadcast_to(keep, (seg.shape[0], LANES)).astype(jnp.bfloat16)
    phi = turned_features(x_ref[:, K], pick_ref, 1.0)
    full = dot(phi, jnp.concatenate([values, ones], axis=1))
    width, masks = values.shape[1], head_masks(value_dim)
    pack_state(
        out_ref,
        [(fold_heads(full[span, :width], masks), full[span, width:]) for span in piece_spans()],
    )


def masks_of(seg_ref, seg_row_ref, begin, block):
    stop = begin + block
    rows = begin + lax.broadcasted_iota(jnp.int32, (block, stop), 0)
    columns = lax.broadcasted_iota(jnp.int32, (block, stop), 1)
    same = seg_ref[begin:stop, :] == seg_row_ref[0, :, :stop]
    return ((rows >= columns) & same).astype(jnp.float32)


def near_kernel(value_dim, block, x_ref, seg_ref, seg_row_ref, top_ref, den_ref):
    length = x_ref.shape[0]
    low = lax.broadcasted_iota(jnp.int32, (block, LANES), 1) < value_dim
    for begin in range(0, length, block):
        stop = begin + block
        mask = masks_of(seg_ref, seg_row_ref, begin, block)
        queries = x_ref[begin:stop, Q] * jnp.bfloat16(FEAT ** (-0.5))
        keys = x_ref[:stop, K]
        ones = jnp.ones((stop, LANES), jnp.bfloat16)
        def pair_step(pair, _):
            first = pl.multiple_of(pair * LANES, LANES)
            span = pl.ds(first, LANES)
            own = pl.ds(2 * LANES + first, LANES)
            values = jnp.concatenate([x_ref[:stop, own], ones], axis=1)
            sides = []
            for head in (2 * pair, 2 * pair + 1):
                scores = dot(own_lanes(queries, FEAT, head), keys, ((1,), (1,)))
                weights = (((0.5 * scores + 1.0) * scores + 1.0) * mask).astype(jnp.bfloat16)
                sides.append(dot(weights, values))
            top_ref[begin:stop, span] = jnp.where(low, sides[0][:, :LANES], sides[1][:, :LANES])
            den_ref[begin:stop, span] = jnp.where(low, sides[0][:, LANES:], sides[1][:, LANES:])

        lax.fori_loop(0, GROUP // 2, pair_step, None)


def far_kernel(value_dim, x_ref, seg_ref, state_ref, top_ref, den_ref, pick_ref, *rest):
    y_ref, inverse_ref, state_wide = rest[-3:]
    width = top_ref.shape[1]
    spread_state(
        state_ref, state_wide, value_dim,
        lambda sums, masks: [jnp.where(mask, sums, 0.0) for mask in masks],
    )
    seg = seg_ref[...]
    keep = (seg == seg[:1, :]).astype(jnp.float32)
    far = dot(upright_features(x_ref[:, Q], pick_ref, FEAT ** (-0.5)), state_wide[...])
    top = top_ref[...] + keep * far[:, :width]
    inverse = 1.0 / (den_ref[...] + keep * far[:, width:])
    y_ref[...] = (top * inverse).astype(y_ref.dtype)
    inverse_ref[...] = inverse


def head_kernel(
    value_dim, x_ref, dy_ref, y_ref, inverse_ref, seg_ref, pick_ref, out_ref, dn_ref, dd_ref
):
    width = dy_ref.shape[1]
    d_top = dy_ref[...].astype(jnp.float32) * inverse_ref[...]
    product = d_top * y_ref[...].astype(jnp.float32)
    large = product.astype(jnp.bfloat16)
    small = (product - large.astype(jnp.float32)).astype(jnp.bfloat16)
    row = lax.broadcasted_iota(jnp.int32, (width, LANES), 0) // value_dim
    lane = lax.broadcasted_iota(jnp.int32, (width, LANES), 1) // FEAT
    adder = jnp.where(row == lane, -1.0, 0.0).astype(jnp.bfloat16)
    d_den = dot(large, adder) + dot(small, adder)
    rounded = d_den.astype(jnp.bfloat16).astype(jnp.float32)
    place = lax.broadcasted_iota(jnp.int32, d_den.shape, 1) % FEAT
    d_den = jnp.where(place < FEAT // 2, rounded, d_den - rounded)
    seg = seg_ref[...]
    keep = (seg == seg[:1, :]).astype(jnp.float32)
    dn_ref[...] = d_top.astype(jnp.bfloat16)
    dd_ref[...] = d_den.astype(jnp.bfloat16)
    d_both = [(d_top * keep).astype(jnp.bfloat16), (d_den * keep).astype(jnp.bfloat16)]
    full = dot(
        turned_features(x_ref[:, Q], pick_ref, FEAT ** (-0.5)), jnp.concatenate(d_both, axis=1)
    )
    masks, own, pieces = head_masks(value_dim), head_mask(FEAT, 0), []
    for span in piece_spans():
        sums = jnp.where(own, full[span, width:], 0.0)
        sums = jnp.sum(sums, axis=1, keepdims=True) * (2 / FEAT)
        pieces.append((fold_heads(full[span, :width], masks), sums))
    pack_state(out_ref, pieces)


def from_features(d_phi, rows, pick_ref, lin):
    x = rows.astype(jnp.float32)
    factors = dot(rows, pick_ref[:, LANES:])
    total, scaled = d_phi[:, :LANES] * lin, []
    for number in range(PIECES - 1):
        span = slice(number * LANES, (number + 1) * LANES)
        piece = d_phi[:, (number + 1) * LANES : (number + 2) * LANES]
        total = total + piece * factors[:, span]
        scaled.append((piece * x).astype(jnp.bfloat16))
    return total + dot(jnp.concatenate(scaled, axis=1), pick_ref[:, LANES:], ((1,), (1,)))


def near_back_kernel(
    value_dim, block, x_ref, dn_ref, dd_ref, seg_ref, seg_row_ref, state_ref, pick_ref,
    dq_ref, dk_ref, dv_ref, state_wide, dq_sum,
):
    length, width = dn_ref.shape
    own = head_mask(FEAT, 0)
    spread_state(
        state_ref, state_wide, value_dim,
        lambda sums, masks: [jnp.where(own, sums, 0.0) * (2 / FEAT)],
    )
    keep = seg_ref[...] == seg_ref[:1, :]
    d_both = jnp.concatenate([dn_ref[...], dd_ref[...]], axis=1)
    d_phi = dot(jnp.where(keep, d_both, jnp.zeros_like(d_both)), state_wide[...], ((1,), (1,)))
    dq_sum[...] = from_features(d_phi, x_ref[:, Q], pick_ref, FEAT ** (-0.5))
    scale = jnp.bfloat16(FEAT ** (-0.5))
    low = lax.broadcasted_iota(jnp.int32, (block, LANES), 1) < value_dim
    for begin in range(0, length, block):
        stop, count = begin + block, length - begin
        key_place = lax.broadcasted_iota(jnp.int32, (block, count), 0)
        query_place = lax.broadcasted_iota(jnp.int32, (block, count), 1)
        same = seg_ref[begin:stop, :] == seg_row_ref[0, :, begin:]
        mask = ((query_place >= key_place) & same).astype(jnp.float32)
        queries = x_ref[begin:, Q] * scale
        keys = x_ref[begin:stop, K]
        dd = dd_ref[begin:, :]
        def pair_step(pair, dk):
            start = pl.multiple_of(pair * LANES, LANES)
            span = pl.ds(start, LANES)
            own = pl.ds(2 * LANES + start, LANES)
            values = x_ref[begin:stop, own]
            dn = dn_ref[begin:, span]
            d_both = jnp.concatenate([dn, dd], axis=1)
            sides = []
            for side in range(2):
                head = 2 * pair + side
                own_keys = own_lanes(keys, FEAT, head)
                ones = own_lanes(jnp.full((block, LANES), 2 / FEAT, jnp.bfloat16), FEAT, head)
                own_values = own_lanes(values, value_dim, side)
                scores = dot(own_keys, queries, ((1,), (1,)))
                weights = (((0.5 * scores + 1.0) * scores + 1.0) * mask).astype(jnp.bfloat16)
                d_weights = dot(
                    jnp.concatenate([own_values, ones], axis=1), d_both, ((1,), (1,))
                )
                d_scores = (d_weights * ((scores + 1.0) * mask)).astype(jnp.bfloat16)
                sides.append(dot(weights, dn))
                dk = dk + own_lanes(dot(d_scores, queries), FEAT, head)
                dq_sum[begin:, :] += dot(d_scores, own_keys * scale, ((0,), (0,)))
            dv_ref[begin:stop, span] = jnp.where(low, sides[0], sides[1])
            return dk

        zeros = jnp.zeros((block, LANES), jnp.float32)
        dk_ref[begin:stop, :] = lax.fori_loop(0, GROUP // 2, pair_step, zeros)
    dq_ref[...] = dq_sum[...].astype(dq_ref.dtype)


def far_back_kernel(
    value_dim, x_ref, seg_ref, state_ref, dq_ref, dk_ref, dv_ref, pick_ref, out_ref, state_wide
):
    length, width = dv_ref.shape
    spread_state(state_ref, state_wide, value_dim, lambda sums, masks: [sums * (1 / LANES)])
    seg = seg_ref[...]
    keep = (seg == seg[-1:, :]).astype(jnp.float32)
    keys = x_ref[:, K]
    ones = jnp.ones((length, LANES), jnp.bfloat16)
    d_phi = dot(jnp.concatenate([x_ref[:, V], ones], axis=1), state_wide[...], ((1,), (1,)))
    dk = dk_ref[...] + keep * from_features(d_phi, keys, pick_ref, 1.0)
    dv = dv_ref[...] + keep * dot(upright_features(keys, pick_ref, 1.0), state_wide[:, :width])
    out_ref[:, Q] = dq_ref[...]
    out_ref[:, K] = dk.astype(out_ref.dtype)
    out_ref[:, V] = dv.astype(out_ref.dtype)


class Attention:
    def __init__(self, rows, length, width):
        self.rows, self.length = rows, length
        self.value_dim = width // HEADS
        self.groups = HEADS // GROUP
        self.wide = GROUP * self.value_dim
        self.across = 2 * LANES + self.wide
        self.block = min(256, length)
        self.count = rows * length
        self.scaled, self.plain = rolls(True), rolls(False)
        self.all = range(self.groups)

    def specs(self, groups):
        def rows_of(columns):
            return pl.BlockSpec((self.length, columns), lambda r, g: (r, g))

        return dict(
            x=rows_of(self.across),
            values=rows_of(self.wide),
            narrow=rows_of(LANES),
            seg=pl.BlockSpec((self.length, 1), lambda r, g: (r, 0)),
            seg_row=pl.BlockSpec((1, 1, self.length), lambda r, g: (r, 0, 0)),
            state=pl.BlockSpec((1, 1, PACKED, LANES), lambda r, g: (r, g, 0, 0)),
            pick=pl.BlockSpec((LANES, WIDE), lambda r, g: (0, 0)),
            turned_pick=pl.BlockSpec((WIDE, LANES), lambda r, g: (0, 0)),
        )

    def shape(self, columns, dtype, groups):
        return jax.ShapeDtypeStruct((self.count, columns * len(groups)), dtype)

    def state_shape(self, groups):
        return jax.ShapeDtypeStruct((self.rows, len(groups), PACKED, LANES), jnp.bfloat16)

    def wide_state(self, columns):
        return pltpu.VMEM((WIDE, columns), jnp.bfloat16)

    def call(self, kernel, groups, specs, outs, out_specs, scratch, passes, name):
        return pl.pallas_call(
            functools.partial(kernel, self.value_dim),
            grid=(self.rows, len(groups)),
            in_specs=specs,
            out_specs=out_specs,
            out_shape=outs,
            scratch_shapes=scratch,
            compiler_params=pltpu.CompilerParams(
                dimension_semantics=("arbitrary", "arbitrary"), vmem_limit_bytes=56 * 2**20
            ),
            cost_estimate=pl.CostEstimate(
                flops=self.rows * len(groups) * GROUP * passes * 2**26 * self.length // 512,
                bytes_accessed=2**21,
                transcendentals=0,
            ),
            name=name,
        )

    def tail(self, x, seg):
        at = self.specs(self.all)
        return self.call(
            tail_kernel, self.all, [at["x"], at["seg"], at["turned_pick"]],
            self.state_shape(self.all), at["state"], [], 5, "attn_tail",
        )(x, seg, self.plain.T)

    def near(self, x, seg, seg_row):
        def kernel(value_dim, *refs):
            near_kernel(value_dim, self.block, *refs)

        at = self.specs(self.all)
        out = self.shape(self.wide, jnp.float32, self.all)
        return self.call(
            kernel, self.all, [at["x"], at["seg"], at["seg_row"]],
            [out, out], [at["values"]] * 2, [], 8, "attn_near",
        )(x, seg, seg_row)

    def far(self, x, seg, state, top, den):
        at = self.specs(self.all)
        return self.call(
            far_kernel, self.all,
            [at["x"], at["seg"], at["state"], at["values"], at["values"], at["pick"]],
            [self.shape(self.wide, dtype, self.all) for dtype in (jnp.bfloat16, jnp.float32)],
            [at["values"]] * 2, [self.wide_state(2 * self.wide)], 8, "attn_far",
        )(x, seg, state, top, den, self.scaled)

    def head(self, x, dy, y, inverse, seg):
        at = self.specs(self.all)
        return self.call(
            head_kernel, self.all,
            [at["x"], at["values"], at["values"], at["values"], at["seg"], at["turned_pick"]],
            [self.state_shape(self.all), self.shape(self.wide, jnp.bfloat16, self.all),
             self.shape(LANES, jnp.bfloat16, self.all)],
            [at["state"], at["values"], at["narrow"]], [], 5, "attn_head",
        )(x, dy, y, inverse, seg, self.scaled.T)

    def near_back(self, x, dn, dd, seg, seg_row, state):
        def kernel(value_dim, *refs):
            near_back_kernel(value_dim, self.block, *refs)

        at, groups = self.specs(self.all), self.all
        return self.call(
            kernel, groups,
            [at["x"], at["values"], at["narrow"], at["seg"], at["seg_row"], at["state"],
             at["pick"]],
            [self.shape(LANES, jnp.bfloat16, groups), self.shape(LANES, jnp.float32, groups),
             self.shape(self.wide, jnp.float32, groups)],
            [at["narrow"], at["narrow"], at["values"]],
            [self.wide_state(self.wide + LANES), pltpu.VMEM((self.length, LANES), jnp.float32)],
            24, "attn_near_back",
        )(x, dn, dd, seg, seg_row, state, self.scaled)

    def far_back(self, x, seg, state, dq, dk, dv):
        at, groups = self.specs(self.all), self.all
        return self.call(
            far_back_kernel, groups,
            [at["x"], at["seg"], at["state"], at["narrow"], at["narrow"], at["values"],
             at["pick"]],
            self.shape(self.across, jnp.bfloat16, groups), at["x"],
            [self.wide_state(self.wide + LANES)], 9, "attn_far_back",
        )(x, seg, state, dq, dk, dv, self.plain)


class Passing:
    def __init__(self, segment_ids, length, reach, size):
        self.ids, self.length, self.reach, self.size = segment_ids, length, reach, size
        self.place = lax.axis_index("seq")

    def id_at(self, device, last):
        position = jnp.clip(device, 0, self.size - 1) * self.length + last * (self.length - 1)
        return lax.dynamic_index_in_dim(self.ids, position, 1, keepdims=False)

    def start(self, own, shift):
        self.shift, self.came = shift, []
        for k in range(1, self.reach + 1):
            goals = [(i, i + shift * k) for i in range(self.size)]
            pairs = [(i, goal) for i, goal in goals if 0 <= goal < self.size]
            self.came.append(lax.ppermute(own, "seq", pairs))

    def end(self, *hold):
        before = self.shift > 0
        own_id, total = self.id_at(self.place, not before), 0.0
        for k, came in enumerate(self.came, 1):
            linked = self.id_at(self.place - self.shift * k, before) == own_id
            came = after(came, *hold) if hold else came
            total = total + jnp.where(linked[:, None, None, None], came.astype(jnp.float32), 0.0)
        return total.astype(jnp.bfloat16)


epsilon = 1e-05


def against(left, matrix):
    return dot(left, matrix, ((1,), (1,)))


def norm_forward(values):
    scale = lax.rsqrt(jnp.mean(values * values, axis=1, keepdims=True) + epsilon)
    return (scale, values * scale)


def norm_backward(d_scaled, gain, scale, normed):
    d_normed = d_scaled * gain
    return scale * (d_normed - normed * jnp.mean(d_normed * normed, axis=1, keepdims=True))


def fold(count):
    return [0] + list(range(1, count, 2)) + list(range(2, count, 2))[::-1]


class Line:
    def __init__(self, axis, axis_size, stride, count):
        self.axis, self.size, self.stride, self.count = axis, axis_size, stride, count
        self.order = fold(count)

    def send(self, array, steps=1):
        pairs = []
        for index in range(self.size):
            place = (index // self.stride) % self.count
            goal = self.order[(self.order.index(place) + steps) % self.count]
            pairs.append((index, index + (goal - place) * self.stride))
        return lax.ppermute(array, self.axis, pairs)

    def place_back(self, steps):
        own = (lax.axis_index(self.axis) // self.stride) % self.count
        rank = jnp.asarray([self.order.index(p) for p in range(self.count)], jnp.int32)[own]
        return jnp.asarray(self.order, jnp.int32)[(rank - steps) % self.count]


class Slice:
    def __init__(self, dp, seq):
        self.dp, self.seq, self.devices = dp, seq, dp * seq
        self.lines = {
            "z": Line("dp", dp, 2, dp // 2),
            "x": Line("dp", dp, 1, 2),
            "y": Line("seq", seq, 2, seq // 2),
            "c": Line("seq", seq, 1, 2),
        }
        if dp % 4 == 0:
            self.lines["w"] = Line("dp", dp, 4, dp // 4)
            self.lines["u"] = Line("dp", dp, 2, 2)

    def device_of(self, back):
        at = {d: self.lines[d].place_back(back[d]) for d in back}
        z = at["z"] if "z" in at else at["w"] * 2 + at["u"]
        return ((z * 2 + at["x"]) * (self.seq // 2) + at["y"]) * 2 + at["c"]


def after(array, *others):
    return lax.optimization_barrier((array, *others))[0]


def assemble(pieces, widths, block, shape):
    arrays = [array for array, _, _ in pieces]
    dtype = arrays[0].dtype
    places = jnp.stack([shape.device_of(n) for _, names, _ in pieces for n in names])
    copies = sum(len(names) * len(spans) for _, names, spans in pieces)
    windows = [
        (min(span[0] for span in spans), max(span[0] + span[1] for span in spans))
        for _, _, spans in pieces
    ]
    held = [(array.shape[0], high - low) for array, (low, high) in zip(arrays, windows)]

    def kernel(places_ref, *refs):
        piece_refs, refs = refs[: len(pieces)], refs[len(pieces) :]
        out_refs, refs = refs[: len(widths)], refs[len(widths) :]
        buffers, (in_sems, out_sems) = refs[: len(pieces)], refs[len(pieces) :]
        loads = []
        for number, piece_ref in enumerate(piece_refs):
            low, high = windows[number]
            load = pltpu.make_async_copy(
                piece_ref.at[:, pl.ds(low, high - low)], buffers[number], in_sems.at[number]
            )
            load.start()
            loads.append(load)
        stores, begin = [], 0
        for number, (load, (_, names, spans)) in enumerate(zip(loads, pieces)):
            load.wait()
            for i in range(len(names)):
                to = pl.multiple_of(places_ref[begin + i] * block, block)
                for low, width, output, column in spans:
                    store = pltpu.make_async_copy(
                        buffers[number].at[pl.ds(i * block, block), pl.ds(low - windows[number][0], width)],
                        out_refs[output].at[pl.ds(to, block), pl.ds(column, width)],
                        out_sems.at[len(stores)],
                    )
                    store.start()
                    stores.append(store)
            begin += len(names)
        for store in stores:
            store.wait()

    size = sum(tall * wide for tall, wide in held) * dtype.itemsize
    return pl.pallas_call(
        kernel,
        out_shape=[jax.ShapeDtypeStruct((shape.devices * block, w), dtype) for w in widths],
        in_specs=[pl.BlockSpec(memory_space=pltpu.SMEM)]
        + [pl.BlockSpec(memory_space=pl.ANY)] * len(pieces),
        out_specs=[pl.BlockSpec(memory_space=pl.ANY)] * len(widths),
        scratch_shapes=[pltpu.VMEM(size, dtype) for size in held]
        + [
            pltpu.SemaphoreType.DMA((len(pieces),)),
            pltpu.SemaphoreType.DMA((copies,)),
        ],
        cost_estimate=pl.CostEstimate(flops=0, bytes_accessed=2 * size, transcendentals=0),
        name="assemble",
    )(places, *arrays)


class Gathering:
    def __init__(self, shape, array, names=None):
        self.shape, self.array = shape, array
        self.names = names or [dict(z=0, x=0, y=0, c=0)]

    def came(self, dim, direct=False, hold=()):
        line, array, out = self.shape.lines[dim], self.array, []
        for step in range(1, line.count):
            array = line.send(self.array, step) if direct else line.send(array)
            if step <= len(hold):
                array = after(array, *hold[step - 1])
            out.append((array, [dict(n, **{dim: step}) for n in self.names]))
        return out

    def along(self, dim, direct=False, hold=()):
        came = self.came(dim, direct, hold)
        array = jnp.concatenate([self.array] + [a for a, _ in came], 0)
        return Gathering(self.shape, array, self.names + [n for _, names in came for n in names])

    def ring(self, dim):
        return RingGathering(self, dim)

    def columns(self, low, high):
        return Gathering(self.shape, self.array[:, low:high], self.names)

    def pieces(self, dim, spans):
        found = [(self.array, self.names)] + self.came(dim)
        return [(array, names, spans) for array, names in found]


class RingGathering:
    def __init__(self, held, dim):
        self.held, self.dim, self.line = held, dim, held.shape.lines[dim]
        self.arrays = [held.array]
        self.came = self.line.send(held.array)

    def next(self, *hold):
        if len(self.arrays) == self.line.count - 1:
            return self.came
        self.arrays.append(after(self.came, *hold))
        self.came = self.line.send(self.arrays[-1])
        return self.arrays[-1]

    def end(self):
        while len(self.arrays) < self.line.count - 1:
            self.next()
        self.arrays.append(self.came)
        names = [dict(n, **{self.dim: s}) for s in range(self.line.count) for n in self.held.names]
        return Gathering(self.held.shape, jnp.concatenate(self.arrays, 0), names)


def spans_of(low, high, homes):
    spans = []
    for begin, width, output, column in homes:
        first, last = max(low, begin), min(high, begin + width)
        if first < last:
            spans.append((first - low, last - first, output, column + first - begin))
    return spans


def side_by_side(widths):
    return [(sum(widths[:i]), width, i, 0) for i, width in enumerate(widths)]


class TwoWays:
    def __init__(self, parts, shape, homes=None, widths=None):
        own = [part.shape[1] for part in parts]
        self.homes, self.widths = homes or side_by_side(own), widths or own
        self.block, self.shape = parts[0].shape[0], shape
        self.columns = sum(own)
        self.cut = -(-self.columns // 2 // LANES) * LANES
        self.held = Gathering(shape, jnp.concatenate(parts, axis=1))

    def first(self, *hold):
        self.held = self.held.along("z", True, [hold] * 8 if hold else ())

    def second(self, *hold):
        hold = [hold] if hold else ()
        self.one = self.held.columns(0, self.cut).along("x", False, hold)
        self.two = self.held.columns(self.cut, self.columns).along("y", False, hold)

    def third(self, *hold):
        hold = [hold] if hold else ()
        self.one, self.two = self.one.along("y", False, hold), self.two.along("x", False, hold)

    def last(self):
        self.ends = [self.one.came("c"), self.two.came("c")]

    def output(self, *outputs):
        homes = [(b, w, outputs.index(o), c) for b, w, o, c in self.homes if o in outputs]
        pieces = []
        for half, low, high, came in (
            (self.one, 0, self.cut, self.ends[0]),
            (self.two, self.cut, self.columns, self.ends[1]),
        ):
            spans = spans_of(low, high, homes)
            found = [(half.array, half.names)] + came
            pieces += [(array, names, spans) for array, names in found if spans]
        return assemble(pieces, [self.widths[o] for o in outputs], self.block, self.shape)


LAYOUT = "cyxwu"


def picker(shape, width):
    block = width // shape.devices
    if block % 16:
        order = jnp.arange(width)
    else:
        names = [dict()]
        for dim in LAYOUT:
            names = [dict(n, **{dim: s}) for n in names for s in range(shape.lines[dim].count)]
        places = jnp.stack([shape.device_of(n) for n in names])
        order = (places[:, None] * block + jnp.arange(block)[None, :]).reshape(width)
    return (jnp.arange(width)[:, None] == order[None, :]).astype(jnp.bfloat16)


def turned_rows(pick, left):
    return dot(pick, left, ((0,), (1,))).astype(jnp.bfloat16)


class Scattering:
    def __init__(self, shape, kept, arrived, number=0):
        count, half, columns = kept.shape
        self.shape, self.dims = shape, LAYOUT[1:]
        form = [shape.lines[d].count for d in self.dims] + [2 * half // shape.devices, columns]
        self.parts = [[(t.reshape([count] + form), number) for t in (kept, arrived)]]

    def beside(self, other):
        self.parts = self.parts + other.parts
        return self

    def piece(self, array, number, step):
        low, high = [0] * array.ndim, list(array.shape)
        for axis, place in ((0, number), (self.axis + 1, step)):
            low[axis], high[axis] = place, place + 1
        rest = array.shape[1 : self.axis + 1] + array.shape[self.axis + 2 :]
        return lax.slice(array, low, high).reshape(rest)

    def terms_of(self, step, came=None):
        found, begin = [], 0
        for terms in self.parts:
            own = [self.piece(t, i, step) for t, i in terms]
            end = begin + own[0].shape[-1]
            own += [] if came is None else [came[..., begin:end]]
            found.append(functools.reduce(jnp.add, [t.astype(jnp.float32) for t in own]))
            begin = end
        return found

    def go(self, terms):
        self.sent = jnp.concatenate([t.astype(jnp.bfloat16) for t in terms], axis=-1)
        self.came = self.line.send(self.sent)

    def start(self, dim, *hold):
        self.line, self.axis, self.step = self.shape.lines[dim], self.dims.index(dim), 1
        self.dims = self.dims.replace(dim, "")
        if hold:
            self.parts = [[(after(t, *hold), i) for t, i in terms] for terms in self.parts]
        self.go(self.terms_of(1))
        return self

    def advance(self, *hold):
        flat = [t for terms in self.parts for t, _ in terms]
        came, *flat = lax.optimization_barrier((self.came, *flat, *hold))[: len(flat) + 1]
        self.parts = [[(flat.pop(0), i) for _, i in terms] for terms in self.parts]
        self.step += 1
        totals = self.terms_of(self.step % self.line.count, came)
        if self.step < self.line.count:
            self.go(totals)
        else:
            self.parts, self.came = [[(total[None], 0)] for total in totals], None
        return self

    def along(self, dim):
        self.start(dim)
        while self.came is not None:
            self.advance()
        return self


def scatter_whole(kept, sent):
    whole = jnp.concatenate([kept, sent], 0).astype(jnp.float32)
    return lax.psum_scatter(whole, ("dp", "seq"), scatter_dimension=0, tiled=True)


FF_TILE = 256


def mlp_kernel(
    block, begins, ends, a_ref, g_ref, at_ref, gt_ref, gate_ref, up_ref, down_ref, *refs
):
    if not begins:
        y_in_ref, da_in_ref, *refs = refs
    if ends:
        x_ref, gain_ref, y_ref, dxo_ref, da_sum, kept_ref, sent_ref, *refs, y_sum = refs
    else:
        y_sum, da_sum, kept_ref, sent_ref, *refs = refs
    hidden_ref, d_gate_ref, d_up_ref = refs
    count = a_ref.shape[0]
    step = pl.program_id(0)

    @pl.when(step == 0)
    def _():
        y_sum[...] = jnp.zeros_like(y_sum) if begins else y_in_ref[...]
        da_sum[...] = jnp.zeros_like(da_sum) if begins else da_in_ref[...]

    def forward_and_back(index, _):
        span = pl.ds(pl.multiple_of(index * block, block), block)
        a, g = a_ref[span, :], g_ref[span, :]
        gate, up = dot(a, gate_ref[...]), dot(a, up_ref[...])
        d_hidden = dot(g, down_ref[...])
        sigma = jax.nn.sigmoid(gate)
        silu = gate * sigma
        hidden = (silu * up).astype(jnp.bfloat16)
        d_gate = (d_hidden * up * (sigma + silu * (1.0 - sigma))).astype(jnp.bfloat16)
        d_up = (d_hidden * silu).astype(jnp.bfloat16)
        hidden_ref[span, :], d_gate_ref[span, :], d_up_ref[span, :] = hidden, d_gate, d_up
        y_sum[span, :] += dot(hidden, down_ref[...], ((1,), (1,)))
        da_sum[span, :] += dot(d_gate, gate_ref[...], ((1,), (1,))) + dot(
            d_up, up_ref[...], ((1,), (1,))
        )

    lax.fori_loop(0, count // block, forward_and_back, None)
    half = at_ref.shape[0] // 2
    part = min(256, half)
    for number, (left, right) in enumerate(
        ((at_ref, d_gate_ref), (at_ref, d_up_ref), (gt_ref, hidden_ref))
    ):

        def products(index, _, number=number, left=left, right=right):
            begin = pl.multiple_of(index * part, part)
            for own, ref in ((0, kept_ref), (half, sent_ref)):
                rows = dot(left[pl.ds(own + begin, part), :], right[...])
                ref[number, pl.ds(begin, part), :] = rows.astype(jnp.bfloat16)

        lax.fori_loop(0, half // part, products, None)
    if not ends:
        return

    @pl.when(step == pl.num_programs(0) - 1)
    def _():
        def finish(index, _):
            span = pl.ds(pl.multiple_of(index * 128, 128), 128)
            x = x_ref[span, :]
            y_ref[span, :] = (x + y_sum[span, :]).astype(y_ref.dtype)
            scale = lax.rsqrt(jnp.mean(x * x, axis=1, keepdims=True) + epsilon)
            normed = x * scale
            d_normed = da_sum[span, :] * gain_ref[...]
            mean = jnp.mean(d_normed * normed, axis=1, keepdims=True)
            dx = g_ref[span, :].astype(jnp.float32) + scale * (d_normed - normed * mean)
            da_sum[span, :] = dx
            dxo_ref[span, :] = dx.astype(dxo_ref.dtype)

        lax.fori_loop(0, count // 128, finish, None)


def feed_forward(a, g, a_turned, g_turned, weights, tiles, sums=None, ending=None):
    count, width = a.shape
    half = width // 2

    def held(rows, columns):
        return pl.BlockSpec((rows, columns), lambda j: (0, 0), pipeline_mode=pl.Buffered(1))

    def tile(first):
        return pl.BlockSpec((width, FF_TILE), lambda j: (0, first + j))

    def shape(dtype):
        return jax.ShapeDtypeStruct((count, width), dtype)

    full = held(count, width)
    given = [a, g, a_turned, g_turned] + [array for array, _ in weights]
    specs = [full, full] + [held(width, count)] * 2 + [tile(first) for _, first in weights]
    scratch = [pltpu.VMEM((count, FF_TILE), jnp.bfloat16)] * 3
    if sums is not None:
        given, specs = given + list(sums), specs + [full] * 2
    if ending is not None:
        given, specs = given + list(ending), specs + [full, held(1, width)]
        outs = [shape(jnp.bfloat16), shape(jnp.bfloat16), shape(jnp.float32)]
        scratch = scratch + [pltpu.VMEM((count, width), jnp.float32)]
    else:
        outs = [shape(jnp.float32)] * 2
    hidden = tiles * FF_TILE
    return pl.pallas_call(
        functools.partial(mlp_kernel, min(512, count), sums is None, ending is not None),
        grid=(tiles,),
        in_specs=specs,
        out_specs=[full] * len(outs)
        + [pl.BlockSpec((3, half, FF_TILE), lambda j: (0, 0, j))] * 2,
        out_shape=outs + [jax.ShapeDtypeStruct((3, half, hidden), jnp.bfloat16)] * 2,
        scratch_shapes=scratch,
        compiler_params=pltpu.CompilerParams(
            dimension_semantics=("arbitrary",), vmem_limit_bytes=60 * 2**20
        ),
        cost_estimate=pl.CostEstimate(
            flops=18 * count * width * hidden,
            bytes_accessed=12 * width * hidden + 20 * count * width,
            transcendentals=count * hidden,
        ),
        name="mlp",
    )(*given)


def gain_gradient(weights, gradients, gain):
    products = jnp.sum(weights.astype(jnp.float32) * gradients, axis=1)
    return products / gain.astype(jnp.float32)


def per_device(
    shape,
    layer_input,
    segment_ids,
    gain_attn,
    w_query,
    w_key,
    w_value,
    w_out,
    gain_mlp,
    w_gate,
    w_up,
    w_down,
    grad_output,
):
    rows, shard_len, width = layer_input.shape
    count = rows * shard_len
    narrow, hidden = HEADS * FEAT, w_gate.shape[1]
    attention = Attention(rows, shard_len, width)
    groups, wide, across = attention.groups, attention.wide, attention.across
    gains = jnp.pad(jnp.stack([gain_attn, gain_mlp], axis=1), ((0, 0), (0, LANES - 2)))
    first_parts = [w_query, w_key, w_value, gains]
    homes, grouped = [], []
    for g in range(groups):
        for part, begin, size, place in (
            (w_query, 0, LANES, 0),
            (w_key, narrow, LANES, LANES),
            (w_value, 2 * narrow, wide, 2 * LANES),
        ):
            homes.append((begin + g * size, size, 0, g * across + place))
            grouped.append(part[:, g * size : (g + 1) * size])
    homes.append((groups * across, LANES, 0, groups * across))
    spare = ((0, 0), (0, -hidden % FF_TILE))
    gate_part, up_part, down_part = (
        jnp.pad(part, spare) for part in (w_gate, w_up, w_down.T)
    )
    tiles = gate_part.shape[1] // FF_TILE
    ringed = gains.shape[0] % 16 == 0
    if ringed:
        early = TwoWays(first_parts, shape, homes, [groups * across + LANES])
        rest = TwoWays([gate_part, w_out, up_part], shape)
        early.first()
        early.second()
        early.third()
        begun = [early.one.array, early.two.array]
        rest.first(*begun)
        down = Gathering(shape, down_part).along("x", False, [begun])
        early.last()
        (gathered,) = early.output(0)
    else:
        first_part = jnp.concatenate(grouped + [gains], axis=1)
        gathered, out_w, gate_w, up_w, down_w = (
            lax.all_gather(part, ("dp", "seq"), axis=0, tiled=True)
            for part in (first_part, w_out, gate_part, up_part, down_part)
        )
    qkv_w = gathered[:, : groups * across]
    gain_one = gathered[:, groups * across].astype(jnp.float32)[None, :]
    gain_two = gathered[:, groups * across + 1].astype(jnp.float32)[None, :]

    pick = picker(shape, width)
    cotangent = grad_output.reshape(count, width)
    tokens = layer_input.reshape(count, width).astype(jnp.float32)
    scale_one, normed_one = norm_forward(tokens)
    a_one = (normed_one * gain_one).astype(jnp.bfloat16)
    a_one = after(a_one, rest.held.array, down.array) if ringed else a_one
    qkv = jnp.dot(a_one, qkv_w, preferred_element_type=jnp.float32).astype(jnp.bfloat16)
    place = lax.axis_index("seq")
    own_seg = lax.dynamic_slice_in_dim(segment_ids, place * shard_len, shard_len, 1)
    seg, seg_row = own_seg.reshape(count, 1), own_seg.reshape(rows, 1, shard_len)
    reach = min(shape.seq - 1, -(-(LONGEST - 1) // shard_len))
    states = Passing(segment_ids, shard_len, reach, shape.seq)
    if ringed:
        down = down.along("y", False, [[qkv]])
        tail = attention.tail(after(qkv, down.array), seg)
        rest.second(tail)
        states.start(tail, 1)
        ring = down.ring("z")
        turn = ring.next(tail)
        top, den = attention.near(
            after(qkv, rest.one.array, rest.two.array, turn), seg, seg_row
        )
        turn = ring.next(den)
        earlier = after(states.end(den), turn)
        mixed_cat, inverse = attention.far(qkv, seg, earlier, top, den)
        turned_mixed, turned_one = turned_rows(pick, mixed_cat), turned_rows(pick, a_one)
        rest.third(turned_mixed, turned_one)
        rest.last()
        down = ring.end()
        down_ends = down.pieces("c", [(0, tiles * FF_TILE, 0, 0)])
        (out_w,) = rest.output(1)
    else:
        tail = attention.tail(qkv, seg)
        states.start(tail, 1)
        earlier = states.end()
        top, den = attention.near(qkv, seg, seg_row)
        mixed_cat, inverse = attention.far(qkv, seg, earlier, top, den)
        turned_mixed, turned_one = turned_rows(pick, mixed_cat), turned_rows(pick, a_one)
    x_two = tokens + jnp.dot(mixed_cat, out_w, preferred_element_type=jnp.float32)
    scale_two, normed_two = norm_forward(x_two)
    a_two = (normed_two * gain_two).astype(jnp.bfloat16)
    a_turned = turned_rows(pick, a_two)
    if ringed:
        gate_w, up_w = rest.output(0, 2)
        (down_w,) = assemble(down_ends, [tiles * FF_TILE], down_part.shape[0], shape)
    result, d_branch, d_x_two, kept, sent = feed_forward(
        a_two,
        cotangent,
        a_turned,
        turned_rows(pick, cotangent),
        [(gate_w, 0), (up_w, 0), (down_w, 0)],
        tiles,
        None,
        (x_two, gain_two),
    )
    half = width // 2
    d_mixed = against(d_branch, out_w).astype(jnp.bfloat16)
    ahead, d_top, d_den = attention.head(qkv, d_mixed, mixed_cat, inverse, seg)
    states.start(ahead, -1)
    own = after(d_branch, ahead) if ringed else d_branch
    out_sent, out_kept = (
        dot(t, own).astype(jnp.bfloat16) for t in (turned_mixed[half:], turned_mixed[:half])
    )
    if ringed:
        send_core = shape.lines["c"].send
        arrived, out_arrived = send_core(sent), send_core(out_sent)
        arrived = after(arrived, out_sent, out_kept)
        gate_sum, up_sum, down_sum = (Scattering(shape, kept, arrived, i) for i in range(3))
        gate_sum.beside(Scattering(shape, out_kept[None], out_arrived[None])).start("y")
        up_sum.start("x")
        down_sum.start("u")
        d_top = after(d_top, gate_sum.sent, up_sum.sent, down_sum.sent)
        d_near = attention.near_back(qkv, d_top, d_den, seg, seg_row, earlier)
        near = d_near[0]
        gate_sum.advance(near).start("x")
        up_sum.advance(near).start("y")
        down_sum.advance(near).start("w")
        later = after(states.end(near), down_sum.sent, gate_sum.sent, up_sum.sent)

        d_qkv = attention.far_back(qkv, seg, later, *d_near)
        own_sent = dot(turned_one[half:], d_qkv).astype(jnp.bfloat16)
        own_kept = dot(turned_one[:half], d_qkv).astype(jnp.bfloat16)
        both = gate_sum.advance(own_kept).beside(up_sum.advance(own_kept)).start("u")
        arrived = after(send_core(own_sent), own_kept)
        down_sum.advance(both.sent).start("x")
        arrived = after(arrived, down_sum.sent)
        qkv_a, qkv_b = (
            Scattering(shape, own_kept[None, :, low : low + across], arrived[None, :, low : low + across])
            for low in (0, across)
        )
        qkv_a.start("y")
        qkv_b.start("x")
        d_qkv = after(d_qkv, qkv_a.sent, qkv_b.sent)
        d_a_one = against(d_qkv[:, :across], qkv_w[:, :across])
        qkv_b.advance(d_a_one).start("y")
        qkv_a.advance(d_a_one).start("x")
        d_qkv = after(d_qkv, qkv_b.sent, qkv_a.sent)
        d_a_one = d_a_one + against(d_qkv[:, across:], qkv_w[:, across:])
        both.advance(d_a_one).start("w")
        down_sum.advance(both.sent).start("y")
        qkv_sum = qkv_a.advance(both.sent).beside(qkv_b.advance(both.sent)).start("u")
        down_sum.advance(both.sent)
        qkv_sum.advance().start("w")
        both.advance()
        qkv_sum.advance()
        grad_qkv = [terms[0][0][0] for terms in qkv_sum.parts]
        grad_gate, grad_out, grad_up = (terms[0][0][0] for terms in both.parts)
        grad_down = down_sum.parts[0][0][0][0][:, :hidden]
        grad_gate, grad_up = grad_gate[:, :hidden], grad_up[:, :hidden]
    else:
        later = states.end()
        d_near = attention.near_back(qkv, d_top, d_den, seg, seg_row, earlier)
        grad_gate, grad_up, grad_down = (
            scatter_whole(kept[i], sent[i])[:, :hidden] for i in range(3)
        )
        grad_out = scatter_whole(out_kept, out_sent)
        d_qkv = attention.far_back(qkv, seg, later, *d_near)
        whole = scatter_whole(dot(turned_one[:half], d_qkv), dot(turned_one[half:], d_qkv))
        grad_qkv = [whole[:, g * across : (g + 1) * across] for g in range(groups)]
        d_a_one = against(d_qkv, qkv_w)
    d_tokens = d_x_two + norm_backward(d_a_one, gain_one, scale_one, normed_one)
    return (
        result.reshape(rows, shard_len, width),
        d_tokens.reshape(rows, shard_len, width),
        gain_gradient(jnp.concatenate(grouped, axis=1), jnp.concatenate(grad_qkv, axis=1), gain_attn),
        jnp.concatenate([part[:, Q] for part in grad_qkv], axis=1),
        jnp.concatenate([part[:, K] for part in grad_qkv], axis=1),
        jnp.concatenate([part[:, V] for part in grad_qkv], axis=1),
        grad_out,
        gain_gradient(
            jnp.concatenate([w_gate, w_up], axis=1),
            jnp.concatenate([grad_gate, grad_up], axis=1),
            gain_mlp,
        ),
        grad_gate,
        grad_up,
        grad_down.T,
    )


def solution(mesh):
    placed = (
        P("dp", "seq", None),
        P("dp", None),
        P(("dp", "seq")),
        P(("dp", "seq"), None),
        P(("dp", "seq"), None),
        P(("dp", "seq"), None),
        P(("dp", "seq"), None),
        P(("dp", "seq")),
        P(("dp", "seq"), None),
        P(("dp", "seq"), None),
        P(None, ("dp", "seq")),
        P("dp", "seq", None),
    )
    return jax.shard_map(
        functools.partial(per_device, Slice(mesh.shape["dp"], mesh.shape["seq"])),
        mesh=mesh,
        in_specs=placed,
        out_specs=(
            P("dp", "seq", None),
            P("dp", "seq", None),
            P(("dp", "seq")),
            P(("dp", "seq"), None),
            P(("dp", "seq"), None),
            P(("dp", "seq"), None),
            P(("dp", "seq"), None),
            P(("dp", "seq")),
            P(("dp", "seq"), None),
            P(("dp", "seq"), None),
            P(None, ("dp", "seq")),
        ),
        check_vma=False,
    )
```
